32 devices in a mesh: dp: 16 (over z, y, core), mp: 2 (over x).
Axes of the slice: x: 2, y: 2, z: 4, core: 2. Of those that a mesh axis runs over, the one named last changes fastest.
Arguments:
- tokens: float32 [16384, 1472], P(('dp', 'mp')), may hold values from -6 to 6
- cotangent: float32 [16384, 1472], P(('dp', 'mp')), may hold values from -6 to 6
- doc_lengths: int32 [16, 4], P('dp'), may hold values from 1 to 512, 1024 in all within a row
- pad_mask: int32 [16, 1024], P('dp'), may hold values 0 or 1
- attn_gain: float32 [1472], replicated, may hold values from 0.5 to 1.5
- qkv_weight: bfloat16 [1472, 3, 384], P(None, None, 'mp'), may hold values from -0.078125 to 0.078125
- rel_table: float32 [32, 6], P(None, 'mp'), may hold values from -6 to 6
- out_weight: bfloat16 [1472, 384], P(None, 'mp'), may hold values from -0.4375 to 0.4375
- ff_gain: float32 [1472], replicated, may hold values from 0.5 to 1.5
- ff_in_weight: bfloat16 [1472, 2, 3584], P(None, None, 'mp'), may hold values from -0.15625 to 0.15625
- ff_out_weight: bfloat16 [1472, 3584], P(None, 'mp'), may hold values from -0.1875 to 0.1875
Outputs:
- result: float32 [16384, 1472], P(('dp', 'mp'))
- input_grad: float32 [16384, 1472], P(('dp', 'mp'))
- attn_gain_grad: float32 [1472], replicated
- qkv_weight_grad: float32 [1472, 3, 384], P('dp', None, 'mp')
- rel_table_grad: float32 [32, 6], replicated
- out_weight_grad: float32 [1472, 384], P('dp', 'mp')
- ff_gain_grad: float32 [1472], replicated
- ff_in_grad: float32 [1472, 2, 3584], P('dp', None, 'mp')
- ff_out_grad: float32 [1472, 3584], P('dp', 'mp')
The draws below stay inside these ranges and needn't reach their ends.
All inputs are finite; a program needn't handle non-finite values. No bound on the sum of `pad_mask` on one device may be relied on, other than what follows from the above.
Results may differ from the reference program's by a relative error of at most 0.035.
Values may be sent and summed in bfloat16 or wider, within the bound.
A program may use at most 256 MiB of HBM per device.

```python
import math
import jax
import jax.numpy as jnp
import numpy as np
from jax import lax

D = 1472
HEADS = 6
DK = 64
FF = 3584
BUCKETS = 32
MAXDIST = 128
DOCS_SEQ = 4
SEQ_LEN = 1024
SEQS = 16
TOKENS = 16384


def with_ends(values, stream_key, smallest, top_value):
    longest = values.shape.index(max(values.shape))
    spots = []
    for shift in (0, 1):
        where = [jax.random.randint(jax.random.fold_in(stream_key, axis), (), 0, length) for axis, length in enumerate(values.shape)]
        where[longest] = (where[longest] + shift) % values.shape[longest]
        spots.append(tuple(where))
    return values.at[spots[0]].set(smallest).at[spots[1]].set(top_value)


def steps_of(key, extent, split, low, largest):
    level = 1.0
    for dim, shards_of in split:
        draws = jax.random.uniform(jax.random.fold_in(jax.random.fold_in(key, 6), dim), (shards_of,), jnp.float32, low / len(split), largest / len(split))
        level = level * jnp.repeat(jnp.exp(draws), extent[dim] // shards_of).reshape((-1,) + (1,) * (len(extent) - 1 - dim))
    return level


def split_up(amount, total, bound, lean):
    weights = [(1 << 20) // math.isqrt(rank ** lean) + 1 for rank in range(2, amount + 1)]
    surplus, counts = total - bound - (amount - 1), [1] * (amount - 1)
    while surplus > 0:
        free = [i for i in range(amount - 1) if counts[i] < bound]
        pool, remaining = sum([weights[i] for i in free]), surplus
        for i in free:
            addition = min(bound - counts[i], max(1, remaining * weights[i] // pool), surplus)
            counts[i] = counts[i] + addition
            surplus = surplus - addition
    return np.array([bound] + counts)


def uneven_parts(own_key, count, total, most, skew):
    if count == 2:
        one = jax.random.randint(own_key, (), max(1, total - most), min(most, total - 1) + 1)
        return jnp.stack([one, total - one])
    sizes = jnp.asarray(split_up(count, total, most, skew), jnp.int32)
    twos = (count - 1) // 2
    source_of, receiver = sizes[1:1 + 2 * twos:2], sizes[2:2 + 2 * twos:2]
    room = jnp.minimum(source_of - 1, most - receiver)
    passed = jax.random.randint(jax.random.fold_in(own_key, 1), (twos,), 0, 1 << 20) % (room + 1)
    sizes = sizes.at[1:1 + 2 * twos:2].set(source_of - passed).at[2:2 + 2 * twos:2].set(receiver + passed)
    return sizes[jax.random.permutation(jax.random.fold_in(own_key, 2), count)]


def centred(own_key, extent, deviation, bound, cuts=(), held_as=jnp.bfloat16):
    drawn = jax.random.normal(own_key, extent, jnp.float32) * deviation
    if len(cuts) > 0:
        drawn = steps_of(own_key, extent, cuts, -0.22, 0.18) * drawn
    return jnp.clip(drawn, min=-bound, max=bound).astype(held_as)


def setup_inputs(seed: int = 0) -> dict:
    splits = jax.random.split(jax.random.key(seed), 12)
    return {
        "tokens": centred(splits[0], (TOKENS, D), 1.0, 6.0, ((0, 32),), jnp.float32),
        "cotangent": centred(splits[1], (TOKENS, D), 1.0, 6.0, ((0, 32),), jnp.float32),
        "doc_lengths": jax.vmap(lambda own: uneven_parts(own, DOCS_SEQ, SEQ_LEN, SEQ_LEN // 2, 2))(jax.random.split(splits[2], SEQS)).reshape((SEQS, DOCS_SEQ)).astype(jnp.int32),
        "pad_mask": with_ends((jax.random.randint(splits[3], (SEQS, SEQ_LEN), 0, 8) < 7).astype(jnp.int32), jax.random.fold_in(splits[3], 1), 0, 1),
        "attn_gain": jnp.clip(1.0 + 0.1 * jax.random.normal(splits[4], (D,), jnp.float32), 0.5, 1.5),
        "qkv_weight": centred(splits[5], (D, 3, HEADS * DK), (4 * D) ** -0.5, 0.078125, ((2, 2),)),
        "rel_table": centred(splits[6], (BUCKETS, HEADS), 1.0, 6.0, ((1, 2),), jnp.float32),
        "out_weight": centred(splits[7], (D, HEADS * DK), (HEADS * DK // 2) ** -0.5, 0.4375, ((1, 2),)),
        "ff_gain": jnp.clip(1.0 + 0.1 * jax.random.normal(splits[8], (D,), jnp.float32), 0.5, 1.5),
        "ff_in_weight": centred(splits[9], (D, 2, FF), D ** -0.5, 0.15625, ((2, 2),)),
        "ff_out_weight": centred(splits[10], (D, FF), (FF // 3) ** -0.5, 0.1875, ((1, 2),)),
    }


norm_eps = 1e-06
top_precision = lax.Precision.HIGHEST

@jax.custom_vjp
def low(v):
    return lax.optimization_barrier(v.astype(jnp.bfloat16)).astype(jnp.float32)

@jax.custom_vjp
def low_back(v):
    return v

def low_keep(v):
    return (low(v), None)

def low_pass(kept, grad):
    return (grad,)

def back_keep(v):
    return (v, None)

def back_low(kept, grad):
    return (low(grad),)
low.defvjp(low_keep, low_pass)
low_back.defvjp(back_keep, back_low)

def offset_buckets(length, buckets, reach):
    offsets = np.arange(-(length - 1), length)
    half_range = buckets // 2
    upper_half = (offsets > 0).astype(np.int32) * half_range
    distance = np.abs(offsets)
    exact_range = half_range // 2
    safe_dist = np.maximum(distance, 1)
    log_bucket = exact_range + (np.log(safe_dist / exact_range) / np.log(reach / exact_range) * (half_range - exact_range)).astype(np.int32)
    log_bucket = np.minimum(log_bucket, half_range - 1)
    return (upper_half + np.where(distance < exact_range, distance, log_bucket)).astype(np.int32)

def rms_scale(residual_in, gain):
    return residual_in * lax.rsqrt(lax.optimization_barrier(jnp.mean(residual_in * residual_in, axis=-1, keepdims=True)) + norm_eps) * gain

def layer(residual_in, gain_attn, qkv_full, rel_full, out_full, gain_ff, ffin_full, ffout_full, allowed, bucket_ids):
    seq_len = residual_in.shape[0]
    normed = low(rms_scale(residual_in, gain_attn))
    projected = jnp.dot(normed, qkv_full.reshape(D, 3 * HEADS * DK), precision=top_precision)
    projected = low(low_back(projected)).reshape(seq_len, 3, HEADS, DK)
    queries = projected[:, 0]
    key_rows = projected[:, 1]
    value_rows = projected[:, 2]
    bias = jnp.transpose(rel_full[bucket_ids], (2, 0, 1))
    scores = jnp.einsum('qhd,khd->hqk', queries, key_rows, precision=top_precision) + bias
    scores = low_back(scores)
    masked = jnp.where(allowed[None], scores, -1000000000.0)
    probs = jax.nn.softmax(masked, axis=-1)
    context = jnp.einsum('hqk,khd->qhd', low(probs), value_rows, precision=top_precision).reshape(seq_len, HEADS * DK)
    context = low(low_back(context))
    attn_out = low_back(jnp.dot(context, out_full.T, precision=top_precision))
    middle = residual_in + attn_out
    normed_ff = low(rms_scale(middle, gain_ff))
    gate_up = low_back(jnp.einsum('sd,dtf->stf', normed_ff, ffin_full, precision=top_precision))
    hidden = low(jax.nn.gelu(gate_up[:, 0], approximate=True) * gate_up[:, 1])
    ff_out = low_back(jnp.dot(hidden, ffout_full.T, precision=top_precision))
    return middle + ff_out

def add_pair(running, update):
    return running + update

def reference(tokens, cotangent, doc_lengths, pad_mask, attn_gain, qkv_weight, rel_table, out_weight, ff_gain, ff_in_weight, ff_out_weight):
    params = (attn_gain, qkv_weight.astype(jnp.float32), rel_table, out_weight.astype(jnp.float32), ff_gain, ff_in_weight.astype(jnp.float32), ff_out_weight.astype(jnp.float32))
    table = offset_buckets(SEQ_LEN, BUCKETS, MAXDIST)
    grid_pos = np.arange(SEQ_LEN)
    bucket_ids = jnp.asarray(table[grid_pos[None, :] - grid_pos[:, None] + SEQ_LEN - 1])
    position = jnp.arange(SEQ_LEN, dtype=jnp.int32)

    def one_sequence(totals, inputs):
        rows_in, cot_rows, lengths, valid = inputs
        bounds = jnp.cumsum(lengths)
        doc_of = lax.optimization_barrier(jnp.sum((position[:, None] >= bounds[None, :]).astype(jnp.int32), axis=1))
        allowed = (doc_of[:, None] == doc_of[None, :]) & ((valid[None, :] == 1) | (position[:, None] == position[None, :]))

        def apply(rows_arg, gain_attn, qkv_full, rel_full, out_full, gain_ff, ffin_full, ffout_full):
            return layer(rows_arg, gain_attn, qkv_full, rel_full, out_full, gain_ff, ffin_full, ffout_full, allowed, bucket_ids)
        output, pullback = jax.vjp(apply, rows_in, params[0], params[1], params[2], params[3], params[4], params[5], params[6])
        grads = pullback(cot_rows)
        new_totals = jax.tree.map(add_pair, totals, tuple(grads[1:]))
        return (new_totals, (output, grads[0]))
    zero_totals = jax.tree.map(jnp.zeros_like, params)
    totals, (outputs, input_grads) = lax.scan(one_sequence, zero_totals, (tokens.reshape(SEQS, SEQ_LEN, D), cotangent.reshape(SEQS, SEQ_LEN, D), doc_lengths, pad_mask))
    return (outputs.reshape(TOKENS, D), input_grads.reshape(TOKENS, D), totals[0], totals[1], totals[2], totals[3], totals[4], totals[5], totals[6])
```

```python
import functools

import jax
import jax.numpy as jnp
import numpy as np
from jax import lax
from jax.experimental import pallas as pl
from jax.experimental.pallas import tpu as pltpu
from jax.sharding import PartitionSpec as P

MAXDIST = 128
norm_eps = 1e-06
BLK = 256
SPAN = 6 * BLK
REACH = 2
BF = jnp.bfloat16
F32 = jnp.float32
VMEM_LIMIT = 56 << 20


def bucket_of(offsets, buckets, reach):
    half_range = buckets // 2
    upper_half = (offsets > 0).astype(np.int32) * half_range
    distance = np.abs(offsets)
    exact_range = half_range // 2
    safe_dist = np.maximum(distance, 1)
    log_bucket = exact_range + (
        np.log(safe_dist / exact_range) / np.log(reach / exact_range) * (half_range - exact_range)
    ).astype(np.int32)
    log_bucket = np.minimum(log_bucket, half_range - 1)
    return (upper_half + np.where(distance < exact_range, distance, log_bucket)).astype(np.int32)


def lane_buckets(buckets):
    lanes = np.arange(SPAN)
    shifted = np.where(lanes < 5 * BLK, lanes, lanes - SPAN)
    return bucket_of(REACH * BLK - shifted, buckets, MAXDIST).reshape(1, SPAN)


def dot(a, b, contract):
    return lax.dot_general(a, b, (contract, ((), ())), preferred_element_type=F32)


def diagonal_of(key_block, query_block, x, blocks):
    half = blocks // 2
    key_true = lax.rem(key_block + half * x, blocks)
    query_true = lax.rem(query_block + half * x, blocks)
    return jnp.clip(key_true - query_true, -REACH, REACH) + REACH


def attn_fwd_kernel(
    heads, dk, buckets, blocks,
    x_ref, rel_ref, bid_ref, doc_ref, code_ref, q_ref, k_ref, v_ref,
    e_ref, inv_ref, ctx_ref,
    table, vt, mask, score, acc,
):
    qb, h = pl.program_id(0), pl.program_id(1)
    x = x_ref[0]

    @pl.when((qb == 0) & (h == 0))
    def _():
        vt[...] = v_ref[...].astype(F32).T.astype(BF)
        ids = bid_ref[...]
        for hh in range(heads):
            line = jnp.zeros((1, SPAN), F32)
            for b in range(buckets):
                line = jnp.where(ids == b, rel_ref[b, hh], line)
            rows = pltpu.roll(
                jnp.broadcast_to(line, (BLK, SPAN)), 0, 1, stride=1, stride_axis=0
            )
            for d in range(5):
                table[hh, d] = rows[:, BLK * (4 - d) : BLK * (5 - d)]

    @pl.when(h == 0)
    def _():
        row = lax.broadcasted_iota(jnp.int32, (BLK, BLK), 0)
        col = lax.broadcasted_iota(jnp.int32, (BLK, BLK), 1)
        for kb in range(blocks):
            same = code_ref[kb * BLK : (kb + 1) * BLK, :] == doc_ref[...]
            diag = (row + kb * BLK) == (col + qb * BLK)
            mask[kb * BLK : (kb + 1) * BLK, :] = jnp.where(same | diag, 0.0, -1000000000.0)

    lane = lax.broadcasted_iota(jnp.int32, q_ref.shape, 1)
    qm = jnp.where(lane // dk == h, q_ref[...], jnp.zeros_like(q_ref[...]))
    peak = None
    for kb in range(blocks):
        rows = slice(kb * BLK, (kb + 1) * BLK)
        s = dot(k_ref[rows, :], qm, ((1,), (1,)))
        s = s + table[h, diagonal_of(kb, qb, x, blocks)] + mask[rows, :]
        score[rows, :] = s
        top = jnp.max(s, axis=0, keepdims=True)
        peak = top if peak is None else jnp.maximum(peak, top)
    total = jnp.zeros((1, BLK), F32)
    ctx = jnp.zeros((dk, BLK), F32)
    hrows = pl.ds(pl.multiple_of(h * dk, dk), dk)
    for kb in range(blocks):
        rows = slice(kb * BLK, (kb + 1) * BLK)
        e = jnp.exp(score[rows, :] - peak)
        total = total + jnp.sum(e, axis=0, keepdims=True)
        e_low = e.astype(BF)
        e_ref[0, 0, rows, :] = e_low
        ctx = ctx + dot(vt[hrows, rows], e_low, ((1,), (0,)))
    inv = 1.0 / total
    inv_ref[0, 0] = inv
    acc[hrows, :] = ctx * inv

    @pl.when(h == heads - 1)
    def _():
        ctx_ref[...] = acc[...].T.astype(BF)


def attn_fwd(x, rel, doc, code, q, k, v, heads, dk):
    seq, cols = q.shape
    blocks = seq // BLK
    buckets = rel.shape[0]
    bids = jnp.asarray(lane_buckets(buckets))
    whole = lambda i, h: (0, 0)
    return pl.pallas_call(
        functools.partial(attn_fwd_kernel, heads, dk, buckets, blocks),
        grid=(blocks, heads),
        in_specs=[
            pl.BlockSpec(memory_space=pltpu.SMEM),
            pl.BlockSpec(memory_space=pltpu.SMEM),
            pl.BlockSpec((1, SPAN), whole),
            pl.BlockSpec((1, BLK), lambda i, h: (0, i)),
            pl.BlockSpec((seq, 1), whole),
            pl.BlockSpec((BLK, cols), lambda i, h: (i, 0)),
            pl.BlockSpec((seq, cols), whole),
            pl.BlockSpec((seq, cols), whole),
        ],
        out_specs=[
            pl.BlockSpec((1, 1, seq, BLK), lambda i, h: (h, i, 0, 0)),
            pl.BlockSpec((1, 1, 1, BLK), lambda i, h: (h, i, 0, 0)),
            pl.BlockSpec((BLK, cols), lambda i, h: (i, 0)),
        ],
        out_shape=[
            jax.ShapeDtypeStruct((heads, blocks, seq, BLK), BF),
            jax.ShapeDtypeStruct((heads, blocks, 1, BLK), F32),
            jax.ShapeDtypeStruct((seq, cols), BF),
        ],
        scratch_shapes=[
            pltpu.VMEM((heads, 5, BLK, BLK), F32),
            pltpu.VMEM((cols, seq), BF),
            pltpu.VMEM((seq, BLK), F32),
            pltpu.VMEM((seq, BLK), F32),
            pltpu.VMEM((cols, BLK), F32),
        ],
        compiler_params=pltpu.CompilerParams(vmem_limit_bytes=VMEM_LIMIT),
        cost_estimate=pl.CostEstimate(
            flops=16 * heads * seq * seq * dk,
            bytes_accessed=2 * heads * seq * seq + 8 * seq * cols,
            transcendentals=heads * seq * seq,
        ),
    )(x, rel, bids, doc, code, q, k, v)


def attn_bwd_kernel(
    heads, dk, buckets, blocks,
    x_ref, bid_ref, q_ref, k_ref, v_ref, dc_ref, e_ref, inv_ref,
    dq_ref, dk_ref, dv_ref, rel_ref,
    kt, dct, dp, dka, dva, dqa, tally,
):
    qb, h = pl.program_id(0), pl.program_id(1)
    x = x_ref[0]

    @pl.when((qb == 0) & (h == 0))
    def _():
        kt[...] = k_ref[...].astype(F32).T.astype(BF)
        dka[...] = jnp.zeros_like(dka)
        dva[...] = jnp.zeros_like(dva)
        tally[...] = jnp.zeros_like(tally)

    @pl.when(h == 0)
    def _():
        dct[...] = dc_ref[...].astype(F32).T

    lane = lax.broadcasted_iota(jnp.int32, q_ref.shape, 1)
    qm = jnp.where(lane // dk == h, q_ref[...], jnp.zeros_like(q_ref[...]))
    row = lax.broadcasted_iota(jnp.int32, dct.shape, 0)
    inv = inv_ref[0, 0]
    ds_t = jnp.where(row // dk == h, dct[...] * inv, 0.0)
    scaled_t = ds_t.astype(BF)
    scaled = ds_t.T.astype(BF)
    inner = jnp.zeros((1, BLK), F32)
    for kb in range(blocks):
        rows = slice(kb * BLK, (kb + 1) * BLK)
        g = dot(v_ref[rows, :], scaled_t, ((1,), (0,)))
        dp[rows, :] = g
        inner = inner + jnp.sum(e_ref[0, 0, rows, :].astype(F32) * g, axis=0, keepdims=True)
    inner = inner * inv
    hrows = pl.ds(pl.multiple_of(h * dk, dk), dk)
    dq = jnp.zeros((dk, BLK), F32)
    for kb in range(blocks):
        rows = slice(kb * BLK, (kb + 1) * BLK)
        e = e_ref[0, 0, rows, :]
        ds = (e.astype(F32) * (dp[rows, :] - inner)).astype(BF)
        dka[rows, :] += dot(ds, qm, ((1,), (0,)))
        dva[rows, :] += dot(e, scaled, ((1,), (0,)))
        dq = dq + dot(kt[hrows, rows], ds, ((1,), (0,)))
        tally[h, diagonal_of(kb, qb, x, blocks)] += ds.astype(F32)
    dqa[hrows, :] = dq

    @pl.when(h == heads - 1)
    def _():
        dq_ref[...] = dqa[...].T.astype(BF)

    @pl.when((h == heads - 1) & (qb == blocks - 1))
    def _():
        dk_ref[...] = dka[...].astype(BF)
        dv_ref[...] = dva[...].astype(BF)
        ids = bid_ref[...]
        hot = ids == lax.broadcasted_iota(jnp.int32, (buckets, SPAN), 0)
        out_lane = lax.broadcasted_iota(jnp.int32, rel_ref.shape, 1)
        sub = lax.broadcasted_iota(jnp.int32, (8, SPAN), 0)
        out = jnp.zeros(rel_ref.shape, F32)
        for hh in range(heads):
            line = jnp.zeros((8, SPAN), F32)
            for a in range(BLK // 8):
                group = slice(8 * a, 8 * a + 8)
                parts = [tally[hh, d, group, :] for d in (4, 3, 2, 1, 0)]
                strip = jnp.concatenate(parts + [jnp.zeros((8, BLK), F32)], axis=1)
                line = line + (strip if a == 0 else pltpu.roll(strip, SPAN - 8 * a, 1))
            for bit in (1, 2, 4):
                line = jnp.where((sub & bit) != 0, pltpu.roll(line, SPAN - bit, 1), line)
            sums = jnp.sum(line, axis=0, keepdims=True)
            col = jnp.sum(jnp.where(hot, sums, 0.0), axis=1, keepdims=True)
            out = jnp.where(out_lane == hh, col, out)
        rel_ref[...] = out


def attn_bwd(x, q, k, v, dctx, e, inv, buckets, heads, dk):
    seq, cols = q.shape
    blocks = seq // BLK
    bids = jnp.asarray(lane_buckets(buckets))
    whole = lambda i, h: (0, 0)
    return pl.pallas_call(
        functools.partial(attn_bwd_kernel, heads, dk, buckets, blocks),
        grid=(blocks, heads),
        in_specs=[
            pl.BlockSpec(memory_space=pltpu.SMEM),
            pl.BlockSpec((1, SPAN), whole),
            pl.BlockSpec((BLK, cols), lambda i, h: (i, 0)),
            pl.BlockSpec((seq, cols), whole),
            pl.BlockSpec((seq, cols), whole),
            pl.BlockSpec((BLK, cols), lambda i, h: (i, 0)),
            pl.BlockSpec((1, 1, seq, BLK), lambda i, h: (h, i, 0, 0)),
            pl.BlockSpec((1, 1, 1, BLK), lambda i, h: (h, i, 0, 0)),
        ],
        out_specs=[
            pl.BlockSpec((BLK, cols), lambda i, h: (i, 0)),
            pl.BlockSpec((seq, cols), whole),
            pl.BlockSpec((seq, cols), whole),
            pl.BlockSpec((buckets, 128), whole),
        ],
        out_shape=[
            jax.ShapeDtypeStruct((seq, cols), BF),
            jax.ShapeDtypeStruct((seq, cols), BF),
            jax.ShapeDtypeStruct((seq, cols), BF),
            jax.ShapeDtypeStruct((buckets, 128), F32),
        ],
        scratch_shapes=[
            pltpu.VMEM((cols, seq), BF),
            pltpu.VMEM((cols, BLK), F32),
            pltpu.VMEM((seq, BLK), F32),
            pltpu.VMEM((seq, cols), F32),
            pltpu.VMEM((seq, cols), F32),
            pltpu.VMEM((cols, BLK), F32),
            pltpu.VMEM((heads, 5, BLK, BLK), F32),
        ],
        compiler_params=pltpu.CompilerParams(vmem_limit_bytes=VMEM_LIMIT),
        cost_estimate=pl.CostEstimate(
            flops=32 * heads * seq * seq * dk,
            bytes_accessed=2 * heads * seq * seq + 14 * seq * cols,
            transcendentals=0,
        ),
    )(x, bids, q, k, v, dctx, e, inv)


def ff_kernel(steps, aliased, *refs):
    if aliased:
        refs = refs[:5] + refs[7:]
    x_ref, c_ref, wg_ref, wu_ref, wo_ref, hid_ref, dgu_ref, out_ref, din_ref, out_acc, din_acc = refs
    j = pl.program_id(0)
    gate = dot(x_ref[...], wg_ref[...], ((1,), (0,)))
    up = dot(x_ref[...], wu_ref[...], ((1,), (0,)))
    dh = dot(c_ref[...], wo_ref[...], ((1,), (0,)))
    scale = np.float32(np.sqrt(2 / np.pi))
    sq = gate * gate
    t = jnp.tanh(scale * gate * (1.0 + 0.044715 * sq))
    half = 0.5 * (1.0 + t)
    act = gate * half
    slope = half + 0.5 * gate * (1.0 - t * t) * (scale * (1.0 + (3 * 0.044715) * sq))
    hid = (act * up).astype(BF)
    dg = (dh * up * slope).astype(BF)
    du = (dh * act).astype(BF)
    hid_ref[...] = hid
    dgu_ref[0] = dg
    dgu_ref[1] = du
    out = dot(hid, wo_ref[...], ((1,), (1,)))
    din = dot(dg, wg_ref[...], ((1,), (1,))) + dot(du, wu_ref[...], ((1,), (1,)))

    @pl.when(j == 0)
    def _():
        out_acc[...] = out
        din_acc[...] = din

    @pl.when(j > 0)
    def _():
        out_acc[...] += out
        din_acc[...] += din

    @pl.when(j == steps - 1)
    def _():
        out_ref[...] = out_acc[...].astype(out_ref.dtype)
        din_ref[...] = din_acc[...].astype(din_ref.dtype)


def ff_part(part, total, x, c, w2, wo, carried, sum_dtype):
    rows, d = x.shape
    f = wo.shape[1]
    steps = f // BLK
    whole = lambda j: (0, 0)
    in_specs = [
        pl.BlockSpec((rows, d), whole),
        pl.BlockSpec((rows, d), whole),
        pl.BlockSpec((None, d, BLK), lambda j: (0, 0, j)),
        pl.BlockSpec((None, d, BLK), lambda j: (1, 0, j)),
        pl.BlockSpec((d, BLK), lambda j: (0, j)),
    ]
    args = [x, c, w2, w2, wo]
    aliases = {}
    if carried is not None:
        in_specs += [pl.BlockSpec(memory_space=pl.ANY)] * 2
        args += list(carried)
        aliases = {5: 0, 6: 1}
    return pl.pallas_call(
        functools.partial(ff_kernel, steps, carried is not None),
        grid=(steps,),
        in_specs=in_specs,
        out_specs=[
            pl.BlockSpec((rows, BLK), lambda j: (part, j)),
            pl.BlockSpec((2, rows, BLK), lambda j: (0, part, j)),
            pl.BlockSpec((rows, d), whole),
            pl.BlockSpec((rows, d), whole),
        ],
        out_shape=[
            jax.ShapeDtypeStruct((total, f), BF),
            jax.ShapeDtypeStruct((2, total, f), BF),
            jax.ShapeDtypeStruct((rows, d), sum_dtype),
            jax.ShapeDtypeStruct((rows, d), sum_dtype),
        ],
        scratch_shapes=[pltpu.VMEM((rows, d), F32), pltpu.VMEM((rows, d), F32)],
        input_output_aliases=aliases,
        compiler_params=pltpu.CompilerParams(vmem_limit_bytes=VMEM_LIMIT),
        cost_estimate=pl.CostEstimate(
            flops=12 * rows * d * f,
            bytes_accessed=6 * d * f + 6 * rows * f + 12 * rows * d,
            transcendentals=rows * f,
        ),
    )(*args)


def rms_scale(v, gain):
    return v * lax.rsqrt(jnp.mean(v * v, axis=-1, keepdims=True) + norm_eps) * gain


def rms_back(v, gain, c):
    r = lax.rsqrt(jnp.mean(v * v, axis=-1, keepdims=True) + norm_eps)
    n = v * r
    cg = c * gain
    return r * (cg - n * jnp.mean(cg * n, axis=-1, keepdims=True)), c * n


def halving_masks(n):
    bits = n.bit_length() - 1
    if n == 16:
        return [1, 2, 4, 12]
    return [1 << b for b in range(bits)]


def coordinates(me, masks):
    k = len(masks)
    combos = {}
    for value in range(1 << k):
        d = 0
        for i in range(k):
            if value >> i & 1:
                d ^= masks[i]
        combos[d] = value
    coords = []
    for i in range(k):
        bits = [b for b in range(k) if combos[1 << b] >> i & 1]
        total = me & 0
        for b in bits:
            total = total ^ ((me >> b) & 1)
        coords.append(total)
    order = []
    for flat in range(1 << k):
        d = 0
        for i in range(k):
            if flat >> (k - 1 - i) & 1:
                d ^= masks[i]
        order.append(d)
    return coords, order


def take(array, index):
    return lax.dynamic_index_in_dim(array, index, 0, keepdims=False)


def per_device(
    tokens,
    cotangent,
    doc_lengths,
    pad_mask,
    attn_gain,
    qkv_weight,
    rel_table,
    out_weight,
    ff_gain,
    ff_in_weight,
    ff_out_weight,
):
    rows, d = tokens.shape
    n_dp = lax.axis_size("dp")
    n_mp = lax.axis_size("mp")
    seq = rows * n_mp
    cols = qkv_weight.shape[2]
    buckets, heads = rel_table.shape
    dk = cols // heads
    x = lax.axis_index("mp")
    me = lax.axis_index("dp")
    xs = x.astype(jnp.int32).reshape(1)
    masks = halving_masks(n_dp)
    coords, order = coordinates(me, masks)
    shard = d // n_dp
    shard_pad = -(-shard // 16) * 16

    def swap(v):
        return lax.ppermute(v, "mp", [(0, 1), (1, 0)])

    def hop(v, mask):
        return lax.ppermute(v, "dp", [(i, i ^ mask) for i in range(n_dp)])

    def after(v, *first):
        return lax.optimization_barrier((v,) + first)[0]

    def by_dest(a):
        r = a.shape[0]
        t = a.T.reshape(n_dp, shard, r)
        t = jnp.concatenate([t[o : o + 1] for o in order], axis=0)
        t = jnp.pad(t, ((0, 0), (0, shard_pad - shard), (0, 0)))
        t = t.reshape(2, n_dp // 2 * shard_pad, r)
        return take(t, 1 - coords[0]), take(t, coords[0])

    def halve(send, keep):
        width = send.shape[-1]
        shape = (2,) * (len(masks) - 1) + (shard_pad, width)
        parts = [keep.reshape(shape), hop(send, masks[0]).reshape(shape)]
        for i in range(1, len(masks)):
            away = sum(take(p, 1 - coords[i]).astype(F32) for p in parts).astype(BF)
            parts = [take(p, coords[i]) for p in parts]
            parts.append(hop(away, masks[i]))
        return sum(p.astype(F32) for p in parts)[:shard]

    tok_low = tokens.astype(BF)
    tok_far = swap(tok_low)
    w_out_far = swap(after(out_weight, tok_far))
    out_low = cotangent.astype(BF)
    cot_far = swap(after(out_low, tok_far))
    w2 = jnp.transpose(ff_in_weight, (1, 0, 2))
    wq, wk, wv = (qkv_weight[:, i, :] for i in range(3))

    bounds = jnp.cumsum(doc_lengths[0])
    position = lax.rem(jnp.arange(seq, dtype=jnp.int32) + rows * x, seq)
    doc_of = jnp.sum((position[:, None] >= bounds[None, :]).astype(jnp.int32), axis=1)
    valid = jnp.concatenate(
        [lax.dynamic_slice(pad_mask[0], (rows * x,), (rows,)),
         lax.dynamic_slice(pad_mask[0], (rows * (1 - x),), (rows,))]
    )
    code = jnp.where(valid == 1, doc_of, -1).reshape(seq, 1)
    doc_row = doc_of.reshape(1, seq)

    far = tok_far.astype(F32)
    normed = jnp.concatenate(
        [rms_scale(tokens, attn_gain).astype(BF), rms_scale(far, attn_gain).astype(BF)], axis=0
    )

    def project(w):
        return jnp.dot(normed, w, preferred_element_type=F32).astype(BF)

    q, k, v = project(wq), project(wk), project(wv)
    e, inv, ctx = attn_fwd(xs, rel_table, doc_row, code, q, k, v, heads, dk)
    ctx_far = swap(ctx)
    ctx_far = jnp.concatenate([ctx_far[rows:], ctx_far[:rows]], axis=0)

    def out_proj(r):
        return jnp.einsum("sc,dc->sd", ctx[r], out_weight, preferred_element_type=F32) + jnp.einsum(
            "sc,dc->sd", ctx_far[r], w_out_far, preferred_element_type=F32
        )

    middle = tokens + out_proj(slice(0, rows))
    near_ff = rms_scale(middle, ff_gain).astype(BF)
    far_ff = rms_scale(far + out_proj(slice(rows, seq)), ff_gain).astype(BF)

    hid, dgu, out_near, din_near = ff_part(0, seq, near_ff, out_low, w2, ff_out_weight, None, F32)
    hid, dgu, out_far, din_far = ff_part(
        1, seq, far_ff, cot_far, w2, ff_out_weight, (hid, dgu), BF
    )
    din_back = swap(din_far)
    out_back = swap(after(out_far, din_back))

    c_send, c_keep = by_dest(jnp.concatenate([out_low, cot_far], axis=0))
    f_send, f_keep = by_dest(jnp.concatenate([near_ff, far_ff], axis=0))

    def grad_pair(send, keep, g):
        return (
            jnp.dot(send, g, preferred_element_type=F32).astype(BF),
            jnp.dot(keep, g, preferred_element_type=F32).astype(BF),
        )

    ffo = halve(*grad_pair(c_send, c_keep, hid))
    ffg = halve(*grad_pair(f_send, f_keep, dgu[0]))
    ffu = halve(*grad_pair(f_send, f_keep, dgu[1]))
    ffi = jnp.stack([ffg, ffu], axis=1)

    result = middle + out_near + out_back.astype(F32)
    grad_mid, gain_rows = rms_back(middle, ff_gain, din_near + din_back.astype(F32))
    ff_gain_part = jnp.sum(gain_rows, axis=0)
    grad_middle = cotangent + grad_mid
    attn_low = grad_middle.astype(BF)
    dctx_near = jnp.dot(attn_low, out_weight, preferred_element_type=F32).astype(BF)
    dctx_far = swap(jnp.dot(attn_low, w_out_far, preferred_element_type=F32).astype(BF))
    dctx = jnp.concatenate([dctx_near, dctx_far], axis=0)
    dq, dkk, dv, rel_part = attn_bwd(xs, q, k, v, dctx, e, inv, buckets, heads, dk)

    a_send, a_keep = by_dest(attn_low)
    out_near_ctx, out_far_ctx = ctx[:rows], ctx_far[:rows]
    o_keep = [jnp.dot(a_keep, c, preferred_element_type=F32) for c in (out_near_ctx, out_far_ctx)]
    o_send = jnp.concatenate(
        [jnp.dot(a_send, c, preferred_element_type=F32).astype(BF) for c in (out_near_ctx, out_far_ctx)],
        axis=1,
    )
    o_back = hop(o_send, masks[0]).astype(F32)
    o_near = o_keep[0] + o_back[:, :cols]
    o_far = swap((o_keep[1] + o_back[:, cols:]).astype(BF))
    o_half = o_near + o_far.astype(F32)

    n_send, n_keep = by_dest(normed)
    dproj = jnp.concatenate([dq, dkk, dv], axis=1)
    qkv_send = jnp.dot(n_send, dproj, preferred_element_type=F32)
    qkv_keep = jnp.dot(n_keep, dproj, preferred_element_type=F32)

    w_flat = jnp.concatenate([wq, wk, wv], axis=1)
    dn_near = jnp.einsum("sc,dc->sd", dproj[:rows], w_flat, preferred_element_type=F32)
    dn_far = jnp.einsum("sc,dc->sd", dproj[rows:], w_flat, preferred_element_type=F32).astype(BF)
    dn = dn_near + swap(dn_far).astype(F32)
    grad_tok, attn_gain_rows = rms_back(tokens, attn_gain, dn)
    input_grad = grad_middle + grad_tok
    attn_gain_part = jnp.sum(attn_gain_rows, axis=0)

    shape = (2,) * (len(masks) - 1) + (shard_pad, 4 * cols)
    recv = hop(qkv_send.astype(BF), masks[0]).astype(F32)
    both = jnp.concatenate([qkv_keep + recv, o_half], axis=1).reshape(shape)
    parts = [both]
    for i in range(1, len(masks)):
        away = sum(take(p, 1 - coords[i]).astype(F32) for p in parts).astype(BF)
        parts = [take(p, coords[i]) for p in parts]
        parts.append(hop(away, masks[i]))
    last = sum(p.astype(F32) for p in parts)[:shard]
    grad_qkv = last[:, : 3 * cols].reshape(shard, 3, cols)
    grad_out = last[:, 3 * cols :]

    rel_all = jnp.zeros((buckets, heads * n_mp), F32)
    rel_all = lax.dynamic_update_slice(
        rel_all, rel_part[:, :heads], (jnp.int32(0), x.astype(jnp.int32) * heads)
    )
    small = jnp.concatenate([attn_gain_part, ff_gain_part, rel_all.reshape(-1)])
    pad = -small.shape[0] % 128
    small = jnp.pad(small, (0, pad)).reshape(-1, 128)
    small = small + swap(small)
    for mask in masks:
        small = small + hop(small, mask)
    small = small.reshape(-1)
    return (
        result,
        input_grad,
        small[:d],
        grad_qkv,
        small[2 * d : 2 * d + rel_all.size].reshape(rel_all.shape),
        grad_out,
        small[d : 2 * d],
        ffi,
        ffo,
    )


def solution(mesh):
    return jax.shard_map(
        per_device,
        mesh=mesh,
        in_specs=(
            P(("dp", "mp"), None),
            P(("dp", "mp"), None),
            P("dp", None),
            P("dp", None),
            P(),
            P(None, None, "mp"),
            P(None, "mp"),
            P(None, "mp"),
            P(),
            P(None, None, "mp"),
            P(None, "mp"),
        ),
        out_specs=(
            P(("dp", "mp"), None),
            P(("dp", "mp"), None),
            P(),
            P("dp", None, "mp"),
            P(),
            P("dp", "mp"),
            P(),
            P("dp", None, "mp"),
            P("dp", "mp"),
        ),
        check_vma=False,
    )
```

```python
import functools

import jax
import jax.numpy as jnp
import numpy as np
from jax import lax
from jax.experimental import pallas as pl
from jax.experimental.pallas import tpu as pltpu
from jax.sharding import PartitionSpec as P

MAXDIST = 128
norm_eps = 1e-06
BLK = 256
SPAN = 6 * BLK
REACH = 2
BF = jnp.bfloat16
F32 = jnp.float32
VMEM_LIMIT = 56 << 20
FF_VMEM = 63 << 20


def bucket_of(offsets, buckets, reach):
    half_range = buckets // 2
    upper_half = (offsets > 0).astype(np.int32) * half_range
    distance = np.abs(offsets)
    exact_range = half_range // 2
    safe_dist = np.maximum(distance, 1)
    log_bucket = exact_range + (
        np.log(safe_dist / exact_range) / np.log(reach / exact_range) * (half_range - exact_range)
    ).astype(np.int32)
    log_bucket = np.minimum(log_bucket, half_range - 1)
    return (upper_half + np.where(distance < exact_range, distance, log_bucket)).astype(np.int32)


def lane_buckets(buckets):
    lanes = np.arange(SPAN)
    shifted = np.where(lanes < 5 * BLK, lanes, lanes - SPAN)
    return bucket_of(REACH * BLK - shifted, buckets, MAXDIST).reshape(1, SPAN)


def dot(a, b, contract):
    return lax.dot_general(a, b, (contract, ((), ())), preferred_element_type=F32)


def diagonal_of(key_block, query_block, x, blocks):
    half = blocks // 2
    key_true = lax.rem(key_block + half * x, blocks)
    query_true = lax.rem(query_block + half * x, blocks)
    return jnp.clip(key_true - query_true, -REACH, REACH) + REACH


def attn_fwd_kernel(
    heads, dk, buckets, blocks,
    x_ref, rel_ref, bid_ref, doc_ref, code_ref, q_ref, k_ref, v_ref,
    e_ref, inv_ref, ctx_ref,
    table, vt, mask, score, acc,
):
    qb, h = pl.program_id(0), pl.program_id(1)
    x = x_ref[0]

    @pl.when((qb == 0) & (h == 0))
    def _():
        vt[...] = v_ref[...].astype(F32).T.astype(BF)
        ids = bid_ref[...]
        for hh in range(heads):
            line = jnp.zeros((1, SPAN), F32)
            for b in range(buckets):
                line = jnp.where(ids == b, rel_ref[b, hh], line)
            rows = pltpu.roll(
                jnp.broadcast_to(line, (BLK, SPAN)), 0, 1, stride=1, stride_axis=0
            )
            for d in range(5):
                table[hh, d] = rows[:, BLK * (4 - d) : BLK * (5 - d)]

    @pl.when(h == 0)
    def _():
        row = lax.broadcasted_iota(jnp.int32, (BLK, BLK), 0)
        col = lax.broadcasted_iota(jnp.int32, (BLK, BLK), 1)
        for kb in range(blocks):
            same = code_ref[kb * BLK : (kb + 1) * BLK, :] == doc_ref[...]
            diag = (row + kb * BLK) == (col + qb * BLK)
            mask[kb * BLK : (kb + 1) * BLK, :] = jnp.where(same | diag, 0.0, -1000000000.0)

    lane = lax.broadcasted_iota(jnp.int32, q_ref.shape, 1)
    qm = jnp.where(lane // dk == h, q_ref[...], jnp.zeros_like(q_ref[...]))
    peak = None
    for kb in range(blocks):
        rows = slice(kb * BLK, (kb + 1) * BLK)
        s = dot(k_ref[rows, :], qm, ((1,), (1,)))
        s = s + table[h, diagonal_of(kb, qb, x, blocks)] + mask[rows, :]
        score[rows, :] = s
        top = jnp.max(s, axis=0, keepdims=True)
        peak = top if peak is None else jnp.maximum(peak, top)
    total = jnp.zeros((1, BLK), F32)
    ctx = jnp.zeros((dk, BLK), F32)
    hrows = pl.ds(pl.multiple_of(h * dk, dk), dk)
    for kb in range(blocks):
        rows = slice(kb * BLK, (kb + 1) * BLK)
        e = jnp.exp(score[rows, :] - peak)
        total = total + jnp.sum(e, axis=0, keepdims=True)
        e_low = e.astype(BF)
        e_ref[0, 0, rows, :] = e_low
        ctx = ctx + dot(vt[hrows, rows], e_low, ((1,), (0,)))
    inv = 1.0 / total
    inv_ref[0, 0] = inv
    acc[hrows, :] = ctx * inv

    @pl.when(h == heads - 1)
    def _():
        ctx_ref[...] = acc[...].T.astype(BF)


def attn_fwd(x, rel, doc, code, q, k, v, heads, dk):
    seq, cols = q.shape
    blocks = seq // BLK
    buckets = rel.shape[0]
    bids = jnp.asarray(lane_buckets(buckets))
    whole = lambda i, h: (0, 0)
    return pl.pallas_call(
        functools.partial(attn_fwd_kernel, heads, dk, buckets, blocks),
        grid=(blocks, heads),
        in_specs=[
            pl.BlockSpec(memory_space=pltpu.SMEM),
            pl.BlockSpec(memory_space=pltpu.SMEM),
            pl.BlockSpec((1, SPAN), whole),
            pl.BlockSpec((1, BLK), lambda i, h: (0, i)),
            pl.BlockSpec((seq, 1), whole),
            pl.BlockSpec((BLK, cols), lambda i, h: (i, 0)),
            pl.BlockSpec((seq, cols), whole),
            pl.BlockSpec((seq, cols), whole),
        ],
        out_specs=[
            pl.BlockSpec((1, 1, seq, BLK), lambda i, h: (h, i, 0, 0)),
            pl.BlockSpec((1, 1, 1, BLK), lambda i, h: (h, i, 0, 0)),
            pl.BlockSpec((BLK, cols), lambda i, h: (i, 0)),
        ],
        out_shape=[
            jax.ShapeDtypeStruct((heads, blocks, seq, BLK), BF),
            jax.ShapeDtypeStruct((heads, blocks, 1, BLK), F32),
            jax.ShapeDtypeStruct((seq, cols), BF),
        ],
        scratch_shapes=[
            pltpu.VMEM((heads, 5, BLK, BLK), F32),
            pltpu.VMEM((cols, seq), BF),
            pltpu.VMEM((seq, BLK), F32),
            pltpu.VMEM((seq, BLK), F32),
            pltpu.VMEM((cols, BLK), F32),
        ],
        compiler_params=pltpu.CompilerParams(vmem_limit_bytes=VMEM_LIMIT),
        cost_estimate=pl.CostEstimate(
            flops=16 * heads * seq * seq * dk,
            bytes_accessed=2 * heads * seq * seq + 8 * seq * cols,
            transcendentals=heads * seq * seq,
        ),
    )(x, rel, bids, doc, code, q, k, v)


def attn_bwd_kernel(
    heads, dk, buckets, blocks,
    x_ref, bid_ref, q_ref, k_ref, v_ref, dc_ref, e_ref, inv_ref,
    dq_ref, dk_ref, dv_ref, rel_ref,
    kt, dct, dp, dka, dva, dqa, tally,
):
    qb, h = pl.program_id(0), pl.program_id(1)
    x = x_ref[0]

    @pl.when((qb == 0) & (h == 0))
    def _():
        kt[...] = k_ref[...].astype(F32).T.astype(BF)
        dka[...] = jnp.zeros_like(dka)
        dva[...] = jnp.zeros_like(dva)
        tally[...] = jnp.zeros_like(tally)

    @pl.when(h == 0)
    def _():
        dct[...] = dc_ref[...].astype(F32).T

    lane = lax.broadcasted_iota(jnp.int32, q_ref.shape, 1)
    qm = jnp.where(lane // dk == h, q_ref[...], jnp.zeros_like(q_ref[...]))
    row = lax.broadcasted_iota(jnp.int32, dct.shape, 0)
    inv = inv_ref[0, 0]
    ds_t = jnp.where(row // dk == h, dct[...] * inv, 0.0)
    scaled_t = ds_t.astype(BF)
    scaled = ds_t.T.astype(BF)
    inner = jnp.zeros((1, BLK), F32)
    for kb in range(blocks):
        rows = slice(kb * BLK, (kb + 1) * BLK)
        g = dot(v_ref[rows, :], scaled_t, ((1,), (0,)))
        dp[rows, :] = g
        inner = inner + jnp.sum(e_ref[0, 0, rows, :].astype(F32) * g, axis=0, keepdims=True)
    inner = inner * inv
    hrows = pl.ds(pl.multiple_of(h * dk, dk), dk)
    dq = jnp.zeros((dk, BLK), F32)
    for kb in range(blocks):
        rows = slice(kb * BLK, (kb + 1) * BLK)
        e = e_ref[0, 0, rows, :]
        ds = (e.astype(F32) * (dp[rows, :] - inner)).astype(BF)
        dka[rows, :] += dot(ds, qm, ((1,), (0,)))
        dva[rows, :] += dot(e, scaled, ((1,), (0,)))
        dq = dq + dot(kt[hrows, rows], ds, ((1,), (0,)))
        tally[h, diagonal_of(kb, qb, x, blocks)] += ds.astype(F32)
    dqa[hrows, :] = dq

    @pl.when(h == heads - 1)
    def _():
        dq_ref[...] = dqa[...].T.astype(BF)

    @pl.when((h == heads - 1) & (qb == blocks - 1))
    def _():
        dk_ref[...] = dka[...].astype(BF)
        dv_ref[...] = dva[...].astype(BF)
        ids = bid_ref[...]
        hot = ids == lax.broadcasted_iota(jnp.int32, (buckets, SPAN), 0)
        out_lane = lax.broadcasted_iota(jnp.int32, rel_ref.shape, 1)
        sub = lax.broadcasted_iota(jnp.int32, (8, SPAN), 0)
        out = jnp.zeros(rel_ref.shape, F32)
        for hh in range(heads):
            line = jnp.zeros((8, SPAN), F32)
            for a in range(BLK // 8):
                group = slice(8 * a, 8 * a + 8)
                parts = [tally[hh, d, group, :] for d in (4, 3, 2, 1, 0)]
                strip = jnp.concatenate(parts + [jnp.zeros((8, BLK), F32)], axis=1)
                line = line + (strip if a == 0 else pltpu.roll(strip, SPAN - 8 * a, 1))
            for bit in (1, 2, 4):
                line = jnp.where((sub & bit) != 0, pltpu.roll(line, SPAN - bit, 1), line)
            sums = jnp.sum(line, axis=0, keepdims=True)
            col = jnp.sum(jnp.where(hot, sums, 0.0), axis=1, keepdims=True)
            out = jnp.where(out_lane == hh, col, out)
        rel_ref[...] = out


def attn_bwd(x, q, k, v, dctx, e, inv, buckets, heads, dk):
    seq, cols = q.shape
    blocks = seq // BLK
    bids = jnp.asarray(lane_buckets(buckets))
    whole = lambda i, h: (0, 0)
    return pl.pallas_call(
        functools.partial(attn_bwd_kernel, heads, dk, buckets, blocks),
        grid=(blocks, heads),
        in_specs=[
            pl.BlockSpec(memory_space=pltpu.SMEM),
            pl.BlockSpec((1, SPAN), whole),
            pl.BlockSpec((BLK, cols), lambda i, h: (i, 0)),
            pl.BlockSpec((seq, cols), whole),
            pl.BlockSpec((seq, cols), whole),
            pl.BlockSpec((BLK, cols), lambda i, h: (i, 0)),
            pl.BlockSpec((1, 1, seq, BLK), lambda i, h: (h, i, 0, 0)),
            pl.BlockSpec((1, 1, 1, BLK), lambda i, h: (h, i, 0, 0)),
        ],
        out_specs=[
            pl.BlockSpec((BLK, cols), lambda i, h: (i, 0)),
            pl.BlockSpec((seq, cols), whole),
            pl.BlockSpec((seq, cols), whole),
            pl.BlockSpec((buckets, 128), whole),
        ],
        out_shape=[
            jax.ShapeDtypeStruct((seq, cols), BF),
            jax.ShapeDtypeStruct((seq, cols), BF),
            jax.ShapeDtypeStruct((seq, cols), BF),
            jax.ShapeDtypeStruct((buckets, 128), F32),
        ],
        scratch_shapes=[
            pltpu.VMEM((cols, seq), BF),
            pltpu.VMEM((cols, BLK), F32),
            pltpu.VMEM((seq, BLK), F32),
            pltpu.VMEM((seq, cols), F32),
            pltpu.VMEM((seq, cols), F32),
            pltpu.VMEM((cols, BLK), F32),
            pltpu.VMEM((heads, 5, BLK, BLK), F32),
        ],
        compiler_params=pltpu.CompilerParams(vmem_limit_bytes=VMEM_LIMIT),
        cost_estimate=pl.CostEstimate(
            flops=32 * heads * seq * seq * dk,
            bytes_accessed=2 * heads * seq * seq + 14 * seq * cols,
            transcendentals=0,
        ),
    )(x, bids, q, k, v, dctx, e, inv)


def flip(index, mask):
    out = index
    bit = 1
    while bit <= mask:
        if mask & bit:
            out = out + bit * (1 - 2 * (index // bit % 2))
        bit *= 2
    return out


GROUP_MASKS = (1, 2, 4, 12)


def group_coords(g):
    b = [g // (1 << i) % 2 for i in range(4)]
    return [b[0], b[1], (b[2] + b[3]) % 2, b[3]]


def block_position(k):
    b = [k >> i & 1 for i in range(4)]
    c = [b[0], b[1], b[2] ^ b[3], b[3]]
    return c[0] * 8 + c[1] * 4 + c[2] * 2 + c[3]


def ff_kernel(
    steps, extra,
    x_ref, c_ref, xt_ref, ct_ref, wg_ref, wu_ref, wo_hbm,
    grads_ref, din_hbm, near_hbm, far_hbm,
    wo, hid, dg, du, din, stage, r1, r2, r3, r4, xs, xr, of,
    wo_sem, s1, s2, s3, s4, t1, t2, t3, t4, xsem, osem,
):
    j = pl.program_id(0)
    last = j == steps - 1
    total, f = hid.shape
    rows = total // 2
    d = xt_ref.shape[0]
    shard = d // 16
    dp, mp = lax.axis_index("dp"), lax.axis_index("mp")
    a = group_coords(dp // extra)
    peers = [flip(dp, m * extra) for m in GROUP_MASKS]
    bufs = (r1, r2, r3, r4)
    sends, recvs = (s1, s2, s3, s4), (t1, t2, t3, t4)
    mesh = pl.DeviceIdType.MESH

    def wo_copy(i):
        cols = pl.ds(pl.multiple_of(i * BLK, BLK), BLK)
        return pltpu.make_async_copy(wo_hbm.at[:, cols], wo.at[:, cols], wo_sem.at[i])

    def hop(level, s, w):
        half = 8 >> level
        away = pl.ds((1 - a[level]) * half, half)
        src = stage.at[w, away] if level == 0 else bufs[level - 1].at[s, away]
        return pltpu.make_async_remote_copy(
            src_ref=src,
            dst_ref=bufs[level].at[s],
            send_sem=sends[level].at[s],
            recv_sem=recvs[level].at[s],
            device_id=(peers[level], mp),
            device_id_type=mesh,
        )

    def absorb(level, step, w):
        s = step * 3 + w
        half = 8 >> level
        copy = hop(level, s, w)
        copy.wait_recv()
        copy.wait_send()
        keep = pl.ds(a[level] * half, half)
        kept = stage[w, keep] if level == 0 else bufs[level - 1][s, keep]
        both = kept.astype(F32) + bufs[level][s].astype(F32)
        if level < 3:
            bufs[level][s] = both.astype(BF)
            hop(level + 1, s, w).start()
        else:
            cols = pl.ds(pl.multiple_of(step * BLK, BLK), BLK)
            grads_ref[w, :, cols] = both[0]

    def absorb_step(level, step):
        def one(w, carry):
            absorb(level, step, w)
            return carry

        lax.fori_loop(0, 3, one, 0)

    @pl.when(j == 0)
    def _():
        barrier = pltpu.get_barrier_semaphore()
        for peer in peers:
            pl.semaphore_signal(barrier, inc=1, device_id=(peer, mp), device_id_type=mesh)
        pl.semaphore_signal(barrier, inc=1, device_id=(dp, 1 - mp), device_id_type=mesh)
        pl.semaphore_wait(barrier, 5)
        for i in range(steps):
            wo_copy(i).start()
        din[...] = jnp.zeros_like(din)
        stage[...] = jnp.zeros_like(stage)

    wo_copy(j).wait()
    cols = pl.ds(pl.multiple_of(j * BLK, BLK), BLK)
    scale = np.float32(np.sqrt(2 / np.pi))
    for r in range(total // BLK):
        rs = slice(r * BLK, (r + 1) * BLK)
        gate = dot(x_ref[rs, :], wg_ref[...], ((1,), (0,)))
        up = dot(x_ref[rs, :], wu_ref[...], ((1,), (0,)))
        dh = dot(c_ref[rs, :], wo[:, cols], ((1,), (0,)))
        sq = gate * gate
        t = jnp.tanh(scale * gate * (1.0 + 0.044715 * sq))
        half = 0.5 * (1.0 + t)
        act = gate * half
        slope = half + 0.5 * gate * (1.0 - t * t) * (scale * (1.0 + (3 * 0.044715) * sq))
        hid[rs, cols] = (act * up).astype(BF)
        dgr = (dh * up * slope).astype(BF)
        dur = (dh * act).astype(BF)
        dg[rs, :] = dgr
        du[rs, :] = dur
        din[rs, :] += dot(dgr, wg_ref[...], ((1,), (1,))) + dot(dur, wu_ref[...], ((1,), (1,)))

    x_copy = pltpu.make_async_remote_copy(
        src_ref=xs,
        dst_ref=xr,
        send_sem=xsem.at[0],
        recv_sem=xsem.at[1],
        device_id=(dp, 1 - mp),
        device_id_type=mesh,
    )

    @pl.when(last)
    def _():
        xs[...] = din[rows:, :].astype(BF)
        x_copy.start()

    @pl.when(j > 0)
    def _():
        absorb(0, j - 1, 2)

    per = 4 * shard
    for w in range(3):
        left = ct_ref if w == 0 else xt_ref
        right = hid[:, cols] if w == 0 else (dg[...] if w == 1 else du[...])
        for q in range(4):
            part = dot(left[q * per : (q + 1) * per, :], right, ((1,), (0,)))
            for k in range(4):
                stage[w, block_position(4 * q + k), 0:shard, :] = part[
                    k * shard : (k + 1) * shard
                ].astype(BF)
        hop(0, j * 3 + w, w).start()
        if w > 0:
            absorb(0, j, w - 1)

    for level, lag in ((1, 3), (2, 4), (3, 5)):
        @pl.when(j >= lag)
        def _():
            absorb_step(level, j - lag)

    @pl.when(last)
    def _():
        end = steps - 1
        absorb(0, end, 2)
        for r in (2, 3):
            rs = slice(r * BLK, (r + 1) * BLK)
            o = dot(hid[rs, :], wo[...], ((1,), (1,)))
            of[(r - 2) * BLK : (r - 1) * BLK, :] = o.astype(BF)
        far_copy = pltpu.make_async_copy(of, far_hbm, osem.at[0])
        far_copy.start()
        absorb_step(1, end - 2)
        absorb_step(2, end - 3)
        absorb_step(3, end - 4)
        for r in (0, 1):
            rs = slice(r * BLK, (r + 1) * BLK)
            o = dot(hid[rs, :], wo[...], ((1,), (1,)))
            din[rows + r * BLK : rows + (r + 1) * BLK, :] = o
        near_copy = pltpu.make_async_copy(din.at[rows:], near_hbm, osem.at[1])
        near_copy.start()
        absorb_step(1, end - 1)
        absorb_step(2, end - 2)
        absorb_step(3, end - 3)
        absorb_step(1, end)
        absorb_step(2, end - 1)
        absorb_step(3, end - 2)
        x_copy.wait()
        din[:rows, :] += xr[...].astype(F32)
        din_copy = pltpu.make_async_copy(din.at[:rows], din_hbm, osem.at[2])
        din_copy.start()
        absorb_step(2, end)
        absorb_step(3, end - 1)
        absorb_step(3, end)
        far_copy.wait()
        near_copy.wait()
        din_copy.wait()


def ff_all(x, c, xt, ct, w2, wo, extra):
    total, dpad = x.shape
    d = xt.shape[0]
    f = wo.shape[1]
    rows = total // 2
    steps = f // BLK
    chunks = 3 * steps
    shard = d // 16
    spad = -(-shard // 16) * 16
    one = pl.Buffered(1)
    whole = lambda j: (0, 0)
    dma = pltpu.SemaphoreType.DMA
    any_spec = pl.BlockSpec(memory_space=pl.ANY)
    return pl.pallas_call(
        functools.partial(ff_kernel, steps, extra),
        grid=(steps,),
        in_specs=[
            pl.BlockSpec((total, dpad), whole, pipeline_mode=one),
            pl.BlockSpec((total, dpad), whole, pipeline_mode=one),
            pl.BlockSpec((d, total), whole, pipeline_mode=one),
            pl.BlockSpec((d, total), whole, pipeline_mode=one),
            pl.BlockSpec((None, dpad, BLK), lambda j: (0, 0, j)),
            pl.BlockSpec((None, dpad, BLK), lambda j: (1, 0, j)),
            any_spec,
        ],
        out_specs=[
            pl.BlockSpec((3, spad, f), lambda j: (0, 0, 0)),
            any_spec,
            any_spec,
            any_spec,
        ],
        out_shape=[
            jax.ShapeDtypeStruct((3, spad, f), F32),
            jax.ShapeDtypeStruct((rows, dpad), F32),
            jax.ShapeDtypeStruct((rows, dpad), F32),
            jax.ShapeDtypeStruct((rows, dpad), BF),
        ],
        scratch_shapes=[
            pltpu.VMEM((dpad, f), BF),
            pltpu.VMEM((total, f), BF),
            pltpu.VMEM((total, BLK), BF),
            pltpu.VMEM((total, BLK), BF),
            pltpu.VMEM((total, dpad), F32),
            pltpu.VMEM((3, 16, spad, BLK), BF),
            pltpu.VMEM((chunks, 8, spad, BLK), BF),
            pltpu.VMEM((chunks, 4, spad, BLK), BF),
            pltpu.VMEM((chunks, 2, spad, BLK), BF),
            pltpu.VMEM((chunks, 1, spad, BLK), BF),
            pltpu.VMEM((rows, dpad), BF),
            pltpu.VMEM((rows, dpad), BF),
            pltpu.VMEM((rows, dpad), BF),
            dma((steps,)),
            dma((chunks,)), dma((chunks,)), dma((chunks,)), dma((chunks,)),
            dma((chunks,)), dma((chunks,)), dma((chunks,)), dma((chunks,)),
            dma((2,)),
            dma((3,)),
        ],
        compiler_params=pltpu.CompilerParams(
            vmem_limit_bytes=FF_VMEM, collective_id=0, has_side_effects=True
        ),
        cost_estimate=pl.CostEstimate(
            flops=18 * total * d * f,
            bytes_accessed=6 * d * f + 16 * total * d,
            transcendentals=total * f,
        ),
    )(x, c, xt, ct, w2, w2, wo)


def rms_scale(v, gain):
    return v * lax.rsqrt(jnp.mean(v * v, axis=-1, keepdims=True) + norm_eps) * gain


def rms_back(v, gain, c):
    r = lax.rsqrt(jnp.mean(v * v, axis=-1, keepdims=True) + norm_eps)
    n = v * r
    cg = c * gain
    return r * (cg - n * jnp.mean(cg * n, axis=-1, keepdims=True)), c * n


def take(array, index):
    return lax.dynamic_index_in_dim(array, index, 0, keepdims=False)


def per_device(
    tokens,
    cotangent,
    doc_lengths,
    pad_mask,
    attn_gain,
    qkv_weight,
    rel_table,
    out_weight,
    ff_gain,
    ff_in_weight,
    ff_out_weight,
):
    rows, d = tokens.shape
    n_dp = lax.axis_size("dp")
    n_mp = lax.axis_size("mp")
    seq = rows * n_mp
    cols = qkv_weight.shape[2]
    buckets, heads = rel_table.shape
    dk = cols // heads
    x = lax.axis_index("mp")
    me = lax.axis_index("dp")
    xs = x.astype(jnp.int32).reshape(1)
    bits = n_dp.bit_length() - 1
    shard = d // n_dp
    extra = n_dp // 16
    pad_d = -d % BLK

    def swap(v):
        return lax.ppermute(v, "mp", [(0, 1), (1, 0)])

    def hop(v, mask):
        return lax.ppermute(v, "dp", [(i, i ^ mask) for i in range(n_dp)])

    def after(v, *first):
        return lax.optimization_barrier((v,) + first)[0]

    def bit(b):
        return (me >> b) & 1

    def reduce_rest(parts, low_bits):
        for b in reversed(range(low_bits)):
            halves = [p.reshape((2, p.shape[0] // 2) + p.shape[1:]) for p in parts]
            away = sum(take(p, 1 - bit(b)).astype(F32) for p in halves).astype(BF)
            parts = [take(p, bit(b)) for p in halves] + [hop(away, 1 << b)]
        return sum(p.astype(F32) for p in parts)[0]

    def reduce_core_first(parts):
        parts = [p.reshape((2,) * bits + p.shape[1:]) for p in parts]
        for b in range(bits):
            axis = bits - 1 - b
            pick = lambda p, i: lax.dynamic_index_in_dim(p, i, axis, keepdims=False)
            away = sum(pick(p, 1 - bit(b)).astype(F32) for p in parts).astype(BF)
            parts = [pick(p, bit(b)) for p in parts] + [hop(away, 1 << b)]
        return sum(p.astype(F32) for p in parts)

    tok_low = tokens.astype(BF)
    tok_far = swap(tok_low)
    w_out_far = swap(after(out_weight, tok_far))
    out_low = cotangent.astype(BF)
    cot_far = swap(after(out_low, tok_far))
    w2 = jnp.pad(jnp.transpose(ff_in_weight, (1, 0, 2)), ((0, 0), (0, pad_d), (0, 0)))
    wo = jnp.pad(ff_out_weight, ((0, pad_d), (0, 0)))
    c_all = jnp.concatenate([out_low, cot_far], axis=0)
    c_t = c_all.T
    c_all = jnp.pad(c_all, ((0, 0), (0, pad_d)))
    wq, wk, wv = (qkv_weight[:, i, :] for i in range(3))

    bounds = jnp.cumsum(doc_lengths[0])
    position = lax.rem(jnp.arange(seq, dtype=jnp.int32) + rows * x, seq)
    doc_of = jnp.sum((position[:, None] >= bounds[None, :]).astype(jnp.int32), axis=1)
    valid = jnp.concatenate(
        [lax.dynamic_slice(pad_mask[0], (rows * x,), (rows,)),
         lax.dynamic_slice(pad_mask[0], (rows * (1 - x),), (rows,))]
    )
    code = jnp.where(valid == 1, doc_of, -1).reshape(seq, 1)
    doc_row = doc_of.reshape(1, seq)

    far = tok_far.astype(F32)
    normed = jnp.concatenate(
        [rms_scale(tokens, attn_gain).astype(BF), rms_scale(far, attn_gain).astype(BF)], axis=0
    )

    def project(w):
        return jnp.dot(normed, w, preferred_element_type=F32).astype(BF)

    q, k, v = project(wq), project(wk), project(wv)
    e, inv, ctx = attn_fwd(xs, rel_table, doc_row, code, q, k, v, heads, dk)
    ctx_far = swap(ctx)
    ctx_far = jnp.concatenate([ctx_far[rows:], ctx_far[:rows]], axis=0)

    def out_proj(r):
        return jnp.einsum("sc,dc->sd", ctx[r], out_weight, preferred_element_type=F32) + jnp.einsum(
            "sc,dc->sd", ctx_far[r], w_out_far, preferred_element_type=F32
        )

    middle = tokens + out_proj(slice(0, rows))
    near_ff = rms_scale(middle, ff_gain).astype(BF)
    far_ff = rms_scale(far + out_proj(slice(rows, seq)), ff_gain).astype(BF)

    x_all = jnp.concatenate([near_ff, far_ff], axis=0)
    grads, din, out_near, out_far = ff_all(
        jnp.pad(x_all, ((0, 0), (0, pad_d))), c_all, x_all.T, c_t, w2, wo, extra
    )
    out_back = swap(out_far)

    def finish(g):
        g = g[: d // 16]
        if extra == 1:
            return g
        return reduce_rest([g.reshape(extra, shard, g.shape[1])], extra.bit_length() - 1)

    ffo = finish(grads[0])
    ffi = jnp.stack([finish(grads[1]), finish(grads[2])], axis=1)

    grad_mid, gain_rows = rms_back(middle, ff_gain, din[:, :d])
    result = middle + out_near[:, :d] + out_back[:, :d].astype(F32)
    ff_gain_part = jnp.sum(gain_rows, axis=0)
    grad_middle = cotangent + grad_mid
    attn_low = grad_middle.astype(BF)
    dctx_near = jnp.dot(attn_low, out_weight, preferred_element_type=F32).astype(BF)
    dctx_far = swap(jnp.dot(attn_low, w_out_far, preferred_element_type=F32).astype(BF))
    dctx = jnp.concatenate([dctx_near, dctx_far], axis=0)
    dq, dkk, dv, rel_part = attn_bwd(xs, q, k, v, dctx, e, inv, buckets, heads, dk)

    o_both = jnp.einsum(
        "sd,sc->dc",
        attn_low,
        jnp.concatenate([ctx[:rows], ctx_far[:rows]], axis=1),
        preferred_element_type=F32,
    )
    o_half = o_both[:, :cols] + swap(o_both[:, cols:].astype(BF)).astype(F32)
    dproj = jnp.concatenate([dq, dkk, dv], axis=1)
    qkv_part = jnp.einsum("sd,sc->dc", normed, dproj, preferred_element_type=F32)
    both = jnp.concatenate([qkv_part, o_half], axis=1).astype(BF)
    both = jnp.pad(both.reshape(n_dp, shard, 4 * cols), ((0, 0), (0, -shard % 16), (0, 0)))

    w_flat = jnp.concatenate([wq, wk, wv], axis=1)
    dn_near = jnp.einsum("sc,dc->sd", dproj[:rows], w_flat, preferred_element_type=F32)
    dn_far = jnp.einsum("sc,dc->sd", dproj[rows:], w_flat, preferred_element_type=F32).astype(BF)
    dn = dn_near + swap(dn_far).astype(F32)
    grad_tok, attn_gain_rows = rms_back(tokens, attn_gain, dn)
    input_grad = grad_middle + grad_tok
    attn_gain_part = jnp.sum(attn_gain_rows, axis=0)

    last = reduce_core_first([both])[:shard]
    grad_qkv = last[:, : 3 * cols].reshape(shard, 3, cols)
    grad_out = last[:, 3 * cols :]

    rel_all = jnp.zeros((buckets, heads * n_mp), F32)
    rel_all = lax.dynamic_update_slice(
        rel_all, rel_part[:, :heads], (jnp.int32(0), x.astype(jnp.int32) * heads)
    )
    small = jnp.concatenate([attn_gain_part, ff_gain_part, rel_all.reshape(-1)])
    pad = -small.shape[0] % 128
    small = jnp.pad(small, (0, pad)).reshape(-1, 128)
    small = small + swap(small)
    for b in range(bits):
        small = small + hop(small, 1 << b)
    small = small.reshape(-1)
    return (
        result,
        input_grad,
        small[:d],
        grad_qkv,
        small[2 * d : 2 * d + rel_all.size].reshape(rel_all.shape),
        grad_out,
        small[d : 2 * d],
        ffi,
        ffo,
    )


def solution(mesh):
    return jax.shard_map(
        per_device,
        mesh=mesh,
        in_specs=(
            P(("dp", "mp"), None),
            P(("dp", "mp"), None),
            P("dp", None),
            P("dp", None),
            P(),
            P(None, None, "mp"),
            P(None, "mp"),
            P(None, "mp"),
            P(),
            P(None, None, "mp"),
            P(None, "mp"),
        ),
        out_specs=(
            P(("dp", "mp"), None),
            P(("dp", "mp"), None),
            P(),
            P("dp", None, "mp"),
            P(),
            P("dp", "mp"),
            P(),
            P("dp", None, "mp"),
            P("dp", "mp"),
        ),
        check_vma=False,
    )
```

```python
import functools

import jax
import jax.numpy as jnp
import numpy as np
from jax import lax
from jax.experimental import pallas as pl
from jax.experimental.pallas import tpu as pltpu
from jax.sharding import PartitionSpec as P

MAXDIST = 128
norm_eps = 1e-06
BLK = 256
SPAN = 6 * BLK
REACH = 2
BF = jnp.bfloat16
F32 = jnp.float32
VMEM_LIMIT = 56 << 20
FF_VMEM = 63 << 20


def bucket_of(offsets, buckets, reach):
    half_range = buckets // 2
    upper_half = (offsets > 0).astype(np.int32) * half_range
    distance = np.abs(offsets)
    exact_range = half_range // 2
    safe_dist = np.maximum(distance, 1)
    log_bucket = exact_range + (
        np.log(safe_dist / exact_range) / np.log(reach / exact_range) * (half_range - exact_range)
    ).astype(np.int32)
    log_bucket = np.minimum(log_bucket, half_range - 1)
    return (upper_half + np.where(distance < exact_range, distance, log_bucket)).astype(np.int32)


def lane_buckets(buckets):
    lanes = np.arange(SPAN)
    shifted = np.where(lanes < 5 * BLK, lanes, lanes - SPAN)
    return bucket_of(REACH * BLK - shifted, buckets, MAXDIST).reshape(1, SPAN)


def dot(a, b, contract):
    return lax.dot_general(a, b, (contract, ((), ())), preferred_element_type=F32)


def diagonal_of(key_block, query_block, x, blocks):
    half = blocks // 2
    key_true = lax.rem(key_block + half * x, blocks)
    query_true = lax.rem(query_block + half * x, blocks)
    return jnp.clip(key_true - query_true, -REACH, REACH) + REACH


def attn_fwd_kernel(
    heads, dk, buckets, blocks,
    x_ref, rel_ref, bid_ref, doc_ref, code_ref, q_ref, k_ref, v_ref,
    e_ref, inv_ref, ctx_ref,
    table, vt, mask, score, acc,
):
    qb, h = pl.program_id(0), pl.program_id(1)
    x = x_ref[0]

    @pl.when((qb == 0) & (h == 0))
    def _():
        vt[...] = v_ref[...].astype(F32).T.astype(BF)
        ids = bid_ref[...]
        for hh in range(heads):
            line = jnp.zeros((1, SPAN), F32)
            for b in range(buckets):
                line = jnp.where(ids == b, rel_ref[b, hh], line)
            rows = pltpu.roll(
                jnp.broadcast_to(line, (BLK, SPAN)), 0, 1, stride=1, stride_axis=0
            )
            for d in range(5):
                table[hh, d] = rows[:, BLK * (4 - d) : BLK * (5 - d)]

    @pl.when(h == 0)
    def _():
        row = lax.broadcasted_iota(jnp.int32, (BLK, BLK), 0)
        col = lax.broadcasted_iota(jnp.int32, (BLK, BLK), 1)
        for kb in range(blocks):
            same = code_ref[kb * BLK : (kb + 1) * BLK, :] == doc_ref[...]
            diag = (row + kb * BLK) == (col + qb * BLK)
            mask[kb * BLK : (kb + 1) * BLK, :] = jnp.where(same | diag, 0.0, -1000000000.0)

    lane = lax.broadcasted_iota(jnp.int32, q_ref.shape, 1)
    qm = jnp.where(lane // dk == h, q_ref[...], jnp.zeros_like(q_ref[...]))
    peak = None
    for kb in range(blocks):
        rows = slice(kb * BLK, (kb + 1) * BLK)
        s = dot(k_ref[rows, :], qm, ((1,), (1,)))
        s = s + table[h, diagonal_of(kb, qb, x, blocks)] + mask[rows, :]
        score[rows, :] = s
        top = jnp.max(s, axis=0, keepdims=True)
        peak = top if peak is None else jnp.maximum(peak, top)
    total = jnp.zeros((1, BLK), F32)
    ctx = jnp.zeros((dk, BLK), F32)
    hrows = pl.ds(pl.multiple_of(h * dk, dk), dk)
    for kb in range(blocks):
        rows = slice(kb * BLK, (kb + 1) * BLK)
        e = jnp.exp(score[rows, :] - peak)
        total = total + jnp.sum(e, axis=0, keepdims=True)
        e_low = e.astype(BF)
        e_ref[0, 0, rows, :] = e_low
        ctx = ctx + dot(vt[hrows, rows], e_low, ((1,), (0,)))
    inv = 1.0 / total
    inv_ref[0, 0] = inv
    acc[hrows, :] = ctx * inv

    @pl.when(h == heads - 1)
    def _():
        ctx_ref[...] = acc[...].T.astype(BF)


def attn_fwd(x, rel, doc, code, q, k, v, heads, dk):
    seq, cols = q.shape
    blocks = seq // BLK
    buckets = rel.shape[0]
    bids = jnp.asarray(lane_buckets(buckets))
    whole = lambda i, h: (0, 0)
    return pl.pallas_call(
        functools.partial(attn_fwd_kernel, heads, dk, buckets, blocks),
        grid=(blocks, heads),
        in_specs=[
            pl.BlockSpec(memory_space=pltpu.SMEM),
            pl.BlockSpec(memory_space=pltpu.SMEM),
            pl.BlockSpec((1, SPAN), whole),
            pl.BlockSpec((1, BLK), lambda i, h: (0, i)),
            pl.BlockSpec((seq, 1), whole),
            pl.BlockSpec((BLK, cols), lambda i, h: (i, 0)),
            pl.BlockSpec((seq, cols), whole),
            pl.BlockSpec((seq, cols), whole),
        ],
        out_specs=[
            pl.BlockSpec((1, 1, seq, BLK), lambda i, h: (h, i, 0, 0)),
            pl.BlockSpec((1, 1, 1, BLK), lambda i, h: (h, i, 0, 0)),
            pl.BlockSpec((BLK, cols), lambda i, h: (i, 0)),
        ],
        out_shape=[
            jax.ShapeDtypeStruct((heads, blocks, seq, BLK), BF),
            jax.ShapeDtypeStruct((heads, blocks, 1, BLK), F32),
            jax.ShapeDtypeStruct((seq, cols), BF),
        ],
        scratch_shapes=[
            pltpu.VMEM((heads, 5, BLK, BLK), F32),
            pltpu.VMEM((cols, seq), BF),
            pltpu.VMEM((seq, BLK), F32),
            pltpu.VMEM((seq, BLK), F32),
            pltpu.VMEM((cols, BLK), F32),
        ],
        compiler_params=pltpu.CompilerParams(vmem_limit_bytes=VMEM_LIMIT),
        cost_estimate=pl.CostEstimate(
            flops=16 * heads * seq * seq * dk,
            bytes_accessed=2 * heads * seq * seq + 8 * seq * cols,
            transcendentals=heads * seq * seq,
        ),
    )(x, rel, bids, doc, code, q, k, v)


def flip(index, mask):
    out = index
    bit = 1
    while bit <= mask:
        if mask & bit:
            out = out + bit * (1 - 2 * (index // bit % 2))
        bit *= 2
    return out


GROUP_MASKS = (1, 2, 4, 12)


def group_coords(g):
    b = [g // (1 << i) % 2 for i in range(4)]
    return [b[0], b[1], (b[2] + b[3]) % 2, b[3]]


def block_position(k):
    b = [k >> i & 1 for i in range(4)]
    c = [b[0], b[1], b[2] ^ b[3], b[3]]
    return c[0] * 8 + c[1] * 4 + c[2] * 2 + c[3]


def ff_kernel(
    steps, extra,
    x_ref, c_ref, xt_ref, ct_ref, wg_ref, wu_ref, wo_hbm,
    grads_ref, din_hbm, near_hbm, far_hbm,
    wo, hid, dg, du, din, stage, r1, r2, r3, r4, xs, xr, of,
    wo_sem, s1, s2, s3, s4, t1, t2, t3, t4, xsem, osem,
):
    j = pl.program_id(0)
    last = j == steps - 1
    total, f = hid.shape
    rows = total // 2
    d = xt_ref.shape[0]
    shard = d // 16
    dp, mp = lax.axis_index("dp"), lax.axis_index("mp")
    a = group_coords(dp // extra)
    peers = [flip(dp, m * extra) for m in GROUP_MASKS]
    bufs = (r1, r2, r3, r4)
    sends, recvs = (s1, s2, s3, s4), (t1, t2, t3, t4)
    mesh = pl.DeviceIdType.MESH

    def wo_copy(i):
        cols = pl.ds(pl.multiple_of(i * BLK, BLK), BLK)
        return pltpu.make_async_copy(wo_hbm.at[:, cols], wo.at[:, cols], wo_sem.at[i])

    def hop(level, s, w):
        half = 8 >> level
        away = pl.ds((1 - a[level]) * half, half)
        src = stage.at[w, away] if level == 0 else bufs[level - 1].at[s, away]
        return pltpu.make_async_remote_copy(
            src_ref=src,
            dst_ref=bufs[level].at[s],
            send_sem=sends[level].at[s],
            recv_sem=recvs[level].at[s],
            device_id=(peers[level], mp),
            device_id_type=mesh,
        )

    def absorb(level, step, w):
        s = step * 3 + w
        half = 8 >> level
        copy = hop(level, s, w)
        copy.wait_recv()
        copy.wait_send()
        keep = pl.ds(a[level] * half, half)
        kept = stage[w, keep] if level == 0 else bufs[level - 1][s, keep]
        both = kept.astype(F32) + bufs[level][s].astype(F32)
        if level < 3:
            bufs[level][s] = both.astype(BF)
            hop(level + 1, s, w).start()
        else:
            cols = pl.ds(pl.multiple_of(step * BLK, BLK), BLK)
            grads_ref[w, :, cols] = both[0]

    def absorb_step(level, step):
        def one(w, carry):
            absorb(level, step, w)
            return carry

        lax.fori_loop(0, 3, one, 0)

    @pl.when(j == 0)
    def _():
        barrier = pltpu.get_barrier_semaphore()
        for peer in peers:
            pl.semaphore_signal(barrier, inc=1, device_id=(peer, mp), device_id_type=mesh)
        pl.semaphore_signal(barrier, inc=1, device_id=(dp, 1 - mp), device_id_type=mesh)
        pl.semaphore_wait(barrier, 5)
        for i in range(steps):
            wo_copy(i).start()
        din[...] = jnp.zeros_like(din)
        stage[...] = jnp.zeros_like(stage)

    wo_copy(j).wait()
    cols = pl.ds(pl.multiple_of(j * BLK, BLK), BLK)
    scale = np.float32(np.sqrt(2 / np.pi))
    for r in range(total // BLK):
        rs = slice(r * BLK, (r + 1) * BLK)
        gate = dot(x_ref[rs, :], wg_ref[...], ((1,), (0,)))
        up = dot(x_ref[rs, :], wu_ref[...], ((1,), (0,)))
        dh = dot(c_ref[rs, :], wo[:, cols], ((1,), (0,)))
        sq = gate * gate
        t = jnp.tanh(scale * gate * (1.0 + 0.044715 * sq))
        half = 0.5 * (1.0 + t)
        act = gate * half
        slope = half + 0.5 * gate * (1.0 - t * t) * (scale * (1.0 + (3 * 0.044715) * sq))
        hid[rs, cols] = (act * up).astype(BF)
        dgr = (dh * up * slope).astype(BF)
        dur = (dh * act).astype(BF)
        dg[rs, :] = dgr
        du[rs, :] = dur
        din[rs, :] += dot(dgr, wg_ref[...], ((1,), (1,))) + dot(dur, wu_ref[...], ((1,), (1,)))

    x_copy = pltpu.make_async_remote_copy(
        src_ref=xs,
        dst_ref=xr,
        send_sem=xsem.at[0],
        recv_sem=xsem.at[1],
        device_id=(dp, 1 - mp),
        device_id_type=mesh,
    )

    @pl.when(last)
    def _():
        xs[...] = din[rows:, :].astype(BF)
        x_copy.start()

    @pl.when(j > 0)
    def _():
        absorb(0, j - 1, 2)

    per = 4 * shard
    for w in range(3):
        left = ct_ref if w == 0 else xt_ref
        right = hid[:, cols] if w == 0 else (dg[...] if w == 1 else du[...])
        for q in range(4):
            part = dot(left[q * per : (q + 1) * per, :], right, ((1,), (0,)))
            for k in range(4):
                stage[w, block_position(4 * q + k), 0:shard, :] = part[
                    k * shard : (k + 1) * shard
                ].astype(BF)
        hop(0, j * 3 + w, w).start()
        if w > 0:
            absorb(0, j, w - 1)

    for level, lag in ((1, 3), (2, 4), (3, 5)):
        @pl.when(j >= lag)
        def _():
            absorb_step(level, j - lag)

    @pl.when(last)
    def _():
        end = steps - 1
        absorb(0, end, 2)
        for r in (2, 3):
            rs = slice(r * BLK, (r + 1) * BLK)
            o = dot(hid[rs, :], wo[...], ((1,), (1,)))
            of[(r - 2) * BLK : (r - 1) * BLK, :] = o.astype(BF)
        far_copy = pltpu.make_async_copy(of, far_hbm, osem.at[0])
        far_copy.start()
        absorb_step(1, end - 2)
        absorb_step(2, end - 3)
        absorb_step(3, end - 4)
        for r in (0, 1):
            rs = slice(r * BLK, (r + 1) * BLK)
            o = dot(hid[rs, :], wo[...], ((1,), (1,)))
            din[rows + r * BLK : rows + (r + 1) * BLK, :] = o
        near_copy = pltpu.make_async_copy(din.at[rows:], near_hbm, osem.at[1])
        near_copy.start()
        absorb_step(1, end - 1)
        absorb_step(2, end - 2)
        absorb_step(3, end - 3)
        absorb_step(1, end)
        absorb_step(2, end - 1)
        absorb_step(3, end - 2)
        x_copy.wait()
        din[:rows, :] += xr[...].astype(F32)
        din_copy = pltpu.make_async_copy(din.at[:rows], din_hbm, osem.at[2])
        din_copy.start()
        absorb_step(2, end)
        absorb_step(3, end - 1)
        absorb_step(3, end)
        far_copy.wait()
        near_copy.wait()
        din_copy.wait()


def ff_all(x, c, xt, ct, w2, wo, extra):
    total, dpad = x.shape
    d = xt.shape[0]
    f = wo.shape[1]
    rows = total // 2
    steps = f // BLK
    chunks = 3 * steps
    shard = d // 16
    spad = -(-shard // 16) * 16
    one = pl.Buffered(1)
    whole = lambda j: (0, 0)
    dma = pltpu.SemaphoreType.DMA
    any_spec = pl.BlockSpec(memory_space=pl.ANY)
    return pl.pallas_call(
        functools.partial(ff_kernel, steps, extra),
        grid=(steps,),
        in_specs=[
            pl.BlockSpec((total, dpad), whole, pipeline_mode=one),
            pl.BlockSpec((total, dpad), whole, pipeline_mode=one),
            pl.BlockSpec((d, total), whole, pipeline_mode=one),
            pl.BlockSpec((d, total), whole, pipeline_mode=one),
            pl.BlockSpec((None, dpad, BLK), lambda j: (0, 0, j)),
            pl.BlockSpec((None, dpad, BLK), lambda j: (1, 0, j)),
            any_spec,
        ],
        out_specs=[
            pl.BlockSpec((3, spad, f), lambda j: (0, 0, 0)),
            any_spec,
            any_spec,
            any_spec,
        ],
        out_shape=[
            jax.ShapeDtypeStruct((3, spad, f), F32),
            jax.ShapeDtypeStruct((rows, dpad), F32),
            jax.ShapeDtypeStruct((rows, dpad), F32),
            jax.ShapeDtypeStruct((rows, dpad), BF),
        ],
        scratch_shapes=[
            pltpu.VMEM((dpad, f), BF),
            pltpu.VMEM((total, f), BF),
            pltpu.VMEM((total, BLK), BF),
            pltpu.VMEM((total, BLK), BF),
            pltpu.VMEM((total, dpad), F32),
            pltpu.VMEM((3, 16, spad, BLK), BF),
            pltpu.VMEM((chunks, 8, spad, BLK), BF),
            pltpu.VMEM((chunks, 4, spad, BLK), BF),
            pltpu.VMEM((chunks, 2, spad, BLK), BF),
            pltpu.VMEM((chunks, 1, spad, BLK), BF),
            pltpu.VMEM((rows, dpad), BF),
            pltpu.VMEM((rows, dpad), BF),
            pltpu.VMEM((rows, dpad), BF),
            dma((steps,)),
            dma((chunks,)), dma((chunks,)), dma((chunks,)), dma((chunks,)),
            dma((chunks,)), dma((chunks,)), dma((chunks,)), dma((chunks,)),
            dma((2,)),
            dma((3,)),
        ],
        compiler_params=pltpu.CompilerParams(
            vmem_limit_bytes=FF_VMEM, collective_id=0, has_side_effects=True
        ),
        cost_estimate=pl.CostEstimate(
            flops=18 * total * d * f,
            bytes_accessed=6 * d * f + 16 * total * d,
            transcendentals=total * f,
        ),
    )(x, c, xt, ct, w2, w2, wo)


def tail_kernel(
    heads, dk, buckets, blocks, extra,
    bid_ref, q_ref, k_ref, v_ref, e_ref, inv_ref, wo_ref, wof_ref, ctx_ref, ctxf_ref, ag_ref, fg_ref,
    din_hbm, mid_hbm, cot_hbm, tok_hbm, nrm_hbm, wfl_hbm, far_hbm,
    ig_hbm, g_ref, small_ref, back_hbm,
    f1, f2, f3, nrm, wfl, alow, dctx, dcs, osend, orecv, gsum, fsum,
    kt, dct, dp_s, dka, dva, dqa, tally, dproj, grad, dns, dnr,
    stage, t1, t2, t3, t4, sb, rb,
    lsem, xs_sem, xr_sem, cs_sem, cr_sem, bs_sem, br_sem,
):
    qb, h = pl.program_id(0), pl.program_id(1)
    dp, x = lax.axis_index("dp"), lax.axis_index("mp")
    rows, d = f2.shape
    cols = dctx.shape[1]
    shard = d // 16
    mesh = pl.DeviceIdType.MESH
    a = group_coords(dp // extra)
    peers = [flip(dp, m * extra) for m in GROUP_MASKS]
    other = (dp, 1 - x)
    bufs = (stage, t1, t2, t3, t4)

    def remote(src, dst, send, recv, who):
        return pltpu.make_async_remote_copy(
            src_ref=src, dst_ref=dst, send_sem=send, recv_sem=recv, device_id=who, device_id_type=mesh
        )

    def local(i):
        src, dst = (
            (din_hbm, f1), (mid_hbm, f2), (cot_hbm, f3), (tok_hbm, f2), (nrm_hbm, nrm), (wfl_hbm, wfl)
        )[i]
        return pltpu.make_async_copy(src, dst, lsem.at[i])

    dctx_copy = remote(dcs, dctx.at[pl.ds(rows, rows)], xs_sem.at[0], xr_sem.at[0], other)
    o_copy = remote(osend, orecv, xs_sem.at[1], xr_sem.at[1], other)
    back_copy = remote(far_hbm, back_hbm, xs_sem.at[2], xr_sem.at[2], other)

    def dn_copy(r):
        return remote(dns.at[r], dnr.at[r], xs_sem.at[3 + r], xr_sem.at[3 + r], other)

    def hop(level):
        half = 8 >> level
        away = pl.ds((1 - a[level]) * half, half)
        return remote(
            bufs[level].at[away], bufs[level + 1], cs_sem.at[level], cr_sem.at[level], (peers[level], x)
        )

    def absorb(level):
        half = 8 >> level
        copy = hop(level)
        copy.wait()
        both = bufs[level][pl.ds(a[level] * half, half)].astype(F32) + bufs[level + 1][...].astype(F32)
        if level < 3:
            bufs[level + 1][...] = both.astype(BF)
            hop(level + 1).start()
        else:
            g_ref[...] = both[0]

    def round_copy(i):
        who = other if i == 4 else (peers[i], x)
        return remote(sb.at[i], rb.at[i], bs_sem.at[i], br_sem.at[i], who)

    def round_end(i):
        round_copy(i).wait()
        sb[i + 1] = sb[i] + rb[i]
        if i < 4:
            round_copy(i + 1).start()

    def out_copy(r):
        rs = pl.ds(r * BLK, BLK)
        return pltpu.make_async_copy(f3.at[rs], ig_hbm.at[rs], lsem.at[6 + r])

    @pl.when((qb == 0) & (h == 0))
    def _():
        barrier = pltpu.get_barrier_semaphore()
        for i in range(3):
            local(i).start()
        for peer in peers:
            pl.semaphore_signal(barrier, inc=1, device_id=(peer, x), device_id_type=mesh)
        pl.semaphore_signal(barrier, inc=1, device_id=other, device_id_type=mesh)
        pl.semaphore_wait(barrier, 5)
        kt[...] = k_ref[...].astype(F32).T.astype(BF)
        dka[...] = jnp.zeros_like(dka)
        dva[...] = jnp.zeros_like(dva)
        tally[...] = jnp.zeros_like(tally)
        stage[...] = jnp.zeros_like(stage)
        fsum[...] = jnp.zeros_like(fsum)
        gsum[...] = jnp.zeros_like(gsum)
        for i in range(3):
            local(i).wait()
        for r in range(rows // BLK):
            rs = slice(r * BLK, (r + 1) * BLK)
            v = f2[rs, :]
            c = f1[rs, :d]
            scale = lax.rsqrt(jnp.mean(v * v, axis=-1, keepdims=True) + norm_eps)
            n = v * scale
            cg = c * fg_ref[...]
            m = jnp.mean(cg * n, axis=-1, keepdims=True)
            gm = f3[rs, :] + scale * (cg - n * m)
            fsum[...] += jnp.sum(c * n, axis=0, keepdims=True)
            f1[rs, :d] = gm
            alow[rs, :] = gm.astype(BF)
        for i in range(3, 6):
            local(i).start()
        dcs[...] = dot(alow[...], wof_ref[...], ((1,), (0,))).astype(BF)
        dctx_copy.start()
        dctx[:rows, :] = dot(alow[...], wo_ref[...], ((1,), (0,))).astype(BF)
        osend[...] = dot(alow[...], ctxf_ref[...], ((0,), (0,))).astype(BF)
        grad[:, 3 * cols : 4 * cols] = dot(alow[...], ctx_ref[...], ((0,), (0,)))
        dctx_copy.wait()
        o_copy.start()
        back_copy.start()

    qrows = pl.ds(pl.multiple_of(qb * BLK, BLK), BLK)

    @pl.when(h == 0)
    def _():
        dct[...] = dctx[qrows, :].astype(F32).T

    lane = lax.broadcasted_iota(jnp.int32, q_ref.shape, 1)
    qm = jnp.where(lane // dk == h, q_ref[...], jnp.zeros_like(q_ref[...]))
    row = lax.broadcasted_iota(jnp.int32, dct.shape, 0)
    inv = inv_ref[0, 0]
    ds_t = jnp.where(row // dk == h, dct[...] * inv, 0.0)
    scaled_t = ds_t.astype(BF)
    scaled = ds_t.T.astype(BF)
    inner = jnp.zeros((1, BLK), F32)
    for kb in range(blocks):
        krows = slice(kb * BLK, (kb + 1) * BLK)
        g = dot(v_ref[krows, :], scaled_t, ((1,), (0,)))
        dp_s[krows, :] = g
        inner = inner + jnp.sum(e_ref[0, 0, krows, :].astype(F32) * g, axis=0, keepdims=True)
    inner = inner * inv
    hrows = pl.ds(pl.multiple_of(h * dk, dk), dk)
    dq = jnp.zeros((dk, BLK), F32)
    q_true = (qb + blocks // 2 * x) % blocks
    for kb in range(blocks):
        krows = slice(kb * BLK, (kb + 1) * BLK)
        e = e_ref[0, 0, krows, :]
        ds = (e.astype(F32) * (dp_s[krows, :] - inner)).astype(BF)
        dka[krows, :] += dot(ds, qm, ((1,), (0,)))
        dva[krows, :] += dot(e, scaled, ((1,), (0,)))
        dq = dq + dot(kt[hrows, krows], ds, ((1,), (0,)))
        diag = (kb + blocks // 2 * x) % blocks - q_true + blocks - 1
        tally[h, diag] += ds.astype(F32)
    dqa[hrows, :] = dq

    @pl.when(h == heads - 1)
    def _():
        dproj[qrows, 0:cols] = dqa[...].T.astype(BF)

    @pl.when((h == heads - 1) & (qb == blocks - 1))
    def _():
        dproj[:, cols : 2 * cols] = dka[...].astype(BF)
        dproj[:, 2 * cols : 3 * cols] = dva[...].astype(BF)
        for i in range(3, 6):
            local(i).wait()
        for r in range(rows // BLK):
            rs = slice(rows + r * BLK, rows + (r + 1) * BLK)
            part = dot(dproj[rs, :], wfl[...], ((1,), (1,)))
            dns[r] = part.astype(BF)
            dn_copy(r).start()
            gsum[...] += jnp.sum(nrm[rs, :].astype(F32) * part, axis=0, keepdims=True)
        step = 3 * 128
        for c in range(0, d, step):
            cs = slice(c, min(c + step, d))
            grad[cs, 0 : 3 * cols] = dot(nrm[:, cs], dproj[...], ((0,), (0,)))
        o_copy.wait()
        grad[:, 3 * cols : 4 * cols] += orecv[...].astype(F32)
        for k in range(16):
            stage[block_position(k), 0:shard, :] = grad[k * shard : (k + 1) * shard, :].astype(BF)
        hop(0).start()
        for r in range(rows // BLK):
            rs = slice(r * BLK, (r + 1) * BLK)
            part = dot(dproj[rs, :], wfl[...], ((1,), (1,)))
            f3[rs, :] = part
            gsum[...] += jnp.sum(nrm[rs, :].astype(F32) * part, axis=0, keepdims=True)
        absorb(0)
        ids = bid_ref[...]
        hot = ids == lax.broadcasted_iota(jnp.int32, (buckets, SPAN), 0)
        out_lane = lax.broadcasted_iota(jnp.int32, (buckets, 128), 1)
        sub = lax.broadcasted_iota(jnp.int32, (8, SPAN), 0)
        out = jnp.zeros((buckets, 128), F32)
        for hh in range(heads):
            line = jnp.zeros((8, SPAN), F32)
            for g in range(BLK // 8):
                group = slice(8 * g, 8 * g + 8)
                t = [tally[hh, i, group, :] for i in range(7)]
                parts = [t[5] + t[6], t[4], t[3], t[2], t[1] + t[0]]
                strip = jnp.concatenate(parts + [jnp.zeros((8, BLK), F32)], axis=1)
                line = line + (strip if g == 0 else pltpu.roll(strip, SPAN - 8 * g, 1))
            for bit in (1, 2, 4):
                line = jnp.where((sub // bit) % 2 == 1, pltpu.roll(line, SPAN - bit, 1), line)
            sums = jnp.sum(line, axis=0, keepdims=True)
            col = jnp.sum(jnp.where(hot, sums, 0.0), axis=1, keepdims=True)
            out = jnp.where(out_lane == x * heads + hh, col, out)
        sb[0] = jnp.zeros(sb.shape[1:], F32)
        sb[0, 0:buckets, :] = out
        again = gsum[...] / ag_ref[...]
        lines = -(-d // 128)
        for i in range(lines):
            n = min(128, d - 128 * i)
            sb[0, buckets + i : buckets + i + 1, 0:n] = again[:, 128 * i : 128 * i + n]
            sb[0, buckets + lines + i : buckets + lines + i + 1, 0:n] = fsum[:, 128 * i : 128 * i + n]
        round_copy(0).start()
        absorb(1)
        round_end(0)
        round_end(1)
        for r in range(rows // BLK):
            rs = slice(r * BLK, (r + 1) * BLK)
            dn_copy(r).wait()
            c = f3[rs, :] + dnr[r].astype(F32)
            v = f2[rs, :]
            scale = lax.rsqrt(jnp.mean(v * v, axis=-1, keepdims=True) + norm_eps)
            n = v * scale
            cg = c * ag_ref[...]
            m = jnp.mean(cg * n, axis=-1, keepdims=True)
            f3[rs, :] = f1[rs, :d] + scale * (cg - n * m)
            out_copy(r).start()
            if r == 0:
                absorb(2)
                round_end(2)
                round_end(3)
        absorb(3)
        round_end(4)
        small_ref[...] = sb[5]
        back_copy.wait()
        for r in range(rows // BLK):
            out_copy(r).wait()


def tail(q, k, v, e, inv, wo, wof, ctx, ctxf, again, fgain, din, mid, cot, tok, nrm, wfl, far,
         buckets, heads, dk, extra):
    seq, cols = q.shape
    rows, d = tok.shape
    dpad = din.shape[1]
    blocks = seq // BLK
    shard = d // 16
    spad = -(-shard // 16) * 16
    lines = -(-(buckets + 2 * -(-d // 128)) // 8) * 8
    bids = jnp.asarray(lane_buckets(buckets))
    one = pl.Buffered(1)
    whole = lambda i, h: (0, 0)
    dma = pltpu.SemaphoreType.DMA
    any_spec = pl.BlockSpec(memory_space=pl.ANY)

    def full(v):
        return pl.BlockSpec(v.shape, whole, pipeline_mode=one)

    return pl.pallas_call(
        functools.partial(tail_kernel, heads, dk, buckets, blocks, extra),
        grid=(blocks, heads),
        in_specs=[
            full(bids),
            pl.BlockSpec((BLK, cols), lambda i, h: (i, 0)),
            full(k),
            full(v),
            pl.BlockSpec((1, 1, seq, BLK), lambda i, h: (h, i, 0, 0)),
            pl.BlockSpec((1, 1, 1, BLK), lambda i, h: (h, i, 0, 0)),
            full(wo),
            full(wof),
            full(ctx),
            full(ctxf),
            full(again),
            full(fgain),
        ]
        + [any_spec] * 7,
        out_specs=[
            any_spec,
            pl.BlockSpec((spad, 4 * cols), whole),
            pl.BlockSpec((lines, 128), whole),
            any_spec,
        ],
        out_shape=[
            jax.ShapeDtypeStruct((rows, d), F32),
            jax.ShapeDtypeStruct((spad, 4 * cols), F32),
            jax.ShapeDtypeStruct((lines, 128), F32),
            jax.ShapeDtypeStruct(far.shape, BF),
        ],
        scratch_shapes=[
            pltpu.VMEM((rows, dpad), F32),
            pltpu.VMEM((rows, d), F32),
            pltpu.VMEM((rows, d), F32),
            pltpu.VMEM((seq, d), BF),
            pltpu.VMEM((d, 3 * cols), BF),
            pltpu.VMEM((rows, d), BF),
            pltpu.VMEM((seq, cols), BF),
            pltpu.VMEM((rows, cols), BF),
            pltpu.VMEM((d, cols), BF),
            pltpu.VMEM((d, cols), BF),
            pltpu.VMEM((1, d), F32),
            pltpu.VMEM((1, d), F32),
            pltpu.VMEM((cols, seq), BF),
            pltpu.VMEM((cols, BLK), F32),
            pltpu.VMEM((seq, BLK), F32),
            pltpu.VMEM((seq, cols), F32),
            pltpu.VMEM((seq, cols), F32),
            pltpu.VMEM((cols, BLK), F32),
            pltpu.VMEM((heads, 7, BLK, BLK), F32),
            pltpu.VMEM((seq, 3 * cols), BF),
            pltpu.VMEM((d, 4 * cols), F32),
            pltpu.VMEM((rows // BLK, BLK, d), BF),
            pltpu.VMEM((rows // BLK, BLK, d), BF),
            pltpu.VMEM((16, spad, 4 * cols), BF),
            pltpu.VMEM((8, spad, 4 * cols), BF),
            pltpu.VMEM((4, spad, 4 * cols), BF),
            pltpu.VMEM((2, spad, 4 * cols), BF),
            pltpu.VMEM((1, spad, 4 * cols), BF),
            pltpu.VMEM((6, lines, 128), F32),
            pltpu.VMEM((5, lines, 128), F32),
            dma((6 + rows // BLK,)),
            dma((3 + rows // BLK,)),
            dma((3 + rows // BLK,)),
            dma((4,)), dma((4,)),
            dma((5,)), dma((5,)),
        ],
        compiler_params=pltpu.CompilerParams(
            vmem_limit_bytes=FF_VMEM, collective_id=1, has_side_effects=True
        ),
        cost_estimate=pl.CostEstimate(
            flops=32 * heads * seq * seq * dk + 8 * seq * d * 3 * cols,
            bytes_accessed=2 * heads * seq * seq + 30 * rows * d,
            transcendentals=0,
        ),
    )(bids, q, k, v, e, inv, wo, wof, ctx, ctxf, again, fgain, din, mid, cot, tok, nrm, wfl, far)


def rms_scale(v, gain):
    return v * lax.rsqrt(jnp.mean(v * v, axis=-1, keepdims=True) + norm_eps) * gain


def take(array, index):
    return lax.dynamic_index_in_dim(array, index, 0, keepdims=False)


def per_device(
    tokens,
    cotangent,
    doc_lengths,
    pad_mask,
    attn_gain,
    qkv_weight,
    rel_table,
    out_weight,
    ff_gain,
    ff_in_weight,
    ff_out_weight,
):
    rows, d = tokens.shape
    n_dp = lax.axis_size("dp")
    n_mp = lax.axis_size("mp")
    seq = rows * n_mp
    cols = qkv_weight.shape[2]
    buckets, heads = rel_table.shape
    dk = cols // heads
    x = lax.axis_index("mp")
    me = lax.axis_index("dp")
    xs = x.astype(jnp.int32).reshape(1)
    bits = n_dp.bit_length() - 1
    shard = d // n_dp
    extra = n_dp // 16
    pad_d = -d % BLK

    def swap(v):
        return lax.ppermute(v, "mp", [(0, 1), (1, 0)])

    def hop(v, mask):
        return lax.ppermute(v, "dp", [(i, i ^ mask) for i in range(n_dp)])

    def after(v, *first):
        return lax.optimization_barrier((v,) + first)[0]

    def bit(b):
        return (me >> b) & 1

    def reduce_rest(parts, low_bits):
        for b in reversed(range(low_bits)):
            halves = [p.reshape((2, p.shape[0] // 2) + p.shape[1:]) for p in parts]
            away = sum(take(p, 1 - bit(b)).astype(F32) for p in halves).astype(BF)
            parts = [take(p, bit(b)) for p in halves] + [hop(away, 1 << b)]
        return sum(p.astype(F32) for p in parts)[0]

    tok_low = tokens.astype(BF)
    tok_far = swap(tok_low)
    w_out_far = swap(after(out_weight, tok_far))
    out_low = cotangent.astype(BF)
    cot_far = swap(after(out_low, tok_far))
    w2 = jnp.pad(jnp.transpose(ff_in_weight, (1, 0, 2)), ((0, 0), (0, pad_d), (0, 0)))
    wo = jnp.pad(ff_out_weight, ((0, pad_d), (0, 0)))
    c_all = jnp.concatenate([out_low, cot_far], axis=0)
    c_t = c_all.T
    c_all = jnp.pad(c_all, ((0, 0), (0, pad_d)))
    wq, wk, wv = (qkv_weight[:, i, :] for i in range(3))

    bounds = jnp.cumsum(doc_lengths[0])
    position = lax.rem(jnp.arange(seq, dtype=jnp.int32) + rows * x, seq)
    doc_of = jnp.sum((position[:, None] >= bounds[None, :]).astype(jnp.int32), axis=1)
    valid = jnp.concatenate(
        [lax.dynamic_slice(pad_mask[0], (rows * x,), (rows,)),
         lax.dynamic_slice(pad_mask[0], (rows * (1 - x),), (rows,))]
    )
    code = jnp.where(valid == 1, doc_of, -1).reshape(seq, 1)
    doc_row = doc_of.reshape(1, seq)

    far = tok_far.astype(F32)
    normed = jnp.concatenate(
        [rms_scale(tokens, attn_gain).astype(BF), rms_scale(far, attn_gain).astype(BF)], axis=0
    )

    def project(w):
        return jnp.dot(normed, w, preferred_element_type=F32).astype(BF)

    q, k, v = project(wq), project(wk), project(wv)
    e, inv, ctx = attn_fwd(xs, rel_table, doc_row, code, q, k, v, heads, dk)
    ctx_far = swap(ctx)
    ctx_far = jnp.concatenate([ctx_far[rows:], ctx_far[:rows]], axis=0)

    def out_proj(r):
        return jnp.einsum("sc,dc->sd", ctx[r], out_weight, preferred_element_type=F32) + jnp.einsum(
            "sc,dc->sd", ctx_far[r], w_out_far, preferred_element_type=F32
        )

    middle = tokens + out_proj(slice(0, rows))
    near_ff = rms_scale(middle, ff_gain).astype(BF)
    far_ff = rms_scale(far + out_proj(slice(rows, seq)), ff_gain).astype(BF)

    x_all = jnp.concatenate([near_ff, far_ff], axis=0)
    grads, din, out_near, out_far = ff_all(
        jnp.pad(x_all, ((0, 0), (0, pad_d))), c_all, x_all.T, c_t, w2, wo, extra
    )
    def finish(g):
        g = g[: d // 16]
        if extra == 1:
            return g
        return reduce_rest([g.reshape(extra, shard, g.shape[1])], extra.bit_length() - 1)

    ffo = finish(grads[0])
    ffi = jnp.stack([finish(grads[1]), finish(grads[2])], axis=1)

    w_flat = jnp.concatenate([wq, wk, wv], axis=1)
    input_grad, last, small, out_back = tail(
        q, k, v, e, inv, out_weight, w_out_far, ctx[:rows], ctx_far[:rows],
        attn_gain.reshape(1, d), ff_gain.reshape(1, d),
        din, middle, cotangent, tokens, normed, w_flat, out_far,
        buckets, heads, dk, extra,
    )
    result = middle + out_near[:, :d] + out_back[:, :d].astype(F32)
    last = finish(last)
    grad_qkv = last[:, : 3 * cols].reshape(shard, 3, cols)
    grad_out = last[:, 3 * cols :]
    for b in range(extra.bit_length() - 1):
        small = small + hop(small, 1 << b)
    lines = -(-d // 128)
    rel_grad = small[:buckets, : heads * n_mp]
    attn_gain_grad = small[buckets : buckets + lines].reshape(-1)[:d]
    ff_gain_grad = small[buckets + lines : buckets + 2 * lines].reshape(-1)[:d]
    return (
        result,
        input_grad,
        attn_gain_grad,
        grad_qkv,
        rel_grad,
        grad_out,
        ff_gain_grad,
        ffi,
        ffo,
    )


def solution(mesh):
    return jax.shard_map(
        per_device,
        mesh=mesh,
        in_specs=(
            P(("dp", "mp"), None),
            P(("dp", "mp"), None),
            P("dp", None),
            P("dp", None),
            P(),
            P(None, None, "mp"),
            P(None, "mp"),
            P(None, "mp"),
            P(),
            P(None, None, "mp"),
            P(None, "mp"),
        ),
        out_specs=(
            P(("dp", "mp"), None),
            P(("dp", "mp"), None),
            P(),
            P("dp", None, "mp"),
            P(),
            P("dp", "mp"),
            P(),
            P("dp", None, "mp"),
            P("dp", "mp"),
        ),
        check_vma=False,
    )
```

```python
import functools

import jax
import jax.numpy as jnp
import numpy as np
from jax import lax
from jax.experimental import pallas as pl
from jax.experimental.pallas import tpu as pltpu
from jax.sharding import PartitionSpec as P

MAXDIST = 128
norm_eps = 1e-06
BLK = 256
SPAN = 6 * BLK
REACH = 2
BF = jnp.bfloat16
F32 = jnp.float32
FF_VMEM = 63 << 20
FF_DONE = 3


def bucket_of(offsets, buckets, reach):
    half_range = buckets // 2
    upper_half = (offsets > 0).astype(np.int32) * half_range
    distance = np.abs(offsets)
    exact_range = half_range // 2
    safe_dist = np.maximum(distance, 1)
    log_bucket = exact_range + (
        np.log(safe_dist / exact_range) / np.log(reach / exact_range) * (half_range - exact_range)
    ).astype(np.int32)
    log_bucket = np.minimum(log_bucket, half_range - 1)
    return (upper_half + np.where(distance < exact_range, distance, log_bucket)).astype(np.int32)


def lane_buckets(buckets):
    lanes = np.arange(SPAN)
    shifted = np.where(lanes < 5 * BLK, lanes, lanes - SPAN)
    return bucket_of(REACH * BLK - shifted, buckets, MAXDIST).reshape(1, SPAN)


def dot(a, b, contract):
    return lax.dot_general(a, b, (contract, ((), ())), preferred_element_type=F32)


def flip(index, mask):
    out = index
    bit = 1
    while bit <= mask:
        if mask & bit:
            out = out + bit * (1 - 2 * (index // bit % 2))
        bit *= 2
    return out


GROUP_MASKS = (1, 2, 4, 12)


def group_coords(g):
    b = [g // (1 << i) % 2 for i in range(4)]
    return [b[0], b[1], (b[2] + b[3]) % 2, b[3]]


def block_position(k):
    b = [k >> i & 1 for i in range(4)]
    c = [b[0], b[1], b[2] ^ b[3], b[3]]
    return c[0] * 8 + c[1] * 4 + c[2] * 2 + c[3]


def column(line):
    return jnp.broadcast_to(line, (8, line.shape[1])).T[:, 0:1]


def norm_scale(v):
    return lax.rsqrt(jnp.mean(v * v, axis=0, keepdims=True) + norm_eps)


def lanes(block):
    return pl.ds(pl.multiple_of(block * BLK, BLK), BLK)


def remote(src, dst, send, recv, who):
    return pltpu.make_async_remote_copy(
        src_ref=src,
        dst_ref=dst,
        send_sem=send,
        recv_sem=recv,
        device_id=who,
        device_id_type=pl.DeviceIdType.MESH,
    )


def meet(devices):
    barrier = pltpu.get_barrier_semaphore()
    for who in devices:
        pl.semaphore_signal(barrier, inc=1, device_id=who, device_id_type=pl.DeviceIdType.MESH)
    pl.semaphore_wait(barrier, len(devices))


def front_kernel(
    heads, dk, buckets, blocks,
    rel_ref, len_ref, bid_ref, pad_ref, ag_ref, fg_ref, wq_ref, wo_ref,
    tok_hbm, far_hbm, cot_hbm,
    e_ref, inv_ref, qkv_ref, ctx_hbm, nrm_hbm, xt_hbm, mid_hbm, ct_hbm, wall_hbm,
    f1, fb, f3, cl, nrm, table, padc, mask, score, agc, fgc, wall, wn, call, xo,
    lsem, osem, wsend, wrecv, csend, crecv,
):
    qb, h = pl.program_id(0), pl.program_id(1)
    dp, x = lax.axis_index("dp"), lax.axis_index("mp")
    d, rows = f1.shape
    cols = heads * dk
    half = cols // 2
    core = dp % 2
    other = (dp, 1 - x)
    sibling = (dp + 1 - 2 * core, x)
    near_blocks = blocks // 2
    part = pl.ds(core * half, half)
    far_part = pl.ds(cols + core * half, half)

    def local(i):
        src, dst = ((tok_hbm, f1), (far_hbm, fb), (cot_hbm, f3))[i]
        return pltpu.make_async_copy(src, dst, lsem.at[i])

    def out(i):
        src, dst = (
            (call, ctx_hbm), (nrm, nrm_hbm), (f1, mid_hbm), (cl, ct_hbm.at[:, pl.ds(0, rows)]), (wall, wall_hbm)
        )[i]
        return pltpu.make_async_copy(src, dst, osem.at[i])

    def xt_out(b):
        return pltpu.make_async_copy(xo.at[:, lanes(b)], xt_hbm.at[:, lanes(b)], osem.at[5 + b])

    w_copy = remote(wo_ref.at[part], wall.at[far_part], wsend.at[0], wrecv.at[0], other)
    w_pass = remote(wall.at[far_part], wall.at[far_part], wsend.at[1], wrecv.at[1], sibling)
    c_copy = remote(cl.at[:, pl.ds(0, BLK)], ct_hbm.at[:, pl.ds(rows, BLK)], wsend.at[2], wrecv.at[2], other)

    def ctx_copy(b):
        there = (b + near_blocks) % blocks
        return remote(
            call.at[pl.ds(0, cols), lanes(b)], call.at[pl.ds(cols, cols), lanes(there)],
            csend.at[b], crecv.at[b], other,
        )

    @pl.when((qb == 0) & (h == 0))
    def _():
        for i in (2, 0, 1):
            local(i).start()
        meet([other, sibling])
        w_copy.start()
        wall[0:cols, :] = wo_ref[...]
        local(2).wait()
        cl[...] = f3[...].astype(BF)
        c_copy.start()
        out(3).start()
        agc[...] = column(ag_ref[...])
        fgc[...] = column(fg_ref[...])
        local(0).wait()
        local(1).wait()
        for b in range(blocks):
            ls = slice(b * BLK, (b + 1) * BLK)
            v = f1[:, ls] if b < near_blocks else fb[:, b * BLK - rows : (b + 1) * BLK - rows].astype(F32)
            nrm[:, ls] = (v * norm_scale(v) * agc[...]).astype(BF)
            qkv_ref[:, ls] = dot(wq_ref[...], nrm[:, ls], ((1,), (0,))).astype(BF)
        out(1).start()
        for i in range(2):
            start = (1 - x) * rows if i else x * rows
            line = pad_ref[:, pl.ds(pl.multiple_of(start, BLK), rows)].astype(F32)
            padc[i * rows : (i + 1) * rows, :] = jnp.broadcast_to(line, (8, rows)).T
        ids = bid_ref[...]
        for hh in range(heads):
            line = jnp.zeros((1, SPAN), F32)
            for b in range(buckets):
                line = jnp.where(ids == b, rel_ref[b, hh], line)
            turned = pltpu.roll(
                jnp.broadcast_to(line, (BLK, SPAN)), 0, 1, stride=1, stride_axis=0
            )
            for i in range(7):
                g = min(max(i - 1, 0), 4)
                table[hh, i] = turned[:, BLK * (4 - g) : BLK * (5 - g)]

    @pl.when((qb == 1) & (h == 0))
    def _():
        w_copy.wait()
        w_pass.start()

    q_true = (qb + near_blocks * x) % blocks

    @pl.when(h == 0)
    def _():
        q_pos = q_true * BLK + lax.broadcasted_iota(jnp.int32, (1, BLK), 1)
        k_iota = lax.broadcasted_iota(jnp.int32, (BLK, BLK), 0)
        for kb in range(blocks):
            k_pos = (kb + near_blocks * x) % blocks * BLK + k_iota
            bound = 0
            q_doc = jnp.zeros((1, BLK), jnp.int32)
            k_doc = jnp.zeros((BLK, BLK), jnp.int32)
            for i in range(len_ref.shape[1]):
                bound = bound + len_ref[0, i]
                q_doc = q_doc + (q_pos >= bound).astype(jnp.int32)
                k_doc = k_doc + (k_pos >= bound).astype(jnp.int32)
            krows = slice(kb * BLK, (kb + 1) * BLK)
            seen = (padc[krows, 0:1] > 0.5) | (k_pos == q_pos)
            mask[krows, :] = jnp.where((k_doc == q_doc) & seen, 0.0, -1000000000.0)

    def head_rows(group):
        return pl.ds(pl.multiple_of(group * cols + h * dk, dk), dk)

    qh = qkv_ref[head_rows(0), lanes(qb)]
    peak = None
    for kb in range(blocks):
        krows = slice(kb * BLK, (kb + 1) * BLK)
        s = dot(qkv_ref[head_rows(1), krows], qh, ((0,), (0,)))
        diag = (kb + near_blocks * x) % blocks - q_true + blocks - 1
        s = s + table[h, diag] + mask[krows, :]
        score[krows, :] = s
        top = jnp.max(s, axis=0, keepdims=True)
        peak = top if peak is None else jnp.maximum(peak, top)
    total = jnp.zeros((1, BLK), F32)
    ctx = jnp.zeros((dk, BLK), F32)
    for kb in range(blocks):
        krows = slice(kb * BLK, (kb + 1) * BLK)
        e = jnp.exp(score[krows, :] - peak)
        total = total + jnp.sum(e, axis=0, keepdims=True)
        e_low = e.astype(BF)
        e_ref[0, 0, krows, :] = e_low
        ctx = ctx + dot(qkv_ref[head_rows(2), krows], e_low, ((1,), (0,)))
    inv = 1.0 / total
    inv_ref[0, 0] = inv
    call[head_rows(0), lanes(qb)] = (ctx * inv).astype(BF)

    @pl.when(h == heads - 1)
    def _():
        ctx_copy(qb).start()

    @pl.when((h == heads - 1) & (qb == blocks - 1))
    def _():
        w_pass.wait()
        wn[...] = wall[...].astype(F32).T.astype(BF)
        out(4).start()
        for i in range(blocks):
            b = (i + near_blocks) % blocks
            ctx_copy(i).wait()
            ls = slice(b * BLK, (b + 1) * BLK)
            v = dot(wn[...], call[:, ls], ((1,), (0,)))
            if b < near_blocks:
                v = v + f1[:, ls]
                f1[:, ls] = v
            else:
                v = v + fb[:, b * BLK - rows : (b + 1) * BLK - rows].astype(F32)
            xo[:, ls] = (v * norm_scale(v) * fgc[...]).astype(BF)
            xt_out(b).start()
        out(0).start()
        out(2).start()
        c_copy.wait()
        for i in range(5):
            out(i).wait()
        for b in range(blocks):
            xt_out(b).wait()


def front(rel, lengths, pad, again, fgain, wq, wo, tok, far, cot, heads, dk):
    d, rows = tok.shape
    seq = 2 * rows
    cols = heads * dk
    blocks = seq // BLK
    buckets = rel.shape[0]
    bids = jnp.asarray(lane_buckets(buckets))
    one = pl.Buffered(1)
    dma = pltpu.SemaphoreType.DMA
    any_spec = pl.BlockSpec(memory_space=pl.ANY)
    smem = pl.BlockSpec(memory_space=pltpu.SMEM)

    def full(v):
        return pl.BlockSpec(v.shape, lambda i, h: (0, 0), pipeline_mode=one)

    return pl.pallas_call(
        functools.partial(front_kernel, heads, dk, buckets, blocks),
        grid=(blocks, heads),
        in_specs=[smem, smem, full(bids), full(pad), full(again), full(fgain), full(wq), full(wo)]
        + [any_spec] * 3,
        out_specs=[
            pl.BlockSpec((1, 1, seq, BLK), lambda i, h: (h, i, 0, 0)),
            pl.BlockSpec((1, 1, 1, BLK), lambda i, h: (h, i, 0, 0)),
            pl.BlockSpec((3 * cols, seq), lambda i, h: (0, 0)),
        ]
        + [any_spec] * 6,
        out_shape=[
            jax.ShapeDtypeStruct((heads, blocks, seq, BLK), BF),
            jax.ShapeDtypeStruct((heads, blocks, 1, BLK), F32),
            jax.ShapeDtypeStruct((3 * cols, seq), BF),
            jax.ShapeDtypeStruct((2 * cols, seq), BF),
            jax.ShapeDtypeStruct((d, seq), BF),
            jax.ShapeDtypeStruct((d, seq), BF),
            jax.ShapeDtypeStruct((d, rows), F32),
            jax.ShapeDtypeStruct((d, seq), BF),
            jax.ShapeDtypeStruct((2 * cols, d), BF),
        ],
        scratch_shapes=[
            pltpu.VMEM((d, rows), F32),
            pltpu.VMEM((d, rows), BF),
            pltpu.VMEM((d, rows), F32),
            pltpu.VMEM((d, rows), BF),
            pltpu.VMEM((d, seq), BF),
            pltpu.VMEM((heads, 7, BLK, BLK), F32),
            pltpu.VMEM((seq, 8), F32),
            pltpu.VMEM((seq, BLK), F32),
            pltpu.VMEM((seq, BLK), F32),
            pltpu.VMEM((d, 1), F32),
            pltpu.VMEM((d, 1), F32),
            pltpu.VMEM((2 * cols, d), BF),
            pltpu.VMEM((d, 2 * cols), BF),
            pltpu.VMEM((2 * cols, seq), BF),
            pltpu.VMEM((d, seq), BF),
            dma((3,)), dma((5 + blocks,)), dma((3,)), dma((3,)), dma((blocks,)), dma((blocks,)),
        ],
        compiler_params=pltpu.CompilerParams(
            vmem_limit_bytes=FF_VMEM, collective_id=2, has_side_effects=True
        ),
        cost_estimate=pl.CostEstimate(
            flops=16 * heads * seq * seq * dk + 10 * seq * d * cols,
            bytes_accessed=2 * heads * seq * seq + 30 * rows * d,
            transcendentals=heads * seq * seq,
        ),
    )(rel, lengths, bids, pad, again, fgain, wq, wo, tok, far, cot)


def ff_kernel(
    steps, done, extra,
    xt_ref, wg_ref, wu_ref, ct_hbm, wo_hbm,
    grads_ref, din_hbm, near_hbm, far_hbm, hand_hbm,
    ct, wo, hid, dg, du, din, stage, r1, r2, r3, r4, xs, xr, of, nf,
    csem, wo_sem, s1, s2, s3, s4, t1, t2, t3, t4, xsem, osem, hsem,
):
    i = pl.program_id(0)
    phase, j = i // steps, i % steps
    f, total = hid.shape
    rows = total // 2
    d = xt_ref.shape[0]
    shard = d // 16
    dp, mp = lax.axis_index("dp"), lax.axis_index("mp")
    a = group_coords(dp // extra)
    peers = [flip(dp, m * extra) for m in GROUP_MASKS]
    other = (dp, 1 - mp)
    bufs = (r1, r2, r3, r4)
    sends, recvs = (s1, s2, s3, s4), (t1, t2, t3, t4)
    end = steps - 1

    def wo_copy(n):
        return pltpu.make_async_copy(wo_hbm.at[:, lanes(n)], wo.at[:, lanes(n)], wo_sem.at[n])

    def c_local(n):
        size = (BLK, rows)[n]
        part = pl.ds((rows, 0)[n], size)
        return pltpu.make_async_copy(ct_hbm.at[:, part], ct.at[:, part], csem.at[n])

    c_far = remote(
        ct_hbm.at[:, pl.ds(BLK, BLK)], ct.at[:, pl.ds(rows + BLK, BLK)], csem.at[2], csem.at[3], other
    )

    def hop(level, s, w):
        half = 8 >> level
        away = pl.ds((1 - a[level]) * half, half)
        src = stage.at[w, away] if level == 0 else bufs[level - 1].at[s, away]
        return remote(src, bufs[level].at[s], sends[level].at[s], recvs[level].at[s], (peers[level], mp))

    def hand_copy(s):
        return pltpu.make_async_copy(r1.at[s], hand_hbm.at[s - 3 * done], hsem.at[s - 3 * done])

    def absorb(level, step, w):
        s = step * 3 + w
        half = 8 >> level
        copy = hop(level, s, w)
        copy.wait_recv()
        copy.wait_send()
        keep = pl.ds(a[level] * half, half)
        kept = stage[w, keep] if level == 0 else bufs[level - 1][s, keep]
        both = kept.astype(F32) + bufs[level][s].astype(F32)
        if level == 3:
            grads_ref[w, :, lanes(step)] = both[0]
            return
        bufs[level][s] = both.astype(BF)
        if level > 0:
            hop(level + 1, s, w).start()
            return
        if isinstance(step, int):
            hand_copy(s).start()
            return

        @pl.when(step < done)
        def _():
            hop(1, s, w).start()

        @pl.when(step >= done)
        def _():
            hand_copy(s).start()

    def absorb_step(level, step):
        def one(w, carry):
            absorb(level, step, w)
            return carry

        lax.fori_loop(0, 3, one, 0)

    @pl.when(i == 0)
    def _():
        meet([(p, mp) for p in peers] + [other])
        c_far.start()
        c_local(0).start()
        for n in range(steps):
            wo_copy(n).start()
        c_local(1).start()
        din[...] = jnp.zeros_like(din)
        stage[...] = jnp.zeros_like(stage)
        c_local(0).wait()

    @pl.when(phase == 0)
    def _():
        wo_copy(j).wait()

    @pl.when(i == steps)
    def _():
        c_far.wait()

    scale = np.float32(np.sqrt(2 / np.pi))
    frows = lanes(j)

    def block(tok, acc):
        gate = dot(wg_ref[...], xt_ref[:, tok], ((0,), (0,)))
        up = dot(wu_ref[...], xt_ref[:, tok], ((0,), (0,)))
        dh = dot(wo[:, frows], ct[:, tok], ((0,), (0,)))
        sq = gate * gate
        t = jnp.tanh(scale * gate * (1.0 + 0.044715 * sq))
        half = 0.5 * (1.0 + t)
        act = gate * half
        slope = half + 0.5 * gate * (1.0 - t * t) * (scale * (1.0 + (3 * 0.044715) * sq))
        hid[frows, tok] = (act * up).astype(BF)
        dgr = (dh * (up * slope)).astype(BF)
        dur = (dh * act).astype(BF)
        dg[frows, tok] = dgr
        du[frows, tok] = dur
        din[:, acc] += dot(wg_ref[...], dgr, ((1,), (0,))) + dot(wu_ref[...], dur, ((1,), (0,)))

    x_copy = remote(xs, xr, xsem.at[0], xsem.at[1], other)

    @pl.when(phase < 2)
    def _():
        block(lanes(phase + rows // BLK), lanes(phase))

    @pl.when(i == 2 * steps - 1)
    def _():
        xs[...] = din[...].astype(BF)
        x_copy.start()
        din[...] = jnp.zeros_like(din)
        c_local(1).wait()

    per = 4 * shard

    @pl.when(phase == 2)
    def _():
        for n in range(rows // BLK):
            block(pl.ds(n * BLK, BLK), pl.ds(n * BLK, BLK))

        @pl.when(j > 0)
        def _():
            absorb(0, j - 1, 2)

        for w in range(3):
            right = (hid, dg, du)[w][frows, :]
            for q in range(4):
                rs = slice(q * per, (q + 1) * per)
                left = ct[rs, :] if w == 0 else xt_ref[rs, :]
                part = dot(left, right, ((1,), (1,)))
                for k in range(4):
                    stage[w, block_position(4 * q + k), 0:shard, :] = part[
                        k * shard : (k + 1) * shard
                    ].astype(BF)
            hop(0, j * 3 + w, w).start()
            if w > 0:
                absorb(0, j, w - 1)

        for when, events in ((3, ((1, 0),)), (5, ((1, 1), (2, 0))), (6, ((3, 0),))):
            @pl.when(j == when)
            def _():
                for level, step in events:
                    absorb_step(level, step)

    @pl.when(i == 3 * steps - 1)
    def _():
        absorb(0, end, 2)

        def out_part(n):
            return dot(wo[...], hid[:, n * BLK : (n + 1) * BLK], ((1,), (0,)))

        half = rows // BLK
        for n in range(half):
            of[:, n * BLK : (n + 1) * BLK] = out_part(half + n).astype(BF)
        far_copy = pltpu.make_async_copy(of, far_hbm, osem.at[0])
        far_copy.start()
        absorb_step(1, 2)
        absorb_step(2, 1)
        x_copy.wait()
        din[...] += xr[...].astype(F32)
        din_copy = pltpu.make_async_copy(din, din_hbm, osem.at[2])
        din_copy.start()
        nf[:, 0:BLK] = out_part(0)
        absorb_step(2, 2)
        absorb_step(3, 1)
        for n in range(1, half):
            nf[:, n * BLK : (n + 1) * BLK] = out_part(n)
        near_copy = pltpu.make_async_copy(nf, near_hbm, osem.at[1])
        near_copy.start()
        absorb_step(3, 2)

        def flush(s, carry):
            hand_copy(s).wait()
            return carry

        lax.fori_loop(3 * done, 3 * steps, flush, 0)
        far_copy.wait()
        near_copy.wait()
        din_copy.wait()


def ff_all(xt, ct, w2, wo, extra):
    d, total = xt.shape
    f = wo.shape[1]
    rows = total // 2
    steps = f // BLK
    done = FF_DONE
    chunks = 3 * steps
    kept = 3 * done
    shard = d // 16
    spad = -(-shard // 16) * 16
    dma = pltpu.SemaphoreType.DMA
    any_spec = pl.BlockSpec(memory_space=pl.ANY)
    return pl.pallas_call(
        functools.partial(ff_kernel, steps, done, extra),
        grid=(3 * steps,),
        in_specs=[
            pl.BlockSpec((d, total), lambda i: (0, 0), pipeline_mode=pl.Buffered(1)),
            pl.BlockSpec((None, d, BLK), lambda i: (0, 0, i % steps)),
            pl.BlockSpec((None, d, BLK), lambda i: (1, 0, i % steps)),
            any_spec,
            any_spec,
        ],
        out_specs=[pl.BlockSpec((3, spad, done * BLK), lambda i: (0, 0, 0))] + [any_spec] * 4,
        out_shape=[
            jax.ShapeDtypeStruct((3, spad, done * BLK), F32),
            jax.ShapeDtypeStruct((d, rows), F32),
            jax.ShapeDtypeStruct((d, rows), F32),
            jax.ShapeDtypeStruct((d, rows), BF),
            jax.ShapeDtypeStruct((chunks - kept, 8, spad, BLK), BF),
        ],
        scratch_shapes=[
            pltpu.VMEM((d, total), BF),
            pltpu.VMEM((d, f), BF),
            pltpu.VMEM((f, total), BF),
            pltpu.VMEM((f, total), BF),
            pltpu.VMEM((f, total), BF),
            pltpu.VMEM((d, rows), F32),
            pltpu.VMEM((3, 16, spad, BLK), BF),
            pltpu.VMEM((chunks, 8, spad, BLK), BF),
            pltpu.VMEM((kept, 4, spad, BLK), BF),
            pltpu.VMEM((kept, 2, spad, BLK), BF),
            pltpu.VMEM((kept, 1, spad, BLK), BF),
            pltpu.VMEM((d, rows), BF),
            pltpu.VMEM((d, rows), BF),
            pltpu.VMEM((d, rows), BF),
            pltpu.VMEM((d, rows), F32),
            dma((4,)),
            dma((steps,)),
            dma((chunks,)), dma((kept,)), dma((kept,)), dma((kept,)),
            dma((chunks,)), dma((kept,)), dma((kept,)), dma((kept,)),
            dma((2,)),
            dma((3,)),
            dma((chunks - kept,)),
        ],
        compiler_params=pltpu.CompilerParams(
            vmem_limit_bytes=FF_VMEM, collective_id=0, has_side_effects=True
        ),
        cost_estimate=pl.CostEstimate(
            flops=18 * total * d * f,
            bytes_accessed=6 * d * f + 16 * total * d,
            transcendentals=total * f,
        ),
    )(xt, w2, w2, ct, wo)


def tail_kernel(
    heads, dk, buckets, blocks, extra, later,
    bid_ref, qkv_ref, e_ref, inv_ref, wall_ref, ctx_ref, wq_ref, ag_ref, fg_ref,
    din_hbm, mid_hbm, cot_hbm, tok_hbm, nrm_hbm, far_hbm, hand_hbm,
    ig_hbm, g_ref, small_ref, grads_ref, back_hbm,
    f1, f2, f3, nrm, wn, alow, dctx, dcs, osend, orecv, gsum, fsum, agc, fgc,
    dp_s, dkv, tally, dproj, grad, dns, dnr,
    stage, t1, t2, t3, t4, hk, h2, h3, h4, sb, rb,
    lsem, ksem, xs_sem, xr_sem, cs_sem, cr_sem, bs_sem, br_sem, hs2, hs3, hs4, hr2, hr3, hr4,
):
    qb, h = pl.program_id(0), pl.program_id(1)
    step_id = qb * heads + h
    dp, x = lax.axis_index("dp"), lax.axis_index("mp")
    d, rows = f2.shape
    seq = 2 * rows
    cols = heads * dk
    shard = d // 16
    a = group_coords(dp // extra)
    peers = [flip(dp, m * extra) for m in GROUP_MASKS]
    other = (dp, 1 - x)
    bufs = (stage, t1, t2, t3, t4)
    hbufs = (None, hk, h2, h3, h4)
    hsends, hrecvs = (None, hs2, hs3, hs4), (None, hr2, hr3, hr4)
    near_blocks = blocks // 2

    def local(i):
        src, dst = ((din_hbm, f1), (mid_hbm, f2), (cot_hbm, f3), (tok_hbm, f2), (nrm_hbm, nrm))[i]
        return pltpu.make_async_copy(src, dst, lsem.at[i])

    dctx_copy = remote(dcs, dctx.at[:, pl.ds(rows, rows)], xs_sem.at[0], xr_sem.at[0], other)
    o_copy = remote(osend, orecv, xs_sem.at[1], xr_sem.at[1], other)
    back_copy = remote(far_hbm, back_hbm, xs_sem.at[2], xr_sem.at[2], other)

    def dn_copy(r):
        return remote(dns.at[r], dnr.at[r], xs_sem.at[3 + r], xr_sem.at[3 + r], other)

    def hop(level):
        half = 8 >> level
        away = pl.ds((1 - a[level]) * half, half)
        return remote(
            bufs[level].at[away], bufs[level + 1], cs_sem.at[level], cr_sem.at[level], (peers[level], x)
        )

    def absorb(level):
        half = 8 >> level
        hop(level).wait()
        both = bufs[level][pl.ds(a[level] * half, half)].astype(F32) + bufs[level + 1][...].astype(F32)
        if level < 3:
            bufs[level + 1][...] = both.astype(BF)
            hop(level + 1).start()
        else:
            for i in range(4):
                g_ref[i] = both[0, :, i * cols : (i + 1) * cols]

    def keep_copy(s):
        return pltpu.make_async_copy(hand_hbm.at[s, pl.ds(a[1] * 4, 4)], hk.at[s], ksem.at[s])

    def hand_hop(level, s):
        half = 8 >> level
        away = pl.ds((1 - a[level]) * half, half)
        src = hand_hbm.at[s, away] if level == 1 else hbufs[level].at[s, away]
        return remote(src, hbufs[level + 1].at[s], hsends[level].at[s], hrecvs[level].at[s], (peers[level], x))

    def hand_start(block):
        def one(w, carry):
            keep_copy(block * 3 + w).start()
            hand_hop(1, block * 3 + w).start()
            return carry

        lax.fori_loop(0, 3, one, 0)

    def hand_absorb(level, block):
        def one(w, carry):
            s = block * 3 + w
            half = 8 >> level
            hand_hop(level, s).wait()
            if level == 1:
                keep_copy(s).wait()
                kept = hk[s]
            else:
                kept = hbufs[level][s, pl.ds(a[level] * half, half)]
            both = kept.astype(F32) + hbufs[level + 1][s].astype(F32)
            if level < 3:
                hbufs[level + 1][s] = both.astype(BF)
                hand_hop(level + 1, s).start()
            else:
                grads_ref[w, :, block * BLK : (block + 1) * BLK] = both[0]
            return carry

        lax.fori_loop(0, 3, one, 0)

    def round_copy(i):
        who = other if i == 4 else (peers[i], x)
        return remote(sb.at[i], rb.at[i], bs_sem.at[i], br_sem.at[i], who)

    def round_end(i):
        round_copy(i).wait()
        sb[i + 1] = sb[i] + rb[i]
        if i < 4:
            round_copy(i + 1).start()

    def out_copy(r):
        return pltpu.make_async_copy(f3.at[:, lanes(r)], ig_hbm.at[:, lanes(r)], lsem.at[5 + r])

    def lane_sum(v):
        total = v[:, 0:128]
        for i in range(1, v.shape[1] // 128):
            total = total + v[:, i * 128 : (i + 1) * 128]
        return total

    def dn_part(b):
        ls = slice(b * BLK, (b + 1) * BLK)
        part = dot(wn[...], dproj[:, ls], ((1,), (0,)))
        gsum[...] += lane_sum(nrm[:, ls].astype(F32) * part)
        return part

    @pl.when(step_id == 0)
    def _():
        for i in range(3):
            local(i).start()
        meet([(p, x) for p in peers] + [other])
        hand_start(0)
        if later > 1:
            hand_start(1)
        dkv[...] = jnp.zeros_like(dkv)
        tally[...] = jnp.zeros_like(tally)
        stage[...] = jnp.zeros_like(stage)
        fsum[...] = jnp.zeros_like(fsum)
        gsum[...] = jnp.zeros_like(gsum)
        agc[...] = column(ag_ref[...])
        fgc[...] = column(fg_ref[...])
        for i in range(3):
            local(i).wait()
        for r in range(near_blocks):
            ls = slice(r * BLK, (r + 1) * BLK)
            v = f2[:, ls]
            c = f1[:, ls]
            scale = norm_scale(v)
            n = v * scale
            cg = c * fgc[...]
            m = jnp.mean(cg * n, axis=0, keepdims=True)
            gm = f3[:, ls] + scale * (cg - n * m)
            fsum[...] += lane_sum(c * n)
            f1[:, ls] = gm
            alow[:, ls] = gm.astype(BF)
        for i in range(3, 5):
            local(i).start()
        dcs[...] = dot(wall_ref[cols : 2 * cols, :], alow[...], ((1,), (0,))).astype(BF)
        dctx_copy.start()
        dctx[:, :rows] = dot(wall_ref[0:cols, :], alow[...], ((1,), (0,))).astype(BF)
        osend[...] = dot(alow[...], ctx_ref[cols : 2 * cols, :rows], ((1,), (1,))).astype(BF)
        grad[:, 3 * cols : 4 * cols] = dot(alow[...], ctx_ref[0:cols, :rows], ((1,), (1,)))
        wn[...] = wq_ref[...].astype(F32).T.astype(BF)
        dctx_copy.wait()
        o_copy.start()
        back_copy.start()

    def head_rows(group):
        return pl.ds(pl.multiple_of(group * cols + h * dk, dk), dk)

    inv = inv_ref[0, 0]
    qh = qkv_ref[head_rows(0), lanes(qb)]
    scaled = (dctx[head_rows(0), lanes(qb)].astype(F32) * inv).astype(BF)
    inner = jnp.zeros((1, BLK), F32)
    for kb in range(blocks):
        krows = slice(kb * BLK, (kb + 1) * BLK)
        g = dot(qkv_ref[head_rows(2), krows], scaled, ((0,), (0,)))
        dp_s[krows, :] = g
        inner = inner + jnp.sum(e_ref[0, 0, krows, :].astype(F32) * g, axis=0, keepdims=True)
    inner = inner * inv
    dq = jnp.zeros((dk, BLK), F32)
    q_true = (qb + near_blocks * x) % blocks
    for kb in range(blocks):
        krows = slice(kb * BLK, (kb + 1) * BLK)
        e = e_ref[0, 0, krows, :]
        ds = (e.astype(F32) * (dp_s[krows, :] - inner)).astype(BF)
        dkv[head_rows(0), krows] += dot(qh, ds, ((1,), (1,)))
        dkv[head_rows(1), krows] += dot(scaled, e, ((1,), (1,)))
        dq = dq + dot(qkv_ref[head_rows(1), krows], ds, ((1,), (0,)))
        diag = (kb + near_blocks * x) % blocks - q_true + blocks - 1
        tally[h, diag] += ds.astype(F32)
    dproj[head_rows(0), lanes(qb)] = dq.astype(BF)

    @pl.when(step_id == 5)
    def _():
        hand_absorb(1, 0)
        if later > 2:
            hand_start(2)

    @pl.when(step_id == blocks * heads - 1)
    def _():
        dproj[cols : 3 * cols, :] = dkv[...].astype(BF)
        for i in range(3, 5):
            local(i).wait()
        for r in range(near_blocks):
            dns[r] = dn_part(near_blocks + r).astype(BF)
            dn_copy(r).start()
        if later > 1:
            hand_absorb(1, 1)
        if later > 3:
            hand_start(3)
        grad[:, 0 : 3 * cols] = dot(nrm[...], dproj[...], ((1,), (1,)))
        o_copy.wait()
        grad[:, 3 * cols : 4 * cols] += orecv[...].astype(F32)
        for k in range(16):
            stage[block_position(k), 0:shard, :] = grad[k * shard : (k + 1) * shard, :].astype(BF)
        hop(0).start()
        hand_absorb(2, 0)
        for r in range(near_blocks):
            f3[:, r * BLK : (r + 1) * BLK] = dn_part(r)
        absorb(0)
        if later > 1:
            hand_absorb(2, 1)
        hand_absorb(3, 0)
        ids = bid_ref[...]
        hot = ids == lax.broadcasted_iota(jnp.int32, (buckets, SPAN), 0)
        out_lane = lax.broadcasted_iota(jnp.int32, (buckets, 128), 1)
        sub = lax.broadcasted_iota(jnp.int32, (8, SPAN), 0)
        out = jnp.zeros((buckets, 128), F32)
        for hh in range(heads):
            line = jnp.zeros((8, SPAN), F32)
            for g in range(BLK // 8):
                group = slice(8 * g, 8 * g + 8)
                t = [tally[hh, i, group, :] for i in range(7)]
                parts = [t[5] + t[6], t[4], t[3], t[2], t[1] + t[0]]
                strip = jnp.concatenate(parts + [jnp.zeros((8, BLK), F32)], axis=1)
                line = line + (strip if g == 0 else pltpu.roll(strip, SPAN - 8 * g, 1))
            for bit in (1, 2, 4):
                line = jnp.where((sub // bit) % 2 == 1, pltpu.roll(line, SPAN - bit, 1), line)
            sums = jnp.sum(line, axis=0, keepdims=True)
            col = jnp.sum(jnp.where(hot, sums, 0.0), axis=1, keepdims=True)
            out = jnp.where(out_lane == x * heads + hh, col, out)
        sb[0] = jnp.zeros(sb.shape[1:], F32)
        sb[0, 0:buckets, :] = out
        again = jnp.sum(gsum[...].T, axis=0, keepdims=True) / ag_ref[...]
        fgain = jnp.sum(fsum[...].T, axis=0, keepdims=True)
        lines = -(-d // 128)
        for i in range(lines):
            n = min(128, d - 128 * i)
            sb[0, buckets + i : buckets + i + 1, 0:n] = again[:, 128 * i : 128 * i + n]
            sb[0, buckets + lines + i : buckets + lines + i + 1, 0:n] = fgain[:, 128 * i : 128 * i + n]
        round_copy(0).start()
        if later > 2:
            hand_absorb(1, 2)
        round_end(0)
        if later > 1:
            hand_absorb(3, 1)
        round_end(1)
        if later > 2:
            hand_absorb(2, 2)
        round_end(2)
        if later > 3:
            hand_absorb(1, 3)
        absorb(1)
        round_end(3)
        if later > 2:
            hand_absorb(3, 2)
        round_end(4)
        small_ref[...] = sb[5]
        if later > 3:
            hand_absorb(2, 3)
        for r in range(near_blocks):
            ls = slice(r * BLK, (r + 1) * BLK)
            dn_copy(r).wait()
            c = f3[:, ls] + dnr[r].astype(F32)
            v = f2[:, ls]
            scale = norm_scale(v)
            n = v * scale
            cg = c * agc[...]
            m = jnp.mean(cg * n, axis=0, keepdims=True)
            f3[:, ls] = f1[:, ls] + scale * (cg - n * m)
            out_copy(r).start()
            if r == 0:
                absorb(2)
                if later > 3:
                    hand_absorb(3, 3)
        absorb(3)
        back_copy.wait()
        for r in range(near_blocks):
            out_copy(r).wait()


def tail(qkv, e, inv, wall, ctx, wq, again, fgain, din, mid, cot, tok, nrm, far, hand,
         buckets, heads, dk, extra):
    d, rows = tok.shape
    seq = 2 * rows
    cols = heads * dk
    blocks = seq // BLK
    near = blocks // 2
    shard = d // 16
    spad = -(-shard // 16) * 16
    chunks = hand.shape[0]
    later = chunks // 3
    lines = -(-(buckets + 2 * -(-d // 128)) // 8) * 8
    bids = jnp.asarray(lane_buckets(buckets))
    one = pl.Buffered(1)
    dma = pltpu.SemaphoreType.DMA
    any_spec = pl.BlockSpec(memory_space=pl.ANY)

    def full(v):
        return pl.BlockSpec(v.shape, lambda i, h: (0, 0), pipeline_mode=one)

    return pl.pallas_call(
        functools.partial(tail_kernel, heads, dk, buckets, blocks, extra, later),
        grid=(blocks, heads),
        in_specs=[
            full(bids),
            full(qkv),
            pl.BlockSpec((1, 1, seq, BLK), lambda i, h: (h, i, 0, 0)),
            pl.BlockSpec((1, 1, 1, BLK), lambda i, h: (h, i, 0, 0)),
            full(wall),
            full(ctx),
            full(wq),
            full(again),
            full(fgain),
        ]
        + [any_spec] * 7,
        out_specs=[
            any_spec,
            pl.BlockSpec((4, spad, cols), lambda i, h: (0, 0, 0)),
            pl.BlockSpec((lines, 128), lambda i, h: (0, 0)),
            pl.BlockSpec((3, spad, later * BLK), lambda i, h: (0, 0, 0)),
            any_spec,
        ],
        out_shape=[
            jax.ShapeDtypeStruct((d, rows), F32),
            jax.ShapeDtypeStruct((4, spad, cols), F32),
            jax.ShapeDtypeStruct((lines, 128), F32),
            jax.ShapeDtypeStruct((3, spad, later * BLK), F32),
            jax.ShapeDtypeStruct(far.shape, BF),
        ],
        scratch_shapes=[
            pltpu.VMEM((d, rows), F32),
            pltpu.VMEM((d, rows), F32),
            pltpu.VMEM((d, rows), F32),
            pltpu.VMEM((d, seq), BF),
            pltpu.VMEM((d, 3 * cols), BF),
            pltpu.VMEM((d, rows), BF),
            pltpu.VMEM((cols, seq), BF),
            pltpu.VMEM((cols, rows), BF),
            pltpu.VMEM((d, cols), BF),
            pltpu.VMEM((d, cols), BF),
            pltpu.VMEM((d, 128), F32),
            pltpu.VMEM((d, 128), F32),
            pltpu.VMEM((d, 1), F32),
            pltpu.VMEM((d, 1), F32),
            pltpu.VMEM((seq, BLK), F32),
            pltpu.VMEM((2 * cols, seq), F32),
            pltpu.VMEM((heads, 7, BLK, BLK), F32),
            pltpu.VMEM((3 * cols, seq), BF),
            pltpu.VMEM((d, 4 * cols), F32),
            pltpu.VMEM((near, d, BLK), BF),
            pltpu.VMEM((near, d, BLK), BF),
            pltpu.VMEM((16, spad, 4 * cols), BF),
            pltpu.VMEM((8, spad, 4 * cols), BF),
            pltpu.VMEM((4, spad, 4 * cols), BF),
            pltpu.VMEM((2, spad, 4 * cols), BF),
            pltpu.VMEM((1, spad, 4 * cols), BF),
            pltpu.VMEM((chunks, 4, spad, BLK), BF),
            pltpu.VMEM((chunks, 4, spad, BLK), BF),
            pltpu.VMEM((chunks, 2, spad, BLK), BF),
            pltpu.VMEM((chunks, 1, spad, BLK), BF),
            pltpu.VMEM((6, lines, 128), F32),
            pltpu.VMEM((5, lines, 128), F32),
            dma((5 + near,)),
            dma((chunks,)),
            dma((3 + near,)), dma((3 + near,)),
            dma((4,)), dma((4,)),
            dma((5,)), dma((5,)),
            dma((chunks,)), dma((chunks,)), dma((chunks,)),
            dma((chunks,)), dma((chunks,)), dma((chunks,)),
        ],
        compiler_params=pltpu.CompilerParams(
            vmem_limit_bytes=FF_VMEM, collective_id=1, has_side_effects=True
        ),
        cost_estimate=pl.CostEstimate(
            flops=32 * heads * seq * seq * dk + 8 * seq * d * 3 * cols,
            bytes_accessed=2 * heads * seq * seq + 30 * rows * d,
            transcendentals=0,
        ),
    )(bids, qkv, e, inv, wall, ctx, wq, again, fgain, din, mid, cot, tok, nrm, far, hand)


def take(array, index):
    return lax.dynamic_index_in_dim(array, index, 0, keepdims=False)


def per_device(
    tokens,
    cotangent,
    doc_lengths,
    pad_mask,
    attn_gain,
    qkv_weight,
    rel_table,
    out_weight,
    ff_gain,
    ff_in_weight,
    ff_out_weight,
):
    rows, d = tokens.shape
    n_dp = lax.axis_size("dp")
    n_mp = lax.axis_size("mp")
    cols = qkv_weight.shape[2]
    buckets, heads = rel_table.shape
    dk = cols // heads
    me = lax.axis_index("dp")
    shard = d // n_dp
    extra = n_dp // 16

    def hop(v, mask):
        return lax.ppermute(v, "dp", [(i, i ^ mask) for i in range(n_dp)])

    def bit(b):
        return (me >> b) & 1

    def reduce_rest(parts, low_bits):
        for b in reversed(range(low_bits)):
            halves = [p.reshape((2, p.shape[0] // 2) + p.shape[1:]) for p in parts]
            away = sum(take(p, 1 - bit(b)).astype(F32) for p in halves).astype(BF)
            parts = [take(p, bit(b)) for p in halves] + [hop(away, 1 << b)]
        return sum(p.astype(F32) for p in parts)[0]

    def finish(g):
        g = g[: d // 16]
        if extra == 1:
            return g
        return reduce_rest([g.reshape(extra, shard, g.shape[1])], extra.bit_length() - 1)

    tok = tokens.T
    cot = cotangent.T
    far = lax.ppermute(tok.astype(BF), "mp", [(0, 1), (1, 0)])
    w2 = jnp.transpose(ff_in_weight, (1, 0, 2))
    wq = jnp.transpose(qkv_weight, (1, 2, 0)).reshape(3 * cols, d)
    again, fgain = attn_gain.reshape(1, d), ff_gain.reshape(1, d)

    e, inv, qkv, ctx, nrm, xt, mid, ct, wall = front(
        rel_table, doc_lengths, pad_mask, again, fgain, wq, out_weight.T, tok, far, cot, heads, dk
    )
    early, din, near_out, far_out, hand = ff_all(xt, ct, w2, ff_out_weight, extra)
    input_grad, last, small, late, back = tail(
        qkv, e, inv, wall, ctx, wq, again, fgain, din, mid, cot, tok, nrm, far_out, hand,
        buckets, heads, dk, extra,
    )
    result = (mid + near_out + back.astype(F32)).T

    ffo, ffg, ffu = (finish(jnp.concatenate([early[i], late[i]], axis=1)) for i in range(3))
    grad_qkv = jnp.stack([finish(last[i]) for i in range(3)], axis=1)
    for b in range(extra.bit_length() - 1):
        small = small + hop(small, 1 << b)
    lines = -(-d // 128)
    return (
        result,
        input_grad.T,
        small[buckets : buckets + lines].reshape(-1)[:d],
        grad_qkv,
        small[:buckets, : heads * n_mp],
        finish(last[3]),
        small[buckets + lines : buckets + 2 * lines].reshape(-1)[:d],
        jnp.stack([ffg, ffu], axis=1),
        ffo,
    )


def solution(mesh):
    return jax.shard_map(
        per_device,
        mesh=mesh,
        in_specs=(
            P(("dp", "mp"), None),
            P(("dp", "mp"), None),
            P("dp", None),
            P("dp", None),
            P(),
            P(None, None, "mp"),
            P(None, "mp"),
            P(None, "mp"),
            P(),
            P(None, None, "mp"),
            P(None, "mp"),
        ),
        out_specs=(
            P(("dp", "mp"), None),
            P(("dp", "mp"), None),
            P(),
            P("dp", None, "mp"),
            P(),
            P("dp", "mp"),
            P(),
            P("dp", None, "mp"),
            P("dp", "mp"),
        ),
        check_vma=False,
    )
```

```python
import functools

import jax
import jax.numpy as jnp
import numpy as np
from jax import lax
from jax.experimental import pallas as pl
from jax.experimental.pallas import tpu as pltpu
from jax.sharding import PartitionSpec as P

MAXDIST = 128
norm_eps = 1e-06
BLK = 256
SPAN = 6 * BLK
REACH = 2
BF = jnp.bfloat16
F32 = jnp.float32
FF_VMEM = 63 << 20
FF_DONE = 2


def bucket_of(offsets, buckets, reach):
    half_range = buckets // 2
    upper_half = (offsets > 0).astype(np.int32) * half_range
    distance = np.abs(offsets)
    exact_range = half_range // 2
    safe_dist = np.maximum(distance, 1)
    log_bucket = exact_range + (
        np.log(safe_dist / exact_range) / np.log(reach / exact_range) * (half_range - exact_range)
    ).astype(np.int32)
    log_bucket = np.minimum(log_bucket, half_range - 1)
    return (upper_half + np.where(distance < exact_range, distance, log_bucket)).astype(np.int32)


def lane_buckets(buckets):
    lanes = np.arange(SPAN)
    shifted = np.where(lanes < 5 * BLK, lanes, lanes - SPAN)
    return bucket_of(REACH * BLK - shifted, buckets, MAXDIST).reshape(1, SPAN)


def dot(a, b, contract):
    return lax.dot_general(a, b, (contract, ((), ())), preferred_element_type=F32)


def flip(index, mask):
    out = index
    bit = 1
    while bit <= mask:
        if mask & bit:
            out = out + bit * (1 - 2 * (index // bit % 2))
        bit *= 2
    return out


GROUP_MASKS = (1, 2, 4, 12)


def group_coords(g):
    b = [g // (1 << i) % 2 for i in range(4)]
    return [b[0], b[1], (b[2] + b[3]) % 2, b[3]]


Y_FIRST = (0, 1, 2, 3)
Z_FIRST = (0, 2, 3, 1)


def block_position(k, order):
    b = [k >> i & 1 for i in range(4)]
    c = [b[0], b[1], b[2] ^ b[3], b[3]]
    return sum(c[order[i]] << (3 - i) for i in range(4))


def column(line):
    return jnp.broadcast_to(line, (8, line.shape[1])).T[:, 0:1]


def norm_scale(v):
    return lax.rsqrt(jnp.mean(v * v, axis=0, keepdims=True) + norm_eps)


def lanes(block):
    return pl.ds(pl.multiple_of(block * BLK, BLK), BLK)


def remote(src, dst, send, recv, who):
    return pltpu.make_async_remote_copy(
        src_ref=src,
        dst_ref=dst,
        send_sem=send,
        recv_sem=recv,
        device_id=who,
        device_id_type=pl.DeviceIdType.MESH,
    )


def meet(devices):
    barrier = pltpu.get_barrier_semaphore()
    for who in devices:
        pl.semaphore_signal(barrier, inc=1, device_id=who, device_id_type=pl.DeviceIdType.MESH)
    pl.semaphore_wait(barrier, len(devices))


def front_kernel(
    heads, dk, buckets, blocks,
    rel_ref, len_ref, bid_ref, pad_ref, ag_ref, fg_ref, wq_ref, wo_ref,
    tok_hbm, far_hbm, cot_hbm,
    e_ref, inv_ref, qkv_ref, ctx_hbm, nrm_hbm, xt_hbm, mid_hbm, ct_hbm, wall_hbm,
    f1, fb, f3, cl, nrm, table, padc, mask, score, agc, fgc, wall, wn, call, xo,
    lsem, osem, wsend, wrecv, csend, crecv,
):
    qb, h = pl.program_id(0), pl.program_id(1)
    dp, x = lax.axis_index("dp"), lax.axis_index("mp")
    d, rows = f1.shape
    cols = heads * dk
    half = cols // 2
    core = dp % 2
    other = (dp, 1 - x)
    sibling = (dp + 1 - 2 * core, x)
    near_blocks = blocks // 2
    part = pl.ds(core * half, half)
    far_part = pl.ds(cols + core * half, half)

    def local(i):
        src, dst = ((tok_hbm, f1), (far_hbm, fb), (cot_hbm, f3))[i]
        return pltpu.make_async_copy(src, dst, lsem.at[i])

    def out(i):
        src, dst = (
            (call, ctx_hbm), (nrm, nrm_hbm), (f1, mid_hbm), (cl, ct_hbm.at[:, pl.ds(0, rows)]), (wall, wall_hbm)
        )[i]
        return pltpu.make_async_copy(src, dst, osem.at[i])

    def xt_out(b):
        return pltpu.make_async_copy(xo.at[:, lanes(b)], xt_hbm.at[:, lanes(b)], osem.at[5 + b])

    w_copy = remote(wo_ref.at[part], wall.at[far_part], wsend.at[0], wrecv.at[0], other)
    w_pass = remote(wall.at[far_part], wall.at[far_part], wsend.at[1], wrecv.at[1], sibling)
    c_copy = remote(cl.at[:, pl.ds(0, BLK)], ct_hbm.at[:, pl.ds(rows, BLK)], wsend.at[2], wrecv.at[2], other)

    def ctx_copy(b):
        there = (b + near_blocks) % blocks
        return remote(
            call.at[pl.ds(0, cols), lanes(b)], call.at[pl.ds(cols, cols), lanes(there)],
            csend.at[b], crecv.at[b], other,
        )

    @pl.when((qb == 0) & (h == 0))
    def _():
        for i in (2, 0, 1):
            local(i).start()
        meet([other, sibling])
        w_copy.start()
        wall[0:cols, :] = wo_ref[...]
        local(2).wait()
        cl[...] = f3[...].astype(BF)
        c_copy.start()
        out(3).start()
        agc[...] = column(ag_ref[...])
        fgc[...] = column(fg_ref[...])
        local(0).wait()
        local(1).wait()
        for b in range(blocks):
            ls = slice(b * BLK, (b + 1) * BLK)
            v = f1[:, ls] if b < near_blocks else fb[:, b * BLK - rows : (b + 1) * BLK - rows].astype(F32)
            nrm[:, ls] = (v * norm_scale(v) * agc[...]).astype(BF)
            qkv_ref[:, ls] = dot(wq_ref[...], nrm[:, ls], ((1,), (0,))).astype(BF)
        out(1).start()
        for i in range(2):
            start = (1 - x) * rows if i else x * rows
            line = pad_ref[:, pl.ds(pl.multiple_of(start, BLK), rows)].astype(F32)
            padc[i * rows : (i + 1) * rows, :] = jnp.broadcast_to(line, (8, rows)).T
        ids = bid_ref[...]
        for hh in range(heads):
            line = jnp.zeros((1, SPAN), F32)
            for b in range(buckets):
                line = jnp.where(ids == b, rel_ref[b, hh], line)
            turned = pltpu.roll(
                jnp.broadcast_to(line, (BLK, SPAN)), 0, 1, stride=1, stride_axis=0
            )
            for i in range(7):
                g = min(max(i - 1, 0), 4)
                table[hh, i] = turned[:, BLK * (4 - g) : BLK * (5 - g)]

    @pl.when((qb == 1) & (h == 0))
    def _():
        w_copy.wait()
        w_pass.start()

    q_true = (qb + near_blocks * x) % blocks

    @pl.when(h == 0)
    def _():
        q_pos = q_true * BLK + lax.broadcasted_iota(jnp.int32, (1, BLK), 1)
        k_iota = lax.broadcasted_iota(jnp.int32, (BLK, BLK), 0)
        for kb in range(blocks):
            k_pos = (kb + near_blocks * x) % blocks * BLK + k_iota
            bound = 0
            q_doc = jnp.zeros((1, BLK), jnp.int32)
            k_doc = jnp.zeros((BLK, BLK), jnp.int32)
            for i in range(len_ref.shape[1]):
                bound = bound + len_ref[0, i]
                q_doc = q_doc + (q_pos >= bound).astype(jnp.int32)
                k_doc = k_doc + (k_pos >= bound).astype(jnp.int32)
            krows = slice(kb * BLK, (kb + 1) * BLK)
            seen = (padc[krows, 0:1] > 0.5) | (k_pos == q_pos)
            mask[krows, :] = jnp.where((k_doc == q_doc) & seen, 0.0, -1000000000.0)

    def head_rows(group):
        return pl.ds(pl.multiple_of(group * cols + h * dk, dk), dk)

    qh = qkv_ref[head_rows(0), lanes(qb)]
    peak = None
    for kb in range(blocks):
        krows = slice(kb * BLK, (kb + 1) * BLK)
        s = dot(qkv_ref[head_rows(1), krows], qh, ((0,), (0,)))
        diag = (kb + near_blocks * x) % blocks - q_true + blocks - 1
        s = s + table[h, diag] + mask[krows, :]
        score[krows, :] = s
        top = jnp.max(s, axis=0, keepdims=True)
        peak = top if peak is None else jnp.maximum(peak, top)
    total = jnp.zeros((1, BLK), F32)
    ctx = jnp.zeros((dk, BLK), F32)
    for kb in range(blocks):
        krows = slice(kb * BLK, (kb + 1) * BLK)
        e = jnp.exp(score[krows, :] - peak)
        total = total + jnp.sum(e, axis=0, keepdims=True)
        e_low = e.astype(BF)
        e_ref[0, 0, krows, :] = e_low
        ctx = ctx + dot(qkv_ref[head_rows(2), krows], e_low, ((1,), (0,)))
    inv = 1.0 / total
    inv_ref[0, 0] = inv
    call[head_rows(0), lanes(qb)] = (ctx * inv).astype(BF)

    @pl.when(h == heads - 1)
    def _():
        ctx_copy(qb).start()

    @pl.when((h == heads - 1) & (qb == blocks - 1))
    def _():
        w_pass.wait()
        wn[...] = wall[...].astype(F32).T.astype(BF)
        out(4).start()
        for i in range(blocks):
            b = (i + near_blocks) % blocks
            ctx_copy(i).wait()
            ls = slice(b * BLK, (b + 1) * BLK)
            v = dot(wn[...], call[:, ls], ((1,), (0,)))
            if b < near_blocks:
                v = v + f1[:, ls]
                f1[:, ls] = v
            else:
                v = v + fb[:, b * BLK - rows : (b + 1) * BLK - rows].astype(F32)
            xo[:, ls] = (v * norm_scale(v) * fgc[...]).astype(BF)
            xt_out(b).start()
        out(0).start()
        out(2).start()
        c_copy.wait()
        for i in range(5):
            out(i).wait()
        for b in range(blocks):
            xt_out(b).wait()


def front(rel, lengths, pad, again, fgain, wq, wo, tok, far, cot, heads, dk):
    d, rows = tok.shape
    seq = 2 * rows
    cols = heads * dk
    blocks = seq // BLK
    buckets = rel.shape[0]
    bids = jnp.asarray(lane_buckets(buckets))
    one = pl.Buffered(1)
    dma = pltpu.SemaphoreType.DMA
    any_spec = pl.BlockSpec(memory_space=pl.ANY)
    smem = pl.BlockSpec(memory_space=pltpu.SMEM)

    def full(v):
        return pl.BlockSpec(v.shape, lambda i, h: (0, 0), pipeline_mode=one)

    return pl.pallas_call(
        functools.partial(front_kernel, heads, dk, buckets, blocks),
        grid=(blocks, heads),
        in_specs=[smem, smem, full(bids), full(pad), full(again), full(fgain), full(wq), full(wo)]
        + [any_spec] * 3,
        out_specs=[
            pl.BlockSpec((1, 1, seq, BLK), lambda i, h: (h, i, 0, 0)),
            pl.BlockSpec((1, 1, 1, BLK), lambda i, h: (h, i, 0, 0)),
            pl.BlockSpec((3 * cols, seq), lambda i, h: (0, 0)),
        ]
        + [any_spec] * 6,
        out_shape=[
            jax.ShapeDtypeStruct((heads, blocks, seq, BLK), BF),
            jax.ShapeDtypeStruct((heads, blocks, 1, BLK), F32),
            jax.ShapeDtypeStruct((3 * cols, seq), BF),
            jax.ShapeDtypeStruct((2 * cols, seq), BF),
            jax.ShapeDtypeStruct((d, seq), BF),
            jax.ShapeDtypeStruct((d, seq), BF),
            jax.ShapeDtypeStruct((d, rows), F32),
            jax.ShapeDtypeStruct((d, seq), BF),
            jax.ShapeDtypeStruct((2 * cols, d), BF),
        ],
        scratch_shapes=[
            pltpu.VMEM((d, rows), F32),
            pltpu.VMEM((d, rows), BF),
            pltpu.VMEM((d, rows), F32),
            pltpu.VMEM((d, rows), BF),
            pltpu.VMEM((d, seq), BF),
            pltpu.VMEM((heads, 7, BLK, BLK), F32),
            pltpu.VMEM((seq, 8), F32),
            pltpu.VMEM((seq, BLK), F32),
            pltpu.VMEM((seq, BLK), F32),
            pltpu.VMEM((d, 1), F32),
            pltpu.VMEM((d, 1), F32),
            pltpu.VMEM((2 * cols, d), BF),
            pltpu.VMEM((d, 2 * cols), BF),
            pltpu.VMEM((2 * cols, seq), BF),
            pltpu.VMEM((d, seq), BF),
            dma((3,)), dma((5 + blocks,)), dma((3,)), dma((3,)), dma((blocks,)), dma((blocks,)),
        ],
        compiler_params=pltpu.CompilerParams(
            vmem_limit_bytes=FF_VMEM, collective_id=2, has_side_effects=True
        ),
        cost_estimate=pl.CostEstimate(
            flops=16 * heads * seq * seq * dk + 10 * seq * d * cols,
            bytes_accessed=2 * heads * seq * seq + 30 * rows * d,
            transcendentals=heads * seq * seq,
        ),
    )(rel, lengths, bids, pad, again, fgain, wq, wo, tok, far, cot)


def ff_kernel(
    steps, done, extra,
    xt_hbm, w_hbm, ct_hbm, wo_hbm,
    grads_ref, din_hbm, near_hbm, far_hbm, back_hbm, mid_hbm, hand_hbm,
    xt, ct, wg, wu, wo, hid, dg, du, din, stage, r1, r2, r3, r4, xs, xr, of,
    csem, wsem, s1, s2, s3, s4, t1, t2, t3, t4, xsem, osem, hsem,
):
    f, total = hid.shape
    rows = total // 2
    chunks = rows // BLK
    d = xt.shape[0]
    shard = d // 16
    dp, mp = lax.axis_index("dp"), lax.axis_index("mp")
    a = group_coords(dp // extra)
    peers = [flip(dp, m * extra) for m in GROUP_MASKS]
    other = (dp, 1 - mp)
    bufs = (r1, r2, r3, r4)
    sends, recvs = (s1, s2, s3, s4), (t1, t2, t3, t4)
    end = steps - 1

    def weight_copy(kind, n):
        src, dst = ((w_hbm.at[0], wg), (w_hbm.at[1], wu), (wo_hbm, wo))[kind]
        return pltpu.make_async_copy(src.at[:, lanes(n)], dst.at[:, lanes(n)], wsem.at[kind, n])

    def tok_copy(n):
        src, dst, start, size = (
            (xt_hbm, xt, rows, BLK), (ct_hbm, ct, rows, BLK),
            (xt_hbm, xt, rows + BLK, BLK), (xt_hbm, xt, 0, rows), (ct_hbm, ct, 0, rows),
        )[n]
        part = pl.ds(start, size)
        return pltpu.make_async_copy(src.at[:, part], dst.at[:, part], csem.at[n])

    c_far = remote(
        ct_hbm.at[:, pl.ds(BLK, BLK)], ct.at[:, pl.ds(rows + BLK, BLK)], csem.at[5], csem.at[6], other
    )
    x_copy = remote(xs, xr, xsem.at[0], xsem.at[1], other)
    back_copy = remote(of, back_hbm, xsem.at[2], xsem.at[3], other)

    def hop(level, s, w):
        half = 8 >> level
        away = pl.ds((1 - a[level]) * half, half)
        src = stage.at[w, away] if level == 0 else bufs[level - 1].at[s, away]
        return remote(src, bufs[level].at[s], sends[level].at[s], recvs[level].at[s], (peers[level], mp))

    def hand_copy(s):
        if isinstance(s, int) and s < 3 * done + 3:
            return pltpu.make_async_copy(r2.at[s], mid_hbm.at[s - 3 * done], hsem.at[s - 3 * done])
        return pltpu.make_async_copy(r1.at[s], hand_hbm.at[s - 3 * done - 3], hsem.at[s - 3 * done])

    def absorb_first(step):
        for w in range(3):
            s = step * 3 + w
            copy = hop(0, s, w)
            copy.wait_recv()
            copy.wait_send()
        keep = pl.ds(a[0] * 8, 8)
        for w in range(3):
            s = step * 3 + w
            r1[s] = stage[w, keep] + r1[s]

        def onward():
            for w in range(3):
                hop(1, step * 3 + w, w).start()

        def aside():
            for w in range(3):
                hand_copy(step * 3 + w).start()

        if isinstance(step, int):
            onward() if step <= done else aside()
        else:
            pl.when(step <= done)(onward)
            pl.when(step > done)(aside)

    def absorb(level, step):
        def one(w, carry):
            s = step * 3 + w
            half = 8 >> level
            copy = hop(level, s, w)
            copy.wait_recv()
            copy.wait_send()
            kept = bufs[level - 1][s, pl.ds(a[level] * half, half)]
            if level < 3:
                bufs[level][s] = kept + bufs[level][s]
                if step < done:
                    hop(level + 1, s, w).start()
            else:
                both = kept.astype(F32) + bufs[level][s].astype(F32)
                grads_ref[w, :, lanes(step)] = both[0]
            return carry

        lax.fori_loop(0, 3, one, 0)

    scale = np.float32(np.sqrt(2 / np.pi))

    def forward(j, tok):
        fcols = lanes(j)
        gate = dot(wg[:, fcols], xt[:, tok], ((0,), (0,)))
        up = dot(wu[:, fcols], xt[:, tok], ((0,), (0,)))
        dh = dot(wo[:, fcols], ct[:, tok], ((0,), (0,)))
        return gate, up, dh

    def pointwise(j, tok, values):
        gate, up, dh = values
        frows = lanes(j)
        sq = gate * gate
        t = jnp.tanh(scale * gate * (1.0 + 0.044715 * sq))
        half = 0.5 * (1.0 + t)
        act = gate * half
        slope = half + 0.5 * gate * (1.0 - t * t) * (scale * (1.0 + (3 * 0.044715) * sq))
        hid[frows, tok] = (act * up).astype(BF)
        dg[frows, tok] = (dh * (up * slope)).astype(BF)
        du[frows, tok] = (dh * act).astype(BF)

    def backward(j, tok, acc):
        rs = lanes(j)
        din[:, acc] += dot(wg[:, rs], dg[rs, tok], ((1,), (0,))) + dot(wu[:, rs], du[rs, tok], ((1,), (0,)))

    def far_lanes(t):
        return lanes(t // steps + chunks), lanes(t // steps)

    def near(j):
        parts = [pl.ds(n * BLK, BLK) for n in range(chunks)]
        values = [forward(j, p) for p in parts]
        for p, v in zip(parts, values):
            pointwise(j, p, v)
        for p in parts:
            backward(j, p, p)

    per = 4 * shard

    def grads(j, order):
        for w in range(3):
            right = (hid, dg, du)[w][lanes(j), :]
            for q in range(4):
                rs = slice(q * per, (q + 1) * per)
                left = ct[rs, :] if w == 0 else xt[rs, :]
                part = dot(left, right, ((1,), (1,)))
                for k in range(4):
                    stage[w, block_position(4 * q + k, order), 0:shard, :] = part[
                        k * shard : (k + 1) * shard
                    ].astype(BF)
        for w in range(3):
            hop(0, j * 3 + w, w).start()

    def out_part(n):
        return dot(wo[...], hid[:, n * BLK : (n + 1) * BLK], ((1,), (0,)))

    def weights_wait(j):
        for kind in range(3):
            weight_copy(kind, j).wait()

    meet([(p, mp) for p in peers] + [other])
    c_far.start()
    tok_copy(0).start()
    tok_copy(1).start()
    for n in range(steps):
        for kind in range(3):
            weight_copy(kind, n).start()
        if n == 0:
            tok_copy(2).start()
    tok_copy(3).start()
    tok_copy(4).start()
    din[...] = jnp.zeros_like(din)
    stage[...] = jnp.zeros_like(stage)
    tok_copy(0).wait()
    tok_copy(1).wait()
    weights_wait(0)
    tok0, acc0 = far_lanes(0)
    pointwise(0, tok0, forward(0, tok0))

    def far_step(t, carry):
        j = t % steps

        @pl.when(t < steps)
        def _():
            weights_wait(j)

        @pl.when(t == steps)
        def _():
            tok_copy(2).wait()
            c_far.wait()

        tok, _ = far_lanes(t)
        before, acc = far_lanes(t - 1)
        values = forward(j, tok)
        backward((t - 1) % steps, before, acc)
        pointwise(j, tok, values)
        return carry

    lax.fori_loop(1, chunks * steps, far_step, 0)
    tok_copy(3).wait()
    tok_copy(4).wait()
    last, acc = far_lanes(chunks * steps - 1)
    backward(end, last, acc)
    xs[...] = din[...].astype(BF)
    x_copy.start()
    din[...] = jnp.zeros_like(din)
    near(0)

    def near_step(j, carry):
        grads(j, Y_FIRST)
        near(j + 1)
        absorb_first(j)

        @pl.when(j == 3)
        def _():
            absorb(1, 0)
            of[...] = out_part(chunks).astype(BF)

        @pl.when(j == 4)
        def _():
            x_copy.wait()
            back_copy.start()

        @pl.when(j == 5)
        def _():
            absorb(1, 1)
            absorb(2, 0)

        return carry

    lax.fori_loop(0, end, near_step, 0)
    din[...] += xr[...].astype(F32)
    din_copy = pltpu.make_async_copy(din, din_hbm, osem.at[2])
    din_copy.start()
    grads(end, Z_FIRST)
    xs[:, 0:BLK] = out_part(chunks + 1).astype(BF)
    far_copy = pltpu.make_async_copy(xs.at[:, pl.ds(0, BLK)], far_hbm, osem.at[0])
    far_copy.start()
    absorb_first(end)
    din_copy.wait()
    din[:, 0:BLK] = out_part(0)
    absorb(2, 1)
    absorb(3, 0)
    for n in range(1, chunks):
        din[:, n * BLK : (n + 1) * BLK] = out_part(n)
    near_copy = pltpu.make_async_copy(din, near_hbm, osem.at[1])
    near_copy.start()
    absorb(1, done)
    for w in range(3):
        hand_copy(3 * done + w).start()
    absorb(3, 1)
    far_copy.wait()
    near_copy.wait()

    def flush(s, carry):
        hand_copy(s).wait()
        return carry

    lax.fori_loop(3 * done + 3, 3 * steps, flush, 0)
    for w in range(3):
        hand_copy(3 * done + w).wait()
    back_copy.wait()


def ff_all(xt, ct, w2, wo, extra):
    d, total = xt.shape
    f = wo.shape[1]
    rows = total // 2
    steps = f // BLK
    done = FF_DONE
    chunks = 3 * steps
    kept = 3 * done
    shard = d // 16
    spad = -(-shard // 16) * 16
    dma = pltpu.SemaphoreType.DMA
    any_spec = pl.BlockSpec(memory_space=pl.ANY)
    return pl.pallas_call(
        functools.partial(ff_kernel, steps, done, extra),
        in_specs=[any_spec] * 4,
        out_specs=[pl.BlockSpec(memory_space=pltpu.VMEM)] + [any_spec] * 6,
        out_shape=[
            jax.ShapeDtypeStruct((3, spad, done * BLK), F32),
            jax.ShapeDtypeStruct((d, rows), F32),
            jax.ShapeDtypeStruct((d, rows), F32),
            jax.ShapeDtypeStruct((d, BLK), BF),
            jax.ShapeDtypeStruct((d, BLK), BF),
            jax.ShapeDtypeStruct((3, 4, spad, BLK), BF),
            jax.ShapeDtypeStruct((chunks - kept - 3, 8, spad, BLK), BF),
        ],
        scratch_shapes=[
            pltpu.VMEM((d, total), BF),
            pltpu.VMEM((d, total), BF),
            pltpu.VMEM((d, f), BF),
            pltpu.VMEM((d, f), BF),
            pltpu.VMEM((d, f), BF),
            pltpu.VMEM((f, total), BF),
            pltpu.VMEM((f, total), BF),
            pltpu.VMEM((f, total), BF),
            pltpu.VMEM((d, rows), F32),
            pltpu.VMEM((3, 16, spad, BLK), BF),
            pltpu.VMEM((chunks, 8, spad, BLK), BF),
            pltpu.VMEM((kept + 3, 4, spad, BLK), BF),
            pltpu.VMEM((kept, 2, spad, BLK), BF),
            pltpu.VMEM((kept, 1, spad, BLK), BF),
            pltpu.VMEM((d, rows), BF),
            pltpu.VMEM((d, rows), BF),
            pltpu.VMEM((d, BLK), BF),
            dma((7,)),
            dma((3, steps)),
            dma((chunks,)), dma((kept + 3,)), dma((kept,)), dma((kept,)),
            dma((chunks,)), dma((kept + 3,)), dma((kept,)), dma((kept,)),
            dma((4,)),
            dma((3,)),
            dma((chunks - kept,)),
        ],
        compiler_params=pltpu.CompilerParams(
            vmem_limit_bytes=FF_VMEM, collective_id=0, has_side_effects=True
        ),
        cost_estimate=pl.CostEstimate(
            flops=18 * total * d * f,
            bytes_accessed=6 * d * f + 16 * total * d,
            transcendentals=total * f,
        ),
    )(xt, w2, ct, wo)


def tail_kernel(
    heads, dk, buckets, blocks, extra,
    bid_ref, qkv_ref, e_ref, inv_ref, wall_ref, ctx_ref, wq_ref, ag_ref, fg_ref,
    din_hbm, mid_hbm, cot_hbm, tok_hbm, nrm_hbm, far_hbm, part_hbm, hand_hbm,
    ig_hbm, g_ref, small_ref, grads_ref, back_hbm,
    f1, f2, f3, nrm, wn, alow, dctx, dcs, osend, orecv, gsum, fsum, agc, fgc,
    dp_s, dkv, tally, dproj, grad, dns, dnr,
    stage, t1, t2, t3, t4, hk, hm, h2, h3, h4, sb, rb,
    lsem, ksem, xs_sem, xr_sem, cs_sem, cr_sem, bs_sem, br_sem, hs2, hs3, hs4, hr2, hr3, hr4,
):
    qb, h = pl.program_id(0), pl.program_id(1)
    step_id = qb * heads + h
    dp, x = lax.axis_index("dp"), lax.axis_index("mp")
    d, rows = f2.shape
    seq = 2 * rows
    cols = heads * dk
    shard = d // 16
    a = group_coords(dp // extra)
    peers = [flip(dp, m * extra) for m in GROUP_MASKS]
    other = (dp, 1 - x)
    bufs = (stage, t1, t2, t3, t4)
    hsends, hrecvs = (None, hs2, hs3, hs4), (None, hr2, hr3, hr4)
    near_blocks = blocks // 2

    def local(i):
        src, dst = ((din_hbm, f1), (mid_hbm, f2), (cot_hbm, f3), (tok_hbm, f2), (nrm_hbm, nrm))[i]
        return pltpu.make_async_copy(src, dst, lsem.at[i])

    dctx_copy = remote(dcs, dctx.at[:, pl.ds(rows, rows)], xs_sem.at[0], xr_sem.at[0], other)
    o_copy = remote(osend, orecv, xs_sem.at[1], xr_sem.at[1], other)

    def back_copy(i):
        part = pl.ds(i * 128, 128)
        return remote(far_hbm.at[:, part], back_hbm.at[:, part], xs_sem.at[2 + i], xr_sem.at[2 + i], other)

    def dn_copy(r):
        return remote(dns.at[r], dnr.at[r], xs_sem.at[4 + r], xr_sem.at[4 + r], other)

    def hop(level):
        half = 8 >> level
        away = pl.ds((1 - a[level]) * half, half)
        return remote(
            bufs[level].at[away], bufs[level + 1], cs_sem.at[level], cr_sem.at[level], (peers[level], x)
        )

    def absorb(level):
        half = 8 >> level
        hop(level).wait()
        kept = bufs[level][pl.ds(a[level] * half, half)]
        if level < 3:
            bufs[level + 1][...] = kept + bufs[level + 1][...]
            hop(level + 1).start()
        else:
            both = kept.astype(F32) + bufs[level + 1][...].astype(F32)
            for i in range(4):
                g_ref[i] = both[0, :, i * cols : (i + 1) * cols]

    def order_of(block):
        return Z_FIRST if block == 4 else Y_FIRST

    def keep_copy(block, w):
        s = block * 3 + w
        if block == 0:
            return pltpu.make_async_copy(part_hbm.at[w, pl.ds(a[2] * 2, 2)], hm.at[w], ksem.at[s])
        keep = pl.ds(a[order_of(block)[1]] * 4, 4)
        return pltpu.make_async_copy(hand_hbm.at[s - 3, keep], hk.at[s - 3], ksem.at[s])

    def hand_hop(level, block, w):
        s = block * 3 + w
        half = 8 >> level
        c = order_of(block)[level]
        away = pl.ds((1 - a[c]) * half, half)
        if level == 1:
            src, dst = hand_hbm.at[s - 3, away], h2.at[s - 3]
        elif level == 2:
            src, dst = part_hbm.at[w, away] if block == 0 else h2.at[s - 3, away], h3.at[s]
        else:
            src, dst = h3.at[s, away], h4.at[s]
        return remote(src, dst, hsends[level].at[s], hrecvs[level].at[s], (peers[c], x))

    def hand_start(block):
        def one(w, carry):
            keep_copy(block, w).start()
            hand_hop(2 if block == 0 else 1, block, w).start()
            return carry

        lax.fori_loop(0, 3, one, 0)

    def hand_absorb(level, block):
        def one(w, carry):
            s = block * 3 + w
            half = 8 >> level
            keep = pl.ds(a[order_of(block)[level]] * half, half)
            hand_hop(level, block, w).wait()
            if level == (2 if block == 0 else 1):
                keep_copy(block, w).wait()
                kept = hm[w] if block == 0 else hk[s - 3]
            else:
                kept = h2[s - 3, keep] if level == 2 else h3[s, keep]
            if level == 1:
                h2[s - 3] = kept + h2[s - 3]
            elif level == 2:
                h3[s] = kept + h3[s]
            else:
                both = kept.astype(F32) + h4[s].astype(F32)
                grads_ref[w, :, block * BLK : (block + 1) * BLK] = both[0]
            if level < 3:
                hand_hop(level + 1, block, w).start()
            return carry

        lax.fori_loop(0, 3, one, 0)

    def round_copy(i):
        who = other if i == 4 else (peers[(0, 2, 3, 1)[i]], x)
        return remote(sb.at[i], rb.at[i], bs_sem.at[i], br_sem.at[i], who)

    def round_end(i):
        round_copy(i).wait()
        sb[i + 1] = sb[i] + rb[i]
        if i < 4:
            round_copy(i + 1).start()

    def out_copy(r):
        return pltpu.make_async_copy(f3.at[:, lanes(r)], ig_hbm.at[:, lanes(r)], lsem.at[5 + r])

    def lane_sum(v):
        total = v[:, 0:128]
        for i in range(1, v.shape[1] // 128):
            total = total + v[:, i * 128 : (i + 1) * 128]
        return total

    def dn_part(b):
        ls = slice(b * BLK, (b + 1) * BLK)
        part = dot(wn[...], dproj[:, ls], ((1,), (0,)))
        gsum[...] += lane_sum(nrm[:, ls].astype(F32) * part)
        return part

    @pl.when(step_id == 0)
    def _():
        for i in range(3):
            local(i).start()
        meet([(p, x) for p in peers] + [other])
        back_copy(0).start()
        for block in (0, 4, 1, 2, 3):
            hand_start(block)
        dkv[...] = jnp.zeros_like(dkv)
        tally[...] = jnp.zeros_like(tally)
        stage[...] = jnp.zeros_like(stage)
        fsum[...] = jnp.zeros_like(fsum)
        gsum[...] = jnp.zeros_like(gsum)
        agc[...] = column(ag_ref[...])
        fgc[...] = column(fg_ref[...])
        for i in range(3):
            local(i).wait()
        for r in range(near_blocks):
            ls = slice(r * BLK, (r + 1) * BLK)
            v = f2[:, ls]
            c = f1[:, ls]
            scale = norm_scale(v)
            n = v * scale
            cg = c * fgc[...]
            m = jnp.mean(cg * n, axis=0, keepdims=True)
            gm = f3[:, ls] + scale * (cg - n * m)
            fsum[...] += lane_sum(c * n)
            f1[:, ls] = gm
            alow[:, ls] = gm.astype(BF)
        for i in range(3, 5):
            local(i).start()
        dcs[...] = dot(wall_ref[cols : 2 * cols, :], alow[...], ((1,), (0,))).astype(BF)
        dctx_copy.start()
        dctx[:, :rows] = dot(wall_ref[0:cols, :], alow[...], ((1,), (0,))).astype(BF)
        osend[...] = dot(alow[...], ctx_ref[cols : 2 * cols, :rows], ((1,), (1,))).astype(BF)
        grad[:, 3 * cols : 4 * cols] = dot(alow[...], ctx_ref[0:cols, :rows], ((1,), (1,)))
        wn[...] = wq_ref[...].astype(F32).T.astype(BF)
        dctx_copy.wait()
        o_copy.start()
        back_copy(1).start()

    def head_rows(group):
        return pl.ds(pl.multiple_of(group * cols + h * dk, dk), dk)

    inv = inv_ref[0, 0]
    qh = qkv_ref[head_rows(0), lanes(qb)]
    scaled = (dctx[head_rows(0), lanes(qb)].astype(F32) * inv).astype(BF)
    inner = jnp.zeros((1, BLK), F32)
    for kb in range(blocks):
        krows = slice(kb * BLK, (kb + 1) * BLK)
        g = dot(qkv_ref[head_rows(2), krows], scaled, ((0,), (0,)))
        dp_s[krows, :] = g
        inner = inner + jnp.sum(e_ref[0, 0, krows, :].astype(F32) * g, axis=0, keepdims=True)
    inner = inner * inv
    dq = jnp.zeros((dk, BLK), F32)
    q_true = (qb + near_blocks * x) % blocks
    for kb in range(blocks):
        krows = slice(kb * BLK, (kb + 1) * BLK)
        e = e_ref[0, 0, krows, :]
        ds = (e.astype(F32) * (dp_s[krows, :] - inner)).astype(BF)
        dkv[head_rows(0), krows] += dot(qh, ds, ((1,), (1,)))
        dkv[head_rows(1), krows] += dot(scaled, e, ((1,), (1,)))
        dq = dq + dot(qkv_ref[head_rows(1), krows], ds, ((1,), (0,)))
        diag = (kb + near_blocks * x) % blocks - q_true + blocks - 1
        tally[h, diag] += ds.astype(F32)
    dproj[head_rows(0), lanes(qb)] = dq.astype(BF)

    for when, events in (
        (2, ((2, 0),)), (5, ((1, 1),)), (7, ((1, 4),)), (9, ((3, 0),)), (10, ((2, 1), (1, 2))),
    ):
        @pl.when(step_id == when)
        def _():
            for level, block in events:
                hand_absorb(level, block)

    @pl.when(step_id == blocks * heads - 1)
    def _():
        dproj[cols : 3 * cols, :] = dkv[...].astype(BF)
        for i in range(3, 5):
            local(i).wait()
        for r in range(near_blocks):
            dns[r] = dn_part(near_blocks + r).astype(BF)
            dn_copy(r).start()
        grad[:, 0 : 3 * cols] = dot(nrm[...], dproj[...], ((1,), (1,)))
        o_copy.wait()
        grad[:, 3 * cols : 4 * cols] += orecv[...].astype(F32)
        for k in range(16):
            stage[block_position(k, Y_FIRST), 0:shard, :] = grad[k * shard : (k + 1) * shard, :].astype(BF)
        hop(0).start()
        hand_absorb(2, 4)
        for r in range(near_blocks):
            f3[:, r * BLK : (r + 1) * BLK] = dn_part(r)
        absorb(0)
        hand_absorb(3, 1)
        hand_absorb(2, 2)
        ids = bid_ref[...]
        hot = ids == lax.broadcasted_iota(jnp.int32, (buckets, SPAN), 0)
        out_lane = lax.broadcasted_iota(jnp.int32, (buckets, 128), 1)
        sub = lax.broadcasted_iota(jnp.int32, (8, SPAN), 0)
        out = jnp.zeros((buckets, 128), F32)
        for hh in range(heads):
            line = jnp.zeros((8, SPAN), F32)
            for g in range(BLK // 8):
                group = slice(8 * g, 8 * g + 8)
                t = [tally[hh, i, group, :] for i in range(7)]
                parts = [t[5] + t[6], t[4], t[3], t[2], t[1] + t[0]]
                strip = jnp.concatenate(parts + [jnp.zeros((8, BLK), F32)], axis=1)
                line = line + (strip if g == 0 else pltpu.roll(strip, SPAN - 8 * g, 1))
            for bit in (1, 2, 4):
                line = jnp.where((sub // bit) % 2 == 1, pltpu.roll(line, SPAN - bit, 1), line)
            sums = jnp.sum(line, axis=0, keepdims=True)
            col = jnp.sum(jnp.where(hot, sums, 0.0), axis=1, keepdims=True)
            out = jnp.where(out_lane == x * heads + hh, col, out)
        sb[0] = jnp.zeros(sb.shape[1:], F32)
        sb[0, 0:buckets, :] = out
        again = jnp.sum(gsum[...].T, axis=0, keepdims=True) / ag_ref[...]
        fgain = jnp.sum(fsum[...].T, axis=0, keepdims=True)
        lines = -(-d // 128)
        for i in range(lines):
            n = min(128, d - 128 * i)
            sb[0, buckets + i : buckets + i + 1, 0:n] = again[:, 128 * i : 128 * i + n]
            sb[0, buckets + lines + i : buckets + lines + i + 1, 0:n] = fgain[:, 128 * i : 128 * i + n]
        round_copy(0).start()
        hand_absorb(1, 3)
        round_end(0)
        hand_absorb(3, 2)
        round_end(1)
        hand_absorb(2, 3)
        round_end(2)

        def last_norm(r):
            ls = slice(r * BLK, (r + 1) * BLK)
            dn_copy(r).wait()
            c = f3[:, ls] + dnr[r].astype(F32)
            v = f2[:, ls]
            scale = norm_scale(v)
            n = v * scale
            cg = c * agc[...]
            m = jnp.mean(cg * n, axis=0, keepdims=True)
            f3[:, ls] = f1[:, ls] + scale * (cg - n * m)
            out_copy(r).start()

        absorb(1)
        last_norm(0)
        round_end(3)
        hand_absorb(3, 4)
        hand_absorb(3, 3)
        absorb(2)
        for r in range(1, near_blocks):
            last_norm(r)
        round_end(4)
        small_ref[...] = sb[5]
        absorb(3)
        for i in range(2):
            back_copy(i).wait()
        for r in range(near_blocks):
            out_copy(r).wait()


def tail(qkv, e, inv, wall, ctx, wq, again, fgain, din, mid, cot, tok, nrm, far, half_way, hand,
         buckets, heads, dk, extra):
    d, rows = tok.shape
    seq = 2 * rows
    cols = heads * dk
    blocks = seq // BLK
    near = blocks // 2
    shard = d // 16
    spad = -(-shard // 16) * 16
    chunks = hand.shape[0]
    later = chunks // 3 + 1
    lines = -(-(buckets + 2 * -(-d // 128)) // 8) * 8
    bids = jnp.asarray(lane_buckets(buckets))
    one = pl.Buffered(1)
    dma = pltpu.SemaphoreType.DMA
    any_spec = pl.BlockSpec(memory_space=pl.ANY)

    def full(v):
        return pl.BlockSpec(v.shape, lambda i, h: (0, 0), pipeline_mode=one)

    return pl.pallas_call(
        functools.partial(tail_kernel, heads, dk, buckets, blocks, extra),
        grid=(blocks, heads),
        in_specs=[
            full(bids),
            full(qkv),
            pl.BlockSpec((1, 1, seq, BLK), lambda i, h: (h, i, 0, 0)),
            pl.BlockSpec((1, 1, 1, BLK), lambda i, h: (h, i, 0, 0)),
            full(wall),
            full(ctx),
            full(wq),
            full(again),
            full(fgain),
        ]
        + [any_spec] * 8,
        out_specs=[
            any_spec,
            pl.BlockSpec((4, spad, cols), lambda i, h: (0, 0, 0)),
            pl.BlockSpec((lines, 128), lambda i, h: (0, 0)),
            pl.BlockSpec((3, spad, later * BLK), lambda i, h: (0, 0, 0)),
            any_spec,
        ],
        out_shape=[
            jax.ShapeDtypeStruct((d, rows), F32),
            jax.ShapeDtypeStruct((4, spad, cols), F32),
            jax.ShapeDtypeStruct((lines, 128), F32),
            jax.ShapeDtypeStruct((3, spad, later * BLK), F32),
            jax.ShapeDtypeStruct(far.shape, BF),
        ],
        scratch_shapes=[
            pltpu.VMEM((d, rows), F32),
            pltpu.VMEM((d, rows), F32),
            pltpu.VMEM((d, rows), F32),
            pltpu.VMEM((d, seq), BF),
            pltpu.VMEM((d, 3 * cols), BF),
            pltpu.VMEM((d, rows), BF),
            pltpu.VMEM((cols, seq), BF),
            pltpu.VMEM((cols, rows), BF),
            pltpu.VMEM((d, cols), BF),
            pltpu.VMEM((d, cols), BF),
            pltpu.VMEM((d, 128), F32),
            pltpu.VMEM((d, 128), F32),
            pltpu.VMEM((d, 1), F32),
            pltpu.VMEM((d, 1), F32),
            pltpu.VMEM((seq, BLK), F32),
            pltpu.VMEM((2 * cols, seq), F32),
            pltpu.VMEM((heads, 7, BLK, BLK), F32),
            pltpu.VMEM((3 * cols, seq), BF),
            pltpu.VMEM((d, 4 * cols), F32),
            pltpu.VMEM((near, d, BLK), BF),
            pltpu.VMEM((near, d, BLK), BF),
            pltpu.VMEM((16, spad, 4 * cols), BF),
            pltpu.VMEM((8, spad, 4 * cols), BF),
            pltpu.VMEM((4, spad, 4 * cols), BF),
            pltpu.VMEM((2, spad, 4 * cols), BF),
            pltpu.VMEM((1, spad, 4 * cols), BF),
            pltpu.VMEM((chunks, 4, spad, BLK), BF),
            pltpu.VMEM((3, 2, spad, BLK), BF),
            pltpu.VMEM((chunks, 4, spad, BLK), BF),
            pltpu.VMEM((3 * later, 2, spad, BLK), BF),
            pltpu.VMEM((3 * later, 1, spad, BLK), BF),
            pltpu.VMEM((6, lines, 128), F32),
            pltpu.VMEM((5, lines, 128), F32),
            dma((5 + near,)),
            dma((3 * later,)),
            dma((4 + near,)), dma((4 + near,)),
            dma((4,)), dma((4,)),
            dma((5,)), dma((5,)),
            dma((3 * later,)), dma((3 * later,)), dma((3 * later,)),
            dma((3 * later,)), dma((3 * later,)), dma((3 * later,)),
        ],
        compiler_params=pltpu.CompilerParams(
            vmem_limit_bytes=FF_VMEM, collective_id=1, has_side_effects=True
        ),
        cost_estimate=pl.CostEstimate(
            flops=32 * heads * seq * seq * dk + 8 * seq * d * 3 * cols,
            bytes_accessed=2 * heads * seq * seq + 30 * rows * d,
            transcendentals=0,
        ),
    )(bids, qkv, e, inv, wall, ctx, wq, again, fgain, din, mid, cot, tok, nrm, far, half_way, hand)


def take(array, index):
    return lax.dynamic_index_in_dim(array, index, 0, keepdims=False)


def per_device(
    tokens,
    cotangent,
    doc_lengths,
    pad_mask,
    attn_gain,
    qkv_weight,
    rel_table,
    out_weight,
    ff_gain,
    ff_in_weight,
    ff_out_weight,
):
    rows, d = tokens.shape
    n_dp = lax.axis_size("dp")
    n_mp = lax.axis_size("mp")
    cols = qkv_weight.shape[2]
    buckets, heads = rel_table.shape
    dk = cols // heads
    me = lax.axis_index("dp")
    shard = d // n_dp
    extra = n_dp // 16

    def hop(v, mask):
        return lax.ppermute(v, "dp", [(i, i ^ mask) for i in range(n_dp)])

    def bit(b):
        return (me >> b) & 1

    def reduce_rest(parts, low_bits):
        for b in reversed(range(low_bits)):
            halves = [p.reshape((2, p.shape[0] // 2) + p.shape[1:]) for p in parts]
            away = sum(take(p, 1 - bit(b)).astype(F32) for p in halves).astype(BF)
            parts = [take(p, bit(b)) for p in halves] + [hop(away, 1 << b)]
        return sum(p.astype(F32) for p in parts)[0]

    def finish(g):
        g = g[: d // 16]
        if extra == 1:
            return g
        return reduce_rest([g.reshape(extra, shard, g.shape[1])], extra.bit_length() - 1)

    tok = tokens.T
    cot = cotangent.T
    far = lax.ppermute(tok.astype(BF), "mp", [(0, 1), (1, 0)])
    w2 = jnp.transpose(ff_in_weight, (1, 0, 2))
    wq = jnp.transpose(qkv_weight, (1, 2, 0)).reshape(3 * cols, d)
    again, fgain = attn_gain.reshape(1, d), ff_gain.reshape(1, d)

    e, inv, qkv, ctx, nrm, xt, mid, ct, wall = front(
        rel_table, doc_lengths, pad_mask, again, fgain, wq, out_weight.T, tok, far, cot, heads, dk
    )
    early, din, near_out, far_out, back0, half_way, hand = ff_all(xt, ct, w2, ff_out_weight, extra)
    input_grad, last, small, late, back1 = tail(
        qkv, e, inv, wall, ctx, wq, again, fgain, din, mid, cot, tok, nrm, far_out, half_way, hand,
        buckets, heads, dk, extra,
    )
    back = jnp.concatenate([back0, back1], axis=1)
    result = (mid + near_out + back.astype(F32)).T

    ffo, ffg, ffu = (finish(jnp.concatenate([early[i], late[i]], axis=1)) for i in range(3))
    grad_qkv = jnp.stack([finish(last[i]) for i in range(3)], axis=1)
    for b in range(extra.bit_length() - 1):
        small = small + hop(small, 1 << b)
    lines = -(-d // 128)
    return (
        result,
        input_grad.T,
        small[buckets : buckets + lines].reshape(-1)[:d],
        grad_qkv,
        small[:buckets, : heads * n_mp],
        finish(last[3]),
        small[buckets + lines : buckets + 2 * lines].reshape(-1)[:d],
        jnp.stack([ffg, ffu], axis=1),
        ffo,
    )


def solution(mesh):
    return jax.shard_map(
        per_device,
        mesh=mesh,
        in_specs=(
            P(("dp", "mp"), None),
            P(("dp", "mp"), None),
            P("dp", None),
            P("dp", None),
            P(),
            P(None, None, "mp"),
            P(None, "mp"),
            P(None, "mp"),
            P(),
            P(None, None, "mp"),
            P(None, "mp"),
        ),
        out_specs=(
            P(("dp", "mp"), None),
            P(("dp", "mp"), None),
            P(),
            P("dp", None, "mp"),
            P(),
            P("dp", "mp"),
            P(),
            P("dp", None, "mp"),
            P("dp", "mp"),
        ),
        check_vma=False,
    )
```

```python
import functools

import jax
import jax.numpy as jnp
import numpy as np
from jax import lax
from jax.experimental import pallas as pl
from jax.experimental.pallas import tpu as pltpu
from jax.sharding import PartitionSpec as P

MAXDIST = 128
norm_eps = 1e-06
BLK = 256
SPAN = 6 * BLK
REACH = 2
BF = jnp.bfloat16
F32 = jnp.float32
FF_VMEM = 63 << 20
FF_DONE = 2


def bucket_of(offsets, buckets, reach):
    half_range = buckets // 2
    upper_half = (offsets > 0).astype(np.int32) * half_range
    distance = np.abs(offsets)
    exact_range = half_range // 2
    safe_dist = np.maximum(distance, 1)
    log_bucket = exact_range + (
        np.log(safe_dist / exact_range) / np.log(reach / exact_range) * (half_range - exact_range)
    ).astype(np.int32)
    log_bucket = np.minimum(log_bucket, half_range - 1)
    return (upper_half + np.where(distance < exact_range, distance, log_bucket)).astype(np.int32)


def lane_buckets(buckets):
    lanes = np.arange(SPAN)
    shifted = np.where(lanes < 5 * BLK, lanes, lanes - SPAN)
    return bucket_of(REACH * BLK - shifted, buckets, MAXDIST).reshape(1, SPAN)


def dot(a, b, contract):
    return lax.dot_general(a, b, (contract, ((), ())), preferred_element_type=F32)


def flip(index, mask):
    out = index
    bit = 1
    while bit <= mask:
        if mask & bit:
            out = out + bit * (1 - 2 * (index // bit % 2))
        bit *= 2
    return out


GROUP_MASKS = (1, 2, 4, 12)


def group_coords(g):
    b = [g // (1 << i) % 2 for i in range(4)]
    return [b[0], b[1], (b[2] + b[3]) % 2, b[3]]


Y_FIRST = (0, 1, 2, 3)
Z_FIRST = (0, 2, 3, 1)


def block_position(k, order):
    b = [k >> i & 1 for i in range(4)]
    c = [b[0], b[1], b[2] ^ b[3], b[3]]
    return sum(c[order[i]] << (3 - i) for i in range(4))


def column(line):
    return jnp.broadcast_to(line, (8, line.shape[1])).T[:, 0:1]


def norm_scale(v):
    return lax.rsqrt(jnp.mean(v * v, axis=0, keepdims=True) + norm_eps)


def lanes(block):
    return pl.ds(pl.multiple_of(block * BLK, BLK), BLK)


def remote(src, dst, send, recv, who):
    return pltpu.make_async_remote_copy(
        src_ref=src,
        dst_ref=dst,
        send_sem=send,
        recv_sem=recv,
        device_id=who,
        device_id_type=pl.DeviceIdType.MESH,
    )


def meet(devices):
    barrier = pltpu.get_barrier_semaphore()
    for who in devices:
        pl.semaphore_signal(barrier, inc=1, device_id=who, device_id_type=pl.DeviceIdType.MESH)
    pl.semaphore_wait(barrier, len(devices))


def near_diagonal(offset):
    i = offset + 3
    return i + (6 - i) // 6 - i // 6 - 1


def front_kernel(
    heads, dk, buckets, blocks,
    rel_ref, len_ref, bid_ref, pad_ref, ag_ref, fg_ref, wq_ref, wo_ref,
    tok_hbm, far_hbm, cot_hbm,
    e_ref, inv_ref, qkv_ref, ctx_hbm, nrm_hbm, xt_hbm, mid_hbm, ct_hbm, wall_hbm,
    f1, fb, f3, cl, nrm, table, padc, mask, score, agc, fgc, wall, wn, call, xo,
    lsem, osem, wsend, wrecv, csend, crecv,
):
    qb = pl.program_id(0)
    dp, x = lax.axis_index("dp"), lax.axis_index("mp")
    d, rows = f1.shape
    cols = heads * dk
    half = cols // 2
    core = dp % 2
    other = (dp, 1 - x)
    sibling = (dp + 1 - 2 * core, x)
    near_blocks = blocks // 2
    part = pl.ds(core * half, half)
    far_part = pl.ds(cols + core * half, half)

    def local(i):
        src, dst = ((tok_hbm, f1), (far_hbm, fb), (cot_hbm, f3))[i]
        return pltpu.make_async_copy(src, dst, lsem.at[i])

    def out(i):
        src, dst = (
            (call, ctx_hbm), (nrm, nrm_hbm), (f1, mid_hbm), (cl, ct_hbm.at[:, pl.ds(0, rows)]), (wall, wall_hbm)
        )[i]
        return pltpu.make_async_copy(src, dst, osem.at[i])

    def xt_out(b):
        return pltpu.make_async_copy(xo.at[:, lanes(b)], xt_hbm.at[:, lanes(b)], osem.at[5 + b])

    w_copy = remote(wo_ref.at[part], wall.at[far_part], wsend.at[0], wrecv.at[0], other)
    w_pass = remote(wall.at[far_part], wall.at[far_part], wsend.at[1], wrecv.at[1], sibling)
    c_copy = remote(cl.at[:, pl.ds(0, BLK)], ct_hbm.at[:, pl.ds(rows, BLK)], wsend.at[2], wrecv.at[2], other)

    def ctx_copy(b):
        there = (b + near_blocks) % blocks
        return remote(
            call.at[pl.ds(0, cols), lanes(b)], call.at[pl.ds(cols, cols), lanes(there)],
            csend.at[b], crecv.at[b], other,
        )

    @pl.when(qb == 0)
    def _():
        for i in (2, 0, 1):
            local(i).start()
        meet([other, sibling])
        w_copy.start()
        wall[0:cols, :] = wo_ref[...]
        local(2).wait()
        cl[...] = f3[...].astype(BF)
        c_copy.start()
        out(3).start()
        agc[...] = column(ag_ref[...])
        fgc[...] = column(fg_ref[...])
        local(0).wait()
        local(1).wait()
        for b in range(blocks):
            ls = slice(b * BLK, (b + 1) * BLK)
            v = f1[:, ls] if b < near_blocks else fb[:, b * BLK - rows : (b + 1) * BLK - rows].astype(F32)
            nrm[:, ls] = (v * norm_scale(v) * agc[...]).astype(BF)
            qkv_ref[:, ls] = dot(wq_ref[...], nrm[:, ls], ((1,), (0,))).astype(BF)
        out(1).start()
        for i in range(2):
            start = (1 - x) * rows if i else x * rows
            line = pad_ref[:, pl.ds(pl.multiple_of(start, BLK), rows)].astype(F32)
            padc[i * rows : (i + 1) * rows, :] = jnp.broadcast_to(line, (8, rows)).T
        ids = bid_ref[...]
        for hh in range(heads):
            line = jnp.zeros((1, SPAN), F32)
            for b in range(buckets):
                line = jnp.where(ids == b, rel_ref[b, hh], line)
            turned = pltpu.roll(
                jnp.broadcast_to(line, (BLK, SPAN)), 0, 1, stride=1, stride_axis=0
            )
            for g in range(5):
                table[hh, g] = turned[:, BLK * (4 - g) : BLK * (5 - g)]

    @pl.when(qb == 1)
    def _():
        w_copy.wait()
        w_pass.start()

    q_true = (qb + near_blocks * x) % blocks

    q_pos = q_true * BLK + lax.broadcasted_iota(jnp.int32, (1, BLK), 1)
    k_iota = lax.broadcasted_iota(jnp.int32, (BLK, BLK), 0)
    for kb in range(blocks):
        k_pos = (kb + near_blocks * x) % blocks * BLK + k_iota
        bound = 0
        q_doc = jnp.zeros((1, BLK), jnp.int32)
        k_doc = jnp.zeros((BLK, BLK), jnp.int32)
        for i in range(len_ref.shape[1]):
            bound = bound + len_ref[0, i]
            q_doc = q_doc + (q_pos >= bound).astype(jnp.int32)
            k_doc = k_doc + (k_pos >= bound).astype(jnp.int32)
        krows = slice(kb * BLK, (kb + 1) * BLK)
        seen = (padc[krows, 0:1] > 0.5) | (k_pos == q_pos)
        mask[krows, :] = jnp.where((k_doc == q_doc) & seen, 0.0, -1000000000.0)

    def head_rows(h, group):
        return pl.ds(pl.multiple_of(group * cols + h * dk, dk), dk)

    def diagonal(kb):
        return near_diagonal((kb + near_blocks * x) % blocks - q_true)

    def head(h, carry):
        qh = qkv_ref[head_rows(h, 0), lanes(qb)]
        peak = None
        for kb in range(blocks):
            krows = slice(kb * BLK, (kb + 1) * BLK)
            s = dot(qkv_ref[head_rows(h, 1), krows], qh, ((0,), (0,)))
            diag = diagonal(kb)
            s = s + table[h, diag] + mask[krows, :]
            score[krows, :] = s
            top = jnp.max(s, axis=0, keepdims=True)
            peak = top if peak is None else jnp.maximum(peak, top)
        total = jnp.zeros((1, BLK), F32)
        ctx = jnp.zeros((dk, BLK), F32)
        for kb in range(blocks):
            krows = slice(kb * BLK, (kb + 1) * BLK)
            e = jnp.exp(score[krows, :] - peak)
            total = total + jnp.sum(e, axis=0, keepdims=True)
            e_low = e.astype(BF)
            e_ref[h, 0, krows, :] = e_low
            ctx = ctx + dot(qkv_ref[head_rows(h, 2), krows], e_low, ((1,), (0,)))
        inv = 1.0 / total
        inv_ref[h, 0] = inv
        call[head_rows(h, 0), lanes(qb)] = (ctx * inv).astype(BF)
        return carry

    lax.fori_loop(0, heads, head, 0)
    ctx_copy(qb).start()

    @pl.when(qb == blocks - 1)
    def _():
        w_pass.wait()
        wn[...] = wall[...].astype(F32).T.astype(BF)
        out(4).start()
        for i in range(blocks):
            b = (i + near_blocks) % blocks
            ctx_copy(i).wait()
            ls = slice(b * BLK, (b + 1) * BLK)
            v = dot(wn[...], call[:, ls], ((1,), (0,)))
            if b < near_blocks:
                v = v + f1[:, ls]
                f1[:, ls] = v
            else:
                v = v + fb[:, b * BLK - rows : (b + 1) * BLK - rows].astype(F32)
            xo[:, ls] = (v * norm_scale(v) * fgc[...]).astype(BF)
            xt_out(b).start()
        out(0).start()
        out(2).start()
        c_copy.wait()
        for i in range(5):
            out(i).wait()
        for b in range(blocks):
            xt_out(b).wait()


def front(rel, lengths, pad, again, fgain, wq, wo, tok, far, cot, heads, dk):
    d, rows = tok.shape
    seq = 2 * rows
    cols = heads * dk
    blocks = seq // BLK
    buckets = rel.shape[0]
    bids = jnp.asarray(lane_buckets(buckets))
    one = pl.Buffered(1)
    dma = pltpu.SemaphoreType.DMA
    any_spec = pl.BlockSpec(memory_space=pl.ANY)
    smem = pl.BlockSpec(memory_space=pltpu.SMEM)

    def full(v):
        return pl.BlockSpec(v.shape, lambda i: (0, 0), pipeline_mode=one)

    return pl.pallas_call(
        functools.partial(front_kernel, heads, dk, buckets, blocks),
        grid=(blocks,),
        in_specs=[smem, smem, full(bids), full(pad), full(again), full(fgain), full(wq), full(wo)]
        + [any_spec] * 3,
        out_specs=[
            pl.BlockSpec((heads, 1, seq, BLK), lambda i: (0, i, 0, 0)),
            pl.BlockSpec((heads, 1, 1, BLK), lambda i: (0, i, 0, 0)),
            pl.BlockSpec((3 * cols, seq), lambda i: (0, 0)),
        ]
        + [any_spec] * 6,
        out_shape=[
            jax.ShapeDtypeStruct((heads, blocks, seq, BLK), BF),
            jax.ShapeDtypeStruct((heads, blocks, 1, BLK), F32),
            jax.ShapeDtypeStruct((3 * cols, seq), BF),
            jax.ShapeDtypeStruct((2 * cols, seq), BF),
            jax.ShapeDtypeStruct((d, seq), BF),
            jax.ShapeDtypeStruct((d, seq), BF),
            jax.ShapeDtypeStruct((d, rows), F32),
            jax.ShapeDtypeStruct((d, seq), BF),
            jax.ShapeDtypeStruct((2 * cols, d), BF),
        ],
        scratch_shapes=[
            pltpu.VMEM((d, rows), F32),
            pltpu.VMEM((d, rows), BF),
            pltpu.VMEM((d, rows), F32),
            pltpu.VMEM((d, rows), BF),
            pltpu.VMEM((d, seq), BF),
            pltpu.VMEM((heads, 5, BLK, BLK), F32),
            pltpu.VMEM((seq, 8), F32),
            pltpu.VMEM((seq, BLK), F32),
            pltpu.VMEM((seq, BLK), F32),
            pltpu.VMEM((d, 1), F32),
            pltpu.VMEM((d, 1), F32),
            pltpu.VMEM((2 * cols, d), BF),
            pltpu.VMEM((d, 2 * cols), BF),
            pltpu.VMEM((2 * cols, seq), BF),
            pltpu.VMEM((d, seq), BF),
            dma((3,)), dma((5 + blocks,)), dma((3,)), dma((3,)), dma((blocks,)), dma((blocks,)),
        ],
        compiler_params=pltpu.CompilerParams(
            vmem_limit_bytes=FF_VMEM, collective_id=2, has_side_effects=True
        ),
        cost_estimate=pl.CostEstimate(
            flops=16 * heads * seq * seq * dk + 10 * seq * d * cols,
            bytes_accessed=2 * heads * seq * seq + 30 * rows * d,
            transcendentals=heads * seq * seq,
        ),
    )(rel, lengths, bids, pad, again, fgain, wq, wo, tok, far, cot)


def ff_kernel(
    steps, done, extra,
    xt_hbm, w_hbm, ct_hbm, wo_hbm, mid_hbm, wq_hbm,
    grads_ref, din_hbm, near_hbm, far_hbm, back_hbm, half_hbm, hand_hbm, wfar_hbm,
    xt, ct, wg, wu, wo, hid, dg, du, din, stage, r1, r2, r3, r4, xs, xr, of,
    csem, wsem, s1, s2, s3, s4, t1, t2, t3, t4, xsem, osem, hsem,
):
    f, total = hid.shape
    rows = total // 2
    chunks = rows // BLK
    d = xt.shape[0]
    shard = d // 16
    dp, mp = lax.axis_index("dp"), lax.axis_index("mp")
    a = group_coords(dp // extra)
    peers = [flip(dp, m * extra) for m in GROUP_MASKS]
    other = (dp, 1 - mp)
    core = dp % 2
    sibling = dp + 1 - 2 * core
    bufs = (r1, r2, r3, r4)
    sends, recvs = (s1, s2, s3, s4), (t1, t2, t3, t4)
    end = steps - 1

    def weight_copy(kind, n):
        src, dst = ((w_hbm.at[0], wg), (w_hbm.at[1], wu), (wo_hbm, wo))[kind]
        return pltpu.make_async_copy(src.at[:, lanes(n)], dst.at[:, lanes(n)], wsem.at[kind, n])

    def tok_copy(n):
        src, dst, start, size = (
            (xt_hbm, xt, rows, BLK), (ct_hbm, ct, rows, BLK),
            (xt_hbm, xt, 0, rows), (ct_hbm, ct, 0, rows), (xt_hbm, xt, rows + BLK, BLK),
        )[n]
        part = pl.ds(start, size)
        return pltpu.make_async_copy(src.at[:, part], dst.at[:, part], csem.at[n])

    near_part, far_part = pl.ds(0, rows), pl.ds(rows, rows)
    c_far = remote(
        ct_hbm.at[:, pl.ds(BLK, BLK)], ct.at[:, pl.ds(rows + BLK, BLK)], csem.at[5], csem.at[6], other
    )
    x_copy = remote(xs, xr, xsem.at[0], xsem.at[1], other)
    back_copy = remote(of.at[:, pl.ds(0, 128)], back_hbm, xsem.at[2], xsem.at[3], other)
    wq_rows = wq_hbm.shape[0] // 2
    wq_part = pl.ds(core * wq_rows, wq_rows)
    w_copy = remote(wq_hbm.at[wq_part], wfar_hbm.at[wq_part], xsem.at[4], xsem.at[5], other)
    w_pass = remote(wfar_hbm.at[wq_part], wfar_hbm.at[wq_part], xsem.at[6], xsem.at[7], (sibling, mp))
    mid_copy = pltpu.make_async_copy(mid_hbm, din.at[:, far_part], osem.at[3])

    def hop(level, n):
        half = 8 >> level
        away = pl.ds((1 - a[level]) * half, half)
        src = stage.at[away] if level == 0 else bufs[level - 1].at[n, away]
        return remote(src, bufs[level].at[n], sends[level].at[n], recvs[level].at[n], (peers[level], mp))

    def hand_copy(n):
        if isinstance(n, int) and n == done:
            return pltpu.make_async_copy(r2.at[n], half_hbm, hsem.at[0])
        return pltpu.make_async_copy(r1.at[n], hand_hbm.at[n - done - 1], hsem.at[n - done])

    def absorb_first(n):
        hop(0, n).wait()
        r1[n] = stage[pl.ds(a[0] * 8, 8)] + r1[n]
        if isinstance(n, int):
            hand_copy(n).start()
            return

        @pl.when(n <= done)
        def _():
            hop(1, n).start()

        @pl.when(n > done)
        def _():
            hand_copy(n).start()

    def absorb(level, n):
        half = 8 >> level
        hop(level, n).wait()
        kept = bufs[level - 1][n, pl.ds(a[level] * half, half)]
        if level < 3:
            bufs[level][n] = kept + bufs[level][n]
            if n < done:
                hop(level + 1, n).start()
            else:
                hand_copy(n).start()
        else:
            both = kept.astype(F32) + bufs[level][n].astype(F32)
            for w in range(3):
                grads_ref[w, :, n * BLK : (n + 1) * BLK] = both[0, w]

    scale = np.float32(np.sqrt(2 / np.pi))

    def place(u):
        early, late = u // steps, (u - 4) // steps
        is_far0 = (early == 0) * 1
        is_far1 = (late == 1) * 1
        v = u - steps
        n = v - steps * (u // (2 * steps + 4))
        near_j, near_c = n // 2, n % 2
        j = is_far0 * u + is_far1 * (u - steps - 4) + (1 - is_far0 - is_far1) * near_j
        c = is_far0 * chunks + is_far1 * (chunks + 1) + (1 - is_far0 - is_far1) * near_c
        return j, c

    def substep(u):
        j, c = place(u)
        pj, pc = place(u - 1)
        pj = pj + (u == 0) * 1
        fcols, tok = lanes(j), lanes(c)
        pcols, ptok = lanes(pj), lanes(pc)
        gate = dot(wg[:, fcols], xt[:, tok], ((0,), (0,)))
        up = dot(wu[:, fcols], xt[:, tok], ((0,), (0,)))
        dh = dot(wo[:, fcols], ct[:, tok], ((0,), (0,)))
        backward(pcols, ptok)
        sq = gate * gate
        t = jnp.tanh(scale * gate * (1.0 + 0.044715 * sq))
        half = 0.5 * (1.0 + t)
        act = gate * half
        slope = half + 0.5 * gate * (1.0 - t * t) * (scale * (1.0 + (3 * 0.044715) * sq))
        hid[fcols, tok] = (act * up).astype(BF)
        dg[fcols, tok] = (dh * (up * slope)).astype(BF)
        du[fcols, tok] = (dh * act).astype(BF)

    def backward(rs, tok):
        din[:, tok] += dot(wg[:, rs], dg[rs, tok], ((1,), (0,))) + dot(wu[:, rs], du[rs, tok], ((1,), (0,)))

    per = 4 * shard

    def grads(j):
        z = j // end
        for w in range(3):
            right = (hid, dg, du)[w][lanes(j), :]
            for q in range(4):
                rs = slice(q * per, (q + 1) * per)
                left = ct[rs, :] if w == 0 else xt[rs, :]
                part = dot(left, right, ((1,), (1,)))
                for k in range(4):
                    at = block_position(4 * q + k, Y_FIRST)
                    at = at + z * (block_position(4 * q + k, Z_FIRST) - at)
                    stage[at, w, 0:shard, :] = part[k * shard : (k + 1) * shard].astype(BF)
        hop(0, j).start()

    def out_part(n):
        return dot(wo[...], hid[:, lanes(n)], ((1,), (0,)))

    meet([(p, mp) for p in peers] + [other] + ([(sibling, mp)] if extra > 1 else []))
    c_far.start()
    w_copy.start()
    tok_copy(0).start()
    tok_copy(1).start()
    for n in range(steps):
        for kind in range(3):
            weight_copy(kind, n).start()
    for n in range(2, 5):
        tok_copy(n).start()
    din[...] = jnp.zeros_like(din)
    stage[...] = jnp.zeros_like(stage)
    before = place(-1)[1]
    dg[0:BLK, before * BLK : (before + 1) * BLK] = jnp.zeros((BLK, BLK), BF)
    du[0:BLK, before * BLK : (before + 1) * BLK] = jnp.zeros((BLK, BLK), BF)
    tok_copy(0).wait()
    tok_copy(1).wait()
    count = 2 * chunks * steps
    far_end = 2 * steps + 4

    def step(u, carry):
        @pl.when(u < steps)
        def _():
            for kind in range(3):
                weight_copy(kind, u).wait()

        @pl.when(u == steps)
        def _():
            tok_copy(2).wait()
            tok_copy(3).wait()

        @pl.when(u == steps + 4)
        def _():
            tok_copy(4).wait()
            c_far.wait()

        @pl.when(u < count)
        def _():
            substep(u)

        @pl.when(u == far_end)
        def _():
            xs[...] = din[:, far_part].astype(BF)
            x_copy.start()
            mid_copy.start()

        @pl.when(u == count)
        def _():
            pj, pc = place(count - 1)
            backward(lanes(pj), lanes(pc))

            def one(n, carry):
                of[:, lanes(n)] = out_part(n + chunks).astype(BF)
                return carry

            lax.fori_loop(0, chunks, one, 0)

        n = (u - far_end + 1) // 2

        @pl.when((u >= far_end + 1) & (u % 2 == (far_end + 1) % 2))
        def _():
            absorb_first(n - 1)

        @pl.when((u >= far_end - 1) & (u % 2 == (far_end + 1) % 2))
        def _():
            for at, events in ((3, ((1, 0),)), (5, ((1, 1), (2, 0))), (6, ((2, 1), (3, 0)))):
                @pl.when(n == at)
                def _():
                    for level, block in events:
                        absorb(level, block)

            grads(n)

        @pl.when(u == far_end + 5)
        def _():
            w_copy.wait()
            w_pass.start()

        return carry

    lax.fori_loop(0, count + 2, step, 0)
    x_copy.wait()
    back_copy.start()
    rest = far_hbm.shape[1]
    far_copy = pltpu.make_async_copy(of.at[:, pl.ds(128, rest)], far_hbm, osem.at[0])
    far_copy.start()
    mid_copy.wait()

    def one(n, carry):
        at = lanes(n + chunks)
        din[:, at] = din[:, at] + out_part(n)
        return carry

    lax.fori_loop(0, chunks, one, 0)
    near_copy = pltpu.make_async_copy(din.at[:, far_part], near_hbm, osem.at[1])
    near_copy.start()
    absorb_first(end)
    absorb(1, done)
    din[:, near_part] += xr[...].astype(F32)
    din_copy = pltpu.make_async_copy(din.at[:, near_part], din_hbm, osem.at[2])
    din_copy.start()
    absorb(3, 1)
    w_pass.wait()

    for n in range(done, steps):
        hand_copy(n).wait()
    far_copy.wait()
    near_copy.wait()
    din_copy.wait()
    back_copy.wait()


def ff_all(xt, ct, w2, wo, mid, wq, extra):
    d, total = xt.shape
    f = wo.shape[1]
    rows = total // 2
    steps = f // BLK
    done = FF_DONE
    shard = d // 16
    spad = -(-shard // 16) * 16
    dma = pltpu.SemaphoreType.DMA
    any_spec = pl.BlockSpec(memory_space=pl.ANY)
    return pl.pallas_call(
        functools.partial(ff_kernel, steps, done, extra),
        in_specs=[any_spec] * 6,
        out_specs=[pl.BlockSpec(memory_space=pltpu.VMEM)] + [any_spec] * 7,
        out_shape=[
            jax.ShapeDtypeStruct((3, spad, done * BLK), F32),
            jax.ShapeDtypeStruct((d, rows), F32),
            jax.ShapeDtypeStruct((d, rows), F32),
            jax.ShapeDtypeStruct((d, rows - 128), BF),
            jax.ShapeDtypeStruct((d, 128), BF),
            jax.ShapeDtypeStruct((4, 3, spad, BLK), BF),
            jax.ShapeDtypeStruct((steps - done - 1, 8, 3, spad, BLK), BF),
            jax.ShapeDtypeStruct(wq.shape, BF),
        ],
        scratch_shapes=[
            pltpu.VMEM((d, total), BF),
            pltpu.VMEM((d, total), BF),
            pltpu.VMEM((d, f), BF),
            pltpu.VMEM((d, f), BF),
            pltpu.VMEM((d, f), BF),
            pltpu.VMEM((f, total), BF),
            pltpu.VMEM((f, total), BF),
            pltpu.VMEM((f, total), BF),
            pltpu.VMEM((d, total), F32),
            pltpu.VMEM((16, 3, spad, BLK), BF),
            pltpu.VMEM((steps, 8, 3, spad, BLK), BF),
            pltpu.VMEM((done + 1, 4, 3, spad, BLK), BF),
            pltpu.VMEM((done, 2, 3, spad, BLK), BF),
            pltpu.VMEM((done, 1, 3, spad, BLK), BF),
            pltpu.VMEM((d, rows), BF),
            pltpu.VMEM((d, rows), BF),
            pltpu.VMEM((d, rows), BF),
            dma((7,)),
            dma((3, steps)),
            dma((steps,)), dma((done + 1,)), dma((done,)), dma((done,)),
            dma((steps,)), dma((done + 1,)), dma((done,)), dma((done,)),
            dma((8,)),
            dma((4,)),
            dma((steps - done,)),
        ],
        compiler_params=pltpu.CompilerParams(
            vmem_limit_bytes=FF_VMEM, collective_id=0, has_side_effects=True
        ),
        cost_estimate=pl.CostEstimate(
            flops=18 * total * d * f,
            bytes_accessed=6 * d * f + 16 * total * d,
            transcendentals=total * f,
        ),
    )(xt, w2, ct, wo, mid, wq)


def tail_kernel(
    heads, dk, buckets, blocks, extra, first,
    bid_ref, qkv_ref, e_ref, inv_ref, wall_ref, ctx_ref, ag_ref, fg_ref, early_ref,
    din_hbm, mid_hbm, cot_hbm, tok_hbm, nrm_hbm, wq_hbm, wfar_hbm, near_hbm, back_hbm, far_hbm, part_hbm, hand_hbm,
    ig_hbm, res_hbm, gq_ref, go_ref, small_ref, ffo_ref, ffi_ref,
    f1, f2, f3, f4, nrm, wq, wn, wf, alow, dctx, dcs, osend, orecv, fsum, agc, fgc,
    dp_s, dkv, tally, dproj, dfar, grad, back0, back,
    sa, sb_, a1, a2, a3, a4, b1, b2, b3, b4, hk, hm, h2, h3, h4, sv, rv,
    lsem, ksem, xs_sem, xr_sem, cs_sem, cr_sem, bs_sem, br_sem, hs_sem, hr_sem,
):
    qb = pl.program_id(0)
    dp, x = lax.axis_index("dp"), lax.axis_index("mp")
    d, rows = f2.shape
    cols = heads * dk
    shard = d // 16
    a = group_coords(dp // extra)
    peers = [flip(dp, m * extra) for m in GROUP_MASKS]
    other = (dp, 1 - x)
    near_blocks = blocks // 2
    near_part, far_part = pl.ds(0, rows), pl.ds(rows, rows)
    halves = ((sa, a1, a2, a3, a4), (sb_, b1, b2, b3, b4))
    orders = (Y_FIRST, Z_FIRST)
    copies = (
        (din_hbm, f1), (mid_hbm, f2), (cot_hbm, f3), (tok_hbm, f2), (nrm_hbm, nrm), (wq_hbm, wq), (wfar_hbm, wq),
        (back_hbm, back0), (near_hbm.at[:, pl.ds(0, BLK)], f4), (near_hbm.at[:, pl.ds(BLK, BLK)], f4),
        (f4, res_hbm.at[:, pl.ds(0, BLK)]), (f4, res_hbm.at[:, pl.ds(BLK, BLK)]),
    )

    def local(i):
        return pltpu.make_async_copy(copies[i][0], copies[i][1], lsem.at[i])

    def x_copy(i, src, dst):
        return remote(src, dst, xs_sem.at[i], xr_sem.at[i], other)

    dctx_copy = x_copy(0, dcs, dctx.at[:, far_part])
    o_copy = x_copy(1, osend, orecv)
    dproj_copy = x_copy(2, dproj.at[:, far_part], dfar)

    def back_copy(i):
        part = pl.ds(i * 128, 128)
        return x_copy(3 + i, far_hbm.at[:, part], back.at[:, part])

    def hop(side, level):
        half = 8 >> level
        c = orders[side][level]
        away = pl.ds((1 - a[c]) * half, half)
        bufs = halves[side]
        return remote(
            bufs[level].at[away], bufs[level + 1], cs_sem.at[side, level], cr_sem.at[side, level], (peers[c], x)
        )

    def absorb(side, level):
        half = 8 >> level
        bufs = halves[side]
        hop(side, level).wait()
        kept = bufs[level][pl.ds(a[orders[side][level]] * half, half)]
        if level < 3:
            bufs[level + 1][...] = kept + bufs[level + 1][...]
            hop(side, level + 1).start()
            return
        both = (kept.astype(F32) + bufs[level + 1][...].astype(F32))[0, 0:shard]
        outs = (gq_ref.at[0], gq_ref.at[1]) if side == 0 else (gq_ref.at[2], go_ref)
        for i in range(2):
            outs[i][...] = both[:, i * cols : (i + 1) * cols]

    def order_of(block):
        return Z_FIRST if block == 4 else Y_FIRST

    def keep_copy(block):
        if block == 0:
            return pltpu.make_async_copy(part_hbm.at[pl.ds(a[2] * 2, 2)], hm, ksem.at[0])
        keep = pl.ds(a[order_of(block)[1]] * 4, 4)
        return pltpu.make_async_copy(hand_hbm.at[block - 1, keep], hk.at[block - 1], ksem.at[block])

    def hand_hop(level, block):
        half = 8 >> level
        c = order_of(block)[level]
        away = pl.ds((1 - a[c]) * half, half)
        if level == 1:
            src, dst = hand_hbm.at[block - 1, away], h2.at[block - 1]
        elif level == 2:
            src, dst = part_hbm.at[away] if block == 0 else h2.at[block - 1, away], h3.at[block]
        else:
            src, dst = h3.at[block, away], h4.at[block]
        return remote(src, dst, hs_sem.at[level, block], hr_sem.at[level, block], (peers[c], x))

    def put_grads(w, block, value):
        at = slice(block * BLK, (block + 1) * BLK)
        if w == 0:
            ffo_ref[:, at] = value
        else:
            ffi_ref[:, w - 1, at] = value

    def hand_absorb(level, block):
        half = 8 >> level
        keep = pl.ds(a[order_of(block)[level]] * half, half)
        hand_hop(level, block).wait()
        if level == (2 if block == 0 else 1):
            keep_copy(block).wait()
            kept = hm[...] if block == 0 else hk[block - 1]
        else:
            kept = h2[block - 1, keep] if level == 2 else h3[block, keep]
        if level == 1:
            h2[block - 1] = kept + h2[block - 1]
        elif level == 2:
            h3[block] = kept + h3[block]
        else:
            both = kept.astype(F32) + h4[block].astype(F32)
            for w in range(3):
                put_grads(w, first + block, both[0, w, 0:shard])
        if level < 3:
            hand_hop(level + 1, block).start()

    def round_copy(i):
        who = other if i == 4 else (peers[(0, 2, 3, 1)[i]], x)
        return remote(sv.at[i], rv.at[i], bs_sem.at[i], br_sem.at[i], who)

    def round_end(i):
        round_copy(i).wait()
        sv[i + 1] = sv[i] + rv[i]
        if i < 4:
            round_copy(i + 1).start()

    def out_copy(r):
        return pltpu.make_async_copy(f3.at[:, lanes(r)], ig_hbm.at[:, lanes(r)], lsem.at[len(copies) + r])

    def lane_sum(v):
        total = v[:, 0:128]
        for i in range(1, v.shape[1] // 128):
            total = total + v[:, i * 128 : (i + 1) * 128]
        return total

    @pl.when(qb == 0)
    def _():
        for i in range(3):
            local(i).start()
        meet([(p, x) for p in peers] + [other])
        back_copy(0).start()
        for block in (0, 4, 1, 2, 3):
            hand_hop(2 if block == 0 else 1, block).start()
        agc[...] = column(ag_ref[...])
        fgc[...] = column(fg_ref[...])
        dkv[...] = jnp.zeros_like(dkv)
        tally[...] = jnp.zeros_like(tally)
        sa[...] = jnp.zeros_like(sa)
        sb_[...] = jnp.zeros_like(sb_)
        fsum[...] = jnp.zeros_like(fsum)
        for i in range(3):
            local(i).wait()

        def norm_rows(r, carry):
            ls = lanes(r)
            v = f2[:, ls]
            c = f1[:, ls]
            scale = norm_scale(v)
            n = v * scale
            cg = c * fgc[...]
            m = jnp.mean(cg * n, axis=0, keepdims=True)
            gm = f3[:, ls] + scale * (cg - n * m)
            fsum[...] += lane_sum(c * n)
            f1[:, ls] = gm
            alow[:, ls] = gm.astype(BF)
            return carry

        lax.fori_loop(0, near_blocks, norm_rows, 0)
        dcs[...] = dot(wall_ref[cols : 2 * cols, :], alow[...], ((1,), (0,))).astype(BF)
        dctx_copy.start()
        for i in (3, 4, 5, 7, 8):
            local(i).start()
        for block in (0, 4, 1, 2, 3):
            keep_copy(block).start()
        dctx[:, near_part] = dot(wall_ref[0:cols, :], alow[...], ((1,), (0,))).astype(BF)
        osend[...] = dot(alow[...], ctx_ref[cols : 2 * cols, near_part], ((1,), (1,))).astype(BF)
        o_copy.start()
        grad[:, 3 * cols : 4 * cols] = dot(alow[...], ctx_ref[0:cols, near_part], ((1,), (1,)))
        for w in range(3):
            for block in range(first):
                put_grads(w, block, early_ref[w, 0:shard, block * BLK : (block + 1) * BLK])
        dctx_copy.wait()
        back_copy(1).start()

    @pl.when(qb == 1)
    def _():
        local(5).wait()
        wn[...] = wq[...].astype(F32).T.astype(BF)
        local(6).start()
        hand_absorb(2, 0)

    @pl.when(qb == 2)
    def _():
        local(6).wait()
        wf[...] = wq[...].astype(F32).T.astype(BF)
        hand_absorb(1, 1)
        hand_absorb(1, 4)
        local(7).wait()
        local(8).wait()
        back_copy(0).wait()
        f4[:, 0:128] += back0[...].astype(F32)
        f4[:, 128:BLK] += back[:, 0:128].astype(F32)
        local(10).start()

    @pl.when(qb == 3)
    def _():
        hand_absorb(3, 0)
        hand_absorb(2, 1)

    q_true = (qb + near_blocks * x) % blocks

    def head(h, carry):
        def head_rows(group):
            return pl.ds(pl.multiple_of(group * cols + h * dk, dk), dk)

        inv = inv_ref[h, 0]
        qh = qkv_ref[head_rows(0), lanes(qb)]
        scaled = (dctx[head_rows(0), lanes(qb)].astype(F32) * inv).astype(BF)
        inner = jnp.zeros((1, BLK), F32)
        for kb in range(blocks):
            krows = slice(kb * BLK, (kb + 1) * BLK)
            g = dot(qkv_ref[head_rows(2), krows], scaled, ((0,), (0,)))
            dp_s[krows, :] = g
            inner = inner + jnp.sum(e_ref[h, 0, krows, :].astype(F32) * g, axis=0, keepdims=True)
        inner = inner * inv
        dq = jnp.zeros((dk, BLK), F32)
        for kb in range(blocks):
            krows = slice(kb * BLK, (kb + 1) * BLK)
            e = e_ref[h, 0, krows, :]
            ds = (e.astype(F32) * (dp_s[krows, :] - inner)).astype(BF)
            dkv[head_rows(0), krows] += dot(qh, ds, ((1,), (1,)))
            dkv[head_rows(1), krows] += dot(scaled, e, ((1,), (1,)))
            dq = dq + dot(qkv_ref[head_rows(1), krows], ds, ((1,), (0,)))
            tally[h, near_diagonal((kb + near_blocks * x) % blocks - q_true)] += ds.astype(F32)
        dproj[head_rows(0), lanes(qb)] = dq.astype(BF)
        return carry

    lax.fori_loop(0, heads, head, 0)

    @pl.when(qb == blocks - 1)
    def _():
        dproj[cols : 3 * cols, :] = dkv[...].astype(BF)
        dproj_copy.start()
        back_copy(2).start()
        local(3).wait()
        local(4).wait()
        per = 4 * shard

        def grad_rows(q, carry):
            rs = pl.ds(pl.multiple_of(q * per, 16), per)
            grad[rs, 0 : 3 * cols] = dot(nrm[rs, :], dproj[...], ((1,), (1,)))
            return carry

        lax.fori_loop(0, 4, grad_rows, 0)
        o_copy.wait()
        grad[:, 3 * cols : 4 * cols] += orecv[...].astype(F32)
        for side in range(2):
            for k in range(16):
                halves[side][0][block_position(k, orders[side]), 0:shard, :] = grad[
                    k * shard : (k + 1) * shard, 2 * side * cols : 2 * (side + 1) * cols
                ].astype(BF)
            hop(side, 0).start()
        hand_absorb(1, 2)
        hand_absorb(2, 4)

        def near_rows(r, carry):
            f3[:, lanes(r)] = dot(wn[...], dproj[:, lanes(r)], ((1,), (0,)))
            return carry

        lax.fori_loop(0, near_blocks, near_rows, 0)
        absorb(0, 0)
        absorb(1, 0)
        hand_absorb(1, 3)
        hand_absorb(3, 1)
        hand_absorb(2, 2)
        ids = bid_ref[...]
        hot = ids == lax.broadcasted_iota(jnp.int32, (buckets, SPAN), 0)
        out_lane = lax.broadcasted_iota(jnp.int32, (buckets, 128), 1)
        sub = lax.broadcasted_iota(jnp.int32, (8, SPAN), 0)
        sv[0] = jnp.zeros(sv.shape[1:], F32)

        def bias_sums(hh, carry):
            line = jnp.zeros((8, SPAN), F32)
            for g in range(BLK // 8):
                group = slice(8 * g, 8 * g + 8)
                parts = [tally[hh, i, group, :] for i in (4, 3, 2, 1, 0)]
                strip = jnp.concatenate(parts + [jnp.zeros((8, BLK), F32)], axis=1)
                line = line + (strip if g == 0 else pltpu.roll(strip, SPAN - 8 * g, 1))
            for bit in (1, 2, 4):
                line = jnp.where((sub // bit) % 2 == 1, pltpu.roll(line, SPAN - bit, 1), line)
            sums = jnp.sum(line, axis=0, keepdims=True)
            col = jnp.sum(jnp.where(hot, sums, 0.0), axis=1, keepdims=True)
            sv[0, 0:buckets, :] = jnp.where(out_lane == x * heads + hh, col, sv[0, 0:buckets, :])
            return carry

        lax.fori_loop(0, heads, bias_sums, 0)
        product = wn[...].astype(F32) * grad[:, 0 : 3 * cols]
        again = lane_sum(product[:, 0:512]).T
        rest = product[:, 512 : 3 * cols]
        again = jnp.sum(again, axis=0, keepdims=True) + jnp.sum(rest.T, axis=0, keepdims=True)
        again = again / ag_ref[...]
        fgain = jnp.sum(fsum[...].T, axis=0, keepdims=True)
        lines = -(-d // 128)
        for i in range(lines):
            n = min(128, d - 128 * i)
            sv[0, buckets + i : buckets + i + 1, 0:n] = again[:, 128 * i : 128 * i + n]
            sv[0, buckets + lines + i : buckets + lines + i + 1, 0:n] = fgain[:, 128 * i : 128 * i + n]
        round_copy(0).start()
        absorb(0, 1)
        absorb(1, 1)
        round_end(0)
        hand_absorb(3, 4)
        hand_absorb(2, 3)
        local(10).wait()
        local(9).start()
        round_end(1)
        dproj_copy.wait()

        def last_norm(r, carry):
            ls = lanes(r)
            c = f3[:, ls] + dot(wf[...], dfar[:, ls], ((1,), (0,)))
            v = f2[:, ls]
            scale = norm_scale(v)
            n = v * scale
            cg = c * agc[...]
            m = jnp.mean(cg * n, axis=0, keepdims=True)
            f3[:, ls] = f1[:, ls] + scale * (cg - n * m)
            out_copy(r).start()
            return carry

        lax.fori_loop(0, near_blocks, last_norm, 0)
        absorb(0, 2)
        absorb(1, 2)
        hand_absorb(3, 2)
        round_end(2)
        back_copy(1).wait()
        back_copy(2).wait()
        local(9).wait()
        f4[...] += back[:, 128 : 128 + BLK].astype(F32)
        local(11).start()
        hand_absorb(3, 3)
        round_end(3)
        absorb(0, 3)
        absorb(1, 3)
        round_end(4)
        small_ref[...] = sv[5]
        local(11).wait()
        for r in range(near_blocks):
            out_copy(r).wait()


def tail(qkv, e, inv, wall, ctx, again, fgain, early, din, mid, cot, tok, nrm, wq, wfar, near_out, back, far,
         half_way, hand, buckets, heads, dk, extra, f):
    d, rows = tok.shape
    seq = 2 * rows
    cols = heads * dk
    blocks = seq // BLK
    near = blocks // 2
    shard = d // 16
    spad = -(-shard // 16) * 16
    later = hand.shape[0] + 1
    first = early.shape[2] // BLK
    lines = -(-(buckets + 2 * -(-d // 128)) // 8) * 8
    bids = jnp.asarray(lane_buckets(buckets))
    one = pl.Buffered(1)
    dma = pltpu.SemaphoreType.DMA
    any_spec = pl.BlockSpec(memory_space=pl.ANY)

    def full(v):
        return pl.BlockSpec(v.shape, lambda i: (0,) * len(v.shape), pipeline_mode=one)

    def chain(width):
        return [pltpu.VMEM((n, spad, width), BF) for n in (16, 8, 4, 2, 1)]

    outs = [
        jax.ShapeDtypeStruct((3, shard, cols), F32),
        jax.ShapeDtypeStruct((shard, cols), F32),
        jax.ShapeDtypeStruct((lines, 128), F32),
        jax.ShapeDtypeStruct((shard, f), F32),
        jax.ShapeDtypeStruct((shard, 2, f), F32),
    ]
    a_chain, b_chain = chain(2 * cols), chain(2 * cols)
    return pl.pallas_call(
        functools.partial(tail_kernel, heads, dk, buckets, blocks, extra, first),
        grid=(blocks,),
        in_specs=[
            full(bids),
            full(qkv),
            pl.BlockSpec((heads, 1, seq, BLK), lambda i: (0, i, 0, 0)),
            pl.BlockSpec((heads, 1, 1, BLK), lambda i: (0, i, 0, 0)),
            full(wall),
            full(ctx),
            full(again),
            full(fgain),
            full(early),
        ]
        + [any_spec] * 12,
        out_specs=[any_spec, any_spec] + [full(v) for v in outs],
        out_shape=[jax.ShapeDtypeStruct((d, rows), F32), jax.ShapeDtypeStruct((d, rows), F32)] + outs,
        scratch_shapes=[
            pltpu.VMEM((d, rows), F32),
            pltpu.VMEM((d, rows), F32),
            pltpu.VMEM((d, rows), F32),
            pltpu.VMEM((d, BLK), F32),
            pltpu.VMEM((d, seq), BF),
            pltpu.VMEM((3 * cols, d), BF),
            pltpu.VMEM((d, 3 * cols), BF),
            pltpu.VMEM((d, 3 * cols), BF),
            pltpu.VMEM((d, rows), BF),
            pltpu.VMEM((cols, seq), BF),
            pltpu.VMEM((cols, rows), BF),
            pltpu.VMEM((d, cols), BF),
            pltpu.VMEM((d, cols), BF),
            pltpu.VMEM((d, 128), F32),
            pltpu.VMEM((d, 1), F32),
            pltpu.VMEM((d, 1), F32),
            pltpu.VMEM((seq, BLK), F32),
            pltpu.VMEM((2 * cols, seq), F32),
            pltpu.VMEM((heads, 5, BLK, BLK), F32),
            pltpu.VMEM((3 * cols, seq), BF),
            pltpu.VMEM((3 * cols, rows), BF),
            pltpu.VMEM((d, 4 * cols), F32),
            pltpu.VMEM((d, 128), BF),
            pltpu.VMEM((d, rows - 128), BF),
            a_chain[0],
            b_chain[0],
        ]
        + a_chain[1:]
        + b_chain[1:]
        + [
            pltpu.VMEM((later - 1, 4, 3, spad, BLK), BF),
            pltpu.VMEM((2, 3, spad, BLK), BF),
            pltpu.VMEM((later - 1, 4, 3, spad, BLK), BF),
            pltpu.VMEM((later, 2, 3, spad, BLK), BF),
            pltpu.VMEM((later, 1, 3, spad, BLK), BF),
            pltpu.VMEM((6, lines, 128), F32),
            pltpu.VMEM((5, lines, 128), F32),
            dma((12 + near,)),
            dma((later,)),
            dma((6,)), dma((6,)),
            dma((2, 4)), dma((2, 4)),
            dma((5,)), dma((5,)),
            dma((4, later)), dma((4, later)),
        ],
        compiler_params=pltpu.CompilerParams(
            vmem_limit_bytes=FF_VMEM, collective_id=1, has_side_effects=True
        ),
        cost_estimate=pl.CostEstimate(
            flops=32 * heads * seq * seq * dk + 8 * seq * d * 3 * cols,
            bytes_accessed=2 * heads * seq * seq + 30 * rows * d,
            transcendentals=0,
        ),
    )(bids, qkv, e, inv, wall, ctx, again, fgain, early, din, mid, cot, tok, nrm, wq, wfar, near_out, back, far,
      half_way, hand)


def take(array, index):
    return lax.dynamic_index_in_dim(array, index, 0, keepdims=False)


def per_device(
    tokens,
    cotangent,
    doc_lengths,
    pad_mask,
    attn_gain,
    qkv_weight,
    rel_table,
    out_weight,
    ff_gain,
    ff_in_weight,
    ff_out_weight,
):
    rows, d = tokens.shape
    n_dp = lax.axis_size("dp")
    n_mp = lax.axis_size("mp")
    cols = qkv_weight.shape[2]
    buckets, heads = rel_table.shape
    dk = cols // heads
    me = lax.axis_index("dp")
    shard = d // n_dp
    extra = n_dp // 16

    def hop(v, mask):
        return lax.ppermute(v, "dp", [(i, i ^ mask) for i in range(n_dp)])

    def bit(b):
        return (me >> b) & 1

    def finish(g):
        parts = [g.reshape((extra, shard) + g.shape[1:])]
        for b in reversed(range(extra.bit_length() - 1)):
            halves = [p.reshape((2, p.shape[0] // 2) + p.shape[1:]) for p in parts]
            away = sum(take(p, 1 - bit(b)).astype(F32) for p in halves).astype(BF)
            parts = [take(p, bit(b)) for p in halves] + [hop(away, 1 << b)]
        return sum(p.astype(F32) for p in parts)[0]

    tok = tokens.T
    cot = cotangent.T
    far = lax.ppermute(tok.astype(BF), "mp", [(0, 1), (1, 0)])
    w2 = jnp.transpose(ff_in_weight, (1, 0, 2))
    wq = jnp.transpose(qkv_weight, (1, 2, 0)).reshape(3 * cols, d)
    again, fgain = attn_gain.reshape(1, d), ff_gain.reshape(1, d)

    e, inv, qkv, ctx, nrm, xt, mid, ct, wall = front(
        rel_table, doc_lengths, pad_mask, again, fgain, wq, out_weight.T, tok, far, cot, heads, dk
    )
    early, din, near_out, far_out, back, half_way, hand, wfar = ff_all(
        xt, ct, w2, ff_out_weight, mid, wq, extra
    )
    input_grad, result, grad_qkv, grad_out, small, ffo, ffi = tail(
        qkv, e, inv, wall, ctx, again, fgain, early, din, mid, cot, tok, nrm, wq, wfar, near_out, back, far_out,
        half_way, hand, buckets, heads, dk, extra, ff_out_weight.shape[1],
    )
    grad_qkv = jnp.transpose(grad_qkv, (1, 0, 2))
    if extra > 1:
        grad_qkv, grad_out, ffo, ffi = (finish(g) for g in (grad_qkv, grad_out, ffo, ffi))
    for b in range(extra.bit_length() - 1):
        small = small + hop(small, 1 << b)
    lines = -(-d // 128)
    return (
        result.T,
        input_grad.T,
        small[buckets : buckets + lines].reshape(-1)[:d],
        grad_qkv,
        small[:buckets, : heads * n_mp],
        grad_out,
        small[buckets + lines : buckets + 2 * lines].reshape(-1)[:d],
        ffi,
        ffo,
    )


def solution(mesh):
    return jax.shard_map(
        per_device,
        mesh=mesh,
        in_specs=(
            P(("dp", "mp"), None),
            P(("dp", "mp"), None),
            P("dp", None),
            P("dp", None),
            P(),
            P(None, None, "mp"),
            P(None, "mp"),
            P(None, "mp"),
            P(),
            P(None, None, "mp"),
            P(None, "mp"),
        ),
        out_specs=(
            P(("dp", "mp"), None),
            P(("dp", "mp"), None),
            P(),
            P("dp", None, "mp"),
            P(),
            P("dp", "mp"),
            P(),
            P("dp", None, "mp"),
            P("dp", "mp"),
        ),
        check_vma=False,
    )
```

```python
import functools

import jax
import jax.numpy as jnp
import numpy as np
from jax import lax
from jax.experimental import pallas as pl
from jax.experimental.pallas import tpu as pltpu
from jax.sharding import PartitionSpec as P

MAXDIST = 128
norm_eps = 1e-06
BLK = 256
SPAN = 6 * BLK
REACH = 2
BF = jnp.bfloat16
F32 = jnp.float32
FF_VMEM = 63 << 20


def bucket_of(offsets, buckets, reach):
    half_range = buckets // 2
    upper_half = (offsets > 0).astype(np.int32) * half_range
    distance = np.abs(offsets)
    exact_range = half_range // 2
    safe_dist = np.maximum(distance, 1)
    log_bucket = exact_range + (
        np.log(safe_dist / exact_range) / np.log(reach / exact_range) * (half_range - exact_range)
    ).astype(np.int32)
    log_bucket = np.minimum(log_bucket, half_range - 1)
    return (upper_half + np.where(distance < exact_range, distance, log_bucket)).astype(np.int32)


def lane_buckets(buckets):
    lanes = np.arange(SPAN)
    shifted = np.where(lanes < 5 * BLK, lanes, lanes - SPAN)
    return bucket_of(REACH * BLK - shifted, buckets, MAXDIST).reshape(1, SPAN)


def dot(a, b, contract):
    return lax.dot_general(a, b, (contract, ((), ())), preferred_element_type=F32)


def flip(index, mask):
    out = index
    bit = 1
    while bit <= mask:
        if mask & bit:
            out = out + bit * (1 - 2 * (index // bit % 2))
        bit *= 2
    return out


GROUP_MASKS = (1, 2, 4, 12)


def group_coords(g):
    b = [g // (1 << i) % 2 for i in range(4)]
    return [b[0], b[1], (b[2] + b[3]) % 2, b[3]]


Y_FIRST = (0, 1, 2, 3)
Z_FIRST = (0, 2, 3, 1)
Z_BLOCK = 1
LEVELS = (4, 3, 3, 2)


def order_of(block):
    return Z_FIRST if block == Z_BLOCK else Y_FIRST


def levels_of(block):
    return LEVELS[block] if block < len(LEVELS) else 1


def block_position(k, order):
    b = [k >> i & 1 for i in range(4)]
    c = [b[0], b[1], b[2] ^ b[3], b[3]]
    return sum(c[order[i]] << (3 - i) for i in range(4))


def column(line):
    return jnp.broadcast_to(line, (8, line.shape[1])).T[:, 0:1]


def norm_scale(v):
    return lax.rsqrt(jnp.mean(v * v, axis=0, keepdims=True) + norm_eps)


def lanes(block):
    return pl.ds(pl.multiple_of(block * BLK, BLK), BLK)


def remote(src, dst, send, recv, who):
    return pltpu.make_async_remote_copy(
        src_ref=src,
        dst_ref=dst,
        send_sem=send,
        recv_sem=recv,
        device_id=who,
        device_id_type=pl.DeviceIdType.MESH,
    )


def meet(devices):
    barrier = pltpu.get_barrier_semaphore()
    for who in devices:
        pl.semaphore_signal(barrier, inc=1, device_id=who, device_id_type=pl.DeviceIdType.MESH)
    pl.semaphore_wait(barrier, len(devices))


def near_diagonal(offset):
    i = offset + 3
    return i + (6 - i) // 6 - i // 6 - 1


def front_kernel(
    heads, dk, buckets, blocks,
    rel_ref, len_ref, bid_ref, pad_ref, ag_ref, fg_ref, wq_ref, wo_ref,
    tok_hbm, far_hbm, cot_hbm,
    e_ref, inv_ref, qkv_ref, ctx_hbm, nrm_hbm, xt_hbm, mid_hbm, ct_hbm, wall_hbm,
    f1, fb, f3, cl, nrm, table, padc, mask, score, agc, fgc, wall, wn, call, xo,
    lsem, osem, wsend, wrecv, csend, crecv,
):
    qb = pl.program_id(0)
    dp, x = lax.axis_index("dp"), lax.axis_index("mp")
    d, rows = f1.shape
    cols = heads * dk
    half = cols // 2
    core = dp % 2
    other = (dp, 1 - x)
    sibling = (dp + 1 - 2 * core, x)
    near_blocks = blocks // 2
    part = pl.ds(core * half, half)
    far_part = pl.ds(cols + core * half, half)

    def local(i):
        src, dst = ((tok_hbm, f1), (far_hbm, fb), (cot_hbm, f3))[i]
        return pltpu.make_async_copy(src, dst, lsem.at[i])

    def out(i):
        src, dst = (
            (call, ctx_hbm), (nrm, nrm_hbm), (f1, mid_hbm), (cl, ct_hbm.at[:, pl.ds(0, rows)]), (wall, wall_hbm)
        )[i]
        return pltpu.make_async_copy(src, dst, osem.at[i])

    def xt_out(b):
        return pltpu.make_async_copy(xo.at[:, lanes(b)], xt_hbm.at[:, lanes(b)], osem.at[5 + b])

    w_copy = remote(wo_ref.at[part], wall.at[far_part], wsend.at[0], wrecv.at[0], other)
    w_pass = remote(wall.at[far_part], wall.at[far_part], wsend.at[1], wrecv.at[1], sibling)
    c_copy = remote(cl.at[:, pl.ds(0, BLK)], ct_hbm.at[:, pl.ds(rows, BLK)], wsend.at[2], wrecv.at[2], other)

    def ctx_copy(b):
        there = (b + near_blocks) % blocks
        return remote(
            call.at[pl.ds(0, cols), lanes(b)], call.at[pl.ds(cols, cols), lanes(there)],
            csend.at[b], crecv.at[b], other,
        )

    @pl.when(qb == 0)
    def _():
        for i in (2, 0, 1):
            local(i).start()
        meet([other, sibling])
        w_copy.start()
        wall[0:cols, :] = wo_ref[...]
        local(2).wait()
        cl[...] = f3[...].astype(BF)
        c_copy.start()
        out(3).start()
        agc[...] = column(ag_ref[...])
        fgc[...] = column(fg_ref[...])
        local(0).wait()
        local(1).wait()
        for b in range(blocks):
            ls = slice(b * BLK, (b + 1) * BLK)
            v = f1[:, ls] if b < near_blocks else fb[:, b * BLK - rows : (b + 1) * BLK - rows].astype(F32)
            nrm[:, ls] = (v * norm_scale(v) * agc[...]).astype(BF)
            qkv_ref[:, ls] = dot(wq_ref[...], nrm[:, ls], ((1,), (0,))).astype(BF)
        out(1).start()
        for i in range(2):
            start = (1 - x) * rows if i else x * rows
            line = pad_ref[:, pl.ds(pl.multiple_of(start, BLK), rows)].astype(F32)
            padc[i * rows : (i + 1) * rows, :] = jnp.broadcast_to(line, (8, rows)).T
        ids = bid_ref[...]
        for hh in range(heads):
            line = jnp.zeros((1, SPAN), F32)
            for b in range(buckets):
                line = jnp.where(ids == b, rel_ref[b, hh], line)
            turned = pltpu.roll(
                jnp.broadcast_to(line, (BLK, SPAN)), 0, 1, stride=1, stride_axis=0
            )
            for g in range(5):
                table[hh, g] = turned[:, BLK * (4 - g) : BLK * (5 - g)]

    @pl.when(qb == 1)
    def _():
        w_copy.wait()
        w_pass.start()

    q_true = (qb + near_blocks * x) % blocks

    q_pos = q_true * BLK + lax.broadcasted_iota(jnp.int32, (1, BLK), 1)
    k_iota = lax.broadcasted_iota(jnp.int32, (BLK, BLK), 0)
    for kb in range(blocks):
        k_pos = (kb + near_blocks * x) % blocks * BLK + k_iota
        bound = 0
        q_doc = jnp.zeros((1, BLK), jnp.int32)
        k_doc = jnp.zeros((BLK, BLK), jnp.int32)
        for i in range(len_ref.shape[1]):
            bound = bound + len_ref[0, i]
            q_doc = q_doc + (q_pos >= bound).astype(jnp.int32)
            k_doc = k_doc + (k_pos >= bound).astype(jnp.int32)
        krows = slice(kb * BLK, (kb + 1) * BLK)
        seen = (padc[krows, 0:1] > 0.5) | (k_pos == q_pos)
        mask[krows, :] = jnp.where((k_doc == q_doc) & seen, 0.0, -1000000000.0)

    def head_rows(h, group):
        return pl.ds(pl.multiple_of(group * cols + h * dk, dk), dk)

    def diagonal(kb):
        return near_diagonal((kb + near_blocks * x) % blocks - q_true)

    def head(h, carry):
        qh = qkv_ref[head_rows(h, 0), lanes(qb)]
        peak = None
        for kb in range(blocks):
            krows = slice(kb * BLK, (kb + 1) * BLK)
            s = dot(qkv_ref[head_rows(h, 1), krows], qh, ((0,), (0,)))
            diag = diagonal(kb)
            s = s + table[h, diag] + mask[krows, :]
            score[krows, :] = s
            top = jnp.max(s, axis=0, keepdims=True)
            peak = top if peak is None else jnp.maximum(peak, top)
        total = jnp.zeros((1, BLK), F32)
        ctx = jnp.zeros((dk, BLK), F32)
        for kb in range(blocks):
            krows = slice(kb * BLK, (kb + 1) * BLK)
            e = jnp.exp(score[krows, :] - peak)
            total = total + jnp.sum(e, axis=0, keepdims=True)
            e_low = e.astype(BF)
            e_ref[h, 0, krows, :] = e_low
            ctx = ctx + dot(qkv_ref[head_rows(h, 2), krows], e_low, ((1,), (0,)))
        inv = 1.0 / total
        inv_ref[h, 0] = inv
        call[head_rows(h, 0), lanes(qb)] = (ctx * inv).astype(BF)
        return carry

    lax.fori_loop(0, heads, head, 0)
    ctx_copy(qb).start()

    @pl.when(qb == blocks - 1)
    def _():
        w_pass.wait()
        wn[...] = wall[...].astype(F32).T.astype(BF)
        out(4).start()
        for i in range(blocks):
            b = (i + near_blocks) % blocks
            ctx_copy(i).wait()
            ls = slice(b * BLK, (b + 1) * BLK)
            v = dot(wn[...], call[:, ls], ((1,), (0,)))
            if b < near_blocks:
                v = v + f1[:, ls]
                f1[:, ls] = v
            else:
                v = v + fb[:, b * BLK - rows : (b + 1) * BLK - rows].astype(F32)
            xo[:, ls] = (v * norm_scale(v) * fgc[...]).astype(BF)
            xt_out(b).start()
        out(0).start()
        out(2).start()
        c_copy.wait()
        for i in range(5):
            out(i).wait()
        for b in range(blocks):
            xt_out(b).wait()


def front(rel, lengths, pad, again, fgain, wq, wo, tok, far, cot, heads, dk):
    d, rows = tok.shape
    seq = 2 * rows
    cols = heads * dk
    blocks = seq // BLK
    buckets = rel.shape[0]
    bids = jnp.asarray(lane_buckets(buckets))
    one = pl.Buffered(1)
    dma = pltpu.SemaphoreType.DMA
    any_spec = pl.BlockSpec(memory_space=pl.ANY)
    smem = pl.BlockSpec(memory_space=pltpu.SMEM)

    def full(v):
        return pl.BlockSpec(v.shape, lambda i: (0, 0), pipeline_mode=one)

    return pl.pallas_call(
        functools.partial(front_kernel, heads, dk, buckets, blocks),
        grid=(blocks,),
        in_specs=[smem, smem, full(bids), full(pad), full(again), full(fgain), full(wq), full(wo)]
        + [any_spec] * 3,
        out_specs=[
            pl.BlockSpec((heads, 1, seq, BLK), lambda i: (0, i, 0, 0)),
            pl.BlockSpec((heads, 1, 1, BLK), lambda i: (0, i, 0, 0)),
            pl.BlockSpec((3 * cols, seq), lambda i: (0, 0)),
        ]
        + [any_spec] * 6,
        out_shape=[
            jax.ShapeDtypeStruct((heads, blocks, seq, BLK), BF),
            jax.ShapeDtypeStruct((heads, blocks, 1, BLK), F32),
            jax.ShapeDtypeStruct((3 * cols, seq), BF),
            jax.ShapeDtypeStruct((2 * cols, seq), BF),
            jax.ShapeDtypeStruct((d, seq), BF),
            jax.ShapeDtypeStruct((d, seq), BF),
            jax.ShapeDtypeStruct((d, rows), F32),
            jax.ShapeDtypeStruct((d, seq), BF),
            jax.ShapeDtypeStruct((2 * cols, d), BF),
        ],
        scratch_shapes=[
            pltpu.VMEM((d, rows), F32),
            pltpu.VMEM((d, rows), BF),
            pltpu.VMEM((d, rows), F32),
            pltpu.VMEM((d, rows), BF),
            pltpu.VMEM((d, seq), BF),
            pltpu.VMEM((heads, 5, BLK, BLK), F32),
            pltpu.VMEM((seq, 8), F32),
            pltpu.VMEM((seq, BLK), F32),
            pltpu.VMEM((seq, BLK), F32),
            pltpu.VMEM((d, 1), F32),
            pltpu.VMEM((d, 1), F32),
            pltpu.VMEM((2 * cols, d), BF),
            pltpu.VMEM((d, 2 * cols), BF),
            pltpu.VMEM((2 * cols, seq), BF),
            pltpu.VMEM((d, seq), BF),
            dma((3,)), dma((5 + blocks,)), dma((3,)), dma((3,)), dma((blocks,)), dma((blocks,)),
        ],
        compiler_params=pltpu.CompilerParams(
            vmem_limit_bytes=FF_VMEM, collective_id=2, has_side_effects=True
        ),
        cost_estimate=pl.CostEstimate(
            flops=16 * heads * seq * seq * dk + 10 * seq * d * cols,
            bytes_accessed=2 * heads * seq * seq + 30 * rows * d,
            transcendentals=heads * seq * seq,
        ),
    )(rel, lengths, bids, pad, again, fgain, wq, wo, tok, far, cot)


def ff_kernel(
    steps, extra,
    xt_hbm, w_hbm, ct_hbm, wo_hbm, mid_hbm, wq_hbm,
    grads_ref, din_hbm, near_hbm, far_hbm, back_hbm, quarter_hbm, half_hbm, hand_hbm, wfar_hbm,
    xt, ct, wg, wu, wo, hid, dg, du, din, stage, r1, r2, r3, r4, xs, xr, of,
    csem, wsem, s1, s2, s3, s4, t1, t2, t3, t4, xsem, osem, hsem,
):
    f, total = hid.shape
    rows = total // 2
    chunks = rows // BLK
    d = xt.shape[0]
    shard = d // 16
    dp, mp = lax.axis_index("dp"), lax.axis_index("mp")
    a = group_coords(dp // extra)
    peers = [flip(dp, m * extra) for m in GROUP_MASKS]
    other = (dp, 1 - mp)
    core = dp % 2
    sibling = dp + 1 - 2 * core
    bufs = (r1, r2, r3, r4)
    sends, recvs = (s1, s2, s3, s4), (t1, t2, t3, t4)
    end = steps - 1

    def weight_copy(kind, n):
        src, dst = ((w_hbm.at[0], wg), (w_hbm.at[1], wu), (wo_hbm, wo))[kind]
        return pltpu.make_async_copy(src.at[:, lanes(n)], dst.at[:, lanes(n)], wsem.at[kind, n])

    def tok_copy(n):
        src, dst, start, size = (
            (xt_hbm, xt, rows, BLK), (ct_hbm, ct, rows, BLK),
            (xt_hbm, xt, 0, rows), (ct_hbm, ct, 0, rows), (xt_hbm, xt, rows + BLK, BLK),
        )[n]
        part = pl.ds(start, size)
        return pltpu.make_async_copy(src.at[:, part], dst.at[:, part], csem.at[n])

    near_part, far_part = pl.ds(0, rows), pl.ds(rows, rows)
    c_far = remote(
        ct_hbm.at[:, pl.ds(BLK, BLK)], ct.at[:, pl.ds(rows + BLK, BLK)], csem.at[5], csem.at[6], other
    )
    x_copy = remote(xs, xr, xsem.at[0], xsem.at[1], other)
    back_copy = remote(of.at[:, pl.ds(0, 128)], back_hbm, xsem.at[2], xsem.at[3], other)
    wq_rows = wq_hbm.shape[0] // 2
    wq_part = pl.ds(core * wq_rows, wq_rows)
    w_copy = remote(wq_hbm.at[wq_part], wfar_hbm.at[wq_part], xsem.at[4], xsem.at[5], other)
    w_pass = remote(wfar_hbm.at[wq_part], wfar_hbm.at[wq_part], xsem.at[6], xsem.at[7], (sibling, mp))
    mid_copy = pltpu.make_async_copy(mid_hbm, din.at[:, far_part], osem.at[3])

    deep = len(LEVELS)

    def hop(level, n, order):
        half = 8 >> level
        c = order[level]
        away = pl.ds((1 - a[c]) * half, half)
        src = stage.at[away] if level == 0 else bufs[level - 1].at[n, away]
        return remote(src, bufs[level].at[n], sends[level].at[n], recvs[level].at[n], (peers[c], mp))

    def hand_copy(n):
        level = levels_of(n) if isinstance(n, int) else 1
        dst = (hand_hbm.at[n - deep], half_hbm, quarter_hbm.at[n - 1])[level - 1]
        return pltpu.make_async_copy(bufs[level - 1].at[n], dst, hsem.at[n])

    def absorb_first(n):
        hop(0, n, Y_FIRST).wait()
        r1[n] = stage[pl.ds(a[0] * 8, 8)] + r1[n]
        if isinstance(n, int):
            hand_copy(n).start()
            return

        @pl.when(n == Z_BLOCK)
        def _():
            hop(1, n, Z_FIRST).start()

        @pl.when((n < deep) & (n != Z_BLOCK))
        def _():
            hop(1, n, Y_FIRST).start()

        @pl.when(n >= deep)
        def _():
            hand_copy(n).start()

    def absorb(level, n):
        half = 8 >> level
        order = order_of(n)
        hop(level, n, order).wait()
        kept = bufs[level - 1][n, pl.ds(a[order[level]] * half, half)]
        if level < 3:
            bufs[level][n] = kept + bufs[level][n]
            if level + 1 < levels_of(n):
                hop(level + 1, n, order).start()
            else:
                hand_copy(n).start()
        else:
            both = kept.astype(F32) + bufs[level][n].astype(F32)
            for w in range(3):
                grads_ref[w, :, n * BLK : (n + 1) * BLK] = both[0, w]

    scale = np.float32(np.sqrt(2 / np.pi))

    def place(u):
        early, late = u // steps, (u - 4) // steps
        is_far0 = (early == 0) * 1
        is_far1 = (late == 1) * 1
        v = u - steps
        n = v - steps * (u // (2 * steps + 4))
        near_j, near_c = n // 2, n % 2
        j = is_far0 * u + is_far1 * (u - steps - 4) + (1 - is_far0 - is_far1) * near_j
        c = is_far0 * chunks + is_far1 * (chunks + 1) + (1 - is_far0 - is_far1) * near_c
        return j, c

    def substep(u):
        j, c = place(u)
        pj, pc = place(u - 1)
        pj = pj + (u == 0) * 1
        fcols, tok = lanes(j), lanes(c)
        pcols, ptok = lanes(pj), lanes(pc)
        gate = dot(wg[:, fcols], xt[:, tok], ((0,), (0,)))
        up = dot(wu[:, fcols], xt[:, tok], ((0,), (0,)))
        dh = dot(wo[:, fcols], ct[:, tok], ((0,), (0,)))
        backward(pcols, ptok)
        sq = gate * gate
        t = jnp.tanh(scale * gate * (1.0 + 0.044715 * sq))
        half = 0.5 * (1.0 + t)
        act = gate * half
        slope = half + 0.5 * gate * (1.0 - t * t) * (scale * (1.0 + (3 * 0.044715) * sq))
        hid[fcols, tok] = (act * up).astype(BF)
        dg[fcols, tok] = (dh * (up * slope)).astype(BF)
        du[fcols, tok] = (dh * act).astype(BF)

    def backward(rs, tok):
        din[:, tok] += dot(wg[:, rs], dg[rs, tok], ((1,), (0,))) + dot(wu[:, rs], du[rs, tok], ((1,), (0,)))

    per = 4 * shard

    def grads(j):
        z = (j == Z_BLOCK) * 1
        for w in range(3):
            right = (hid, dg, du)[w][lanes(j), :]
            for q in range(4):
                rs = slice(q * per, (q + 1) * per)
                left = ct[rs, :] if w == 0 else xt[rs, :]
                part = dot(left, right, ((1,), (1,)))
                for k in range(4):
                    at = block_position(4 * q + k, Y_FIRST)
                    at = at + z * (block_position(4 * q + k, Z_FIRST) - at)
                    stage[at, w, 0:shard, :] = part[k * shard : (k + 1) * shard].astype(BF)
        hop(0, j, Y_FIRST).start()

    def out_part(n):
        return dot(wo[...], hid[:, lanes(n)], ((1,), (0,)))

    meet([(p, mp) for p in peers] + [other] + ([(sibling, mp)] if extra > 1 else []))
    c_far.start()
    w_copy.start()
    tok_copy(0).start()
    tok_copy(1).start()
    for n in range(steps):
        for kind in range(3):
            weight_copy(kind, n).start()
    for n in range(2, 5):
        tok_copy(n).start()
    din[...] = jnp.zeros_like(din)
    stage[...] = jnp.zeros_like(stage)
    before = place(-1)[1]
    dg[0:BLK, before * BLK : (before + 1) * BLK] = jnp.zeros((BLK, BLK), BF)
    du[0:BLK, before * BLK : (before + 1) * BLK] = jnp.zeros((BLK, BLK), BF)
    tok_copy(0).wait()
    tok_copy(1).wait()
    count = 2 * chunks * steps
    far_end = 2 * steps + 4

    def step(u, carry):
        @pl.when(u < steps)
        def _():
            for kind in range(3):
                weight_copy(kind, u).wait()

        @pl.when(u == steps)
        def _():
            tok_copy(2).wait()
            tok_copy(3).wait()

        @pl.when(u == steps + 4)
        def _():
            tok_copy(4).wait()
            c_far.wait()

        @pl.when(u < count)
        def _():
            substep(u)

        @pl.when(u == far_end)
        def _():
            xs[...] = din[:, far_part].astype(BF)
            x_copy.start()
            mid_copy.start()

        odd = u % 2 == 1
        late = (u >= 2 * steps + 5) * 1
        m = (u - 13) // 2 - 2 * ((u >= 2 * steps + 7) * 1)
        n = (u - 11) // 2 - 2 * late

        @pl.when(odd & ((u == 13) | (u == 15) | (u >= 2 * steps + 7)))
        def _():
            absorb_first(m)

        for at, events in (
            (21, ((1, 0),)), (23, ((1, 1),)), (25, ((2, 0),)), (27, ((1, 2), (2, 1))),
        ):
            @pl.when(u == at)
            def _():
                for level, block in events:
                    absorb(level, block)

        @pl.when(odd & ((u == 11) | (u == 13) | (u >= 2 * steps + 5)))
        def _():
            grads(n)

        @pl.when(u == far_end + 5)
        def _():
            w_copy.wait()
            w_pass.start()

        return carry

    lax.fori_loop(0, count, step, 0)
    pj, pc = place(count - 1)
    backward(lanes(pj), lanes(pc))

    def far_out(n, carry):
        of[:, lanes(n)] = out_part(n + chunks).astype(BF)
        return carry

    lax.fori_loop(0, chunks, far_out, 0)
    x_copy.wait()
    back_copy.start()
    rest = far_hbm.shape[1]
    far_copy = pltpu.make_async_copy(of.at[:, pl.ds(128, rest)], far_hbm, osem.at[0])
    far_copy.start()
    din[:, near_part] += xr[...].astype(F32)
    din_copy = pltpu.make_async_copy(din.at[:, near_part], din_hbm, osem.at[2])
    din_copy.start()
    mid_copy.wait()

    def near_out(n, carry):
        at = lanes(n + chunks)
        din[:, at] = din[:, at] + out_part(n)
        return carry

    lax.fori_loop(0, chunks, near_out, 0)
    near_copy = pltpu.make_async_copy(din.at[:, far_part], near_hbm, osem.at[1])
    near_copy.start()
    absorb_first(end)
    absorb(3, 0)
    absorb(2, 2)
    absorb(1, 3)
    w_pass.wait()
    for n in range(1, steps):
        hand_copy(n).wait()
    far_copy.wait()
    near_copy.wait()
    din_copy.wait()
    back_copy.wait()


def ff_all(xt, ct, w2, wo, mid, wq, extra):
    d, total = xt.shape
    f = wo.shape[1]
    rows = total // 2
    steps = f // BLK
    deep = len(LEVELS)
    shard = d // 16
    spad = -(-shard // 16) * 16
    dma = pltpu.SemaphoreType.DMA
    any_spec = pl.BlockSpec(memory_space=pl.ANY)
    return pl.pallas_call(
        functools.partial(ff_kernel, steps, extra),
        in_specs=[any_spec] * 6,
        out_specs=[pl.BlockSpec(memory_space=pltpu.VMEM)] + [any_spec] * 8,
        out_shape=[
            jax.ShapeDtypeStruct((3, spad, BLK), F32),
            jax.ShapeDtypeStruct((d, rows), F32),
            jax.ShapeDtypeStruct((d, rows), F32),
            jax.ShapeDtypeStruct((d, rows - 128), BF),
            jax.ShapeDtypeStruct((d, 128), BF),
            jax.ShapeDtypeStruct((2, 2, 3, spad, BLK), BF),
            jax.ShapeDtypeStruct((4, 3, spad, BLK), BF),
            jax.ShapeDtypeStruct((steps - deep, 8, 3, spad, BLK), BF),
            jax.ShapeDtypeStruct(wq.shape, BF),
        ],
        scratch_shapes=[
            pltpu.VMEM((d, total), BF),
            pltpu.VMEM((d, total), BF),
            pltpu.VMEM((d, f), BF),
            pltpu.VMEM((d, f), BF),
            pltpu.VMEM((d, f), BF),
            pltpu.VMEM((f, total), BF),
            pltpu.VMEM((f, total), BF),
            pltpu.VMEM((f, total), BF),
            pltpu.VMEM((d, total), F32),
            pltpu.VMEM((16, 3, spad, BLK), BF),
            pltpu.VMEM((steps, 8, 3, spad, BLK), BF),
            pltpu.VMEM((4, 4, 3, spad, BLK), BF),
            pltpu.VMEM((3, 2, 3, spad, BLK), BF),
            pltpu.VMEM((1, 1, 3, spad, BLK), BF),
            pltpu.VMEM((d, rows), BF),
            pltpu.VMEM((d, rows), BF),
            pltpu.VMEM((d, rows), BF),
            dma((7,)),
            dma((3, steps)),
            dma((steps,)), dma((4,)), dma((3,)), dma((1,)),
            dma((steps,)), dma((4,)), dma((3,)), dma((1,)),
            dma((8,)),
            dma((4,)),
            dma((steps,)),
        ],
        compiler_params=pltpu.CompilerParams(
            vmem_limit_bytes=FF_VMEM, collective_id=0, has_side_effects=True
        ),
        cost_estimate=pl.CostEstimate(
            flops=18 * total * d * f,
            bytes_accessed=6 * d * f + 16 * total * d,
            transcendentals=total * f,
        ),
    )(xt, w2, ct, wo, mid, wq)


def tail_kernel(
    heads, dk, buckets, blocks, extra,
    bid_ref, qkv_ref, e_ref, inv_ref, wall_ref, ctx_ref, ag_ref, fg_ref, early_ref,
    din_hbm, mid_hbm, cot_hbm, tok_hbm, nrm_hbm, wq_hbm, wfar_hbm, near_hbm, back_hbm, far_hbm,
    quarter_hbm, half_hbm, hand_hbm,
    ig_hbm, res_hbm, gq_ref, go_ref, small_ref, ffo_ref, ffi_ref,
    f1, f2, f3, f4, nrm, wq, wn, wf, alow, dctx, dcs, osend, orecv, fsum, agc, fgc,
    dp_s, dkv, tally, dproj, dfar, grad, back0, back,
    sa, sb_, a1, a2, a3, a4, b1, b2, b3, b4, hk, hm, hq, h2, h3, h4, sv, rv,
    lsem, ksem, xs_sem, xr_sem, cs_sem, cr_sem, bs_sem, br_sem, hs_sem, hr_sem,
):
    qb = pl.program_id(0)
    dp, x = lax.axis_index("dp"), lax.axis_index("mp")
    d, rows = f2.shape
    cols = heads * dk
    shard = d // 16
    a = group_coords(dp // extra)
    peers = [flip(dp, m * extra) for m in GROUP_MASKS]
    other = (dp, 1 - x)
    near_blocks = blocks // 2
    near_part, far_part = pl.ds(0, rows), pl.ds(rows, rows)
    halves = ((sa, a1, a2, a3, a4), (sb_, b1, b2, b3, b4))
    orders = (Y_FIRST, Z_FIRST)
    copies = (
        (din_hbm, f1), (mid_hbm, f2), (cot_hbm, f3), (tok_hbm, f2), (nrm_hbm, nrm), (wq_hbm, wq), (wfar_hbm, wq),
        (back_hbm, back0), (near_hbm.at[:, pl.ds(0, BLK)], f4), (near_hbm.at[:, pl.ds(BLK, BLK)], f4),
        (f4, res_hbm.at[:, pl.ds(0, BLK)]), (f4, res_hbm.at[:, pl.ds(BLK, BLK)]),
    )

    def local(i):
        return pltpu.make_async_copy(copies[i][0], copies[i][1], lsem.at[i])

    def x_copy(i, src, dst):
        return remote(src, dst, xs_sem.at[i], xr_sem.at[i], other)

    dctx_copy = x_copy(0, dcs, dctx.at[:, far_part])
    o_copy = x_copy(1, osend, orecv)
    dproj_copy = x_copy(2, dproj.at[:, far_part], dfar)

    def back_copy(i):
        part = pl.ds(i * 128, 128)
        return x_copy(3 + i, far_hbm.at[:, part], back.at[:, part])

    def hop(side, level):
        half = 8 >> level
        c = orders[side][level]
        away = pl.ds((1 - a[c]) * half, half)
        bufs = halves[side]
        return remote(
            bufs[level].at[away], bufs[level + 1], cs_sem.at[side, level], cr_sem.at[side, level], (peers[c], x)
        )

    def absorb(side, level):
        half = 8 >> level
        bufs = halves[side]
        hop(side, level).wait()
        kept = bufs[level][pl.ds(a[orders[side][level]] * half, half)]
        if level < 3:
            bufs[level + 1][...] = kept + bufs[level + 1][...]
            hop(side, level + 1).start()
            return
        both = (kept.astype(F32) + bufs[level + 1][...].astype(F32))[0, 0:shard]
        outs = (gq_ref.at[0], gq_ref.at[1]) if side == 0 else (gq_ref.at[2], go_ref)
        for i in range(2):
            outs[i][...] = both[:, i * cols : (i + 1) * cols]

    deep = len(LEVELS)
    handed = (1, 2, 3, 4, 5, 6)

    def keep_copy(block):
        level = levels_of(block)
        half = 8 >> level
        keep = pl.ds(a[order_of(block)[level]] * half, half)
        if level == 3:
            src, dst = quarter_hbm.at[block - 1, keep], hq.at[block - 1]
        elif level == 2:
            src, dst = half_hbm.at[keep], hm
        else:
            src, dst = hand_hbm.at[block - deep, keep], hk.at[block - deep]
        return pltpu.make_async_copy(src, dst, ksem.at[block])

    def hand_hop(level, block):
        half = 8 >> level
        c = order_of(block)[level]
        away = pl.ds((1 - a[c]) * half, half)
        fresh = level == levels_of(block)
        if level == 1:
            src, dst = hand_hbm.at[block - deep, away], h2.at[block - deep]
        elif level == 2:
            src, dst = half_hbm.at[away] if fresh else h2.at[block - deep, away], h3.at[block - 3]
        else:
            src, dst = quarter_hbm.at[block - 1, away] if fresh else h3.at[block - 3, away], h4.at[block - 1]
        return remote(src, dst, hs_sem.at[level, block], hr_sem.at[level, block], (peers[c], x))

    def put_grads(w, block, value):
        at = slice(block * BLK, (block + 1) * BLK)
        if w == 0:
            ffo_ref[:, at] = value
        else:
            ffi_ref[:, w - 1, at] = value

    def hand_absorb(level, block):
        half = 8 >> level
        keep = pl.ds(a[order_of(block)[level]] * half, half)
        hand_hop(level, block).wait()
        if level == levels_of(block):
            keep_copy(block).wait()
            kept = hk[block - deep] if level == 1 else (hm[...] if level == 2 else hq[block - 1])
        else:
            kept = h2[block - deep, keep] if level == 2 else h3[block - 3, keep]
        if level == 1:
            h2[block - deep] = kept + h2[block - deep]
        elif level == 2:
            h3[block - 3] = kept + h3[block - 3]
        else:
            both = kept.astype(F32) + h4[block - 1].astype(F32)
            for w in range(3):
                put_grads(w, block, both[0, w, 0:shard])
        if level < 3:
            hand_hop(level + 1, block).start()

    def round_copy(i):
        who = other if i == 4 else (peers[(0, 2, 3, 1)[i]], x)
        return remote(sv.at[i], rv.at[i], bs_sem.at[i], br_sem.at[i], who)

    def round_end(i):
        round_copy(i).wait()
        sv[i + 1] = sv[i] + rv[i]
        if i < 4:
            round_copy(i + 1).start()

    def out_copy(r):
        return pltpu.make_async_copy(f3.at[:, lanes(r)], ig_hbm.at[:, lanes(r)], lsem.at[len(copies) + r])

    def lane_sum(v):
        total = v[:, 0:128]
        for i in range(1, v.shape[1] // 128):
            total = total + v[:, i * 128 : (i + 1) * 128]
        return total

    @pl.when(qb == 0)
    def _():
        for i in range(3):
            local(i).start()
        meet([(p, x) for p in peers] + [other])
        back_copy(0).start()
        for block in handed:
            hand_hop(levels_of(block), block).start()
        agc[...] = column(ag_ref[...])
        fgc[...] = column(fg_ref[...])
        dkv[...] = jnp.zeros_like(dkv)
        tally[...] = jnp.zeros_like(tally)
        sa[...] = jnp.zeros_like(sa)
        sb_[...] = jnp.zeros_like(sb_)
        fsum[...] = jnp.zeros_like(fsum)
        for i in range(3):
            local(i).wait()

        def norm_rows(r, carry):
            ls = lanes(r)
            v = f2[:, ls]
            c = f1[:, ls]
            scale = norm_scale(v)
            n = v * scale
            cg = c * fgc[...]
            m = jnp.mean(cg * n, axis=0, keepdims=True)
            gm = f3[:, ls] + scale * (cg - n * m)
            fsum[...] += lane_sum(c * n)
            f1[:, ls] = gm
            alow[:, ls] = gm.astype(BF)
            return carry

        lax.fori_loop(0, near_blocks, norm_rows, 0)
        dcs[...] = dot(wall_ref[cols : 2 * cols, :], alow[...], ((1,), (0,))).astype(BF)
        dctx_copy.start()
        for i in (3, 4, 5, 7, 8):
            local(i).start()
        for block in handed:
            keep_copy(block).start()
        dctx[:, near_part] = dot(wall_ref[0:cols, :], alow[...], ((1,), (0,))).astype(BF)
        osend[...] = dot(alow[...], ctx_ref[cols : 2 * cols, near_part], ((1,), (1,))).astype(BF)
        o_copy.start()
        grad[:, 3 * cols : 4 * cols] = dot(alow[...], ctx_ref[0:cols, near_part], ((1,), (1,)))
        for w in range(3):
            put_grads(w, 0, early_ref[w, 0:shard, :])
        dctx_copy.wait()
        back_copy(1).start()

    @pl.when(qb == 1)
    def _():
        local(5).wait()
        wn[...] = wq[...].astype(F32).T.astype(BF)
        local(6).start()
        hand_absorb(3, 1)
        hand_absorb(3, 2)
        hand_absorb(2, 3)

    @pl.when(qb == 2)
    def _():
        local(6).wait()
        wf[...] = wq[...].astype(F32).T.astype(BF)
        local(7).wait()
        local(8).wait()
        back_copy(0).wait()
        f4[:, 0:128] += back0[...].astype(F32)
        f4[:, 128:BLK] += back[:, 0:128].astype(F32)
        local(10).start()
        hand_absorb(1, 4)

    @pl.when(qb == 3)
    def _():
        hand_absorb(3, 3)

    q_true = (qb + near_blocks * x) % blocks

    def head(h, carry):
        def head_rows(group):
            return pl.ds(pl.multiple_of(group * cols + h * dk, dk), dk)

        inv = inv_ref[h, 0]
        qh = qkv_ref[head_rows(0), lanes(qb)]
        scaled = (dctx[head_rows(0), lanes(qb)].astype(F32) * inv).astype(BF)
        inner = jnp.zeros((1, BLK), F32)
        for kb in range(blocks):
            krows = slice(kb * BLK, (kb + 1) * BLK)
            g = dot(qkv_ref[head_rows(2), krows], scaled, ((0,), (0,)))
            dp_s[krows, :] = g
            inner = inner + jnp.sum(e_ref[h, 0, krows, :].astype(F32) * g, axis=0, keepdims=True)
        inner = inner * inv
        dq = jnp.zeros((dk, BLK), F32)
        for kb in range(blocks):
            krows = slice(kb * BLK, (kb + 1) * BLK)
            e = e_ref[h, 0, krows, :]
            ds = (e.astype(F32) * (dp_s[krows, :] - inner)).astype(BF)
            dkv[head_rows(0), krows] += dot(qh, ds, ((1,), (1,)))
            dkv[head_rows(1), krows] += dot(scaled, e, ((1,), (1,)))
            dq = dq + dot(qkv_ref[head_rows(1), krows], ds, ((1,), (0,)))
            tally[h, near_diagonal((kb + near_blocks * x) % blocks - q_true)] += ds.astype(F32)
        dproj[head_rows(0), lanes(qb)] = dq.astype(BF)
        return carry

    lax.fori_loop(0, heads, head, 0)

    @pl.when(qb == blocks - 1)
    def _():
        dproj[cols : 3 * cols, :] = dkv[...].astype(BF)
        dproj_copy.start()
        back_copy(2).start()
        local(3).wait()
        local(4).wait()
        per = 4 * shard

        def grad_rows(q, carry):
            rs = pl.ds(pl.multiple_of(q * per, 16), per)
            grad[rs, 0 : 3 * cols] = dot(nrm[rs, :], dproj[...], ((1,), (1,)))
            return carry

        lax.fori_loop(0, 4, grad_rows, 0)
        o_copy.wait()
        grad[:, 3 * cols : 4 * cols] += orecv[...].astype(F32)
        for side in range(2):
            for k in range(16):
                halves[side][0][block_position(k, orders[side]), 0:shard, :] = grad[
                    k * shard : (k + 1) * shard, 2 * side * cols : 2 * (side + 1) * cols
                ].astype(BF)
            hop(side, 0).start()
        hand_absorb(1, 5)
        hand_absorb(2, 4)

        def near_rows(r, carry):
            f3[:, lanes(r)] = dot(wn[...], dproj[:, lanes(r)], ((1,), (0,)))
            return carry

        lax.fori_loop(0, near_blocks, near_rows, 0)
        absorb(0, 0)
        absorb(1, 0)
        ids = bid_ref[...]
        hot = ids == lax.broadcasted_iota(jnp.int32, (buckets, SPAN), 0)
        out_lane = lax.broadcasted_iota(jnp.int32, (buckets, 128), 1)
        sub = lax.broadcasted_iota(jnp.int32, (8, SPAN), 0)
        sv[0] = jnp.zeros(sv.shape[1:], F32)

        def bias_sums(hh, carry):
            line = jnp.zeros((8, SPAN), F32)
            for g in range(BLK // 8):
                group = slice(8 * g, 8 * g + 8)
                parts = [tally[hh, i, group, :] for i in (4, 3, 2, 1, 0)]
                strip = jnp.concatenate(parts + [jnp.zeros((8, BLK), F32)], axis=1)
                line = line + (strip if g == 0 else pltpu.roll(strip, SPAN - 8 * g, 1))
            for bit in (1, 2, 4):
                line = jnp.where((sub // bit) % 2 == 1, pltpu.roll(line, SPAN - bit, 1), line)
            sums = jnp.sum(line, axis=0, keepdims=True)
            col = jnp.sum(jnp.where(hot, sums, 0.0), axis=1, keepdims=True)
            sv[0, 0:buckets, :] = jnp.where(out_lane == x * heads + hh, col, sv[0, 0:buckets, :])
            return carry

        lax.fori_loop(0, heads, bias_sums, 0)
        product = wn[...].astype(F32) * grad[:, 0 : 3 * cols]
        again = lane_sum(product[:, 0:512]).T
        rest = product[:, 512 : 3 * cols]
        again = jnp.sum(again, axis=0, keepdims=True) + jnp.sum(rest.T, axis=0, keepdims=True)
        again = again / ag_ref[...]
        fgain = jnp.sum(fsum[...].T, axis=0, keepdims=True)
        lines = -(-d // 128)
        for i in range(lines):
            n = min(128, d - 128 * i)
            sv[0, buckets + i : buckets + i + 1, 0:n] = again[:, 128 * i : 128 * i + n]
            sv[0, buckets + lines + i : buckets + lines + i + 1, 0:n] = fgain[:, 128 * i : 128 * i + n]
        round_copy(0).start()
        hand_absorb(3, 4)
        hand_absorb(2, 5)
        hand_absorb(1, 6)
        round_end(0)
        local(10).wait()
        local(9).start()
        absorb(1, 1)
        dproj_copy.wait()

        def last_norm(r, carry):
            ls = lanes(r)
            c = f3[:, ls] + dot(wf[...], dfar[:, ls], ((1,), (0,)))
            v = f2[:, ls]
            scale = norm_scale(v)
            n = v * scale
            cg = c * agc[...]
            m = jnp.mean(cg * n, axis=0, keepdims=True)
            f3[:, ls] = f1[:, ls] + scale * (cg - n * m)
            out_copy(r).start()
            return carry

        lax.fori_loop(0, near_blocks, last_norm, 0)
        absorb(0, 1)
        hand_absorb(3, 5)
        round_end(1)
        hand_absorb(2, 6)
        absorb(1, 2)
        round_end(2)
        back_copy(1).wait()
        back_copy(2).wait()
        local(9).wait()
        f4[...] += back[:, 128 : 128 + BLK].astype(F32)
        local(11).start()
        absorb(0, 2)
        hand_absorb(3, 6)
        absorb(1, 3)
        round_end(3)
        absorb(0, 3)
        round_end(4)
        small_ref[...] = sv[5]
        local(11).wait()
        for r in range(near_blocks):
            out_copy(r).wait()


def tail(qkv, e, inv, wall, ctx, again, fgain, early, din, mid, cot, tok, nrm, wq, wfar, near_out, back, far,
         quarter, half_way, hand, buckets, heads, dk, extra, f):
    d, rows = tok.shape
    seq = 2 * rows
    cols = heads * dk
    blocks = seq // BLK
    near = blocks // 2
    shard = d // 16
    spad = -(-shard // 16) * 16
    deep = hand.shape[0]
    later = deep + len(LEVELS)
    lines = -(-(buckets + 2 * -(-d // 128)) // 8) * 8
    bids = jnp.asarray(lane_buckets(buckets))
    one = pl.Buffered(1)
    dma = pltpu.SemaphoreType.DMA
    any_spec = pl.BlockSpec(memory_space=pl.ANY)

    def full(v):
        return pl.BlockSpec(v.shape, lambda i: (0,) * len(v.shape), pipeline_mode=one)

    def chain(width):
        return [pltpu.VMEM((n, spad, width), BF) for n in (16, 8, 4, 2, 1)]

    outs = [
        jax.ShapeDtypeStruct((3, shard, cols), F32),
        jax.ShapeDtypeStruct((shard, cols), F32),
        jax.ShapeDtypeStruct((lines, 128), F32),
        jax.ShapeDtypeStruct((shard, f), F32),
        jax.ShapeDtypeStruct((shard, 2, f), F32),
    ]
    a_chain, b_chain = chain(2 * cols), chain(2 * cols)
    return pl.pallas_call(
        functools.partial(tail_kernel, heads, dk, buckets, blocks, extra),
        grid=(blocks,),
        in_specs=[
            full(bids),
            full(qkv),
            pl.BlockSpec((heads, 1, seq, BLK), lambda i: (0, i, 0, 0)),
            pl.BlockSpec((heads, 1, 1, BLK), lambda i: (0, i, 0, 0)),
            full(wall),
            full(ctx),
            full(again),
            full(fgain),
            full(early),
        ]
        + [any_spec] * 13,
        out_specs=[any_spec, any_spec] + [full(v) for v in outs],
        out_shape=[jax.ShapeDtypeStruct((d, rows), F32), jax.ShapeDtypeStruct((d, rows), F32)] + outs,
        scratch_shapes=[
            pltpu.VMEM((d, rows), F32),
            pltpu.VMEM((d, rows), F32),
            pltpu.VMEM((d, rows), F32),
            pltpu.VMEM((d, BLK), F32),
            pltpu.VMEM((d, seq), BF),
            pltpu.VMEM((3 * cols, d), BF),
            pltpu.VMEM((d, 3 * cols), BF),
            pltpu.VMEM((d, 3 * cols), BF),
            pltpu.VMEM((d, rows), BF),
            pltpu.VMEM((cols, seq), BF),
            pltpu.VMEM((cols, rows), BF),
            pltpu.VMEM((d, cols), BF),
            pltpu.VMEM((d, cols), BF),
            pltpu.VMEM((d, 128), F32),
            pltpu.VMEM((d, 1), F32),
            pltpu.VMEM((d, 1), F32),
            pltpu.VMEM((seq, BLK), F32),
            pltpu.VMEM((2 * cols, seq), F32),
            pltpu.VMEM((heads, 5, BLK, BLK), F32),
            pltpu.VMEM((3 * cols, seq), BF),
            pltpu.VMEM((3 * cols, rows), BF),
            pltpu.VMEM((d, 4 * cols), F32),
            pltpu.VMEM((d, 128), BF),
            pltpu.VMEM((d, rows - 128), BF),
            a_chain[0],
            b_chain[0],
        ]
        + a_chain[1:]
        + b_chain[1:]
        + [
            pltpu.VMEM((deep, 4, 3, spad, BLK), BF),
            pltpu.VMEM((2, 3, spad, BLK), BF),
            pltpu.VMEM((2, 1, 3, spad, BLK), BF),
            pltpu.VMEM((deep, 4, 3, spad, BLK), BF),
            pltpu.VMEM((deep + 1, 2, 3, spad, BLK), BF),
            pltpu.VMEM((later - 1, 1, 3, spad, BLK), BF),
            pltpu.VMEM((6, lines, 128), F32),
            pltpu.VMEM((5, lines, 128), F32),
            dma((12 + near,)),
            dma((later,)),
            dma((6,)), dma((6,)),
            dma((2, 4)), dma((2, 4)),
            dma((5,)), dma((5,)),
            dma((4, later)), dma((4, later)),
        ],
        compiler_params=pltpu.CompilerParams(
            vmem_limit_bytes=FF_VMEM, collective_id=1, has_side_effects=True
        ),
        cost_estimate=pl.CostEstimate(
            flops=32 * heads * seq * seq * dk + 8 * seq * d * 3 * cols,
            bytes_accessed=2 * heads * seq * seq + 30 * rows * d,
            transcendentals=0,
        ),
    )(bids, qkv, e, inv, wall, ctx, again, fgain, early, din, mid, cot, tok, nrm, wq, wfar, near_out, back, far,
      quarter, half_way, hand)


def take(array, index):
    return lax.dynamic_index_in_dim(array, index, 0, keepdims=False)


def per_device(
    tokens,
    cotangent,
    doc_lengths,
    pad_mask,
    attn_gain,
    qkv_weight,
    rel_table,
    out_weight,
    ff_gain,
    ff_in_weight,
    ff_out_weight,
):
    rows, d = tokens.shape
    n_dp = lax.axis_size("dp")
    n_mp = lax.axis_size("mp")
    cols = qkv_weight.shape[2]
    buckets, heads = rel_table.shape
    dk = cols // heads
    me = lax.axis_index("dp")
    shard = d // n_dp
    extra = n_dp // 16

    def hop(v, mask):
        return lax.ppermute(v, "dp", [(i, i ^ mask) for i in range(n_dp)])

    def bit(b):
        return (me >> b) & 1

    def finish(g):
        parts = [g.reshape((extra, shard) + g.shape[1:])]
        for b in reversed(range(extra.bit_length() - 1)):
            halves = [p.reshape((2, p.shape[0] // 2) + p.shape[1:]) for p in parts]
            away = sum(take(p, 1 - bit(b)).astype(F32) for p in halves).astype(BF)
            parts = [take(p, bit(b)) for p in halves] + [hop(away, 1 << b)]
        return sum(p.astype(F32) for p in parts)[0]

    tok = tokens.T
    cot = cotangent.T
    far = lax.ppermute(tok.astype(BF), "mp", [(0, 1), (1, 0)])
    w2 = jnp.transpose(ff_in_weight, (1, 0, 2))
    wq = jnp.transpose(qkv_weight, (1, 2, 0)).reshape(3 * cols, d)
    again, fgain = attn_gain.reshape(1, d), ff_gain.reshape(1, d)

    e, inv, qkv, ctx, nrm, xt, mid, ct, wall = front(
        rel_table, doc_lengths, pad_mask, again, fgain, wq, out_weight.T, tok, far, cot, heads, dk
    )
    early, din, near_out, far_out, back, quarter, half_way, hand, wfar = ff_all(
        xt, ct, w2, ff_out_weight, mid, wq, extra
    )
    input_grad, result, grad_qkv, grad_out, small, ffo, ffi = tail(
        qkv, e, inv, wall, ctx, again, fgain, early, din, mid, cot, tok, nrm, wq, wfar, near_out, back, far_out,
        quarter, half_way, hand, buckets, heads, dk, extra, ff_out_weight.shape[1],
    )
    grad_qkv = jnp.transpose(grad_qkv, (1, 0, 2))
    if extra > 1:
        grad_qkv, grad_out, ffo, ffi = (finish(g) for g in (grad_qkv, grad_out, ffo, ffi))
    for b in range(extra.bit_length() - 1):
        small = small + hop(small, 1 << b)
    lines = -(-d // 128)
    return (
        result.T,
        input_grad.T,
        small[buckets : buckets + lines].reshape(-1)[:d],
        grad_qkv,
        small[:buckets, : heads * n_mp],
        grad_out,
        small[buckets + lines : buckets + 2 * lines].reshape(-1)[:d],
        ffi,
        ffo,
    )


def solution(mesh):
    return jax.shard_map(
        per_device,
        mesh=mesh,
        in_specs=(
            P(("dp", "mp"), None),
            P(("dp", "mp"), None),
            P("dp", None),
            P("dp", None),
            P(),
            P(None, None, "mp"),
            P(None, "mp"),
            P(None, "mp"),
            P(),
            P(None, None, "mp"),
            P(None, "mp"),
        ),
        out_specs=(
            P(("dp", "mp"), None),
            P(("dp", "mp"), None),
            P(),
            P("dp", None, "mp"),
            P(),
            P("dp", "mp"),
            P(),
            P("dp", None, "mp"),
            P("dp", "mp"),
        ),
        check_vma=False,
    )
```

```python
import functools

import jax
import jax.numpy as jnp
import numpy as np
from jax import lax
from jax.experimental import pallas as pl
from jax.experimental.pallas import tpu as pltpu
from jax.sharding import PartitionSpec as P

MAXDIST = 128
norm_eps = 1e-06
BLK = 256
SPAN = 6 * BLK
REACH = 2
BF = jnp.bfloat16
F32 = jnp.float32
FF_VMEM = 63 << 20


def bucket_of(offsets, buckets, reach):
    half_range = buckets // 2
    upper_half = (offsets > 0).astype(np.int32) * half_range
    distance = np.abs(offsets)
    exact_range = half_range // 2
    safe_dist = np.maximum(distance, 1)
    log_bucket = exact_range + (
        np.log(safe_dist / exact_range) / np.log(reach / exact_range) * (half_range - exact_range)
    ).astype(np.int32)
    log_bucket = np.minimum(log_bucket, half_range - 1)
    return (upper_half + np.where(distance < exact_range, distance, log_bucket)).astype(np.int32)


def lane_buckets(buckets):
    lanes = np.arange(SPAN)
    shifted = np.where(lanes < 5 * BLK, lanes, lanes - SPAN)
    return bucket_of(REACH * BLK - shifted, buckets, MAXDIST).reshape(1, SPAN)


def dot(a, b, contract):
    return lax.dot_general(a, b, (contract, ((), ())), preferred_element_type=F32)


def flip(index, mask):
    out = index
    bit = 1
    while bit <= mask:
        if mask & bit:
            out = out + bit * (1 - 2 * (index // bit % 2))
        bit *= 2
    return out


GROUP_MASKS = (1, 2, 4, 12)


def group_coords(g):
    b = [g // (1 << i) % 2 for i in range(4)]
    return [b[0], b[1], (b[2] + b[3]) % 2, b[3]]


Y_FIRST = (0, 1, 2, 3)
Z_FIRST = (0, 2, 3, 1)
Z_BLOCK = 1
LEVELS = (4, 3, 3, 2)


def order_of(block):
    return Z_FIRST if block == Z_BLOCK else Y_FIRST


def levels_of(block):
    return LEVELS[block] if block < len(LEVELS) else 1


def block_position(k, order):
    b = [k >> i & 1 for i in range(4)]
    c = [b[0], b[1], b[2] ^ b[3], b[3]]
    return sum(c[order[i]] << (3 - i) for i in range(4))


def column(line):
    return jnp.broadcast_to(line, (8, line.shape[1])).T[:, 0:1]


def norm_scale(v):
    return lax.rsqrt(jnp.mean(v * v, axis=0, keepdims=True) + norm_eps)


def lanes(block):
    return pl.ds(pl.multiple_of(block * BLK, BLK), BLK)


def remote(src, dst, send, recv, who):
    return pltpu.make_async_remote_copy(
        src_ref=src,
        dst_ref=dst,
        send_sem=send,
        recv_sem=recv,
        device_id=who,
        device_id_type=pl.DeviceIdType.MESH,
    )


def meet(devices):
    barrier = pltpu.get_barrier_semaphore()
    for who in devices:
        pl.semaphore_signal(barrier, inc=1, device_id=who, device_id_type=pl.DeviceIdType.MESH)
    pl.semaphore_wait(barrier, len(devices))


def near_diagonal(offset):
    i = offset + 3
    return i + (6 - i) // 6 - i // 6 - 1


def front_kernel(
    heads, dk, buckets, blocks,
    rel_ref, len_ref, bid_ref, pad_ref, ag_ref, fg_ref, wq_ref, wo_ref,
    tok_hbm, far_hbm, cot_hbm,
    e_ref, inv_ref, qkv_ref, ctx_hbm, nrm_hbm, xt_hbm, mid_hbm, ct_hbm, wall_hbm,
    f1, fb, f3, cl, nrm, table, padc, mask, score, agc, fgc, wall, wn, call, xo,
    lsem, osem, wsend, wrecv, csend, crecv,
):
    qb = pl.program_id(0)
    dp, x = lax.axis_index("dp"), lax.axis_index("mp")
    d, rows = f1.shape
    cols = heads * dk
    half = cols // 2
    core = dp % 2
    other = (dp, 1 - x)
    sibling = (dp + 1 - 2 * core, x)
    near_blocks = blocks // 2
    part = pl.ds(core * half, half)
    far_part = pl.ds(cols + core * half, half)

    def local(i):
        src, dst = ((tok_hbm, f1), (far_hbm, fb), (cot_hbm, f3))[i]
        return pltpu.make_async_copy(src, dst, lsem.at[i])

    def out(i):
        src, dst = (
            (call, ctx_hbm), (nrm, nrm_hbm), (f1, mid_hbm), (cl, ct_hbm.at[:, pl.ds(0, rows)]), (wall, wall_hbm)
        )[i]
        return pltpu.make_async_copy(src, dst, osem.at[i])

    def xt_out(b):
        return pltpu.make_async_copy(xo.at[:, lanes(b)], xt_hbm.at[:, lanes(b)], osem.at[5 + b])

    w_copy = remote(wo_ref.at[part], wall.at[far_part], wsend.at[0], wrecv.at[0], other)
    w_pass = remote(wall.at[far_part], wall.at[far_part], wsend.at[1], wrecv.at[1], sibling)
    piece = d // 4

    def c_copy(i):
        rs = pl.ds(i * piece, piece)
        return remote(
            cl.at[rs, pl.ds(0, BLK)], ct_hbm.at[rs, pl.ds(rows, BLK)], wsend.at[2 + i], wrecv.at[2 + i], other
        )

    def ctx_copy(b):
        there = (b + near_blocks) % blocks
        return remote(
            call.at[pl.ds(0, cols), lanes(b)], call.at[pl.ds(cols, cols), lanes(there)],
            csend.at[b], crecv.at[b], other,
        )

    @pl.when(qb == 0)
    def _():
        for i in (2, 0, 1):
            local(i).start()
        meet([other, sibling])
        w_copy.start()
        wall[0:cols, :] = wo_ref[...]
        local(2).wait()
        cl[...] = f3[...].astype(BF)
        c_copy(0).start()
        c_copy(1).start()
        out(3).start()
        agc[...] = column(ag_ref[...])
        fgc[...] = column(fg_ref[...])
        local(0).wait()
        local(1).wait()
        for b in range(blocks):
            ls = slice(b * BLK, (b + 1) * BLK)
            v = f1[:, ls] if b < near_blocks else fb[:, b * BLK - rows : (b + 1) * BLK - rows].astype(F32)
            nrm[:, ls] = (v * norm_scale(v) * agc[...]).astype(BF)
            qkv_ref[:, ls] = dot(wq_ref[...], nrm[:, ls], ((1,), (0,))).astype(BF)
        out(1).start()
        for i in range(2):
            start = (1 - x) * rows if i else x * rows
            line = pad_ref[:, pl.ds(pl.multiple_of(start, BLK), rows)].astype(F32)
            padc[i * rows : (i + 1) * rows, :] = jnp.broadcast_to(line, (8, rows)).T
        ids = bid_ref[...]
        for hh in range(heads):
            line = jnp.zeros((1, SPAN), F32)
            for b in range(buckets):
                line = jnp.where(ids == b, rel_ref[b, hh], line)
            turned = pltpu.roll(
                jnp.broadcast_to(line, (BLK, SPAN)), 0, 1, stride=1, stride_axis=0
            )
            for g in range(5):
                table[hh, g] = turned[:, BLK * (4 - g) : BLK * (5 - g)]

    @pl.when(qb == 1)
    def _():
        w_copy.wait()
        w_pass.start()

    q_true = (qb + near_blocks * x) % blocks

    q_pos = q_true * BLK + lax.broadcasted_iota(jnp.int32, (1, BLK), 1)
    k_iota = lax.broadcasted_iota(jnp.int32, (BLK, BLK), 0)
    for kb in range(blocks):
        k_pos = (kb + near_blocks * x) % blocks * BLK + k_iota
        bound = 0
        q_doc = jnp.zeros((1, BLK), jnp.int32)
        k_doc = jnp.zeros((BLK, BLK), jnp.int32)
        for i in range(len_ref.shape[1]):
            bound = bound + len_ref[0, i]
            q_doc = q_doc + (q_pos >= bound).astype(jnp.int32)
            k_doc = k_doc + (k_pos >= bound).astype(jnp.int32)
        krows = slice(kb * BLK, (kb + 1) * BLK)
        seen = (padc[krows, 0:1] > 0.5) | (k_pos == q_pos)
        mask[krows, :] = jnp.where((k_doc == q_doc) & seen, 0.0, -1000000000.0)

    def head_rows(h, group):
        return pl.ds(pl.multiple_of(group * cols + h * dk, dk), dk)

    def diagonal(kb):
        return near_diagonal((kb + near_blocks * x) % blocks - q_true)

    def head(h, carry):
        qh = qkv_ref[head_rows(h, 0), lanes(qb)]
        peak = None
        for kb in range(blocks):
            krows = slice(kb * BLK, (kb + 1) * BLK)
            s = dot(qkv_ref[head_rows(h, 1), krows], qh, ((0,), (0,)))
            diag = diagonal(kb)
            s = s + table[h, diag] + mask[krows, :]
            score[krows, :] = s
            top = jnp.max(s, axis=0, keepdims=True)
            peak = top if peak is None else jnp.maximum(peak, top)
        total = jnp.zeros((1, BLK), F32)
        ctx = jnp.zeros((dk, BLK), F32)
        for kb in range(blocks):
            krows = slice(kb * BLK, (kb + 1) * BLK)
            e = jnp.exp(score[krows, :] - peak)
            total = total + jnp.sum(e, axis=0, keepdims=True)
            e_low = e.astype(BF)
            e_ref[h, 0, krows, :] = e_low
            ctx = ctx + dot(qkv_ref[head_rows(h, 2), krows], e_low, ((1,), (0,)))
        inv = 1.0 / total
        inv_ref[h, 0] = inv
        call[head_rows(h, 0), lanes(qb)] = (ctx * inv).astype(BF)
        return carry

    lax.fori_loop(0, heads, head, 0)
    ctx_copy(qb).start()

    @pl.when(qb == 1)
    def _():
        c_copy(2).start()

    @pl.when(qb == blocks - 1)
    def _():
        c_copy(3).start()
        w_pass.wait()
        wn[...] = wall[...].astype(F32).T.astype(BF)
        out(4).start()
        for i in range(blocks):
            b = (i + near_blocks) % blocks
            ctx_copy(i).wait()
            ls = slice(b * BLK, (b + 1) * BLK)
            v = dot(wn[...], call[:, ls], ((1,), (0,)))
            if b < near_blocks:
                v = v + f1[:, ls]
                f1[:, ls] = v
            else:
                v = v + fb[:, b * BLK - rows : (b + 1) * BLK - rows].astype(F32)
            xo[:, ls] = (v * norm_scale(v) * fgc[...]).astype(BF)
            xt_out(b).start()
        out(0).start()
        out(2).start()
        for i in range(4):
            c_copy(i).wait()
        for i in range(5):
            out(i).wait()
        for b in range(blocks):
            xt_out(b).wait()


def front(rel, lengths, pad, again, fgain, wq, wo, tok, far, cot, heads, dk):
    d, rows = tok.shape
    seq = 2 * rows
    cols = heads * dk
    blocks = seq // BLK
    buckets = rel.shape[0]
    bids = jnp.asarray(lane_buckets(buckets))
    one = pl.Buffered(1)
    dma = pltpu.SemaphoreType.DMA
    any_spec = pl.BlockSpec(memory_space=pl.ANY)
    smem = pl.BlockSpec(memory_space=pltpu.SMEM)

    def full(v):
        return pl.BlockSpec(v.shape, lambda i: (0, 0), pipeline_mode=one)

    return pl.pallas_call(
        functools.partial(front_kernel, heads, dk, buckets, blocks),
        grid=(blocks,),
        in_specs=[smem, smem, full(bids), full(pad), full(again), full(fgain), full(wq), full(wo)]
        + [any_spec] * 3,
        out_specs=[
            pl.BlockSpec((heads, 1, seq, BLK), lambda i: (0, i, 0, 0)),
            pl.BlockSpec((heads, 1, 1, BLK), lambda i: (0, i, 0, 0)),
            pl.BlockSpec((3 * cols, seq), lambda i: (0, 0)),
        ]
        + [any_spec] * 6,
        out_shape=[
            jax.ShapeDtypeStruct((heads, blocks, seq, BLK), BF),
            jax.ShapeDtypeStruct((heads, blocks, 1, BLK), F32),
            jax.ShapeDtypeStruct((3 * cols, seq), BF),
            jax.ShapeDtypeStruct((2 * cols, seq), BF),
            jax.ShapeDtypeStruct((d, seq), BF),
            jax.ShapeDtypeStruct((d, seq), BF),
            jax.ShapeDtypeStruct((d, rows), F32),
            jax.ShapeDtypeStruct((d, seq), BF),
            jax.ShapeDtypeStruct((2 * cols, d), BF),
        ],
        scratch_shapes=[
            pltpu.VMEM((d, rows), F32),
            pltpu.VMEM((d, rows), BF),
            pltpu.VMEM((d, rows), F32),
            pltpu.VMEM((d, rows), BF),
            pltpu.VMEM((d, seq), BF),
            pltpu.VMEM((heads, 5, BLK, BLK), F32),
            pltpu.VMEM((seq, 8), F32),
            pltpu.VMEM((seq, BLK), F32),
            pltpu.VMEM((seq, BLK), F32),
            pltpu.VMEM((d, 1), F32),
            pltpu.VMEM((d, 1), F32),
            pltpu.VMEM((2 * cols, d), BF),
            pltpu.VMEM((d, 2 * cols), BF),
            pltpu.VMEM((2 * cols, seq), BF),
            pltpu.VMEM((d, seq), BF),
            dma((3,)), dma((5 + blocks,)), dma((6,)), dma((6,)), dma((blocks,)), dma((blocks,)),
        ],
        compiler_params=pltpu.CompilerParams(
            vmem_limit_bytes=FF_VMEM, collective_id=2, has_side_effects=True
        ),
        cost_estimate=pl.CostEstimate(
            flops=16 * heads * seq * seq * dk + 10 * seq * d * cols,
            bytes_accessed=2 * heads * seq * seq + 30 * rows * d,
            transcendentals=heads * seq * seq,
        ),
    )(rel, lengths, bids, pad, again, fgain, wq, wo, tok, far, cot)


def ff_kernel(
    steps, extra,
    xt_hbm, w_hbm, ct_hbm, wo_hbm, mid_hbm, wq_hbm,
    grads_ref, din_hbm, near_hbm, far_hbm, quarter_hbm, half_hbm, hand_hbm, wfar_hbm,
    xt, ct, wg, wu, wo, hid, dg, du, din, stage, r1, r2, r3, r4, xs, xr, of,
    csem, wsem, s1, s2, s3, s4, t1, t2, t3, t4, xsem, osem, hsem,
):
    f, total = hid.shape
    rows = total // 2
    chunks = rows // BLK
    d = xt.shape[0]
    shard = d // 16
    dp, mp = lax.axis_index("dp"), lax.axis_index("mp")
    a = group_coords(dp // extra)
    peers = [flip(dp, m * extra) for m in GROUP_MASKS]
    other = (dp, 1 - mp)
    core = dp % 2
    sibling = dp + 1 - 2 * core
    bufs = (r1, r2, r3, r4)
    sends, recvs = (s1, s2, s3, s4), (t1, t2, t3, t4)
    end = steps - 1

    def weight_copy(kind, n):
        src, dst = ((w_hbm.at[0], wg), (w_hbm.at[1], wu), (wo_hbm, wo))[kind]
        return pltpu.make_async_copy(src.at[:, lanes(n)], dst.at[:, lanes(n)], wsem.at[kind, n])

    def tok_copy(n):
        src, dst, start, size = (
            (xt_hbm, xt, rows, BLK), (ct_hbm, ct, rows, BLK),
            (xt_hbm, xt, 0, rows), (ct_hbm, ct, 0, rows), (xt_hbm, xt, rows + BLK, BLK),
        )[n]
        part = pl.ds(start, size)
        return pltpu.make_async_copy(src.at[:, part], dst.at[:, part], csem.at[n])

    near_part, far_part = pl.ds(0, rows), pl.ds(rows, rows)
    c_far = remote(
        ct_hbm.at[:, pl.ds(BLK, BLK)], ct.at[:, pl.ds(rows + BLK, BLK)], csem.at[5], csem.at[6], other
    )
    x_copy = remote(xs, xr, xsem.at[0], xsem.at[1], other)
    wq_rows = wq_hbm.shape[0] // 2
    wq_part = pl.ds(core * wq_rows, wq_rows)
    w_copy = remote(wq_hbm.at[wq_part], wfar_hbm.at[wq_part], xsem.at[2], xsem.at[3], other)
    w_pass = remote(wfar_hbm.at[wq_part], wfar_hbm.at[wq_part], xsem.at[4], xsem.at[5], (sibling, mp))
    mid_copy = pltpu.make_async_copy(mid_hbm, din.at[:, far_part], osem.at[3])

    deep = len(LEVELS)

    def hop(level, n, order):
        half = 8 >> level
        c = order[level]
        away = pl.ds((1 - a[c]) * half, half)
        src = stage.at[away] if level == 0 else bufs[level - 1].at[n, away]
        return remote(src, bufs[level].at[n], sends[level].at[n], recvs[level].at[n], (peers[c], mp))

    def hand_copy(n):
        level = levels_of(n) if isinstance(n, int) else 1
        dst = (hand_hbm.at[n - deep], half_hbm, quarter_hbm.at[n - 1])[level - 1]
        return pltpu.make_async_copy(bufs[level - 1].at[n], dst, hsem.at[n])

    def absorb_first(n):
        hop(0, n, Y_FIRST).wait()
        r1[n] = stage[pl.ds(a[0] * 8, 8)] + r1[n]
        if isinstance(n, int):
            hand_copy(n).start()
            return

        @pl.when(n == Z_BLOCK)
        def _():
            hop(1, n, Z_FIRST).start()

        @pl.when((n < deep) & (n != Z_BLOCK))
        def _():
            hop(1, n, Y_FIRST).start()

        @pl.when(n >= deep)
        def _():
            hand_copy(n).start()

    def absorb(level, n):
        half = 8 >> level
        order = order_of(n)
        hop(level, n, order).wait()
        kept = bufs[level - 1][n, pl.ds(a[order[level]] * half, half)]
        if level < 3:
            bufs[level][n] = kept + bufs[level][n]
            if level + 1 < levels_of(n):
                hop(level + 1, n, order).start()
            else:
                hand_copy(n).start()
        else:
            both = kept.astype(F32) + bufs[level][n].astype(F32)
            for w in range(3):
                grads_ref[w, :, n * BLK : (n + 1) * BLK] = both[0, w]

    scale = np.float32(np.sqrt(2 / np.pi))

    def place(u):
        early, late = u // steps, (u - 4) // steps
        is_far0 = (early == 0) * 1
        is_far1 = (late == 1) * 1
        v = u - steps
        n = v - steps * (u // (2 * steps + 4))
        near_j, near_c = n // 2, n % 2
        j = is_far0 * u + is_far1 * (u - steps - 4) + (1 - is_far0 - is_far1) * near_j
        c = is_far0 * chunks + is_far1 * (chunks + 1) + (1 - is_far0 - is_far1) * near_c
        return j, c

    def substep(u):
        j, c = place(u)
        pj, pc = place(u - 1)
        pj = pj + (u == 0) * 1
        fcols, tok = lanes(j), lanes(c)
        pcols, ptok = lanes(pj), lanes(pc)
        gate = dot(wg[:, fcols], xt[:, tok], ((0,), (0,)))
        up = dot(wu[:, fcols], xt[:, tok], ((0,), (0,)))
        dh = dot(wo[:, fcols], ct[:, tok], ((0,), (0,)))
        backward(pcols, ptok)
        sq = gate * gate
        t = jnp.tanh(scale * gate * (1.0 + 0.044715 * sq))
        half = 0.5 * (1.0 + t)
        act = gate * half
        slope = half + 0.5 * gate * (1.0 - t * t) * (scale * (1.0 + (3 * 0.044715) * sq))
        hid[fcols, tok] = (act * up).astype(BF)
        dg[fcols, tok] = (dh * (up * slope)).astype(BF)
        du[fcols, tok] = (dh * act).astype(BF)

    def backward(rs, tok):
        din[:, tok] += dot(wg[:, rs], dg[rs, tok], ((1,), (0,))) + dot(wu[:, rs], du[rs, tok], ((1,), (0,)))

    per = 4 * shard

    def grads(j):
        z = (j == Z_BLOCK) * 1
        for w in range(3):
            right = (hid, dg, du)[w][lanes(j), :]
            for q in range(4):
                rs = slice(q * per, (q + 1) * per)
                left = ct[rs, :] if w == 0 else xt[rs, :]
                part = dot(left, right, ((1,), (1,)))
                for k in range(4):
                    at = block_position(4 * q + k, Y_FIRST)
                    at = at + z * (block_position(4 * q + k, Z_FIRST) - at)
                    stage[at, w, 0:shard, :] = part[k * shard : (k + 1) * shard].astype(BF)
        hop(0, j, Y_FIRST).start()

    def out_part(n):
        return dot(wo[...], hid[:, lanes(n)], ((1,), (0,)))

    meet([(p, mp) for p in peers] + [other] + ([(sibling, mp)] if extra > 1 else []))
    c_far.start()
    w_copy.start()
    tok_copy(0).start()
    tok_copy(1).start()
    for n in range(steps):
        for kind in range(3):
            weight_copy(kind, n).start()
    for n in range(2, 5):
        tok_copy(n).start()
    din[...] = jnp.zeros_like(din)
    stage[...] = jnp.zeros_like(stage)
    before = place(-1)[1]
    dg[0:BLK, before * BLK : (before + 1) * BLK] = jnp.zeros((BLK, BLK), BF)
    du[0:BLK, before * BLK : (before + 1) * BLK] = jnp.zeros((BLK, BLK), BF)
    tok_copy(0).wait()
    tok_copy(1).wait()
    count = 2 * chunks * steps
    far_end = 2 * steps + 4

    def step(u, carry):
        @pl.when(u < steps)
        def _():
            for kind in range(3):
                weight_copy(kind, u).wait()

        @pl.when(u == steps)
        def _():
            tok_copy(2).wait()
            tok_copy(3).wait()

        @pl.when(u == steps + 4)
        def _():
            tok_copy(4).wait()
            c_far.wait()

        @pl.when(u < count)
        def _():
            substep(u)

        @pl.when(u == far_end)
        def _():
            xs[...] = din[:, far_part].astype(BF)
            x_copy.start()
            mid_copy.start()

        odd = u % 2 == 1
        late = (u >= 2 * steps + 5) * 1
        m = (u - 13) // 2 - 2 * ((u >= 2 * steps + 7) * 1)
        n = (u - 11) // 2 - 2 * late

        @pl.when(odd & ((u == 13) | (u == 15) | (u >= 2 * steps + 7)))
        def _():
            absorb_first(m)

        for at, events in (
            (21, ((1, 0),)), (23, ((1, 1),)), (25, ((2, 0),)), (27, ((1, 2), (2, 1))),
        ):
            @pl.when(u == at)
            def _():
                for level, block in events:
                    absorb(level, block)

        @pl.when(odd & ((u == 11) | (u == 13) | (u >= 2 * steps + 5)))
        def _():
            grads(n)

        @pl.when(u == far_end + 5)
        def _():
            w_copy.wait()
            w_pass.start()

        return carry

    lax.fori_loop(0, count, step, 0)
    pj, pc = place(count - 1)
    backward(lanes(pj), lanes(pc))

    def far_out(n, carry):
        of[:, lanes(n)] = out_part(n + chunks).astype(BF)
        return carry

    lax.fori_loop(0, chunks, far_out, 0)
    far_copy = pltpu.make_async_copy(of, far_hbm, osem.at[0])
    far_copy.start()
    x_copy.wait()
    din[:, near_part] += xr[...].astype(F32)
    din_copy = pltpu.make_async_copy(din.at[:, near_part], din_hbm, osem.at[2])
    din_copy.start()
    mid_copy.wait()

    def near_out(n, carry):
        at = lanes(n + chunks)
        din[:, at] = din[:, at] + out_part(n)
        return carry

    lax.fori_loop(0, chunks, near_out, 0)
    near_copy = pltpu.make_async_copy(din.at[:, far_part], near_hbm, osem.at[1])
    near_copy.start()
    absorb_first(end)
    absorb(3, 0)
    absorb(2, 2)
    absorb(1, 3)
    w_pass.wait()
    for n in range(1, steps):
        hand_copy(n).wait()
    far_copy.wait()
    near_copy.wait()
    din_copy.wait()


def ff_all(xt, ct, w2, wo, mid, wq, extra):
    d, total = xt.shape
    f = wo.shape[1]
    rows = total // 2
    steps = f // BLK
    deep = len(LEVELS)
    shard = d // 16
    spad = -(-shard // 16) * 16
    dma = pltpu.SemaphoreType.DMA
    any_spec = pl.BlockSpec(memory_space=pl.ANY)
    return pl.pallas_call(
        functools.partial(ff_kernel, steps, extra),
        in_specs=[any_spec] * 6,
        out_specs=[pl.BlockSpec(memory_space=pltpu.VMEM)] + [any_spec] * 7,
        out_shape=[
            jax.ShapeDtypeStruct((3, spad, BLK), F32),
            jax.ShapeDtypeStruct((d, rows), F32),
            jax.ShapeDtypeStruct((d, rows), F32),
            jax.ShapeDtypeStruct((d, rows), BF),
            jax.ShapeDtypeStruct((2, 2, 3, spad, BLK), BF),
            jax.ShapeDtypeStruct((4, 3, spad, BLK), BF),
            jax.ShapeDtypeStruct((steps - deep, 8, 3, spad, BLK), BF),
            jax.ShapeDtypeStruct(wq.shape, BF),
        ],
        scratch_shapes=[
            pltpu.VMEM((d, total), BF),
            pltpu.VMEM((d, total), BF),
            pltpu.VMEM((d, f), BF),
            pltpu.VMEM((d, f), BF),
            pltpu.VMEM((d, f), BF),
            pltpu.VMEM((f, total), BF),
            pltpu.VMEM((f, total), BF),
            pltpu.VMEM((f, total), BF),
            pltpu.VMEM((d, total), F32),
            pltpu.VMEM((16, 3, spad, BLK), BF),
            pltpu.VMEM((steps, 8, 3, spad, BLK), BF),
            pltpu.VMEM((4, 4, 3, spad, BLK), BF),
            pltpu.VMEM((3, 2, 3, spad, BLK), BF),
            pltpu.VMEM((1, 1, 3, spad, BLK), BF),
            pltpu.VMEM((d, rows), BF),
            pltpu.VMEM((d, rows), BF),
            pltpu.VMEM((d, rows), BF),
            dma((7,)),
            dma((3, steps)),
            dma((steps,)), dma((4,)), dma((3,)), dma((1,)),
            dma((steps,)), dma((4,)), dma((3,)), dma((1,)),
            dma((6,)),
            dma((4,)),
            dma((steps,)),
        ],
        compiler_params=pltpu.CompilerParams(
            vmem_limit_bytes=FF_VMEM, collective_id=0, has_side_effects=True
        ),
        cost_estimate=pl.CostEstimate(
            flops=18 * total * d * f,
            bytes_accessed=6 * d * f + 16 * total * d,
            transcendentals=total * f,
        ),
    )(xt, w2, ct, wo, mid, wq)


def tail_kernel(
    heads, dk, buckets, blocks, extra,
    bid_ref, qkv_ref, e_ref, inv_ref, wall_ref, ctx_ref, ag_ref, fg_ref, early_ref,
    din_hbm, mid_hbm, cot_hbm, tok_hbm, nrm_hbm, wq_hbm, wfar_hbm, far_hbm,
    quarter_hbm, half_hbm, hand_hbm,
    ig_hbm, back_hbm, gq_ref, go_ref, small_ref, ffo_ref, ffi_ref,
    f1, f2, f3, nrm, wq, wn, wf, alow, dctx, dcs, osend, orecv, fsum, agc, fgc,
    dp_s, dkv, tally, dproj, dfar, grad,
    sa, sb_, a1, a2, a3, a4, b1, b2, b3, b4, hk, hm, hq, h2, h3, h4, sv, rv,
    lsem, ksem, xs_sem, xr_sem, cs_sem, cr_sem, bs_sem, br_sem, hs_sem, hr_sem,
):
    qb = pl.program_id(0)
    dp, x = lax.axis_index("dp"), lax.axis_index("mp")
    d, rows = f2.shape
    cols = heads * dk
    shard = d // 16
    a = group_coords(dp // extra)
    peers = [flip(dp, m * extra) for m in GROUP_MASKS]
    other = (dp, 1 - x)
    near_blocks = blocks // 2
    near_part, far_part = pl.ds(0, rows), pl.ds(rows, rows)
    halves = ((sa, a1, a2, a3, a4), (sb_, b1, b2, b3, b4))
    orders = (Y_FIRST, Z_FIRST)
    copies = (
        (din_hbm, f1), (mid_hbm, f2), (cot_hbm, f3), (tok_hbm, f2), (nrm_hbm, nrm), (wq_hbm, wq), (wfar_hbm, wq),
    )

    def local(i):
        return pltpu.make_async_copy(copies[i][0], copies[i][1], lsem.at[i])

    def x_copy(i, src, dst):
        return remote(src, dst, xs_sem.at[i], xr_sem.at[i], other)

    dctx_copy = x_copy(0, dcs, dctx.at[:, far_part])
    o_copy = x_copy(1, osend, orecv)
    dproj_copy = x_copy(2, dproj.at[:, far_part], dfar)

    def back_copy(i):
        part = pl.ds(i * 128, 128)
        return x_copy(3 + i, far_hbm.at[:, part], back_hbm.at[:, part])

    def hop(side, level):
        half = 8 >> level
        c = orders[side][level]
        away = pl.ds((1 - a[c]) * half, half)
        bufs = halves[side]
        return remote(
            bufs[level].at[away], bufs[level + 1], cs_sem.at[side, level], cr_sem.at[side, level], (peers[c], x)
        )

    def absorb(side, level):
        half = 8 >> level
        bufs = halves[side]
        hop(side, level).wait()
        kept = bufs[level][pl.ds(a[orders[side][level]] * half, half)]
        if level < 3:
            bufs[level + 1][...] = kept + bufs[level + 1][...]
            hop(side, level + 1).start()
            return
        both = (kept.astype(F32) + bufs[level + 1][...].astype(F32))[0, 0:shard]
        outs = (gq_ref.at[0], gq_ref.at[1]) if side == 0 else (gq_ref.at[2], go_ref)
        for i in range(2):
            outs[i][...] = both[:, i * cols : (i + 1) * cols]

    deep = len(LEVELS)
    handed = (1, 2, 3, 4, 5, 6)

    def keep_copy(block):
        level = levels_of(block)
        half = 8 >> level
        keep = pl.ds(a[order_of(block)[level]] * half, half)
        if level == 3:
            src, dst = quarter_hbm.at[block - 1, keep], hq.at[block - 1]
        elif level == 2:
            src, dst = half_hbm.at[keep], hm
        else:
            src, dst = hand_hbm.at[block - deep, keep], hk.at[block - deep]
        return pltpu.make_async_copy(src, dst, ksem.at[block])

    def hand_hop(level, block):
        half = 8 >> level
        c = order_of(block)[level]
        away = pl.ds((1 - a[c]) * half, half)
        fresh = level == levels_of(block)
        if level == 1:
            src, dst = hand_hbm.at[block - deep, away], h2.at[block - deep]
        elif level == 2:
            src, dst = half_hbm.at[away] if fresh else h2.at[block - deep, away], h3.at[block - 3]
        else:
            src, dst = quarter_hbm.at[block - 1, away] if fresh else h3.at[block - 3, away], h4.at[block - 1]
        return remote(src, dst, hs_sem.at[level, block], hr_sem.at[level, block], (peers[c], x))

    def put_grads(w, block, value):
        at = slice(block * BLK, (block + 1) * BLK)
        if w == 0:
            ffo_ref[:, at] = value
        else:
            ffi_ref[:, w - 1, at] = value

    def hand_absorb(level, block):
        half = 8 >> level
        keep = pl.ds(a[order_of(block)[level]] * half, half)
        hand_hop(level, block).wait()
        if level == levels_of(block):
            keep_copy(block).wait()
            kept = hk[block - deep] if level == 1 else (hm[...] if level == 2 else hq[block - 1])
        else:
            kept = h2[block - deep, keep] if level == 2 else h3[block - 3, keep]
        if level == 1:
            h2[block - deep] = kept + h2[block - deep]
        elif level == 2:
            h3[block - 3] = kept + h3[block - 3]
        else:
            both = kept.astype(F32) + h4[block - 1].astype(F32)
            for w in range(3):
                put_grads(w, block, both[0, w, 0:shard])
        if level < 3:
            hand_hop(level + 1, block).start()

    def round_copy(i):
        who = other if i == 4 else (peers[(0, 2, 3, 1)[i]], x)
        return remote(sv.at[i], rv.at[i], bs_sem.at[i], br_sem.at[i], who)

    def round_end(i):
        round_copy(i).wait()
        sv[i + 1] = sv[i] + rv[i]
        if i < 4:
            round_copy(i + 1).start()

    def out_copy(r):
        return pltpu.make_async_copy(f3.at[:, lanes(r)], ig_hbm.at[:, lanes(r)], lsem.at[len(copies) + r])

    def lane_sum(v):
        total = v[:, 0:128]
        for i in range(1, v.shape[1] // 128):
            total = total + v[:, i * 128 : (i + 1) * 128]
        return total

    @pl.when(qb == 0)
    def _():
        for i in range(3):
            local(i).start()
        meet([(p, x) for p in peers] + [other])
        back_copy(0).start()
        for block in handed:
            hand_hop(levels_of(block), block).start()
        agc[...] = column(ag_ref[...])
        fgc[...] = column(fg_ref[...])
        dkv[...] = jnp.zeros_like(dkv)
        tally[...] = jnp.zeros_like(tally)
        sa[...] = jnp.zeros_like(sa)
        sb_[...] = jnp.zeros_like(sb_)
        fsum[...] = jnp.zeros_like(fsum)
        for i in range(3):
            local(i).wait()

        def norm_rows(r, carry):
            ls = lanes(r)
            v = f2[:, ls]
            c = f1[:, ls]
            scale = norm_scale(v)
            n = v * scale
            cg = c * fgc[...]
            m = jnp.mean(cg * n, axis=0, keepdims=True)
            gm = f3[:, ls] + scale * (cg - n * m)
            fsum[...] += lane_sum(c * n)
            f1[:, ls] = gm
            alow[:, ls] = gm.astype(BF)
            return carry

        lax.fori_loop(0, near_blocks, norm_rows, 0)
        dcs[...] = dot(wall_ref[cols : 2 * cols, :], alow[...], ((1,), (0,))).astype(BF)
        dctx_copy.start()
        for i in (3, 4, 5):
            local(i).start()
        for block in handed:
            keep_copy(block).start()
        dctx[:, near_part] = dot(wall_ref[0:cols, :], alow[...], ((1,), (0,))).astype(BF)
        osend[...] = dot(alow[...], ctx_ref[cols : 2 * cols, near_part], ((1,), (1,))).astype(BF)
        o_copy.start()
        grad[:, 3 * cols : 4 * cols] = dot(alow[...], ctx_ref[0:cols, near_part], ((1,), (1,)))
        for w in range(3):
            put_grads(w, 0, early_ref[w, 0:shard, :])
        dctx_copy.wait()
        back_copy(1).start()

    @pl.when(qb == 1)
    def _():
        local(5).wait()
        wn[...] = wq[...].astype(F32).T.astype(BF)
        local(6).start()
        hand_absorb(2, 3)
        hand_absorb(3, 1)
        hand_absorb(3, 2)
        hand_absorb(1, 4)

    @pl.when(qb == 2)
    def _():
        local(6).wait()
        wf[...] = wq[...].astype(F32).T.astype(BF)

    @pl.when(qb == 3)
    def _():
        hand_absorb(3, 3)
        hand_absorb(2, 4)

    q_true = (qb + near_blocks * x) % blocks

    def head(h, carry):
        def head_rows(group):
            return pl.ds(pl.multiple_of(group * cols + h * dk, dk), dk)

        inv = inv_ref[h, 0]
        qh = qkv_ref[head_rows(0), lanes(qb)]
        scaled = (dctx[head_rows(0), lanes(qb)].astype(F32) * inv).astype(BF)
        inner = jnp.zeros((1, BLK), F32)
        for kb in range(blocks):
            krows = slice(kb * BLK, (kb + 1) * BLK)
            g = dot(qkv_ref[head_rows(2), krows], scaled, ((0,), (0,)))
            dp_s[krows, :] = g
            inner = inner + jnp.sum(e_ref[h, 0, krows, :].astype(F32) * g, axis=0, keepdims=True)
        inner = inner * inv
        dq = jnp.zeros((dk, BLK), F32)
        for kb in range(blocks):
            krows = slice(kb * BLK, (kb + 1) * BLK)
            e = e_ref[h, 0, krows, :]
            ds = (e.astype(F32) * (dp_s[krows, :] - inner)).astype(BF)
            dkv[head_rows(0), krows] += dot(qh, ds, ((1,), (1,)))
            dkv[head_rows(1), krows] += dot(scaled, e, ((1,), (1,)))
            dq = dq + dot(qkv_ref[head_rows(1), krows], ds, ((1,), (0,)))
            tally[h, near_diagonal((kb + near_blocks * x) % blocks - q_true)] += ds.astype(F32)
        dproj[head_rows(0), lanes(qb)] = dq.astype(BF)
        return carry

    lax.fori_loop(0, heads, head, 0)

    @pl.when(qb == blocks - 1)
    def _():
        dproj[cols : 3 * cols, :] = dkv[...].astype(BF)
        dproj_copy.start()
        back_copy(2).start()
        back_copy(3).start()
        hand_absorb(1, 5)
        local(3).wait()
        local(4).wait()
        per = 4 * shard

        def grad_rows(q, carry):
            rs = pl.ds(pl.multiple_of(q * per, 16), per)
            grad[rs, 0 : 3 * cols] = dot(nrm[rs, :], dproj[...], ((1,), (1,)))
            return carry

        lax.fori_loop(0, 4, grad_rows, 0)
        o_copy.wait()
        grad[:, 3 * cols : 4 * cols] += orecv[...].astype(F32)
        for side in range(2):
            for k in range(16):
                halves[side][0][block_position(k, orders[side]), 0:shard, :] = grad[
                    k * shard : (k + 1) * shard, 2 * side * cols : 2 * (side + 1) * cols
                ].astype(BF)
            hop(side, 0).start()

        def near_rows(r, carry):
            f3[:, lanes(r)] = dot(wn[...], dproj[:, lanes(r)], ((1,), (0,)))
            return carry

        lax.fori_loop(0, near_blocks, near_rows, 0)
        absorb(0, 0)
        absorb(1, 0)
        ids = bid_ref[...]
        hot = ids == lax.broadcasted_iota(jnp.int32, (buckets, SPAN), 0)
        out_lane = lax.broadcasted_iota(jnp.int32, (buckets, 128), 1)
        sub = lax.broadcasted_iota(jnp.int32, (8, SPAN), 0)
        sv[0] = jnp.zeros(sv.shape[1:], F32)

        def bias_sums(hh, carry):
            line = jnp.zeros((8, SPAN), F32)
            for g in range(BLK // 8):
                group = slice(8 * g, 8 * g + 8)
                parts = [tally[hh, i, group, :] for i in (4, 3, 2, 1, 0)]
                strip = jnp.concatenate(parts + [jnp.zeros((8, BLK), F32)], axis=1)
                line = line + (strip if g == 0 else pltpu.roll(strip, SPAN - 8 * g, 1))
            for bit in (1, 2, 4):
                line = jnp.where((sub // bit) % 2 == 1, pltpu.roll(line, SPAN - bit, 1), line)
            sums = jnp.sum(line, axis=0, keepdims=True)
            col = jnp.sum(jnp.where(hot, sums, 0.0), axis=1, keepdims=True)
            sv[0, 0:buckets, :] = jnp.where(out_lane == x * heads + hh, col, sv[0, 0:buckets, :])
            return carry

        lax.fori_loop(0, heads, bias_sums, 0)
        product = wn[...].astype(F32) * grad[:, 0 : 3 * cols]
        again = lane_sum(product[:, 0:512]).T
        rest = product[:, 512 : 3 * cols]
        again = jnp.sum(again, axis=0, keepdims=True) + jnp.sum(rest.T, axis=0, keepdims=True)
        again = again / ag_ref[...]
        fgain = jnp.sum(fsum[...].T, axis=0, keepdims=True)
        lines = -(-d // 128)
        for i in range(lines):
            n = min(128, d - 128 * i)
            sv[0, buckets + i : buckets + i + 1, 0:n] = again[:, 128 * i : 128 * i + n]
            sv[0, buckets + lines + i : buckets + lines + i + 1, 0:n] = fgain[:, 128 * i : 128 * i + n]
        round_copy(0).start()
        hand_absorb(3, 4)
        hand_absorb(2, 5)
        hand_absorb(1, 6)
        round_end(0)
        absorb(1, 1)
        dproj_copy.wait()

        def last_norm(r, carry):
            ls = lanes(r)
            c = f3[:, ls] + dot(wf[...], dfar[:, ls], ((1,), (0,)))
            v = f2[:, ls]
            scale = norm_scale(v)
            n = v * scale
            cg = c * agc[...]
            m = jnp.mean(cg * n, axis=0, keepdims=True)
            f3[:, ls] = f1[:, ls] + scale * (cg - n * m)
            out_copy(r).start()
            return carry

        lax.fori_loop(0, near_blocks, last_norm, 0)
        absorb(0, 1)
        hand_absorb(3, 5)
        round_end(1)
        hand_absorb(2, 6)
        absorb(1, 2)
        round_end(2)
        absorb(0, 2)
        hand_absorb(3, 6)
        absorb(1, 3)
        round_end(3)
        absorb(0, 3)
        round_end(4)
        small_ref[...] = sv[5]
        for i in range(4):
            back_copy(i).wait()
        for r in range(near_blocks):
            out_copy(r).wait()


def tail(qkv, e, inv, wall, ctx, again, fgain, early, din, mid, cot, tok, nrm, wq, wfar, far,
         quarter, half_way, hand, buckets, heads, dk, extra, f):
    d, rows = tok.shape
    seq = 2 * rows
    cols = heads * dk
    blocks = seq // BLK
    near = blocks // 2
    shard = d // 16
    spad = -(-shard // 16) * 16
    deep = hand.shape[0]
    later = deep + len(LEVELS)
    lines = -(-(buckets + 2 * -(-d // 128)) // 8) * 8
    bids = jnp.asarray(lane_buckets(buckets))
    one = pl.Buffered(1)
    dma = pltpu.SemaphoreType.DMA
    any_spec = pl.BlockSpec(memory_space=pl.ANY)

    def full(v):
        return pl.BlockSpec(v.shape, lambda i: (0,) * len(v.shape), pipeline_mode=one)

    def chain(width):
        return [pltpu.VMEM((n, spad, width), BF) for n in (16, 8, 4, 2, 1)]

    outs = [
        jax.ShapeDtypeStruct((3, shard, cols), F32),
        jax.ShapeDtypeStruct((shard, cols), F32),
        jax.ShapeDtypeStruct((lines, 128), F32),
        jax.ShapeDtypeStruct((shard, f), F32),
        jax.ShapeDtypeStruct((shard, 2, f), F32),
    ]
    a_chain, b_chain = chain(2 * cols), chain(2 * cols)
    return pl.pallas_call(
        functools.partial(tail_kernel, heads, dk, buckets, blocks, extra),
        grid=(blocks,),
        in_specs=[
            full(bids),
            full(qkv),
            pl.BlockSpec((heads, 1, seq, BLK), lambda i: (0, i, 0, 0)),
            pl.BlockSpec((heads, 1, 1, BLK), lambda i: (0, i, 0, 0)),
            full(wall),
            full(ctx),
            full(again),
            full(fgain),
            full(early),
        ]
        + [any_spec] * 11,
        out_specs=[any_spec, any_spec] + [full(v) for v in outs],
        out_shape=[jax.ShapeDtypeStruct((d, rows), F32), jax.ShapeDtypeStruct((d, rows), BF)] + outs,
        scratch_shapes=[
            pltpu.VMEM((d, rows), F32),
            pltpu.VMEM((d, rows), F32),
            pltpu.VMEM((d, rows), F32),
            pltpu.VMEM((d, seq), BF),
            pltpu.VMEM((3 * cols, d), BF),
            pltpu.VMEM((d, 3 * cols), BF),
            pltpu.VMEM((d, 3 * cols), BF),
            pltpu.VMEM((d, rows), BF),
            pltpu.VMEM((cols, seq), BF),
            pltpu.VMEM((cols, rows), BF),
            pltpu.VMEM((d, cols), BF),
            pltpu.VMEM((d, cols), BF),
            pltpu.VMEM((d, 128), F32),
            pltpu.VMEM((d, 1), F32),
            pltpu.VMEM((d, 1), F32),
            pltpu.VMEM((seq, BLK), F32),
            pltpu.VMEM((2 * cols, seq), F32),
            pltpu.VMEM((heads, 5, BLK, BLK), F32),
            pltpu.VMEM((3 * cols, seq), BF),
            pltpu.VMEM((3 * cols, rows), BF),
            pltpu.VMEM((d, 4 * cols), F32),
            a_chain[0],
            b_chain[0],
        ]
        + a_chain[1:]
        + b_chain[1:]
        + [
            pltpu.VMEM((deep, 4, 3, spad, BLK), BF),
            pltpu.VMEM((2, 3, spad, BLK), BF),
            pltpu.VMEM((2, 1, 3, spad, BLK), BF),
            pltpu.VMEM((deep, 4, 3, spad, BLK), BF),
            pltpu.VMEM((deep + 1, 2, 3, spad, BLK), BF),
            pltpu.VMEM((later - 1, 1, 3, spad, BLK), BF),
            pltpu.VMEM((6, lines, 128), F32),
            pltpu.VMEM((5, lines, 128), F32),
            dma((7 + near,)),
            dma((later,)),
            dma((7,)), dma((7,)),
            dma((2, 4)), dma((2, 4)),
            dma((5,)), dma((5,)),
            dma((4, later)), dma((4, later)),
        ],
        compiler_params=pltpu.CompilerParams(
            vmem_limit_bytes=FF_VMEM, collective_id=1, has_side_effects=True
        ),
        cost_estimate=pl.CostEstimate(
            flops=32 * heads * seq * seq * dk + 8 * seq * d * 3 * cols,
            bytes_accessed=2 * heads * seq * seq + 30 * rows * d,
            transcendentals=0,
        ),
    )(bids, qkv, e, inv, wall, ctx, again, fgain, early, din, mid, cot, tok, nrm, wq, wfar, far,
      quarter, half_way, hand)


def outputs_kernel(near_ref, back_ref, ig_ref, *refs):
    n = (len(refs) - 3) // 2
    sources, res_ref, ig_out, targets, sem = refs[:n], refs[n], refs[n + 1], refs[n + 2 : 2 * n + 2], refs[-1]

    def copy(i):
        return pltpu.make_async_copy(sources[i], targets[i], sem.at[i])

    @pl.when(pl.program_id(0) == 0)
    def _():
        for i in range(n):
            copy(i).start()

    res_ref[...] = near_ref[...] + back_ref[...].astype(F32)
    ig_out[...] = ig_ref[...]

    @pl.when(pl.program_id(0) == pl.num_programs(0) - 1)
    def _():
        for i in range(n):
            copy(i).wait()


def outputs(near, back, ig, *grads):
    d, rows = near.shape
    block = pl.BlockSpec((d // 4, rows), lambda i: (i, 0))
    any_spec = pl.BlockSpec(memory_space=pl.ANY)
    return pl.pallas_call(
        outputs_kernel,
        grid=(4,),
        in_specs=[block] * 3 + [any_spec] * len(grads),
        out_specs=[block] * 2 + [any_spec] * len(grads),
        out_shape=[jax.ShapeDtypeStruct(v.shape, F32) for v in (near, ig) + grads],
        scratch_shapes=[pltpu.SemaphoreType.DMA((len(grads),))],
    )(near, back, ig, *grads)


def take(array, index):
    return lax.dynamic_index_in_dim(array, index, 0, keepdims=False)


def per_device(
    tokens,
    cotangent,
    doc_lengths,
    pad_mask,
    attn_gain,
    qkv_weight,
    rel_table,
    out_weight,
    ff_gain,
    ff_in_weight,
    ff_out_weight,
):
    rows, d = tokens.shape
    n_dp = lax.axis_size("dp")
    n_mp = lax.axis_size("mp")
    cols = qkv_weight.shape[2]
    buckets, heads = rel_table.shape
    dk = cols // heads
    me = lax.axis_index("dp")
    shard = d // n_dp
    extra = n_dp // 16

    def hop(v, mask):
        return lax.ppermute(v, "dp", [(i, i ^ mask) for i in range(n_dp)])

    def bit(b):
        return (me >> b) & 1

    def finish(g):
        parts = [g.reshape((extra, shard) + g.shape[1:])]
        for b in reversed(range(extra.bit_length() - 1)):
            halves = [p.reshape((2, p.shape[0] // 2) + p.shape[1:]) for p in parts]
            away = sum(take(p, 1 - bit(b)).astype(F32) for p in halves).astype(BF)
            parts = [take(p, bit(b)) for p in halves] + [hop(away, 1 << b)]
        return sum(p.astype(F32) for p in parts)[0]

    tok = tokens.T
    cot = cotangent.T
    far = lax.ppermute(tok.astype(BF), "mp", [(0, 1), (1, 0)])
    w2 = jnp.transpose(ff_in_weight, (1, 0, 2))
    wq = jnp.transpose(qkv_weight, (1, 2, 0)).reshape(3 * cols, d)
    again, fgain = attn_gain.reshape(1, d), ff_gain.reshape(1, d)

    e, inv, qkv, ctx, nrm, xt, mid, ct, wall = front(
        rel_table, doc_lengths, pad_mask, again, fgain, wq, out_weight.T, tok, far, cot, heads, dk
    )
    early, din, near_out, far_out, quarter, half_way, hand, wfar = ff_all(
        xt, ct, w2, ff_out_weight, mid, wq, extra
    )
    input_grad, back, grad_qkv, grad_out, small, ffo, ffi = tail(
        qkv, e, inv, wall, ctx, again, fgain, early, din, mid, cot, tok, nrm, wq, wfar, far_out,
        quarter, half_way, hand, buckets, heads, dk, extra, ff_out_weight.shape[1],
    )
    result, input_grad, grad_qkv, grad_out, ffo, ffi = outputs(
        near_out, back, input_grad, grad_qkv, grad_out, ffo, ffi
    )
    grad_qkv = jnp.transpose(grad_qkv, (1, 0, 2))
    if extra > 1:
        grad_qkv, grad_out, ffo, ffi = (finish(g) for g in (grad_qkv, grad_out, ffo, ffi))
    for b in range(extra.bit_length() - 1):
        small = small + hop(small, 1 << b)
    lines = -(-d // 128)
    return (
        result.T,
        input_grad.T,
        small[buckets : buckets + lines].reshape(-1)[:d],
        grad_qkv,
        small[:buckets, : heads * n_mp],
        grad_out,
        small[buckets + lines : buckets + 2 * lines].reshape(-1)[:d],
        ffi,
        ffo,
    )


def solution(mesh):
    return jax.shard_map(
        per_device,
        mesh=mesh,
        in_specs=(
            P(("dp", "mp"), None),
            P(("dp", "mp"), None),
            P("dp", None),
            P("dp", None),
            P(),
            P(None, None, "mp"),
            P(None, "mp"),
            P(None, "mp"),
            P(),
            P(None, None, "mp"),
            P(None, "mp"),
        ),
        out_specs=(
            P(("dp", "mp"), None),
            P(("dp", "mp"), None),
            P(),
            P("dp", None, "mp"),
            P(),
            P("dp", "mp"),
            P(),
            P("dp", None, "mp"),
            P("dp", "mp"),
        ),
        check_vma=False,
    )
```

```python
import functools

import jax
import jax.numpy as jnp
import numpy as np
from jax import lax
from jax.experimental import pallas as pl
from jax.experimental.pallas import tpu as pltpu
from jax.sharding import PartitionSpec as P

MAXDIST = 128
norm_eps = 1e-06
BLK = 256
SPAN = 6 * BLK
REACH = 2
BF = jnp.bfloat16
F32 = jnp.float32
FF_VMEM = 63 << 20


def bucket_of(offsets, buckets, reach):
    half_range = buckets // 2
    upper_half = (offsets > 0).astype(np.int32) * half_range
    distance = np.abs(offsets)
    exact_range = half_range // 2
    safe_dist = np.maximum(distance, 1)
    log_bucket = exact_range + (
        np.log(safe_dist / exact_range) / np.log(reach / exact_range) * (half_range - exact_range)
    ).astype(np.int32)
    log_bucket = np.minimum(log_bucket, half_range - 1)
    return (upper_half + np.where(distance < exact_range, distance, log_bucket)).astype(np.int32)


def lane_buckets(buckets):
    lanes = np.arange(SPAN)
    shifted = np.where(lanes < 5 * BLK, lanes, lanes - SPAN)
    return bucket_of(REACH * BLK - shifted, buckets, MAXDIST).reshape(1, SPAN)


def dot(a, b, contract):
    return lax.dot_general(a, b, (contract, ((), ())), preferred_element_type=F32)


def flip(index, mask):
    out = index
    bit = 1
    while bit <= mask:
        if mask & bit:
            out = out + bit * (1 - 2 * (index // bit % 2))
        bit *= 2
    return out


GROUP_MASKS = (1, 2, 4, 12)


def group_coords(g):
    b = [g // (1 << i) % 2 for i in range(4)]
    return [b[0], b[1], (b[2] + b[3]) % 2, b[3]]


Y_FIRST = (0, 1, 2, 3)
Z_FIRST = (0, 2, 3, 1)
Z_BLOCK = 1
LEVELS = (4, 3, 3, 2)


def order_of(block):
    return Z_FIRST if block == Z_BLOCK else Y_FIRST


def levels_of(block):
    return LEVELS[block] if block < len(LEVELS) else 1


def block_position(k, order):
    b = [k >> i & 1 for i in range(4)]
    c = [b[0], b[1], b[2] ^ b[3], b[3]]
    return sum(c[order[i]] << (3 - i) for i in range(4))


def column(line):
    return jnp.broadcast_to(line, (8, line.shape[1])).T[:, 0:1]


def norm_scale(v):
    return lax.rsqrt(jnp.mean(v * v, axis=0, keepdims=True) + norm_eps)


def lanes(block):
    return pl.ds(pl.multiple_of(block * BLK, BLK), BLK)


def remote(src, dst, send, recv, who):
    return pltpu.make_async_remote_copy(
        src_ref=src,
        dst_ref=dst,
        send_sem=send,
        recv_sem=recv,
        device_id=who,
        device_id_type=pl.DeviceIdType.MESH,
    )


def meet(devices):
    barrier = pltpu.get_barrier_semaphore()
    for who in devices:
        pl.semaphore_signal(barrier, inc=1, device_id=who, device_id_type=pl.DeviceIdType.MESH)
    pl.semaphore_wait(barrier, len(devices))


def near_diagonal(offset):
    i = offset + 3
    return i + (6 - i) // 6 - i // 6 - 1


def front_kernel(
    heads, dk, buckets, blocks,
    rel_ref, len_ref, bid_ref, pad_ref, ag_ref, fg_ref, wq_ref, wo_ref,
    tok_hbm, far_hbm, cot_hbm,
    e_ref, inv_ref, qkv_ref, ctx_hbm, nrm_hbm, xt_hbm, mid_hbm, ct_hbm, wall_hbm,
    f1, fb, f3, cl, nrm, table, padc, mask, score, agc, fgc, wall, wn, call, xo,
    lsem, osem, wsend, wrecv, csend, crecv,
):
    qb = pl.program_id(0)
    dp, x = lax.axis_index("dp"), lax.axis_index("mp")
    d, rows = f1.shape
    cols = heads * dk
    half = cols // 2
    core = dp % 2
    other = (dp, 1 - x)
    sibling = (dp + 1 - 2 * core, x)
    near_blocks = blocks // 2
    part = pl.ds(core * half, half)
    far_part = pl.ds(cols + core * half, half)

    def local(i):
        src, dst = ((tok_hbm, f1), (far_hbm, fb), (cot_hbm, f3))[i]
        return pltpu.make_async_copy(src, dst, lsem.at[i])

    def out(i):
        src, dst = (
            (call, ctx_hbm), (nrm, nrm_hbm), (f1, mid_hbm), (cl, ct_hbm.at[:, pl.ds(0, rows)]), (wall, wall_hbm)
        )[i]
        return pltpu.make_async_copy(src, dst, osem.at[i])

    def xt_out(b):
        return pltpu.make_async_copy(xo.at[:, lanes(b)], xt_hbm.at[:, lanes(b)], osem.at[5 + b])

    w_copy = remote(wo_ref.at[part], wall.at[far_part], wsend.at[0], wrecv.at[0], other)
    w_pass = remote(wall.at[far_part], wall.at[far_part], wsend.at[1], wrecv.at[1], sibling)
    piece = d // 4

    def c_copy(i):
        rs = pl.ds(i * piece, piece)
        return remote(
            cl.at[rs, pl.ds(0, BLK)], ct_hbm.at[rs, pl.ds(rows, BLK)], wsend.at[2 + i], wrecv.at[2 + i], other
        )

    def ctx_copy(b):
        there = (b + near_blocks) % blocks
        return remote(
            call.at[pl.ds(0, cols), lanes(b)], call.at[pl.ds(cols, cols), lanes(there)],
            csend.at[b], crecv.at[b], other,
        )

    @pl.when(qb == 0)
    def _():
        for i in (2, 0, 1):
            local(i).start()
        meet([other, sibling])
        w_copy.start()
        wall[0:cols, :] = wo_ref[...]
        local(2).wait()
        cl[...] = f3[...].astype(BF)
        c_copy(0).start()
        c_copy(1).start()
        out(3).start()
        agc[...] = column(ag_ref[...])
        fgc[...] = column(fg_ref[...])
        local(0).wait()
        local(1).wait()
        for b in range(blocks):
            ls = slice(b * BLK, (b + 1) * BLK)
            v = f1[:, ls] if b < near_blocks else fb[:, b * BLK - rows : (b + 1) * BLK - rows].astype(F32)
            nrm[:, ls] = (v * norm_scale(v) * agc[...]).astype(BF)
            qkv_ref[:, ls] = dot(wq_ref[...], nrm[:, ls], ((1,), (0,))).astype(BF)
        out(1).start()
        for i in range(2):
            start = (1 - x) * rows if i else x * rows
            line = pad_ref[:, pl.ds(pl.multiple_of(start, BLK), rows)].astype(F32)
            padc[i * rows : (i + 1) * rows, :] = jnp.broadcast_to(line, (8, rows)).T
        ids = bid_ref[...]
        for hh in range(heads):
            line = jnp.zeros((1, SPAN), F32)
            for b in range(buckets):
                line = jnp.where(ids == b, rel_ref[b, hh], line)
            turned = pltpu.roll(
                jnp.broadcast_to(line, (BLK, SPAN)), 0, 1, stride=1, stride_axis=0
            )
            for g in range(5):
                table[hh, g] = turned[:, BLK * (4 - g) : BLK * (5 - g)]

    @pl.when(qb == 1)
    def _():
        w_copy.wait()
        w_pass.start()

    q_true = (qb + near_blocks * x) % blocks

    q_pos = q_true * BLK + lax.broadcasted_iota(jnp.int32, (1, BLK), 1)
    k_iota = lax.broadcasted_iota(jnp.int32, (BLK, BLK), 0)
    for kb in range(blocks):
        k_pos = (kb + near_blocks * x) % blocks * BLK + k_iota
        bound = 0
        q_doc = jnp.zeros((1, BLK), jnp.int32)
        k_doc = jnp.zeros((BLK, BLK), jnp.int32)
        for i in range(len_ref.shape[1]):
            bound = bound + len_ref[0, i]
            q_doc = q_doc + (q_pos >= bound).astype(jnp.int32)
            k_doc = k_doc + (k_pos >= bound).astype(jnp.int32)
        krows = slice(kb * BLK, (kb + 1) * BLK)
        seen = (padc[krows, 0:1] > 0.5) | (k_pos == q_pos)
        mask[krows, :] = jnp.where((k_doc == q_doc) & seen, 0.0, -1000000000.0)

    def head_rows(h, group):
        return pl.ds(pl.multiple_of(group * cols + h * dk, dk), dk)

    def diagonal(kb):
        return near_diagonal((kb + near_blocks * x) % blocks - q_true)

    def head(h, carry):
        qh = qkv_ref[head_rows(h, 0), lanes(qb)]
        peak = None
        for kb in range(blocks):
            krows = slice(kb * BLK, (kb + 1) * BLK)
            s = dot(qkv_ref[head_rows(h, 1), krows], qh, ((0,), (0,)))
            diag = diagonal(kb)
            s = s + table[h, diag] + mask[krows, :]
            score[krows, :] = s
            top = jnp.max(s, axis=0, keepdims=True)
            peak = top if peak is None else jnp.maximum(peak, top)
        total = jnp.zeros((1, BLK), F32)
        ctx = jnp.zeros((dk, BLK), F32)
        for kb in range(blocks):
            krows = slice(kb * BLK, (kb + 1) * BLK)
            e = jnp.exp(score[krows, :] - peak)
            total = total + jnp.sum(e, axis=0, keepdims=True)
            e_low = e.astype(BF)
            e_ref[h, 0, krows, :] = e_low
            ctx = ctx + dot(qkv_ref[head_rows(h, 2), krows], e_low, ((1,), (0,)))
        inv = 1.0 / total
        inv_ref[h, 0] = inv
        call[head_rows(h, 0), lanes(qb)] = (ctx * inv).astype(BF)
        return carry

    lax.fori_loop(0, heads, head, 0)
    ctx_copy(qb).start()

    @pl.when(qb == 1)
    def _():
        c_copy(2).start()

    @pl.when(qb == blocks - 1)
    def _():
        c_copy(3).start()
        w_pass.wait()
        wn[...] = wall[...].astype(F32).T.astype(BF)
        out(4).start()
        for i in range(blocks):
            b = (i + near_blocks) % blocks
            ctx_copy(i).wait()
            ls = slice(b * BLK, (b + 1) * BLK)
            v = dot(wn[...], call[:, ls], ((1,), (0,)))
            if b < near_blocks:
                v = v + f1[:, ls]
                f1[:, ls] = v
            else:
                v = v + fb[:, b * BLK - rows : (b + 1) * BLK - rows].astype(F32)
            xo[:, ls] = (v * norm_scale(v) * fgc[...]).astype(BF)
            xt_out(b).start()
        out(0).start()
        out(2).start()
        for i in range(4):
            c_copy(i).wait()
        for i in range(5):
            out(i).wait()
        for b in range(blocks):
            xt_out(b).wait()


def front(rel, lengths, pad, again, fgain, wq, wo, tok, far, cot, heads, dk):
    d, rows = tok.shape
    seq = 2 * rows
    cols = heads * dk
    blocks = seq // BLK
    buckets = rel.shape[0]
    bids = jnp.asarray(lane_buckets(buckets))
    one = pl.Buffered(1)
    dma = pltpu.SemaphoreType.DMA
    any_spec = pl.BlockSpec(memory_space=pl.ANY)
    smem = pl.BlockSpec(memory_space=pltpu.SMEM)

    def full(v):
        return pl.BlockSpec(v.shape, lambda i: (0, 0), pipeline_mode=one)

    return pl.pallas_call(
        functools.partial(front_kernel, heads, dk, buckets, blocks),
        grid=(blocks,),
        in_specs=[smem, smem, full(bids), full(pad), full(again), full(fgain), full(wq), full(wo)]
        + [any_spec] * 3,
        out_specs=[
            pl.BlockSpec((heads, 1, seq, BLK), lambda i: (0, i, 0, 0)),
            pl.BlockSpec((heads, 1, 1, BLK), lambda i: (0, i, 0, 0)),
            pl.BlockSpec((3 * cols, seq), lambda i: (0, 0)),
        ]
        + [any_spec] * 6,
        out_shape=[
            jax.ShapeDtypeStruct((heads, blocks, seq, BLK), BF),
            jax.ShapeDtypeStruct((heads, blocks, 1, BLK), F32),
            jax.ShapeDtypeStruct((3 * cols, seq), BF),
            jax.ShapeDtypeStruct((2 * cols, seq), BF),
            jax.ShapeDtypeStruct((d, seq), BF),
            jax.ShapeDtypeStruct((d, seq), BF),
            jax.ShapeDtypeStruct((d, rows), F32),
            jax.ShapeDtypeStruct((d, seq), BF),
            jax.ShapeDtypeStruct((2 * cols, d), BF),
        ],
        scratch_shapes=[
            pltpu.VMEM((d, rows), F32),
            pltpu.VMEM((d, rows), BF),
            pltpu.VMEM((d, rows), F32),
            pltpu.VMEM((d, rows), BF),
            pltpu.VMEM((d, seq), BF),
            pltpu.VMEM((heads, 5, BLK, BLK), F32),
            pltpu.VMEM((seq, 8), F32),
            pltpu.VMEM((seq, BLK), F32),
            pltpu.VMEM((seq, BLK), F32),
            pltpu.VMEM((d, 1), F32),
            pltpu.VMEM((d, 1), F32),
            pltpu.VMEM((2 * cols, d), BF),
            pltpu.VMEM((d, 2 * cols), BF),
            pltpu.VMEM((2 * cols, seq), BF),
            pltpu.VMEM((d, seq), BF),
            dma((3,)), dma((5 + blocks,)), dma((6,)), dma((6,)), dma((blocks,)), dma((blocks,)),
        ],
        compiler_params=pltpu.CompilerParams(
            vmem_limit_bytes=FF_VMEM, collective_id=2, has_side_effects=True
        ),
        cost_estimate=pl.CostEstimate(
            flops=16 * heads * seq * seq * dk + 10 * seq * d * cols,
            bytes_accessed=2 * heads * seq * seq + 30 * rows * d,
            transcendentals=heads * seq * seq,
        ),
    )(rel, lengths, bids, pad, again, fgain, wq, wo, tok, far, cot)


def ff_kernel(
    steps, extra,
    xt_hbm, w_hbm, ct_hbm, wo_hbm, mid_hbm, wq_hbm,
    grads_ref, din_hbm, near_hbm, far_hbm, quarter_hbm, half_hbm, hand_hbm, wfar_hbm,
    xt, ct, wg, wu, wo, hid, dg, du, din, stage, r1, r2, r3, r4, xs, xr, of,
    csem, wsem, s1, s2, s3, s4, t1, t2, t3, t4, xsem, osem, hsem,
):
    f, total = hid.shape
    rows = total // 2
    chunks = rows // BLK
    d = xt.shape[0]
    shard = d // 16
    dp, mp = lax.axis_index("dp"), lax.axis_index("mp")
    a = group_coords(dp // extra)
    peers = [flip(dp, m * extra) for m in GROUP_MASKS]
    other = (dp, 1 - mp)
    core = dp % 2
    sibling = dp + 1 - 2 * core
    bufs = (r1, r2, r3, r4)
    sends, recvs = (s1, s2, s3, s4), (t1, t2, t3, t4)
    end = steps - 1

    def weight_copy(kind, n):
        src, dst = ((w_hbm.at[0], wg), (w_hbm.at[1], wu), (wo_hbm, wo))[kind]
        return pltpu.make_async_copy(src.at[:, lanes(n)], dst.at[:, lanes(n)], wsem.at[kind, n])

    def tok_copy(n):
        src, dst, start, size = (
            (xt_hbm, xt, rows, BLK), (ct_hbm, ct, rows, BLK),
            (xt_hbm, xt, 0, rows), (ct_hbm, ct, 0, rows), (xt_hbm, xt, rows + BLK, BLK),
        )[n]
        part = pl.ds(start, size)
        return pltpu.make_async_copy(src.at[:, part], dst.at[:, part], csem.at[n])

    near_part, far_part = pl.ds(0, rows), pl.ds(rows, rows)
    c_far = remote(
        ct_hbm.at[:, pl.ds(BLK, BLK)], ct.at[:, pl.ds(rows + BLK, BLK)], csem.at[5], csem.at[6], other
    )
    x_copy = remote(xs, xr, xsem.at[0], xsem.at[1], other)
    wq_rows = wq_hbm.shape[0] // 2
    wq_part = pl.ds(core * wq_rows, wq_rows)
    w_copy = remote(wq_hbm.at[wq_part], wfar_hbm.at[wq_part], xsem.at[2], xsem.at[3], other)
    w_pass = remote(wfar_hbm.at[wq_part], wfar_hbm.at[wq_part], xsem.at[4], xsem.at[5], (sibling, mp))
    mid_copy = pltpu.make_async_copy(mid_hbm, din.at[:, far_part], osem.at[3])

    deep = len(LEVELS)

    def hop(level, n, order):
        half = 8 >> level
        c = order[level]
        away = pl.ds((1 - a[c]) * half, half)
        src = stage.at[away] if level == 0 else bufs[level - 1].at[n, away]
        return remote(src, bufs[level].at[n], sends[level].at[n], recvs[level].at[n], (peers[c], mp))

    def hand_copy(n):
        level = levels_of(n) if isinstance(n, int) else 1
        dst = (hand_hbm.at[n - deep], half_hbm, quarter_hbm.at[n - 1])[level - 1]
        return pltpu.make_async_copy(bufs[level - 1].at[n], dst, hsem.at[n])

    def absorb_first(n):
        hop(0, n, Y_FIRST).wait()
        r1[n] = stage[pl.ds(a[0] * 8, 8)] + r1[n]
        if isinstance(n, int):
            hand_copy(n).start()
            return

        @pl.when(n == Z_BLOCK)
        def _():
            hop(1, n, Z_FIRST).start()

        @pl.when((n < deep) & (n != Z_BLOCK))
        def _():
            hop(1, n, Y_FIRST).start()

        @pl.when(n >= deep)
        def _():
            hand_copy(n).start()

    def absorb(level, n):
        half = 8 >> level
        order = order_of(n)
        hop(level, n, order).wait()
        kept = bufs[level - 1][n, pl.ds(a[order[level]] * half, half)]
        if level < 3:
            bufs[level][n] = kept + bufs[level][n]
            if level + 1 < levels_of(n):
                hop(level + 1, n, order).start()
            else:
                hand_copy(n).start()
        else:
            both = kept.astype(F32) + bufs[level][n].astype(F32)
            for w in range(3):
                grads_ref[w, :, n * BLK : (n + 1) * BLK] = both[0, w]

    scale = np.float32(np.sqrt(2 / np.pi))

    def place(u):
        early, late = u // steps, (u - 4) // steps
        is_far0 = (early == 0) * 1
        is_far1 = (late == 1) * 1
        v = u - steps
        n = v - steps * (u // (2 * steps + 4))
        near_j, near_c = n // 2, n % 2
        j = is_far0 * u + is_far1 * (u - steps - 4) + (1 - is_far0 - is_far1) * near_j
        c = is_far0 * chunks + is_far1 * (chunks + 1) + (1 - is_far0 - is_far1) * near_c
        return j, c

    def substep(u):
        j, c = place(u)
        pj, pc = place(u - 1)
        pj = pj + (u == 0) * 1
        fcols, tok = lanes(j), lanes(c)
        pcols, ptok = lanes(pj), lanes(pc)
        gate = dot(wg[:, fcols], xt[:, tok], ((0,), (0,)))
        up = dot(wu[:, fcols], xt[:, tok], ((0,), (0,)))
        dh = dot(wo[:, fcols], ct[:, tok], ((0,), (0,)))
        backward(pcols, ptok)
        sq = gate * gate
        t = jnp.tanh(scale * gate * (1.0 + 0.044715 * sq))
        half = 0.5 * (1.0 + t)
        act = gate * half
        slope = half + 0.5 * gate * (1.0 - t * t) * (scale * (1.0 + (3 * 0.044715) * sq))
        hid[fcols, tok] = (act * up).astype(BF)
        dg[fcols, tok] = (dh * (up * slope)).astype(BF)
        du[fcols, tok] = (dh * act).astype(BF)

    def backward(rs, tok):
        din[:, tok] += dot(wg[:, rs], dg[rs, tok], ((1,), (0,))) + dot(wu[:, rs], du[rs, tok], ((1,), (0,)))

    per = 4 * shard

    def grads(j):
        z = (j == Z_BLOCK) * 1
        for w in range(3):
            right = (hid, dg, du)[w][lanes(j), :]
            for q in range(4):
                rs = slice(q * per, (q + 1) * per)
                left = ct[rs, :] if w == 0 else xt[rs, :]
                part = dot(left, right, ((1,), (1,)))
                for k in range(4):
                    at = block_position(4 * q + k, Y_FIRST)
                    at = at + z * (block_position(4 * q + k, Z_FIRST) - at)
                    stage[at, w, 0:shard, :] = part[k * shard : (k + 1) * shard].astype(BF)
        hop(0, j, Y_FIRST).start()

    def out_part(n):
        return dot(wo[...], hid[:, lanes(n)], ((1,), (0,)))

    meet([(p, mp) for p in peers] + [other] + ([(sibling, mp)] if extra > 1 else []))
    c_far.start()
    w_copy.start()
    tok_copy(0).start()
    tok_copy(1).start()
    for n in range(steps):
        for kind in range(3):
            weight_copy(kind, n).start()
    for n in range(2, 5):
        tok_copy(n).start()
    din[...] = jnp.zeros_like(din)
    stage[...] = jnp.zeros_like(stage)
    before = place(-1)[1]
    dg[0:BLK, before * BLK : (before + 1) * BLK] = jnp.zeros((BLK, BLK), BF)
    du[0:BLK, before * BLK : (before + 1) * BLK] = jnp.zeros((BLK, BLK), BF)
    tok_copy(0).wait()
    tok_copy(1).wait()
    count = 2 * chunks * steps
    far_end = 2 * steps + 4

    def step(u, carry):
        @pl.when(u < steps)
        def _():
            for kind in range(3):
                weight_copy(kind, u).wait()

        @pl.when(u == steps)
        def _():
            tok_copy(2).wait()
            tok_copy(3).wait()

        @pl.when(u == steps + 4)
        def _():
            tok_copy(4).wait()
            c_far.wait()

        @pl.when(u < count)
        def _():
            substep(u)

        @pl.when(u == far_end)
        def _():
            xs[...] = din[:, far_part].astype(BF)
            x_copy.start()
            mid_copy.start()

        odd = u % 2 == 1
        late = (u >= 2 * steps + 5) * 1
        m = (u - 13) // 2 - 2 * ((u >= 2 * steps + 7) * 1)
        n = (u - 11) // 2 - 2 * late

        @pl.when(odd & ((u == 13) | (u == 15) | (u >= 2 * steps + 7)))
        def _():
            absorb_first(m)

        for at, events in (
            (21, ((1, 0),)), (23, ((1, 1),)), (25, ((2, 0),)), (27, ((1, 2), (2, 1))),
        ):
            @pl.when(u == at)
            def _():
                for level, block in events:
                    absorb(level, block)

        @pl.when(odd & ((u == 11) | (u == 13) | (u >= 2 * steps + 5)))
        def _():
            grads(n)

        @pl.when(u == far_end + 5)
        def _():
            w_copy.wait()
            w_pass.start()

        return carry

    lax.fori_loop(0, count, step, 0)
    pj, pc = place(count - 1)
    backward(lanes(pj), lanes(pc))

    def far_out(n, carry):
        of[:, lanes(n)] = out_part(n + chunks).astype(BF)
        return carry

    lax.fori_loop(0, chunks, far_out, 0)
    far_copy = pltpu.make_async_copy(of, far_hbm, osem.at[0])
    far_copy.start()
    x_copy.wait()
    din[:, near_part] += xr[...].astype(F32)
    din_copy = pltpu.make_async_copy(din.at[:, near_part], din_hbm, osem.at[2])
    din_copy.start()
    mid_copy.wait()

    def near_out(n, carry):
        at = lanes(n + chunks)
        din[:, at] = din[:, at] + out_part(n)
        return carry

    lax.fori_loop(0, chunks, near_out, 0)
    near_copy = pltpu.make_async_copy(din.at[:, far_part], near_hbm, osem.at[1])
    near_copy.start()
    absorb_first(end)
    absorb(3, 0)
    absorb(2, 2)
    absorb(1, 3)
    w_pass.wait()
    for n in range(1, steps):
        hand_copy(n).wait()
    far_copy.wait()
    near_copy.wait()
    din_copy.wait()


def ff_all(xt, ct, w2, wo, mid, wq, extra):
    d, total = xt.shape
    f = wo.shape[1]
    rows = total // 2
    steps = f // BLK
    deep = len(LEVELS)
    shard = d // 16
    spad = -(-shard // 16) * 16
    dma = pltpu.SemaphoreType.DMA
    any_spec = pl.BlockSpec(memory_space=pl.ANY)
    return pl.pallas_call(
        functools.partial(ff_kernel, steps, extra),
        in_specs=[any_spec] * 6,
        out_specs=[pl.BlockSpec(memory_space=pltpu.VMEM)] + [any_spec] * 7,
        out_shape=[
            jax.ShapeDtypeStruct((3, spad, BLK), F32),
            jax.ShapeDtypeStruct((d, rows), F32),
            jax.ShapeDtypeStruct((d, rows), F32),
            jax.ShapeDtypeStruct((d, rows), BF),
            jax.ShapeDtypeStruct((2, 2, 3, spad, BLK), BF),
            jax.ShapeDtypeStruct((4, 3, spad, BLK), BF),
            jax.ShapeDtypeStruct((steps - deep, 8, 3, spad, BLK), BF),
            jax.ShapeDtypeStruct(wq.shape, BF),
        ],
        scratch_shapes=[
            pltpu.VMEM((d, total), BF),
            pltpu.VMEM((d, total), BF),
            pltpu.VMEM((d, f), BF),
            pltpu.VMEM((d, f), BF),
            pltpu.VMEM((d, f), BF),
            pltpu.VMEM((f, total), BF),
            pltpu.VMEM((f, total), BF),
            pltpu.VMEM((f, total), BF),
            pltpu.VMEM((d, total), F32),
            pltpu.VMEM((16, 3, spad, BLK), BF),
            pltpu.VMEM((steps, 8, 3, spad, BLK), BF),
            pltpu.VMEM((4, 4, 3, spad, BLK), BF),
            pltpu.VMEM((3, 2, 3, spad, BLK), BF),
            pltpu.VMEM((1, 1, 3, spad, BLK), BF),
            pltpu.VMEM((d, rows), BF),
            pltpu.VMEM((d, rows), BF),
            pltpu.VMEM((d, rows), BF),
            dma((7,)),
            dma((3, steps)),
            dma((steps,)), dma((4,)), dma((3,)), dma((1,)),
            dma((steps,)), dma((4,)), dma((3,)), dma((1,)),
            dma((6,)),
            dma((4,)),
            dma((steps,)),
        ],
        compiler_params=pltpu.CompilerParams(
            vmem_limit_bytes=FF_VMEM, collective_id=0, has_side_effects=True
        ),
        cost_estimate=pl.CostEstimate(
            flops=18 * total * d * f,
            bytes_accessed=6 * d * f + 16 * total * d,
            transcendentals=total * f,
        ),
    )(xt, w2, ct, wo, mid, wq)


def tail_kernel(
    heads, dk, buckets, blocks, extra,
    bid_ref, qkv_ref, e_ref, inv_ref, wall_ref, ctx_ref, ag_ref, fg_ref, early_ref,
    din_hbm, mid_hbm, cot_hbm, tok_hbm, nrm_hbm, wq_hbm, wfar_hbm, far_hbm,
    quarter_hbm, half_hbm, hand_hbm,
    ig_hbm, back_hbm, gq_ref, go_ref, small_ref, ffo_ref, ffi_ref,
    f1, f2, f3, nrm, wq, wn, wf, alow, dctx, dcs, osend, orecv, fsum, agc, fgc,
    dp_s, dkv, tally, dproj, dfar, grad,
    sa, sb_, a1, a2, a3, a4, b1, b2, b3, b4, hk, hm, hq, h2, h3, h4, sv, rv,
    lsem, ksem, xs_sem, xr_sem, cs_sem, cr_sem, bs_sem, br_sem, hs_sem, hr_sem,
):
    qb = pl.program_id(0)
    dp, x = lax.axis_index("dp"), lax.axis_index("mp")
    d, rows = f2.shape
    cols = heads * dk
    shard = d // 16
    a = group_coords(dp // extra)
    peers = [flip(dp, m * extra) for m in GROUP_MASKS]
    other = (dp, 1 - x)
    near_blocks = blocks // 2
    near_part, far_part = pl.ds(0, rows), pl.ds(rows, rows)
    halves = ((sa, a1, a2, a3, a4), (sb_, b1, b2, b3, b4))
    orders = (Y_FIRST, Z_FIRST)
    copies = (
        (din_hbm, f1), (mid_hbm, f2), (cot_hbm, f3), (tok_hbm, f2), (nrm_hbm, nrm), (wq_hbm, wq), (wfar_hbm, wq),
    )

    def local(i):
        return pltpu.make_async_copy(copies[i][0], copies[i][1], lsem.at[i])

    def x_copy(i, src, dst):
        return remote(src, dst, xs_sem.at[i], xr_sem.at[i], other)

    dctx_copy = x_copy(0, dcs, dctx.at[:, far_part])
    o_copy = x_copy(1, osend, orecv)
    dproj_copy = x_copy(2, dproj.at[:, far_part], dfar)

    def back_copy(i):
        part = pl.ds(i * 128, 128)
        return x_copy(3 + i, far_hbm.at[:, part], back_hbm.at[:, part])

    def hop(side, level):
        half = 8 >> level
        c = orders[side][level]
        away = pl.ds((1 - a[c]) * half, half)
        bufs = halves[side]
        return remote(
            bufs[level].at[away], bufs[level + 1], cs_sem.at[side, level], cr_sem.at[side, level], (peers[c], x)
        )

    def absorb(side, level):
        half = 8 >> level
        bufs = halves[side]
        hop(side, level).wait()
        kept = bufs[level][pl.ds(a[orders[side][level]] * half, half)]
        if level < 3:
            bufs[level + 1][...] = kept + bufs[level + 1][...]
            hop(side, level + 1).start()
            return
        both = (kept.astype(F32) + bufs[level + 1][...].astype(F32))[0, 0:shard]
        outs = (gq_ref.at[0], gq_ref.at[1]) if side == 0 else (gq_ref.at[2], go_ref)
        for i in range(2):
            outs[i][...] = both[:, i * cols : (i + 1) * cols]

    deep = len(LEVELS)
    handed = (1, 2, 3, 4, 5, 6)

    def keep_copy(block):
        level = levels_of(block)
        half = 8 >> level
        keep = pl.ds(a[order_of(block)[level]] * half, half)
        if level == 3:
            src, dst = quarter_hbm.at[block - 1, keep], hq.at[block - 1]
        elif level == 2:
            src, dst = half_hbm.at[keep], hm
        else:
            src, dst = hand_hbm.at[block - deep, keep], hk.at[block - deep]
        return pltpu.make_async_copy(src, dst, ksem.at[block])

    def hand_hop(level, block):
        half = 8 >> level
        c = order_of(block)[level]
        away = pl.ds((1 - a[c]) * half, half)
        fresh = level == levels_of(block)
        if level == 1:
            src, dst = hand_hbm.at[block - deep, away], h2.at[block - deep]
        elif level == 2:
            src, dst = half_hbm.at[away] if fresh else h2.at[block - deep, away], h3.at[block - 3]
        else:
            src, dst = quarter_hbm.at[block - 1, away] if fresh else h3.at[block - 3, away], h4.at[block - 1]
        return remote(src, dst, hs_sem.at[level, block], hr_sem.at[level, block], (peers[c], x))

    def put_grads(w, block, value):
        at = slice(block * BLK, (block + 1) * BLK)
        if w == 0:
            ffo_ref[:, at] = value
        else:
            ffi_ref[:, w - 1, at] = value

    def hand_absorb(level, block):
        half = 8 >> level
        keep = pl.ds(a[order_of(block)[level]] * half, half)
        hand_hop(level, block).wait()
        if level == levels_of(block):
            keep_copy(block).wait()
            kept = hk[block - deep] if level == 1 else (hm[...] if level == 2 else hq[block - 1])
        else:
            kept = h2[block - deep, keep] if level == 2 else h3[block - 3, keep]
        if level == 1:
            h2[block - deep] = kept + h2[block - deep]
        elif level == 2:
            h3[block - 3] = kept + h3[block - 3]
        else:
            both = kept.astype(F32) + h4[block - 1].astype(F32)
            for w in range(3):
                put_grads(w, block, both[0, w, 0:shard])
        if level < 3:
            hand_hop(level + 1, block).start()

    def round_copy(i):
        who = other if i == 4 else (peers[(0, 2, 3, 1)[i]], x)
        return remote(sv.at[i], rv.at[i], bs_sem.at[i], br_sem.at[i], who)

    def round_end(i):
        round_copy(i).wait()
        sv[i + 1] = sv[i] + rv[i]
        if i < 4:
            round_copy(i + 1).start()

    def out_copy(r):
        return pltpu.make_async_copy(f3.at[:, lanes(r)], ig_hbm.at[:, lanes(r)], lsem.at[len(copies) + r])

    def lane_sum(v):
        total = v[:, 0:128]
        for i in range(1, v.shape[1] // 128):
            total = total + v[:, i * 128 : (i + 1) * 128]
        return total

    @pl.when(qb == 0)
    def _():
        for i in range(3):
            local(i).start()
        meet([(p, x) for p in peers] + [other])
        back_copy(0).start()
        for block in handed:
            hand_hop(levels_of(block), block).start()
        agc[...] = column(ag_ref[...])
        fgc[...] = column(fg_ref[...])
        dkv[...] = jnp.zeros_like(dkv)
        tally[...] = jnp.zeros_like(tally)
        sa[...] = jnp.zeros_like(sa)
        sb_[...] = jnp.zeros_like(sb_)
        fsum[...] = jnp.zeros_like(fsum)
        for i in range(3):
            local(i).wait()

        def norm_rows(r, carry):
            ls = lanes(r)
            v = f2[:, ls]
            c = f1[:, ls]
            scale = norm_scale(v)
            n = v * scale
            cg = c * fgc[...]
            m = jnp.mean(cg * n, axis=0, keepdims=True)
            gm = f3[:, ls] + scale * (cg - n * m)
            fsum[...] += lane_sum(c * n)
            f1[:, ls] = gm
            alow[:, ls] = gm.astype(BF)
            return carry

        lax.fori_loop(0, near_blocks, norm_rows, 0)
        dcs[...] = dot(wall_ref[cols : 2 * cols, :], alow[...], ((1,), (0,))).astype(BF)
        dctx_copy.start()
        for i in (3, 4, 5):
            local(i).start()
        for block in handed:
            keep_copy(block).start()
        dctx[:, near_part] = dot(wall_ref[0:cols, :], alow[...], ((1,), (0,))).astype(BF)
        osend[...] = dot(alow[...], ctx_ref[cols : 2 * cols, near_part], ((1,), (1,))).astype(BF)
        o_copy.start()
        grad[:, 3 * cols : 4 * cols] = dot(alow[...], ctx_ref[0:cols, near_part], ((1,), (1,)))
        for w in range(3):
            put_grads(w, 0, early_ref[w, 0:shard, :])
        dctx_copy.wait()
        back_copy(1).start()

    @pl.when(qb == 1)
    def _():
        local(5).wait()
        wn[...] = wq[...].astype(F32).T.astype(BF)
        local(6).start()
        hand_absorb(2, 3)
        hand_absorb(3, 1)
        hand_absorb(3, 2)
        hand_absorb(1, 4)

    @pl.when(qb == 2)
    def _():
        local(6).wait()
        wf[...] = wq[...].astype(F32).T.astype(BF)

    @pl.when(qb == 3)
    def _():
        hand_absorb(3, 3)
        hand_absorb(2, 4)

    q_true = (qb + near_blocks * x) % blocks

    def head(h, carry):
        def head_rows(group):
            return pl.ds(pl.multiple_of(group * cols + h * dk, dk), dk)

        inv = inv_ref[h, 0]
        qh = qkv_ref[head_rows(0), lanes(qb)]
        scaled = (dctx[head_rows(0), lanes(qb)].astype(F32) * inv).astype(BF)
        inner = jnp.zeros((1, BLK), F32)
        for kb in range(blocks):
            krows = slice(kb * BLK, (kb + 1) * BLK)
            g = dot(qkv_ref[head_rows(2), krows], scaled, ((0,), (0,)))
            dp_s[krows, :] = g
            inner = inner + jnp.sum(e_ref[h, 0, krows, :].astype(F32) * g, axis=0, keepdims=True)
        inner = inner * inv
        dq = jnp.zeros((dk, BLK), F32)
        for kb in range(blocks):
            krows = slice(kb * BLK, (kb + 1) * BLK)
            e = e_ref[h, 0, krows, :]
            ds = (e.astype(F32) * (dp_s[krows, :] - inner)).astype(BF)
            dkv[head_rows(0), krows] += dot(qh, ds, ((1,), (1,)))
            dkv[head_rows(1), krows] += dot(scaled, e, ((1,), (1,)))
            dq = dq + dot(qkv_ref[head_rows(1), krows], ds, ((1,), (0,)))
            tally[h, near_diagonal((kb + near_blocks * x) % blocks - q_true)] += ds.astype(F32)
        dproj[head_rows(0), lanes(qb)] = dq.astype(BF)
        return carry

    lax.fori_loop(0, heads, head, 0)

    @pl.when(qb == blocks - 1)
    def _():
        dproj[cols : 3 * cols, :] = dkv[...].astype(BF)
        dproj_copy.start()
        back_copy(2).start()
        back_copy(3).start()
        hand_absorb(1, 5)
        local(3).wait()
        local(4).wait()
        per = 4 * shard

        def grad_rows(q, carry):
            rs = pl.ds(pl.multiple_of(q * per, 16), per)
            grad[rs, 0 : 3 * cols] = dot(nrm[rs, :], dproj[...], ((1,), (1,)))
            return carry

        lax.fori_loop(0, 4, grad_rows, 0)
        o_copy.wait()
        grad[:, 3 * cols : 4 * cols] += orecv[...].astype(F32)
        for side in range(2):
            for k in range(16):
                halves[side][0][block_position(k, orders[side]), 0:shard, :] = grad[
                    k * shard : (k + 1) * shard, 2 * side * cols : 2 * (side + 1) * cols
                ].astype(BF)
            hop(side, 0).start()

        def near_rows(r, carry):
            f3[:, lanes(r)] = dot(wn[...], dproj[:, lanes(r)], ((1,), (0,)))
            return carry

        lax.fori_loop(0, near_blocks, near_rows, 0)
        absorb(0, 0)
        absorb(1, 0)
        ids = bid_ref[...]
        hot = ids == lax.broadcasted_iota(jnp.int32, (buckets, SPAN), 0)
        out_lane = lax.broadcasted_iota(jnp.int32, (buckets, 128), 1)
        sub = lax.broadcasted_iota(jnp.int32, (8, SPAN), 0)
        sv[0] = jnp.zeros(sv.shape[1:], F32)

        def bias_sums(hh, carry):
            line = jnp.zeros((8, SPAN), F32)
            for g in range(BLK // 8):
                group = slice(8 * g, 8 * g + 8)
                parts = [tally[hh, i, group, :] for i in (4, 3, 2, 1, 0)]
                strip = jnp.concatenate(parts + [jnp.zeros((8, BLK), F32)], axis=1)
                line = line + (strip if g == 0 else pltpu.roll(strip, SPAN - 8 * g, 1))
            for bit in (1, 2, 4):
                line = jnp.where((sub // bit) % 2 == 1, pltpu.roll(line, SPAN - bit, 1), line)
            sums = jnp.sum(line, axis=0, keepdims=True)
            col = jnp.sum(jnp.where(hot, sums, 0.0), axis=1, keepdims=True)
            sv[0, 0:buckets, :] = jnp.where(out_lane == x * heads + hh, col, sv[0, 0:buckets, :])
            return carry

        lax.fori_loop(0, heads, bias_sums, 0)
        product = wn[...].astype(F32) * grad[:, 0 : 3 * cols]
        again = lane_sum(product[:, 0:512]).T
        rest = product[:, 512 : 3 * cols]
        again = jnp.sum(again, axis=0, keepdims=True) + jnp.sum(rest.T, axis=0, keepdims=True)
        again = again / ag_ref[...]
        fgain = jnp.sum(fsum[...].T, axis=0, keepdims=True)
        lines = -(-d // 128)
        for i in range(lines):
            n = min(128, d - 128 * i)
            sv[0, buckets + i : buckets + i + 1, 0:n] = again[:, 128 * i : 128 * i + n]
            sv[0, buckets + lines + i : buckets + lines + i + 1, 0:n] = fgain[:, 128 * i : 128 * i + n]
        round_copy(0).start()
        hand_absorb(3, 4)
        hand_absorb(2, 5)
        hand_absorb(1, 6)
        round_end(0)
        absorb(1, 1)
        dproj_copy.wait()

        def last_norm(r, carry):
            ls = lanes(r)
            c = f3[:, ls] + dot(wf[...], dfar[:, ls], ((1,), (0,)))
            v = f2[:, ls]
            scale = norm_scale(v)
            n = v * scale
            cg = c * agc[...]
            m = jnp.mean(cg * n, axis=0, keepdims=True)
            f3[:, ls] = f1[:, ls] + scale * (cg - n * m)
            out_copy(r).start()
            return carry

        lax.fori_loop(0, near_blocks, last_norm, 0)
        absorb(0, 1)
        hand_absorb(3, 5)
        round_end(1)
        hand_absorb(2, 6)
        absorb(1, 2)
        round_end(2)
        absorb(0, 2)
        hand_absorb(3, 6)
        absorb(1, 3)
        round_end(3)
        absorb(0, 3)
        round_end(4)
        small_ref[...] = sv[5]
        for i in range(4):
            back_copy(i).wait()
        for r in range(near_blocks):
            out_copy(r).wait()


def tail(qkv, e, inv, wall, ctx, again, fgain, early, din, mid, cot, tok, nrm, wq, wfar, far,
         quarter, half_way, hand, buckets, heads, dk, extra, f):
    d, rows = tok.shape
    seq = 2 * rows
    cols = heads * dk
    blocks = seq // BLK
    near = blocks // 2
    shard = d // 16
    spad = -(-shard // 16) * 16
    deep = hand.shape[0]
    later = deep + len(LEVELS)
    lines = -(-(buckets + 2 * -(-d // 128)) // 8) * 8
    bids = jnp.asarray(lane_buckets(buckets))
    one = pl.Buffered(1)
    dma = pltpu.SemaphoreType.DMA
    any_spec = pl.BlockSpec(memory_space=pl.ANY)

    def full(v):
        return pl.BlockSpec(v.shape, lambda i: (0,) * len(v.shape), pipeline_mode=one)

    def chain(width):
        return [pltpu.VMEM((n, spad, width), BF) for n in (16, 8, 4, 2, 1)]

    outs = [
        jax.ShapeDtypeStruct((3, shard, cols), F32),
        jax.ShapeDtypeStruct((shard, cols), F32),
        jax.ShapeDtypeStruct((lines, 128), F32),
        jax.ShapeDtypeStruct((shard, f), F32),
        jax.ShapeDtypeStruct((shard, 2, f), F32),
    ]
    a_chain, b_chain = chain(2 * cols), chain(2 * cols)
    return pl.pallas_call(
        functools.partial(tail_kernel, heads, dk, buckets, blocks, extra),
        grid=(blocks,),
        in_specs=[
            full(bids),
            full(qkv),
            pl.BlockSpec((heads, 1, seq, BLK), lambda i: (0, i, 0, 0)),
            pl.BlockSpec((heads, 1, 1, BLK), lambda i: (0, i, 0, 0)),
            full(wall),
            full(ctx),
            full(again),
            full(fgain),
            full(early),
        ]
        + [any_spec] * 11,
        out_specs=[any_spec, any_spec] + [full(v) for v in outs],
        out_shape=[jax.ShapeDtypeStruct((d, rows), F32), jax.ShapeDtypeStruct((d, rows), BF)] + outs,
        scratch_shapes=[
            pltpu.VMEM((d, rows), F32),
            pltpu.VMEM((d, rows), F32),
            pltpu.VMEM((d, rows), F32),
            pltpu.VMEM((d, seq), BF),
            pltpu.VMEM((3 * cols, d), BF),
            pltpu.VMEM((d, 3 * cols), BF),
            pltpu.VMEM((d, 3 * cols), BF),
            pltpu.VMEM((d, rows), BF),
            pltpu.VMEM((cols, seq), BF),
            pltpu.VMEM((cols, rows), BF),
            pltpu.VMEM((d, cols), BF),
            pltpu.VMEM((d, cols), BF),
            pltpu.VMEM((d, 128), F32),
            pltpu.VMEM((d, 1), F32),
            pltpu.VMEM((d, 1), F32),
            pltpu.VMEM((seq, BLK), F32),
            pltpu.VMEM((2 * cols, seq), F32),
            pltpu.VMEM((heads, 5, BLK, BLK), F32),
            pltpu.VMEM((3 * cols, seq), BF),
            pltpu.VMEM((3 * cols, rows), BF),
            pltpu.VMEM((d, 4 * cols), F32),
            a_chain[0],
            b_chain[0],
        ]
        + a_chain[1:]
        + b_chain[1:]
        + [
            pltpu.VMEM((deep, 4, 3, spad, BLK), BF),
            pltpu.VMEM((2, 3, spad, BLK), BF),
            pltpu.VMEM((2, 1, 3, spad, BLK), BF),
            pltpu.VMEM((deep, 4, 3, spad, BLK), BF),
            pltpu.VMEM((deep + 1, 2, 3, spad, BLK), BF),
            pltpu.VMEM((later - 1, 1, 3, spad, BLK), BF),
            pltpu.VMEM((6, lines, 128), F32),
            pltpu.VMEM((5, lines, 128), F32),
            dma((7 + near,)),
            dma((later,)),
            dma((7,)), dma((7,)),
            dma((2, 4)), dma((2, 4)),
            dma((5,)), dma((5,)),
            dma((4, later)), dma((4, later)),
        ],
        compiler_params=pltpu.CompilerParams(
            vmem_limit_bytes=FF_VMEM, collective_id=1, has_side_effects=True
        ),
        cost_estimate=pl.CostEstimate(
            flops=32 * heads * seq * seq * dk + 8 * seq * d * 3 * cols,
            bytes_accessed=2 * heads * seq * seq + 30 * rows * d,
            transcendentals=0,
        ),
    )(bids, qkv, e, inv, wall, ctx, again, fgain, early, din, mid, cot, tok, nrm, wq, wfar, far,
      quarter, half_way, hand)


def outputs_kernel(near_ref, back_ref, ig_ref, ffi_ref, *refs):
    n = (len(refs) - 3) // 2
    sources, res_ref, ig_out, ffi_out, targets = refs[:n], refs[n], refs[n + 1], refs[n + 2], refs[n + 3 :]
    res_ref[...] = near_ref[...] + back_ref[...].astype(F32)
    ig_out[...] = ig_ref[...]
    ffi_out[...] = ffi_ref[...]

    @pl.when(pl.program_id(0) == 0)
    def _():
        for i in range(n):
            targets[i][...] = sources[i][...]


def outputs(near, back, ig, ffi, *grads):
    d, rows = near.shape
    block = pl.BlockSpec((d // 4, rows), lambda i: (i, 0))
    shard, two, f = ffi.shape
    part = pl.BlockSpec((shard // 4, two, f), lambda i: (i, 0, 0))
    one = pl.Buffered(1)
    whole = [pl.BlockSpec(v.shape, lambda i, n=v.ndim: (0,) * n, pipeline_mode=one) for v in grads]
    return pl.pallas_call(
        outputs_kernel,
        grid=(4,),
        in_specs=[block] * 3 + [part] + whole,
        out_specs=[block] * 2 + [part] + whole,
        out_shape=[jax.ShapeDtypeStruct(v.shape, F32) for v in (near, ig, ffi) + grads],
        compiler_params=pltpu.CompilerParams(vmem_limit_bytes=40 << 20),
    )(near, back, ig, ffi, *grads)


def take(array, index):
    return lax.dynamic_index_in_dim(array, index, 0, keepdims=False)


def per_device(
    tokens,
    cotangent,
    doc_lengths,
    pad_mask,
    attn_gain,
    qkv_weight,
    rel_table,
    out_weight,
    ff_gain,
    ff_in_weight,
    ff_out_weight,
):
    rows, d = tokens.shape
    n_dp = lax.axis_size("dp")
    n_mp = lax.axis_size("mp")
    cols = qkv_weight.shape[2]
    buckets, heads = rel_table.shape
    dk = cols // heads
    me = lax.axis_index("dp")
    shard = d // n_dp
    extra = n_dp // 16

    def hop(v, mask):
        return lax.ppermute(v, "dp", [(i, i ^ mask) for i in range(n_dp)])

    def bit(b):
        return (me >> b) & 1

    def finish(g):
        parts = [g.reshape((extra, shard) + g.shape[1:])]
        for b in reversed(range(extra.bit_length() - 1)):
            halves = [p.reshape((2, p.shape[0] // 2) + p.shape[1:]) for p in parts]
            away = sum(take(p, 1 - bit(b)).astype(F32) for p in halves).astype(BF)
            parts = [take(p, bit(b)) for p in halves] + [hop(away, 1 << b)]
        return sum(p.astype(F32) for p in parts)[0]

    tok = tokens.T
    cot = cotangent.T
    far = lax.ppermute(tok.astype(BF), "mp", [(0, 1), (1, 0)])
    w2 = jnp.transpose(ff_in_weight, (1, 0, 2))
    wq = jnp.transpose(qkv_weight, (1, 2, 0)).reshape(3 * cols, d)
    again, fgain = attn_gain.reshape(1, d), ff_gain.reshape(1, d)

    e, inv, qkv, ctx, nrm, xt, mid, ct, wall = front(
        rel_table, doc_lengths, pad_mask, again, fgain, wq, out_weight.T, tok, far, cot, heads, dk
    )
    early, din, near_out, far_out, quarter, half_way, hand, wfar = ff_all(
        xt, ct, w2, ff_out_weight, mid, wq, extra
    )
    input_grad, back, grad_qkv, grad_out, small, ffo, ffi = tail(
        qkv, e, inv, wall, ctx, again, fgain, early, din, mid, cot, tok, nrm, wq, wfar, far_out,
        quarter, half_way, hand, buckets, heads, dk, extra, ff_out_weight.shape[1],
    )
    result, input_grad, ffi, grad_qkv, grad_out, ffo = outputs(
        near_out, back, input_grad, ffi, grad_qkv, grad_out, ffo
    )
    grad_qkv = jnp.transpose(grad_qkv, (1, 0, 2))
    if extra > 1:
        grad_qkv, grad_out, ffo, ffi = (finish(g) for g in (grad_qkv, grad_out, ffo, ffi))
    for b in range(extra.bit_length() - 1):
        small = small + hop(small, 1 << b)
    lines = -(-d // 128)
    return (
        result.T,
        input_grad.T,
        small[buckets : buckets + lines].reshape(-1)[:d],
        grad_qkv,
        small[:buckets, : heads * n_mp],
        grad_out,
        small[buckets + lines : buckets + 2 * lines].reshape(-1)[:d],
        ffi,
        ffo,
    )


def solution(mesh):
    return jax.shard_map(
        per_device,
        mesh=mesh,
        in_specs=(
            P(("dp", "mp"), None),
            P(("dp", "mp"), None),
            P("dp", None),
            P("dp", None),
            P(),
            P(None, None, "mp"),
            P(None, "mp"),
            P(None, "mp"),
            P(),
            P(None, None, "mp"),
            P(None, "mp"),
        ),
        out_specs=(
            P(("dp", "mp"), None),
            P(("dp", "mp"), None),
            P(),
            P("dp", None, "mp"),
            P(),
            P("dp", "mp"),
            P(),
            P("dp", None, "mp"),
            P("dp", "mp"),
        ),
        check_vma=False,
    )
```

```python
import functools

import jax
import jax.numpy as jnp
import numpy as np
from jax import lax
from jax.experimental import pallas as pl
from jax.experimental.pallas import tpu as pltpu
from jax.sharding import PartitionSpec as P

MAXDIST = 128
norm_eps = 1e-06
BLK = 256
SPAN = 6 * BLK
REACH = 2
BF = jnp.bfloat16
F32 = jnp.float32
FF_VMEM = 63 << 20


def bucket_of(offsets, buckets, reach):
    half_range = buckets // 2
    upper_half = (offsets > 0).astype(np.int32) * half_range
    distance = np.abs(offsets)
    exact_range = half_range // 2
    safe_dist = np.maximum(distance, 1)
    log_bucket = exact_range + (
        np.log(safe_dist / exact_range) / np.log(reach / exact_range) * (half_range - exact_range)
    ).astype(np.int32)
    log_bucket = np.minimum(log_bucket, half_range - 1)
    return (upper_half + np.where(distance < exact_range, distance, log_bucket)).astype(np.int32)


def lane_buckets(buckets):
    lanes = np.arange(SPAN)
    shifted = np.where(lanes < 5 * BLK, lanes, lanes - SPAN)
    return bucket_of(REACH * BLK - shifted, buckets, MAXDIST).reshape(1, SPAN)


def dot(a, b, contract):
    return lax.dot_general(a, b, (contract, ((), ())), preferred_element_type=F32)


def flip(index, mask):
    out = index
    bit = 1
    while bit <= mask:
        if mask & bit:
            out = out + bit * (1 - 2 * (index // bit % 2))
        bit *= 2
    return out


GROUP_MASKS = (1, 2, 4, 12)


def group_coords(g):
    b = [g // (1 << i) % 2 for i in range(4)]
    return [b[0], b[1], (b[2] + b[3]) % 2, b[3]]


Y_FIRST = (0, 1, 2, 3)
Z_FIRST = (0, 2, 3, 1)
Z_BLOCK = 1
LEVELS = (4, 3, 3, 2)


def order_of(block):
    return Z_FIRST if block == Z_BLOCK else Y_FIRST


def levels_of(block):
    return LEVELS[block] if block < len(LEVELS) else 1


def block_position(k, order):
    b = [k >> i & 1 for i in range(4)]
    c = [b[0], b[1], b[2] ^ b[3], b[3]]
    return sum(c[order[i]] << (3 - i) for i in range(4))


def column(line):
    return jnp.broadcast_to(line, (8, line.shape[1])).T[:, 0:1]


def norm_scale(v):
    return lax.rsqrt(jnp.mean(v * v, axis=0, keepdims=True) + norm_eps)


def lanes(block):
    return pl.ds(pl.multiple_of(block * BLK, BLK), BLK)


def remote(src, dst, send, recv, who):
    return pltpu.make_async_remote_copy(
        src_ref=src,
        dst_ref=dst,
        send_sem=send,
        recv_sem=recv,
        device_id=who,
        device_id_type=pl.DeviceIdType.MESH,
    )


def meet(devices):
    barrier = pltpu.get_barrier_semaphore()
    for who in devices:
        pl.semaphore_signal(barrier, inc=1, device_id=who, device_id_type=pl.DeviceIdType.MESH)
    pl.semaphore_wait(barrier, len(devices))


def near_diagonal(offset):
    i = offset + 3
    return i + (6 - i) // 6 - i // 6 - 1


def front_kernel(
    heads, dk, buckets, blocks,
    rel_ref, len_ref, bid_ref, pad_ref, ag_ref, fg_ref, wq_ref, wo_ref,
    tok_hbm, far_hbm, cot_hbm,
    e_ref, inv_ref, qkv_ref, ctx_hbm, nrm_hbm, xt_hbm, mid_hbm, ct_hbm, wall_hbm,
    f1, fb, f3, cl, nrm, table, padc, mask, score, agc, fgc, wall, wn, call, xo,
    lsem, osem, wsend, wrecv, csend, crecv,
):
    qb = pl.program_id(0)
    dp, x = lax.axis_index("dp"), lax.axis_index("mp")
    d, rows = f1.shape
    cols = heads * dk
    half = cols // 2
    core = dp % 2
    other = (dp, 1 - x)
    sibling = (dp + 1 - 2 * core, x)
    near_blocks = blocks // 2
    part = pl.ds(core * half, half)
    far_part = pl.ds(cols + core * half, half)

    def local(i):
        src, dst = ((tok_hbm, f1), (far_hbm, fb), (cot_hbm, f3))[i]
        return pltpu.make_async_copy(src, dst, lsem.at[i])

    def out(i):
        src, dst = (
            (call, ctx_hbm), (nrm, nrm_hbm), (f1, mid_hbm), (cl, ct_hbm.at[:, pl.ds(0, rows)]), (wall, wall_hbm)
        )[i]
        return pltpu.make_async_copy(src, dst, osem.at[i])

    def xt_out(b):
        return pltpu.make_async_copy(xo.at[:, lanes(b)], xt_hbm.at[:, lanes(b)], osem.at[5 + b])

    w_copy = remote(wo_ref.at[part], wall.at[far_part], wsend.at[0], wrecv.at[0], other)
    w_pass = remote(wall.at[far_part], wall.at[far_part], wsend.at[1], wrecv.at[1], sibling)
    piece = d // 4

    def c_copy(i):
        rs = pl.ds(i * piece, piece)
        return remote(
            cl.at[rs, pl.ds(0, BLK)], ct_hbm.at[rs, pl.ds(rows, BLK)], wsend.at[2 + i], wrecv.at[2 + i], other
        )

    def ctx_copy(b):
        there = (b + near_blocks) % blocks
        return remote(
            call.at[pl.ds(0, cols), lanes(b)], call.at[pl.ds(cols, cols), lanes(there)],
            csend.at[b], crecv.at[b], other,
        )

    @pl.when(qb == 0)
    def _():
        for i in (2, 0, 1):
            local(i).start()
        meet([other, sibling])
        w_copy.start()
        wall[0:cols, :] = wo_ref[...]
        local(2).wait()
        cl[...] = f3[...].astype(BF)
        c_copy(0).start()
        c_copy(1).start()
        out(3).start()
        agc[...] = column(ag_ref[...])
        fgc[...] = column(fg_ref[...])
        local(0).wait()
        local(1).wait()
        for b in range(blocks):
            ls = slice(b * BLK, (b + 1) * BLK)
            v = f1[:, ls] if b < near_blocks else fb[:, b * BLK - rows : (b + 1) * BLK - rows].astype(F32)
            nrm[:, ls] = (v * norm_scale(v) * agc[...]).astype(BF)
            qkv_ref[:, ls] = dot(wq_ref[...], nrm[:, ls], ((1,), (0,))).astype(BF)
        out(1).start()
        for i in range(2):
            start = (1 - x) * rows if i else x * rows
            line = pad_ref[:, pl.ds(pl.multiple_of(start, BLK), rows)].astype(F32)
            padc[i * rows : (i + 1) * rows, :] = jnp.broadcast_to(line, (8, rows)).T
        ids = bid_ref[...]
        for hh in range(heads):
            line = jnp.zeros((1, SPAN), F32)
            for b in range(buckets):
                line = jnp.where(ids == b, rel_ref[b, hh], line)
            turned = pltpu.roll(
                jnp.broadcast_to(line, (BLK, SPAN)), 0, 1, stride=1, stride_axis=0
            )
            for g in range(5):
                table[hh, g] = turned[:, BLK * (4 - g) : BLK * (5 - g)]

    @pl.when(qb == 1)
    def _():
        w_copy.wait()
        w_pass.start()

    q_true = (qb + near_blocks * x) % blocks

    q_pos = q_true * BLK + lax.broadcasted_iota(jnp.int32, (1, BLK), 1)
    k_iota = lax.broadcasted_iota(jnp.int32, (BLK, BLK), 0)
    for kb in range(blocks):
        k_pos = (kb + near_blocks * x) % blocks * BLK + k_iota
        bound = 0
        q_doc = jnp.zeros((1, BLK), jnp.int32)
        k_doc = jnp.zeros((BLK, BLK), jnp.int32)
        for i in range(len_ref.shape[1]):
            bound = bound + len_ref[0, i]
            q_doc = q_doc + (q_pos >= bound).astype(jnp.int32)
            k_doc = k_doc + (k_pos >= bound).astype(jnp.int32)
        krows = slice(kb * BLK, (kb + 1) * BLK)
        seen = (padc[krows, 0:1] > 0.5) | (k_pos == q_pos)
        mask[krows, :] = jnp.where((k_doc == q_doc) & seen, 0.0, -1000000000.0)

    def head_rows(h, group):
        return pl.ds(pl.multiple_of(group * cols + h * dk, dk), dk)

    def diagonal(kb):
        return near_diagonal((kb + near_blocks * x) % blocks - q_true)

    def head(h, carry):
        qh = qkv_ref[head_rows(h, 0), lanes(qb)]
        peak = None
        for kb in range(blocks):
            krows = slice(kb * BLK, (kb + 1) * BLK)
            s = dot(qkv_ref[head_rows(h, 1), krows], qh, ((0,), (0,)))
            diag = diagonal(kb)
            s = s + table[h, diag] + mask[krows, :]
            score[krows, :] = s
            top = jnp.max(s, axis=0, keepdims=True)
            peak = top if peak is None else jnp.maximum(peak, top)
        total = jnp.zeros((1, BLK), F32)
        ctx = jnp.zeros((dk, BLK), F32)
        for kb in range(blocks):
            krows = slice(kb * BLK, (kb + 1) * BLK)
            e = jnp.exp(score[krows, :] - peak)
            total = total + jnp.sum(e, axis=0, keepdims=True)
            e_low = e.astype(BF)
            e_ref[h, 0, krows, :] = e_low
            ctx = ctx + dot(qkv_ref[head_rows(h, 2), krows], e_low, ((1,), (0,)))
        inv = 1.0 / total
        inv_ref[h, 0] = inv
        call[head_rows(h, 0), lanes(qb)] = (ctx * inv).astype(BF)
        return carry

    lax.fori_loop(0, heads, head, 0)
    ctx_copy(qb).start()

    @pl.when(qb == 1)
    def _():
        c_copy(2).start()

    @pl.when(qb == blocks - 1)
    def _():
        c_copy(3).start()
        w_pass.wait()
        wn[...] = wall[...].astype(F32).T.astype(BF)
        out(4).start()
        for i in range(blocks):
            b = (i + near_blocks) % blocks
            ctx_copy(i).wait()
            ls = slice(b * BLK, (b + 1) * BLK)
            v = dot(wn[...], call[:, ls], ((1,), (0,)))
            if b < near_blocks:
                v = v + f1[:, ls]
                f1[:, ls] = v
            else:
                v = v + fb[:, b * BLK - rows : (b + 1) * BLK - rows].astype(F32)
            xo[:, ls] = (v * norm_scale(v) * fgc[...]).astype(BF)
            xt_out(b).start()
        out(0).start()
        out(2).start()
        for i in range(4):
            c_copy(i).wait()
        for i in range(5):
            out(i).wait()
        for b in range(blocks):
            xt_out(b).wait()


def front(rel, lengths, pad, again, fgain, wq, wo, tok, far, cot, heads, dk):
    d, rows = tok.shape
    seq = 2 * rows
    cols = heads * dk
    blocks = seq // BLK
    buckets = rel.shape[0]
    bids = jnp.asarray(lane_buckets(buckets))
    one = pl.Buffered(1)
    dma = pltpu.SemaphoreType.DMA
    any_spec = pl.BlockSpec(memory_space=pl.ANY)
    smem = pl.BlockSpec(memory_space=pltpu.SMEM)

    def full(v):
        return pl.BlockSpec(v.shape, lambda i: (0, 0), pipeline_mode=one)

    return pl.pallas_call(
        functools.partial(front_kernel, heads, dk, buckets, blocks),
        grid=(blocks,),
        in_specs=[smem, smem, full(bids), full(pad), full(again), full(fgain), full(wq), full(wo)]
        + [any_spec] * 3,
        out_specs=[
            pl.BlockSpec((heads, 1, seq, BLK), lambda i: (0, i, 0, 0)),
            pl.BlockSpec((heads, 1, 1, BLK), lambda i: (0, i, 0, 0)),
            pl.BlockSpec((3 * cols, seq), lambda i: (0, 0)),
        ]
        + [any_spec] * 6,
        out_shape=[
            jax.ShapeDtypeStruct((heads, blocks, seq, BLK), BF),
            jax.ShapeDtypeStruct((heads, blocks, 1, BLK), F32),
            jax.ShapeDtypeStruct((3 * cols, seq), BF),
            jax.ShapeDtypeStruct((2 * cols, seq), BF),
            jax.ShapeDtypeStruct((d, seq), BF),
            jax.ShapeDtypeStruct((d, seq), BF),
            jax.ShapeDtypeStruct((d, rows), F32),
            jax.ShapeDtypeStruct((d, seq), BF),
            jax.ShapeDtypeStruct((2 * cols, d), BF),
        ],
        scratch_shapes=[
            pltpu.VMEM((d, rows), F32),
            pltpu.VMEM((d, rows), BF),
            pltpu.VMEM((d, rows), F32),
            pltpu.VMEM((d, rows), BF),
            pltpu.VMEM((d, seq), BF),
            pltpu.VMEM((heads, 5, BLK, BLK), F32),
            pltpu.VMEM((seq, 8), F32),
            pltpu.VMEM((seq, BLK), F32),
            pltpu.VMEM((seq, BLK), F32),
            pltpu.VMEM((d, 1), F32),
            pltpu.VMEM((d, 1), F32),
            pltpu.VMEM((2 * cols, d), BF),
            pltpu.VMEM((d, 2 * cols), BF),
            pltpu.VMEM((2 * cols, seq), BF),
            pltpu.VMEM((d, seq), BF),
            dma((3,)), dma((5 + blocks,)), dma((6,)), dma((6,)), dma((blocks,)), dma((blocks,)),
        ],
        compiler_params=pltpu.CompilerParams(
            vmem_limit_bytes=FF_VMEM, collective_id=2, has_side_effects=True
        ),
        cost_estimate=pl.CostEstimate(
            flops=16 * heads * seq * seq * dk + 10 * seq * d * cols,
            bytes_accessed=2 * heads * seq * seq + 30 * rows * d,
            transcendentals=heads * seq * seq,
        ),
    )(rel, lengths, bids, pad, again, fgain, wq, wo, tok, far, cot)


def ff_kernel(
    steps, extra,
    xt_hbm, w_hbm, ct_hbm, wo_hbm, mid_hbm, wq_hbm,
    grads_ref, din_hbm, near_hbm, far_hbm, quarter_hbm, half_hbm, hand_hbm, wfar_hbm,
    xt, ct, wg, wu, wo, hid, dg, du, din, stage, r1, r2, r3, r4, xs, xr, of,
    csem, wsem, s1, s2, s3, s4, t1, t2, t3, t4, xsem, osem, hsem,
):
    f, total = hid.shape
    rows = total // 2
    chunks = rows // BLK
    d = xt.shape[0]
    shard = d // 16
    dp, mp = lax.axis_index("dp"), lax.axis_index("mp")
    a = group_coords(dp // extra)
    peers = [flip(dp, m * extra) for m in GROUP_MASKS]
    other = (dp, 1 - mp)
    core = dp % 2
    sibling = dp + 1 - 2 * core
    bufs = (r1, r2, r3, r4)
    sends, recvs = (s1, s2, s3, s4), (t1, t2, t3, t4)
    end = steps - 1

    def weight_copy(kind, n):
        src, dst = ((w_hbm.at[0], wg), (w_hbm.at[1], wu), (wo_hbm, wo))[kind]
        return pltpu.make_async_copy(src.at[:, lanes(n)], dst.at[:, lanes(n)], wsem.at[kind, n])

    def tok_copy(n):
        src, dst, start, size = (
            (xt_hbm, xt, rows, BLK), (ct_hbm, ct, rows, BLK),
            (xt_hbm, xt, 0, rows), (ct_hbm, ct, 0, rows), (xt_hbm, xt, rows + BLK, BLK),
        )[n]
        part = pl.ds(start, size)
        return pltpu.make_async_copy(src.at[:, part], dst.at[:, part], csem.at[n])

    near_part, far_part = pl.ds(0, rows), pl.ds(rows, rows)
    c_far = remote(
        ct_hbm.at[:, pl.ds(BLK, BLK)], ct.at[:, pl.ds(rows + BLK, BLK)], csem.at[5], csem.at[6], other
    )
    x_copy = remote(xs, xr, xsem.at[0], xsem.at[1], other)
    wq_rows = wq_hbm.shape[0] // 2
    wq_part = pl.ds(core * wq_rows, wq_rows)
    w_copy = remote(wq_hbm.at[wq_part], wfar_hbm.at[wq_part], xsem.at[2], xsem.at[3], other)
    w_pass = remote(wfar_hbm.at[wq_part], wfar_hbm.at[wq_part], xsem.at[4], xsem.at[5], (sibling, mp))
    mid_copy = pltpu.make_async_copy(mid_hbm, din.at[:, far_part], osem.at[3])

    deep = len(LEVELS)

    def hop(level, n, order):
        half = 8 >> level
        c = order[level]
        away = pl.ds((1 - a[c]) * half, half)
        src = stage.at[away] if level == 0 else bufs[level - 1].at[n, away]
        return remote(src, bufs[level].at[n], sends[level].at[n], recvs[level].at[n], (peers[c], mp))

    def hand_copy(n):
        level = levels_of(n) if isinstance(n, int) else 1
        dst = (hand_hbm.at[n - deep], half_hbm, quarter_hbm.at[n - 1])[level - 1]
        return pltpu.make_async_copy(bufs[level - 1].at[n], dst, hsem.at[n])

    def absorb_first(n):
        hop(0, n, Y_FIRST).wait()
        r1[n] = stage[pl.ds(a[0] * 8, 8)] + r1[n]
        if isinstance(n, int):
            hand_copy(n).start()
            return

        @pl.when(n == Z_BLOCK)
        def _():
            hop(1, n, Z_FIRST).start()

        @pl.when((n < deep) & (n != Z_BLOCK))
        def _():
            hop(1, n, Y_FIRST).start()

        @pl.when(n >= deep)
        def _():
            hand_copy(n).start()

    def absorb(level, n):
        half = 8 >> level
        order = order_of(n)
        hop(level, n, order).wait()
        kept = bufs[level - 1][n, pl.ds(a[order[level]] * half, half)]
        if level < 3:
            bufs[level][n] = kept + bufs[level][n]
            if level + 1 < levels_of(n):
                hop(level + 1, n, order).start()
            else:
                hand_copy(n).start()
        else:
            both = kept.astype(F32) + bufs[level][n].astype(F32)
            for w in range(3):
                grads_ref[w, :, n * BLK : (n + 1) * BLK] = both[0, w]

    scale = np.float32(np.sqrt(2 / np.pi))

    def place(u):
        early, late = u // steps, (u - 4) // steps
        is_far0 = (early == 0) * 1
        is_far1 = (late == 1) * 1
        v = u - steps
        n = v - steps * (u // (2 * steps + 4))
        near_j, near_c = n // 2, n % 2
        j = is_far0 * u + is_far1 * (u - steps - 4) + (1 - is_far0 - is_far1) * near_j
        c = is_far0 * chunks + is_far1 * (chunks + 1) + (1 - is_far0 - is_far1) * near_c
        return j, c

    def substep(u):
        j, c = place(u)
        pj, pc = place(u - 1)
        pj = pj + (u == 0) * 1
        fcols, tok = lanes(j), lanes(c)
        pcols, ptok = lanes(pj), lanes(pc)
        gate = dot(wg[:, fcols], xt[:, tok], ((0,), (0,)))
        up = dot(wu[:, fcols], xt[:, tok], ((0,), (0,)))
        dh = dot(wo[:, fcols], ct[:, tok], ((0,), (0,)))
        backward(pcols, ptok)
        sq = gate * gate
        t = jnp.tanh(scale * gate * (1.0 + 0.044715 * sq))
        half = 0.5 * (1.0 + t)
        act = gate * half
        slope = half + 0.5 * gate * (1.0 - t * t) * (scale * (1.0 + (3 * 0.044715) * sq))
        hid[fcols, tok] = (act * up).astype(BF)
        dg[fcols, tok] = (dh * (up * slope)).astype(BF)
        du[fcols, tok] = (dh * act).astype(BF)

    def backward(rs, tok):
        din[:, tok] += dot(wg[:, rs], dg[rs, tok], ((1,), (0,))) + dot(wu[:, rs], du[rs, tok], ((1,), (0,)))

    per = 4 * shard

    def grads(j):
        z = (j == Z_BLOCK) * 1
        for w in range(3):
            right = (hid, dg, du)[w][lanes(j), :]
            for q in range(4):
                rs = slice(q * per, (q + 1) * per)
                left = ct[rs, :] if w == 0 else xt[rs, :]
                part = dot(left, right, ((1,), (1,)))
                for k in range(4):
                    at = block_position(4 * q + k, Y_FIRST)
                    at = at + z * (block_position(4 * q + k, Z_FIRST) - at)
                    stage[at, w, 0:shard, :] = part[k * shard : (k + 1) * shard].astype(BF)
        hop(0, j, Y_FIRST).start()

    def out_part(n):
        return dot(wo[...], hid[:, lanes(n)], ((1,), (0,)))

    meet([(p, mp) for p in peers] + [other] + ([(sibling, mp)] if extra > 1 else []))
    c_far.start()
    w_copy.start()
    tok_copy(0).start()
    tok_copy(1).start()
    for n in range(steps):
        for kind in range(3):
            weight_copy(kind, n).start()
    for n in range(2, 5):
        tok_copy(n).start()
    din[...] = jnp.zeros_like(din)
    stage[...] = jnp.zeros_like(stage)
    before = place(-1)[1]
    dg[0:BLK, before * BLK : (before + 1) * BLK] = jnp.zeros((BLK, BLK), BF)
    du[0:BLK, before * BLK : (before + 1) * BLK] = jnp.zeros((BLK, BLK), BF)
    tok_copy(0).wait()
    tok_copy(1).wait()
    count = 2 * chunks * steps
    far_end = 2 * steps + 4

    def step(u, carry):
        @pl.when(u < steps)
        def _():
            for kind in range(3):
                weight_copy(kind, u).wait()

        @pl.when(u == steps)
        def _():
            tok_copy(2).wait()
            tok_copy(3).wait()

        @pl.when(u == steps + 4)
        def _():
            tok_copy(4).wait()
            c_far.wait()

        @pl.when(u < count)
        def _():
            substep(u)

        @pl.when(u == far_end)
        def _():
            xs[...] = din[:, far_part].astype(BF)
            x_copy.start()
            mid_copy.start()

        odd = u % 2 == 1
        late = (u >= 2 * steps + 5) * 1
        m = (u - 13) // 2 - 2 * ((u >= 2 * steps + 7) * 1)
        n = (u - 11) // 2 - 2 * late

        @pl.when(odd & ((u == 13) | (u == 15) | (u >= 2 * steps + 7)))
        def _():
            absorb_first(m)

        for at, events in (
            (21, ((1, 0),)), (23, ((1, 1),)), (25, ((2, 0),)), (27, ((1, 2), (2, 1))),
        ):
            @pl.when(u == at)
            def _():
                for level, block in events:
                    absorb(level, block)

        @pl.when(odd & ((u == 11) | (u == 13) | (u >= 2 * steps + 5)))
        def _():
            grads(n)

        @pl.when(u == far_end + 5)
        def _():
            w_copy.wait()
            w_pass.start()

        return carry

    lax.fori_loop(0, count, step, 0)
    pj, pc = place(count - 1)
    backward(lanes(pj), lanes(pc))

    def far_out(n, carry):
        of[:, lanes(n)] = out_part(n + chunks).astype(BF)
        return carry

    lax.fori_loop(0, chunks, far_out, 0)
    far_copy = pltpu.make_async_copy(of, far_hbm, osem.at[0])
    far_copy.start()
    x_copy.wait()
    din[:, near_part] += xr[...].astype(F32)
    din_copy = pltpu.make_async_copy(din.at[:, near_part], din_hbm, osem.at[2])
    din_copy.start()
    mid_copy.wait()

    def near_out(n, carry):
        at = lanes(n + chunks)
        din[:, at] = din[:, at] + out_part(n)
        return carry

    lax.fori_loop(0, chunks, near_out, 0)
    near_copy = pltpu.make_async_copy(din.at[:, far_part], near_hbm, osem.at[1])
    near_copy.start()
    absorb_first(end)
    absorb(3, 0)
    absorb(2, 2)
    absorb(1, 3)
    w_pass.wait()
    for n in range(1, steps):
        hand_copy(n).wait()
    far_copy.wait()
    near_copy.wait()
    din_copy.wait()


def ff_all(xt, ct, w2, wo, mid, wq, extra):
    d, total = xt.shape
    f = wo.shape[1]
    rows = total // 2
    steps = f // BLK
    deep = len(LEVELS)
    shard = d // 16
    spad = -(-shard // 16) * 16
    dma = pltpu.SemaphoreType.DMA
    any_spec = pl.BlockSpec(memory_space=pl.ANY)
    return pl.pallas_call(
        functools.partial(ff_kernel, steps, extra),
        in_specs=[any_spec] * 6,
        out_specs=[pl.BlockSpec(memory_space=pltpu.VMEM)] + [any_spec] * 7,
        out_shape=[
            jax.ShapeDtypeStruct((3, spad, BLK), F32),
            jax.ShapeDtypeStruct((d, rows), F32),
            jax.ShapeDtypeStruct((d, rows), F32),
            jax.ShapeDtypeStruct((d, rows), BF),
            jax.ShapeDtypeStruct((2, 2, 3, spad, BLK), BF),
            jax.ShapeDtypeStruct((4, 3, spad, BLK), BF),
            jax.ShapeDtypeStruct((steps - deep, 8, 3, spad, BLK), BF),
            jax.ShapeDtypeStruct(wq.shape, BF),
        ],
        scratch_shapes=[
            pltpu.VMEM((d, total), BF),
            pltpu.VMEM((d, total), BF),
            pltpu.VMEM((d, f), BF),
            pltpu.VMEM((d, f), BF),
            pltpu.VMEM((d, f), BF),
            pltpu.VMEM((f, total), BF),
            pltpu.VMEM((f, total), BF),
            pltpu.VMEM((f, total), BF),
            pltpu.VMEM((d, total), F32),
            pltpu.VMEM((16, 3, spad, BLK), BF),
            pltpu.VMEM((steps, 8, 3, spad, BLK), BF),
            pltpu.VMEM((4, 4, 3, spad, BLK), BF),
            pltpu.VMEM((3, 2, 3, spad, BLK), BF),
            pltpu.VMEM((1, 1, 3, spad, BLK), BF),
            pltpu.VMEM((d, rows), BF),
            pltpu.VMEM((d, rows), BF),
            pltpu.VMEM((d, rows), BF),
            dma((7,)),
            dma((3, steps)),
            dma((steps,)), dma((4,)), dma((3,)), dma((1,)),
            dma((steps,)), dma((4,)), dma((3,)), dma((1,)),
            dma((6,)),
            dma((4,)),
            dma((steps,)),
        ],
        compiler_params=pltpu.CompilerParams(
            vmem_limit_bytes=FF_VMEM, collective_id=0, has_side_effects=True
        ),
        cost_estimate=pl.CostEstimate(
            flops=18 * total * d * f,
            bytes_accessed=6 * d * f + 16 * total * d,
            transcendentals=total * f,
        ),
    )(xt, w2, ct, wo, mid, wq)


EVENTS = (
    ((0, 0), ((2, 3), (3, 2))),
    ((0, 2), ((1, 4),)),
    ((2, 0), ((3, 3),)),
    ((2, 1), ((2, 4),)),
    ((3, 2), ((1, 5),)),
)


def tail_kernel(
    heads, dk, buckets, blocks, extra,
    bid_ref, qkv_ref, e_ref, inv_ref, wall_ref, ctx_ref, ag_ref, fg_ref, early_ref,
    din_hbm, mid_hbm, cot_hbm, tok_hbm, nrm_hbm, wq_hbm, wfar_hbm, far_hbm,
    quarter_hbm, half_hbm, hand_hbm,
    ig_hbm, back_hbm, gq_ref, go_ref, small_ref, ffo_ref, ffi_ref,
    f1, f2, f3, nrm, wq, wn, wf, alow, dctx, dcs, osend, orecv, fsum, agc, fgc,
    dp_s, dkv, tally, dproj, dfar, grad,
    sa, sb_, a1, a2, a3, a4, b1, b2, b3, b4, hk, hm, hq, h2, h3, h4, sv, rv,
    lsem, ksem, xs_sem, xr_sem, cs_sem, cr_sem, bs_sem, br_sem, hs_sem, hr_sem,
):
    qb = pl.program_id(0)
    dp, x = lax.axis_index("dp"), lax.axis_index("mp")
    d, rows = f2.shape
    cols = heads * dk
    shard = d // 16
    a = group_coords(dp // extra)
    peers = [flip(dp, m * extra) for m in GROUP_MASKS]
    other = (dp, 1 - x)
    near_blocks = blocks // 2
    near_part, far_part = pl.ds(0, rows), pl.ds(rows, rows)
    halves = ((sa, a1, a2, a3, a4), (sb_, b1, b2, b3, b4))
    orders = (Y_FIRST, Y_FIRST)
    copies = (
        (din_hbm, f1), (mid_hbm, f2), (cot_hbm, f3), (tok_hbm, f2), (nrm_hbm, nrm), (wq_hbm, wq), (wfar_hbm, wq),
    )

    def local(i):
        return pltpu.make_async_copy(copies[i][0], copies[i][1], lsem.at[i])

    def x_copy(i, src, dst):
        return remote(src, dst, xs_sem.at[i], xr_sem.at[i], other)

    dctx_copy = x_copy(0, dcs, dctx.at[:, far_part])
    o_copy = x_copy(1, osend, orecv)
    dproj_copy = x_copy(2, dproj.at[:, far_part], dfar)

    def back_copy(i):
        part = pl.ds(i * 128, 128)
        return x_copy(3 + i, far_hbm.at[:, part], back_hbm.at[:, part])

    def hop(side, level):
        half = 8 >> level
        c = orders[side][level]
        away = pl.ds((1 - a[c]) * half, half)
        bufs = halves[side]
        return remote(
            bufs[level].at[away], bufs[level + 1], cs_sem.at[side, level], cr_sem.at[side, level], (peers[c], x)
        )

    def absorb(side, level):
        half = 8 >> level
        bufs = halves[side]
        hop(side, level).wait()
        kept = bufs[level][pl.ds(a[orders[side][level]] * half, half)]
        if level < 3:
            bufs[level + 1][...] = kept + bufs[level + 1][...]
            hop(side, level + 1).start()
            return
        both = (kept.astype(F32) + bufs[level + 1][...].astype(F32))[0, 0:shard]
        outs = (gq_ref.at[0], gq_ref.at[1]) if side == 0 else (gq_ref.at[2], go_ref)
        for i in range(2):
            outs[i][...] = both[:, i * cols : (i + 1) * cols]

    deep = len(LEVELS)
    handed = (3, 4, 2, 5, 6, 1)

    def keep_copy(block):
        level = levels_of(block)
        half = 8 >> level
        keep = pl.ds(a[order_of(block)[level]] * half, half)
        if level == 3:
            src, dst = quarter_hbm.at[block - 1, keep], hq.at[block - 1]
        elif level == 2:
            src, dst = half_hbm.at[keep], hm
        else:
            src, dst = hand_hbm.at[block - deep, keep], hk.at[block - deep]
        return pltpu.make_async_copy(src, dst, ksem.at[block])

    def hand_hop(level, block):
        half = 8 >> level
        c = order_of(block)[level]
        away = pl.ds((1 - a[c]) * half, half)
        fresh = level == levels_of(block)
        if level == 1:
            src, dst = hand_hbm.at[block - deep, away], h2.at[block - deep]
        elif level == 2:
            src, dst = half_hbm.at[away] if fresh else h2.at[block - deep, away], h3.at[block - 3]
        else:
            src, dst = quarter_hbm.at[block - 1, away] if fresh else h3.at[block - 3, away], h4.at[block - 1]
        return remote(src, dst, hs_sem.at[level, block], hr_sem.at[level, block], (peers[c], x))

    def put_grads(w, block, value):
        at = slice(block * BLK, (block + 1) * BLK)
        if w == 0:
            ffo_ref[:, at] = value
        else:
            ffi_ref[:, w - 1, at] = value

    def hand_absorb(level, block):
        half = 8 >> level
        keep = pl.ds(a[order_of(block)[level]] * half, half)
        hand_hop(level, block).wait()
        if level == levels_of(block):
            keep_copy(block).wait()
            kept = hk[block - deep] if level == 1 else (hm[...] if level == 2 else hq[block - 1])
        else:
            kept = h2[block - deep, keep] if level == 2 else h3[block - 3, keep]
        if level == 1:
            h2[block - deep] = kept + h2[block - deep]
        elif level == 2:
            h3[block - 3] = kept + h3[block - 3]
        else:
            both = kept.astype(F32) + h4[block - 1].astype(F32)
            for w in range(3):
                put_grads(w, block, both[0, w, 0:shard])
        if level < 3:
            hand_hop(level + 1, block).start()

    def round_copy(i):
        who = other if i == 4 else (peers[(0, 2, 3, 1)[i]], x)
        return remote(sv.at[i], rv.at[i], bs_sem.at[i], br_sem.at[i], who)

    def round_end(i):
        round_copy(i).wait()
        sv[i + 1] = sv[i] + rv[i]
        if i < 4:
            round_copy(i + 1).start()

    def out_copy(r):
        return pltpu.make_async_copy(f3.at[:, lanes(r)], ig_hbm.at[:, lanes(r)], lsem.at[len(copies) + r])

    def lane_sum(v):
        total = v[:, 0:128]
        for i in range(1, v.shape[1] // 128):
            total = total + v[:, i * 128 : (i + 1) * 128]
        return total

    @pl.when(qb == 0)
    def _():
        for i in range(3):
            local(i).start()
        meet([(p, x) for p in peers] + [other])
        back_copy(0).start()
        for block in handed[:-1]:
            hand_hop(levels_of(block), block).start()
        agc[...] = column(ag_ref[...])
        fgc[...] = column(fg_ref[...])
        dkv[...] = jnp.zeros_like(dkv)
        tally[...] = jnp.zeros_like(tally)
        sa[...] = jnp.zeros_like(sa)
        sb_[...] = jnp.zeros_like(sb_)
        fsum[...] = jnp.zeros_like(fsum)
        for i in range(3):
            local(i).wait()

        def norm_rows(r, carry):
            ls = lanes(r)
            v = f2[:, ls]
            c = f1[:, ls]
            scale = norm_scale(v)
            n = v * scale
            cg = c * fgc[...]
            m = jnp.mean(cg * n, axis=0, keepdims=True)
            gm = f3[:, ls] + scale * (cg - n * m)
            fsum[...] += lane_sum(c * n)
            f1[:, ls] = gm
            alow[:, ls] = gm.astype(BF)
            return carry

        lax.fori_loop(0, near_blocks, norm_rows, 0)
        dcs[...] = dot(wall_ref[cols : 2 * cols, :], alow[...], ((1,), (0,))).astype(BF)
        dctx_copy.start()
        for i in (3, 4, 5):
            local(i).start()
        for block in handed:
            keep_copy(block).start()
        dctx[:, near_part] = dot(wall_ref[0:cols, :], alow[...], ((1,), (0,))).astype(BF)
        osend[...] = dot(alow[...], ctx_ref[cols : 2 * cols, near_part], ((1,), (1,))).astype(BF)
        o_copy.start()
        grad[:, 3 * cols : 4 * cols] = dot(alow[...], ctx_ref[0:cols, near_part], ((1,), (1,)))
        for w in range(3):
            put_grads(w, 0, early_ref[w, 0:shard, :])
        dctx_copy.wait()
        back_copy(1).start()

    @pl.when(qb == 1)
    def _():
        local(5).wait()
        wn[...] = wq[...].astype(F32).T.astype(BF)
        local(6).start()

    @pl.when(qb == 2)
    def _():
        local(6).wait()
        wf[...] = wq[...].astype(F32).T.astype(BF)

    q_true = (qb + near_blocks * x) % blocks

    def head(h, carry):
        for at, events in EVENTS:
            @pl.when((qb == at[0]) & (h == at[1]))
            def _():
                for level, block in events:
                    hand_absorb(level, block)

        def head_rows(group):
            return pl.ds(pl.multiple_of(group * cols + h * dk, dk), dk)

        inv = inv_ref[h, 0]
        qh = qkv_ref[head_rows(0), lanes(qb)]
        scaled = (dctx[head_rows(0), lanes(qb)].astype(F32) * inv).astype(BF)
        inner = jnp.zeros((1, BLK), F32)
        for kb in range(blocks):
            krows = slice(kb * BLK, (kb + 1) * BLK)
            g = dot(qkv_ref[head_rows(2), krows], scaled, ((0,), (0,)))
            dp_s[krows, :] = g
            inner = inner + jnp.sum(e_ref[h, 0, krows, :].astype(F32) * g, axis=0, keepdims=True)
        inner = inner * inv
        dq = jnp.zeros((dk, BLK), F32)
        for kb in range(blocks):
            krows = slice(kb * BLK, (kb + 1) * BLK)
            e = e_ref[h, 0, krows, :]
            ds = (e.astype(F32) * (dp_s[krows, :] - inner)).astype(BF)
            dkv[head_rows(0), krows] += dot(qh, ds, ((1,), (1,)))
            dkv[head_rows(1), krows] += dot(scaled, e, ((1,), (1,)))
            dq = dq + dot(qkv_ref[head_rows(1), krows], ds, ((1,), (0,)))
            tally[h, near_diagonal((kb + near_blocks * x) % blocks - q_true)] += ds.astype(F32)
        dproj[head_rows(0), lanes(qb)] = dq.astype(BF)
        return carry

    lax.fori_loop(0, heads, head, 0)

    @pl.when(qb == blocks - 1)
    def _():
        dproj[cols : 3 * cols, :] = dkv[...].astype(BF)
        dproj_copy.start()
        back_copy(2).start()
        back_copy(3).start()
        local(3).wait()
        local(4).wait()
        per = 4 * shard

        def grad_rows(q, carry):
            rs = pl.ds(pl.multiple_of(q * per, 16), per)
            grad[rs, 0 : 3 * cols] = dot(nrm[rs, :], dproj[...], ((1,), (1,)))
            return carry

        lax.fori_loop(0, 4, grad_rows, 0)
        o_copy.wait()
        grad[:, 3 * cols : 4 * cols] += orecv[...].astype(F32)
        for side in range(2):
            for k in range(16):
                halves[side][0][block_position(k, orders[side]), 0:shard, :] = grad[
                    k * shard : (k + 1) * shard, 2 * side * cols : 2 * (side + 1) * cols
                ].astype(BF)
            hop(side, 0).start()
        hand_absorb(2, 5)

        def near_rows(r, carry):
            f3[:, lanes(r)] = dot(wn[...], dproj[:, lanes(r)], ((1,), (0,)))
            return carry

        lax.fori_loop(0, near_blocks, near_rows, 0)
        absorb(1, 0)
        absorb(0, 0)
        hand_hop(3, 1).start()
        hand_absorb(1, 6)
        ids = bid_ref[...]
        hot = ids == lax.broadcasted_iota(jnp.int32, (buckets, SPAN), 0)
        out_lane = lax.broadcasted_iota(jnp.int32, (buckets, 128), 1)
        sub = lax.broadcasted_iota(jnp.int32, (8, SPAN), 0)
        sv[0] = jnp.zeros(sv.shape[1:], F32)

        def bias_sums(hh, carry):
            line = jnp.zeros((8, SPAN), F32)
            for g in range(BLK // 8):
                group = slice(8 * g, 8 * g + 8)
                parts = [tally[hh, i, group, :] for i in (4, 3, 2, 1, 0)]
                strip = jnp.concatenate(parts + [jnp.zeros((8, BLK), F32)], axis=1)
                line = line + (strip if g == 0 else pltpu.roll(strip, SPAN - 8 * g, 1))
            for bit in (1, 2, 4):
                line = jnp.where((sub // bit) % 2 == 1, pltpu.roll(line, SPAN - bit, 1), line)
            sums = jnp.sum(line, axis=0, keepdims=True)
            col = jnp.sum(jnp.where(hot, sums, 0.0), axis=1, keepdims=True)
            sv[0, 0:buckets, :] = jnp.where(out_lane == x * heads + hh, col, sv[0, 0:buckets, :])
            return carry

        lax.fori_loop(0, heads, bias_sums, 0)
        product = wn[...].astype(F32) * grad[:, 0 : 3 * cols]
        again = lane_sum(product[:, 0:512]).T
        rest = product[:, 512 : 3 * cols]
        again = jnp.sum(again, axis=0, keepdims=True) + jnp.sum(rest.T, axis=0, keepdims=True)
        again = again / ag_ref[...]
        fgain = jnp.sum(fsum[...].T, axis=0, keepdims=True)
        lines = -(-d // 128)
        for i in range(lines):
            n = min(128, d - 128 * i)
            sv[0, buckets + i : buckets + i + 1, 0:n] = again[:, 128 * i : 128 * i + n]
            sv[0, buckets + lines + i : buckets + lines + i + 1, 0:n] = fgain[:, 128 * i : 128 * i + n]
        round_copy(0).start()
        hand_absorb(3, 4)
        round_end(0)
        absorb(1, 1)
        dproj_copy.wait()

        def last_norm(r, carry):
            ls = lanes(r)
            c = f3[:, ls] + dot(wf[...], dfar[:, ls], ((1,), (0,)))
            v = f2[:, ls]
            scale = norm_scale(v)
            n = v * scale
            cg = c * agc[...]
            m = jnp.mean(cg * n, axis=0, keepdims=True)
            f3[:, ls] = f1[:, ls] + scale * (cg - n * m)
            out_copy(r).start()
            return carry

        lax.fori_loop(0, near_blocks, last_norm, 0)
        absorb(0, 1)
        hand_absorb(3, 5)
        round_end(1)
        hand_absorb(2, 6)
        absorb(1, 2)
        round_end(2)
        absorb(0, 2)
        hand_absorb(3, 1)
        hand_absorb(3, 6)
        absorb(1, 3)
        round_end(3)
        absorb(0, 3)
        round_end(4)
        small_ref[...] = sv[5]
        for i in range(4):
            back_copy(i).wait()
        for r in range(near_blocks):
            out_copy(r).wait()


def tail(qkv, e, inv, wall, ctx, again, fgain, early, din, mid, cot, tok, nrm, wq, wfar, far,
         quarter, half_way, hand, buckets, heads, dk, extra, f):
    d, rows = tok.shape
    seq = 2 * rows
    cols = heads * dk
    blocks = seq // BLK
    near = blocks // 2
    shard = d // 16
    spad = -(-shard // 16) * 16
    deep = hand.shape[0]
    later = deep + len(LEVELS)
    lines = -(-(buckets + 2 * -(-d // 128)) // 8) * 8
    bids = jnp.asarray(lane_buckets(buckets))
    one = pl.Buffered(1)
    dma = pltpu.SemaphoreType.DMA
    any_spec = pl.BlockSpec(memory_space=pl.ANY)

    def full(v):
        return pl.BlockSpec(v.shape, lambda i: (0,) * len(v.shape), pipeline_mode=one)

    def chain(width):
        return [pltpu.VMEM((n, spad, width), BF) for n in (16, 8, 4, 2, 1)]

    outs = [
        jax.ShapeDtypeStruct((3, shard, cols), F32),
        jax.ShapeDtypeStruct((shard, cols), F32),
        jax.ShapeDtypeStruct((lines, 128), F32),
        jax.ShapeDtypeStruct((shard, f), F32),
        jax.ShapeDtypeStruct((shard, 2, f), F32),
    ]
    a_chain, b_chain = chain(2 * cols), chain(2 * cols)
    return pl.pallas_call(
        functools.partial(tail_kernel, heads, dk, buckets, blocks, extra),
        grid=(blocks,),
        in_specs=[
            full(bids),
            full(qkv),
            pl.BlockSpec((heads, 1, seq, BLK), lambda i: (0, i, 0, 0)),
            pl.BlockSpec((heads, 1, 1, BLK), lambda i: (0, i, 0, 0)),
            full(wall),
            full(ctx),
            full(again),
            full(fgain),
            full(early),
        ]
        + [any_spec] * 11,
        out_specs=[any_spec, any_spec] + [full(v) for v in outs],
        out_shape=[jax.ShapeDtypeStruct((d, rows), F32), jax.ShapeDtypeStruct((d, rows), BF)] + outs,
        scratch_shapes=[
            pltpu.VMEM((d, rows), F32),
            pltpu.VMEM((d, rows), F32),
            pltpu.VMEM((d, rows), F32),
            pltpu.VMEM((d, seq), BF),
            pltpu.VMEM((3 * cols, d), BF),
            pltpu.VMEM((d, 3 * cols), BF),
            pltpu.VMEM((d, 3 * cols), BF),
            pltpu.VMEM((d, rows), BF),
            pltpu.VMEM((cols, seq), BF),
            pltpu.VMEM((cols, rows), BF),
            pltpu.VMEM((d, cols), BF),
            pltpu.VMEM((d, cols), BF),
            pltpu.VMEM((d, 128), F32),
            pltpu.VMEM((d, 1), F32),
            pltpu.VMEM((d, 1), F32),
            pltpu.VMEM((seq, BLK), F32),
            pltpu.VMEM((2 * cols, seq), F32),
            pltpu.VMEM((heads, 5, BLK, BLK), F32),
            pltpu.VMEM((3 * cols, seq), BF),
            pltpu.VMEM((3 * cols, rows), BF),
            pltpu.VMEM((d, 4 * cols), F32),
            a_chain[0],
            b_chain[0],
        ]
        + a_chain[1:]
        + b_chain[1:]
        + [
            pltpu.VMEM((deep, 4, 3, spad, BLK), BF),
            pltpu.VMEM((2, 3, spad, BLK), BF),
            pltpu.VMEM((2, 1, 3, spad, BLK), BF),
            pltpu.VMEM((deep, 4, 3, spad, BLK), BF),
            pltpu.VMEM((deep + 1, 2, 3, spad, BLK), BF),
            pltpu.VMEM((later - 1, 1, 3, spad, BLK), BF),
            pltpu.VMEM((6, lines, 128), F32),
            pltpu.VMEM((5, lines, 128), F32),
            dma((7 + near,)),
            dma((later,)),
            dma((7,)), dma((7,)),
            dma((2, 4)), dma((2, 4)),
            dma((5,)), dma((5,)),
            dma((4, later)), dma((4, later)),
        ],
        compiler_params=pltpu.CompilerParams(
            vmem_limit_bytes=FF_VMEM, collective_id=1, has_side_effects=True
        ),
        cost_estimate=pl.CostEstimate(
            flops=32 * heads * seq * seq * dk + 8 * seq * d * 3 * cols,
            bytes_accessed=2 * heads * seq * seq + 30 * rows * d,
            transcendentals=0,
        ),
    )(bids, qkv, e, inv, wall, ctx, again, fgain, early, din, mid, cot, tok, nrm, wq, wfar, far,
      quarter, half_way, hand)


def outputs_kernel(near_ref, back_ref, ig_ref, ffi_ref, rel_ref, *refs):
    n = (len(refs) - 4) // 2
    refs, rel_out = refs[:-1], refs[-1]
    sources, res_ref, ig_out, ffi_out, targets = refs[:n], refs[n], refs[n + 1], refs[n + 2], refs[n + 3 :]
    res_ref[...] = near_ref[...] + back_ref[...].astype(F32)
    ig_out[...] = ig_ref[...]
    ffi_out[...] = ffi_ref[...]

    @pl.when(pl.program_id(0) == 0)
    def _():
        for i in range(n):
            targets[i][...] = sources[i][...]
        rel_out[...] = rel_ref[...].T[0 : rel_out.shape[0], 0 : rel_out.shape[1]]


def outputs(near, back, ig, ffi, small, rel_shape, *grads):
    d, rows = near.shape
    block = pl.BlockSpec((d // 4, rows), lambda i: (i, 0))
    shard, two, f = ffi.shape
    part = pl.BlockSpec((shard // 4, two, f), lambda i: (i, 0, 0))
    one = pl.Buffered(1)
    whole = [pl.BlockSpec(v.shape, lambda i, n=v.ndim: (0,) * n, pipeline_mode=one) for v in grads]
    return pl.pallas_call(
        outputs_kernel,
        grid=(4,),
        in_specs=[block] * 3 + [part, pl.BlockSpec((rel_shape[1], 128), lambda i: (0, 0))] + whole,
        out_specs=[block] * 2 + [part] + whole + [pl.BlockSpec(rel_shape, lambda i: (0, 0))],
        out_shape=[jax.ShapeDtypeStruct(v.shape, F32) for v in (near, ig, ffi) + grads]
        + [jax.ShapeDtypeStruct(rel_shape, F32)],
        compiler_params=pltpu.CompilerParams(vmem_limit_bytes=FF_VMEM),
    )(near, back, ig, ffi, small, *grads)


def take(array, index):
    return lax.dynamic_index_in_dim(array, index, 0, keepdims=False)


def per_device(
    tokens,
    cotangent,
    doc_lengths,
    pad_mask,
    attn_gain,
    qkv_weight,
    rel_table,
    out_weight,
    ff_gain,
    ff_in_weight,
    ff_out_weight,
):
    rows, d = tokens.shape
    n_dp = lax.axis_size("dp")
    n_mp = lax.axis_size("mp")
    cols = qkv_weight.shape[2]
    buckets, heads = rel_table.shape
    dk = cols // heads
    me = lax.axis_index("dp")
    shard = d // n_dp
    extra = n_dp // 16

    def hop(v, mask):
        return lax.ppermute(v, "dp", [(i, i ^ mask) for i in range(n_dp)])

    def bit(b):
        return (me >> b) & 1

    def finish(g):
        parts = [g.reshape((extra, shard) + g.shape[1:])]
        for b in reversed(range(extra.bit_length() - 1)):
            halves = [p.reshape((2, p.shape[0] // 2) + p.shape[1:]) for p in parts]
            away = sum(take(p, 1 - bit(b)).astype(F32) for p in halves).astype(BF)
            parts = [take(p, bit(b)) for p in halves] + [hop(away, 1 << b)]
        return sum(p.astype(F32) for p in parts)[0]

    tok = tokens.T
    cot = cotangent.T
    far = lax.ppermute(tok.astype(BF), "mp", [(0, 1), (1, 0)])
    w2 = jnp.transpose(ff_in_weight, (1, 0, 2))
    wq = jnp.transpose(qkv_weight, (1, 2, 0)).reshape(3 * cols, d)
    again, fgain = attn_gain.reshape(1, d), ff_gain.reshape(1, d)

    e, inv, qkv, ctx, nrm, xt, mid, ct, wall = front(
        rel_table, doc_lengths, pad_mask, again, fgain, wq, out_weight.T, tok, far, cot, heads, dk
    )
    early, din, near_out, far_out, quarter, half_way, hand, wfar = ff_all(
        xt, ct, w2, ff_out_weight, mid, wq, extra
    )
    input_grad, back, grad_qkv, grad_out, small, ffo, ffi = tail(
        qkv, e, inv, wall, ctx, again, fgain, early, din, mid, cot, tok, nrm, wq, wfar, far_out,
        quarter, half_way, hand, buckets, heads, dk, extra, ff_out_weight.shape[1],
    )
    for b in range(extra.bit_length() - 1):
        small = small + hop(small, 1 << b)
    result, input_grad, ffi, grad_qkv, grad_out, ffo, rel_grad = outputs(
        near_out, back, input_grad, ffi, small, (heads * n_mp, buckets), grad_qkv, grad_out, ffo
    )
    grad_qkv = jnp.transpose(grad_qkv, (1, 0, 2))
    if extra > 1:
        grad_qkv, grad_out, ffo, ffi = (finish(g) for g in (grad_qkv, grad_out, ffo, ffi))
    lines = -(-d // 128)
    return (
        result.T,
        input_grad.T,
        small[buckets : buckets + lines].reshape(-1)[:d],
        grad_qkv,
        rel_grad.T,
        grad_out,
        small[buckets + lines : buckets + 2 * lines].reshape(-1)[:d],
        ffi,
        ffo,
    )


def solution(mesh):
    return jax.shard_map(
        per_device,
        mesh=mesh,
        in_specs=(
            P(("dp", "mp"), None),
            P(("dp", "mp"), None),
            P("dp", None),
            P("dp", None),
            P(),
            P(None, None, "mp"),
            P(None, "mp"),
            P(None, "mp"),
            P(),
            P(None, None, "mp"),
            P(None, "mp"),
        ),
        out_specs=(
            P(("dp", "mp"), None),
            P(("dp", "mp"), None),
            P(),
            P("dp", None, "mp"),
            P(),
            P("dp", "mp"),
            P(),
            P("dp", None, "mp"),
            P("dp", "mp"),
        ),
        check_vma=False,
    )
```

```python
import functools

import jax
import jax.numpy as jnp
import numpy as np
from jax import lax
from jax.experimental import pallas as pl
from jax.experimental.pallas import tpu as pltpu
from jax.sharding import PartitionSpec as P

MAXDIST = 128
norm_eps = 1e-06
BLK = 256
SPAN = 6 * BLK
REACH = 2
BF = jnp.bfloat16
F32 = jnp.float32
FF_VMEM = 63 << 20


def bucket_of(offsets, buckets, reach):
    half_range = buckets // 2
    upper_half = (offsets > 0).astype(np.int32) * half_range
    distance = np.abs(offsets)
    exact_range = half_range // 2
    safe_dist = np.maximum(distance, 1)
    log_bucket = exact_range + (
        np.log(safe_dist / exact_range) / np.log(reach / exact_range) * (half_range - exact_range)
    ).astype(np.int32)
    log_bucket = np.minimum(log_bucket, half_range - 1)
    return (upper_half + np.where(distance < exact_range, distance, log_bucket)).astype(np.int32)


def lane_buckets(buckets):
    lanes = np.arange(SPAN)
    shifted = np.where(lanes < 5 * BLK, lanes, lanes - SPAN)
    return bucket_of(REACH * BLK - shifted, buckets, MAXDIST).reshape(1, SPAN)


def dot(a, b, contract):
    return lax.dot_general(a, b, (contract, ((), ())), preferred_element_type=F32)


def flip(index, mask):
    out = index
    bit = 1
    while bit <= mask:
        if mask & bit:
            out = out + bit * (1 - 2 * (index // bit % 2))
        bit *= 2
    return out


GROUP_MASKS = (1, 2, 4, 12)


def group_coords(g):
    b = [g // (1 << i) % 2 for i in range(4)]
    return [b[0], b[1], (b[2] + b[3]) % 2, b[3]]


Y_FIRST = (0, 1, 2, 3)
Z_FIRST = (0, 2, 3, 1)
Z_BLOCK = 1
LEVELS = (4, 3, 3, 2)


def order_of(block):
    return Z_FIRST if block == Z_BLOCK else Y_FIRST


def levels_of(block):
    return LEVELS[block] if block < len(LEVELS) else 1


def block_position(k, order):
    b = [k >> i & 1 for i in range(4)]
    c = [b[0], b[1], b[2] ^ b[3], b[3]]
    return sum(c[order[i]] << (3 - i) for i in range(4))


def column(line):
    return jnp.broadcast_to(line, (8, line.shape[1])).T[:, 0:1]


def norm_scale(v):
    return lax.rsqrt(jnp.mean(v * v, axis=0, keepdims=True) + norm_eps)


def lanes(block):
    return pl.ds(pl.multiple_of(block * BLK, BLK), BLK)


def remote(src, dst, send, recv, who):
    return pltpu.make_async_remote_copy(
        src_ref=src,
        dst_ref=dst,
        send_sem=send,
        recv_sem=recv,
        device_id=who,
        device_id_type=pl.DeviceIdType.MESH,
    )


def meet(devices):
    barrier = pltpu.get_barrier_semaphore()
    for who in devices:
        pl.semaphore_signal(barrier, inc=1, device_id=who, device_id_type=pl.DeviceIdType.MESH)
    pl.semaphore_wait(barrier, len(devices))


def near_diagonal(offset):
    i = offset + 3
    return i + (6 - i) // 6 - i // 6 - 1


def front_kernel(
    heads, dk, buckets, blocks,
    rel_ref, len_ref, bid_ref, pad_ref, ag_ref, fg_ref, wq_ref, wo_ref,
    tok_hbm, far_hbm, cot_hbm,
    e_ref, inv_ref, qkv_ref, ctx_hbm, nrm_hbm, xt_hbm, mid_hbm, ct_hbm, wall_hbm,
    f1, fb, f3, cl, nrm, table, padc, mask, score, agc, fgc, wall, wn, call, xo,
    lsem, osem, wsend, wrecv, csend, crecv,
):
    qb = pl.program_id(0)
    dp, x = lax.axis_index("dp"), lax.axis_index("mp")
    d, rows = f1.shape
    cols = heads * dk
    half = cols // 2
    core = dp % 2
    other = (dp, 1 - x)
    sibling = (dp + 1 - 2 * core, x)
    near_blocks = blocks // 2
    part = pl.ds(core * half, half)
    far_part = pl.ds(cols + core * half, half)

    def local(i):
        src, dst = ((tok_hbm, f1), (far_hbm, fb), (cot_hbm, f3))[i]
        return pltpu.make_async_copy(src, dst, lsem.at[i])

    def out(i):
        src, dst = (
            (call, ctx_hbm), (nrm, nrm_hbm), (f1.at[:, lanes(0)], mid_hbm.at[:, lanes(0)]), (cl, ct_hbm.at[:, pl.ds(0, rows)]), (wall, wall_hbm),
            (f1.at[:, pl.ds(BLK, rows - BLK)], mid_hbm.at[:, pl.ds(BLK, rows - BLK)]),
        )[i]
        return pltpu.make_async_copy(src, dst, osem.at[i])

    def xt_out(b):
        return pltpu.make_async_copy(xo.at[:, lanes(b)], xt_hbm.at[:, lanes(b)], osem.at[6 + b])

    w_copy = remote(wo_ref.at[part], wall.at[far_part], wsend.at[0], wrecv.at[0], other)
    w_pass = remote(wall.at[far_part], wall.at[far_part], wsend.at[1], wrecv.at[1], sibling)
    piece = d // 4

    def c_copy(i):
        rs = pl.ds(i * piece, piece)
        return remote(
            cl.at[rs, pl.ds(0, BLK)], ct_hbm.at[rs, pl.ds(rows, BLK)], wsend.at[2 + i], wrecv.at[2 + i], other
        )

    def ctx_copy(b):
        there = (b + near_blocks) % blocks
        return remote(
            call.at[pl.ds(0, cols), lanes(b)], call.at[pl.ds(cols, cols), lanes(there)],
            csend.at[b], crecv.at[b], other,
        )

    @pl.when(qb == 0)
    def _():
        for i in (2, 0, 1):
            local(i).start()
        meet([other, sibling])
        w_copy.start()
        wall[0:cols, :] = wo_ref[...]
        local(2).wait()
        cl[...] = f3[...].astype(BF)
        c_copy(0).start()
        c_copy(1).start()
        out(3).start()
        agc[...] = column(ag_ref[...])
        fgc[...] = column(fg_ref[...])
        local(0).wait()
        local(1).wait()
        for b in range(blocks):
            ls = slice(b * BLK, (b + 1) * BLK)
            v = f1[:, ls] if b < near_blocks else fb[:, b * BLK - rows : (b + 1) * BLK - rows].astype(F32)
            nrm[:, ls] = (v * norm_scale(v) * agc[...]).astype(BF)
            qkv_ref[:, ls] = dot(wq_ref[...], nrm[:, ls], ((1,), (0,))).astype(BF)
        out(1).start()
        for i in range(2):
            start = (1 - x) * rows if i else x * rows
            line = pad_ref[:, pl.ds(pl.multiple_of(start, BLK), rows)].astype(F32)
            padc[i * rows : (i + 1) * rows, :] = jnp.broadcast_to(line, (8, rows)).T
        ids = bid_ref[...]
        for hh in range(heads):
            line = jnp.zeros((1, SPAN), F32)
            for b in range(buckets):
                line = jnp.where(ids == b, rel_ref[b, hh], line)
            turned = pltpu.roll(
                jnp.broadcast_to(line, (BLK, SPAN)), 0, 1, stride=1, stride_axis=0
            )
            for g in range(5):
                table[hh, g] = turned[:, BLK * (4 - g) : BLK * (5 - g)]

    @pl.when(qb == 1)
    def _():
        w_copy.wait()
        w_pass.start()

    q_true = (qb + near_blocks * x) % blocks

    q_pos = q_true * BLK + lax.broadcasted_iota(jnp.int32, (1, BLK), 1)
    k_iota = lax.broadcasted_iota(jnp.int32, (BLK, BLK), 0)
    for kb in range(blocks):
        k_pos = (kb + near_blocks * x) % blocks * BLK + k_iota
        bound = 0
        q_doc = jnp.zeros((1, BLK), jnp.int32)
        k_doc = jnp.zeros((BLK, BLK), jnp.int32)
        for i in range(len_ref.shape[1]):
            bound = bound + len_ref[0, i]
            q_doc = q_doc + (q_pos >= bound).astype(jnp.int32)
            k_doc = k_doc + (k_pos >= bound).astype(jnp.int32)
        krows = slice(kb * BLK, (kb + 1) * BLK)
        seen = (padc[krows, 0:1] > 0.5) | (k_pos == q_pos)
        mask[krows, :] = jnp.where((k_doc == q_doc) & seen, 0.0, -1000000000.0)

    def head_rows(h, group):
        return pl.ds(pl.multiple_of(group * cols + h * dk, dk), dk)

    def diagonal(kb):
        return near_diagonal((kb + near_blocks * x) % blocks - q_true)

    def head(h, carry):
        qh = qkv_ref[head_rows(h, 0), lanes(qb)]
        peak = None
        for kb in range(blocks):
            krows = slice(kb * BLK, (kb + 1) * BLK)
            s = dot(qkv_ref[head_rows(h, 1), krows], qh, ((0,), (0,)))
            diag = diagonal(kb)
            s = s + table[h, diag] + mask[krows, :]
            score[krows, :] = s
            top = jnp.max(s, axis=0, keepdims=True)
            peak = top if peak is None else jnp.maximum(peak, top)
        total = jnp.zeros((1, BLK), F32)
        ctx = jnp.zeros((dk, BLK), F32)
        for kb in range(blocks):
            krows = slice(kb * BLK, (kb + 1) * BLK)
            e = jnp.exp(score[krows, :] - peak)
            total = total + jnp.sum(e, axis=0, keepdims=True)
            e_low = e.astype(BF)
            e_ref[h, 0, krows, :] = e_low
            ctx = ctx + dot(qkv_ref[head_rows(h, 2), krows], e_low, ((1,), (0,)))
        inv = 1.0 / total
        inv_ref[h, 0] = inv
        call[head_rows(h, 0), lanes(qb)] = (ctx * inv).astype(BF)
        return carry

    lax.fori_loop(0, heads, head, 0)
    ctx_copy(qb).start()

    @pl.when(qb == 1)
    def _():
        c_copy(2).start()

    @pl.when(qb == blocks - 1)
    def _():
        c_copy(3).start()
        w_pass.wait()
        wn[...] = wall[...].astype(F32).T.astype(BF)
        out(4).start()
        for i in range(blocks):
            b = (i + near_blocks) % blocks
            ctx_copy(i).wait()
            ls = slice(b * BLK, (b + 1) * BLK)
            v = dot(wn[...], call[:, ls], ((1,), (0,)))
            if b < near_blocks:
                v = v + f1[:, ls]
                f1[:, ls] = v
                if b == 0:
                    out(2).start()
            else:
                v = v + fb[:, b * BLK - rows : (b + 1) * BLK - rows].astype(F32)
            xo[:, ls] = (v * norm_scale(v) * fgc[...]).astype(BF)
            xt_out(b).start()
        out(0).start()
        out(5).start()
        for i in range(4):
            c_copy(i).wait()
        for i in range(6):
            out(i).wait()
        for b in range(blocks):
            xt_out(b).wait()


def front(rel, lengths, pad, again, fgain, wq, wo, tok, far, cot, heads, dk):
    d, rows = tok.shape
    seq = 2 * rows
    cols = heads * dk
    blocks = seq // BLK
    buckets = rel.shape[0]
    bids = jnp.asarray(lane_buckets(buckets))
    one = pl.Buffered(1)
    dma = pltpu.SemaphoreType.DMA
    any_spec = pl.BlockSpec(memory_space=pl.ANY)
    smem = pl.BlockSpec(memory_space=pltpu.SMEM)

    def full(v):
        return pl.BlockSpec(v.shape, lambda i: (0, 0), pipeline_mode=one)

    return pl.pallas_call(
        functools.partial(front_kernel, heads, dk, buckets, blocks),
        grid=(blocks,),
        in_specs=[smem, smem, full(bids), full(pad), full(again), full(fgain), full(wq), full(wo)]
        + [any_spec] * 3,
        out_specs=[
            pl.BlockSpec((heads, 1, seq, BLK), lambda i: (0, i, 0, 0)),
            pl.BlockSpec((heads, 1, 1, BLK), lambda i: (0, i, 0, 0)),
            pl.BlockSpec((3 * cols, seq), lambda i: (0, 0)),
        ]
        + [any_spec] * 6,
        out_shape=[
            jax.ShapeDtypeStruct((heads, blocks, seq, BLK), BF),
            jax.ShapeDtypeStruct((heads, blocks, 1, BLK), F32),
            jax.ShapeDtypeStruct((3 * cols, seq), BF),
            jax.ShapeDtypeStruct((2 * cols, seq), BF),
            jax.ShapeDtypeStruct((d, seq), BF),
            jax.ShapeDtypeStruct((d, seq), BF),
            jax.ShapeDtypeStruct((d, rows), F32),
            jax.ShapeDtypeStruct((d, seq), BF),
            jax.ShapeDtypeStruct((2 * cols, d), BF),
        ],
        scratch_shapes=[
            pltpu.VMEM((d, rows), F32),
            pltpu.VMEM((d, rows), BF),
            pltpu.VMEM((d, rows), F32),
            pltpu.VMEM((d, rows), BF),
            pltpu.VMEM((d, seq), BF),
            pltpu.VMEM((heads, 5, BLK, BLK), F32),
            pltpu.VMEM((seq, 8), F32),
            pltpu.VMEM((seq, BLK), F32),
            pltpu.VMEM((seq, BLK), F32),
            pltpu.VMEM((d, 1), F32),
            pltpu.VMEM((d, 1), F32),
            pltpu.VMEM((2 * cols, d), BF),
            pltpu.VMEM((d, 2 * cols), BF),
            pltpu.VMEM((2 * cols, seq), BF),
            pltpu.VMEM((d, seq), BF),
            dma((3,)), dma((6 + blocks,)), dma((6,)), dma((6,)), dma((blocks,)), dma((blocks,)),
        ],
        compiler_params=pltpu.CompilerParams(
            vmem_limit_bytes=FF_VMEM, collective_id=2, has_side_effects=True
        ),
        cost_estimate=pl.CostEstimate(
            flops=16 * heads * seq * seq * dk + 10 * seq * d * cols,
            bytes_accessed=2 * heads * seq * seq + 30 * rows * d,
            transcendentals=heads * seq * seq,
        ),
    )(rel, lengths, bids, pad, again, fgain, wq, wo, tok, far, cot)


def ff_kernel(
    steps, extra,
    xt_hbm, w_hbm, ct_hbm, wo_hbm, mid_hbm, wq_hbm,
    grads_ref, din_hbm, near_hbm, far_hbm, quarter_hbm, half_hbm, hand_hbm, wfar_hbm,
    xt, ct, wg, wu, wo, hid, dg, du, din, stage, r1, r2, r3, r4, xs, xr, of,
    csem, wsem, s1, s2, s3, s4, t1, t2, t3, t4, xsem, osem, hsem,
):
    f, total = hid.shape
    rows = total // 2
    chunks = rows // BLK
    d = xt.shape[0]
    shard = d // 16
    dp, mp = lax.axis_index("dp"), lax.axis_index("mp")
    a = group_coords(dp // extra)
    peers = [flip(dp, m * extra) for m in GROUP_MASKS]
    other = (dp, 1 - mp)
    core = dp % 2
    sibling = dp + 1 - 2 * core
    bufs = (r1, r2, r3, r4)
    sends, recvs = (s1, s2, s3, s4), (t1, t2, t3, t4)
    end = steps - 1

    def weight_copy(kind, n):
        src, dst = ((w_hbm.at[0], wg), (w_hbm.at[1], wu), (wo_hbm, wo))[kind]
        return pltpu.make_async_copy(src.at[:, lanes(n)], dst.at[:, lanes(n)], wsem.at[kind, n])

    def tok_copy(n):
        src, dst, start, size = (
            (xt_hbm, xt, rows, BLK), (ct_hbm, ct, rows, BLK),
            (xt_hbm, xt, 0, rows), (ct_hbm, ct, 0, rows), (xt_hbm, xt, rows + BLK, BLK),
        )[n]
        part = pl.ds(start, size)
        return pltpu.make_async_copy(src.at[:, part], dst.at[:, part], csem.at[n])

    near_part, far_part = pl.ds(0, rows), pl.ds(rows, rows)
    c_far = remote(
        ct_hbm.at[:, pl.ds(BLK, BLK)], ct.at[:, pl.ds(rows + BLK, BLK)], csem.at[5], csem.at[6], other
    )
    x_copy = remote(xs, xr, xsem.at[0], xsem.at[1], other)
    wq_rows = wq_hbm.shape[0] // 2
    wq_part = pl.ds(core * wq_rows, wq_rows)
    w_copy = remote(wq_hbm.at[wq_part], wfar_hbm.at[wq_part], xsem.at[2], xsem.at[3], other)
    w_pass = remote(wfar_hbm.at[wq_part], wfar_hbm.at[wq_part], xsem.at[4], xsem.at[5], (sibling, mp))
    mid_copy = pltpu.make_async_copy(mid_hbm, din.at[:, far_part], osem.at[3])

    deep = len(LEVELS)

    def hop(level, n, order):
        half = 8 >> level
        c = order[level]
        away = pl.ds((1 - a[c]) * half, half)
        src = stage.at[away] if level == 0 else bufs[level - 1].at[n, away]
        return remote(src, bufs[level].at[n], sends[level].at[n], recvs[level].at[n], (peers[c], mp))

    def hand_copy(n):
        level = levels_of(n) if isinstance(n, int) else 1
        dst = (hand_hbm.at[n - deep], half_hbm, quarter_hbm.at[n - 1])[level - 1]
        return pltpu.make_async_copy(bufs[level - 1].at[n], dst, hsem.at[n])

    def absorb_first(n):
        hop(0, n, Y_FIRST).wait()
        r1[n] = stage[pl.ds(a[0] * 8, 8)] + r1[n]
        if isinstance(n, int):
            hand_copy(n).start()
            return

        @pl.when(n == Z_BLOCK)
        def _():
            hop(1, n, Z_FIRST).start()

        @pl.when((n < deep) & (n != Z_BLOCK))
        def _():
            hop(1, n, Y_FIRST).start()

        @pl.when(n >= deep)
        def _():
            hand_copy(n).start()

    def absorb(level, n):
        half = 8 >> level
        order = order_of(n)
        hop(level, n, order).wait()
        kept = bufs[level - 1][n, pl.ds(a[order[level]] * half, half)]
        if level < 3:
            bufs[level][n] = kept + bufs[level][n]
            if level + 1 < levels_of(n):
                hop(level + 1, n, order).start()
            else:
                hand_copy(n).start()
        else:
            both = kept.astype(F32) + bufs[level][n].astype(F32)
            for w in range(3):
                grads_ref[w, :, n * BLK : (n + 1) * BLK] = both[0, w]

    scale = np.float32(np.sqrt(2 / np.pi))

    def place(u):
        early, late = u // steps, (u - 4) // steps
        is_far0 = (early == 0) * 1
        is_far1 = (late == 1) * 1
        v = u - steps
        n = v - steps * (u // (2 * steps + 4))
        near_j, near_c = n // 2, n % 2
        j = is_far0 * u + is_far1 * (u - steps - 4) + (1 - is_far0 - is_far1) * near_j
        c = is_far0 * chunks + is_far1 * (chunks + 1) + (1 - is_far0 - is_far1) * near_c
        return j, c

    def substep(u):
        j, c = place(u)
        pj, pc = place(u - 1)
        pj = pj + (u == 0) * 1
        fcols, tok = lanes(j), lanes(c)
        pcols, ptok = lanes(pj), lanes(pc)
        gate = dot(wg[:, fcols], xt[:, tok], ((0,), (0,)))
        up = dot(wu[:, fcols], xt[:, tok], ((0,), (0,)))
        dh = dot(wo[:, fcols], ct[:, tok], ((0,), (0,)))
        backward(pcols, ptok)
        sq = gate * gate
        t = jnp.tanh(scale * gate * (1.0 + 0.044715 * sq))
        half = 0.5 * (1.0 + t)
        act = gate * half
        slope = half + 0.5 * gate * (1.0 - t * t) * (scale * (1.0 + (3 * 0.044715) * sq))
        hid[fcols, tok] = (act * up).astype(BF)
        dg[fcols, tok] = (dh * (up * slope)).astype(BF)
        du[fcols, tok] = (dh * act).astype(BF)

    def backward(rs, tok):
        din[:, tok] += dot(wg[:, rs], dg[rs, tok], ((1,), (0,))) + dot(wu[:, rs], du[rs, tok], ((1,), (0,)))

    per = 4 * shard

    def grads(j):
        z = (j == Z_BLOCK) * 1
        for w in range(3):
            right = (hid, dg, du)[w][lanes(j), :]
            for q in range(4):
                rs = slice(q * per, (q + 1) * per)
                left = ct[rs, :] if w == 0 else xt[rs, :]
                part = dot(left, right, ((1,), (1,)))
                for k in range(4):
                    at = block_position(4 * q + k, Y_FIRST)
                    at = at + z * (block_position(4 * q + k, Z_FIRST) - at)
                    stage[at, w, 0:shard, :] = part[k * shard : (k + 1) * shard].astype(BF)
        hop(0, j, Y_FIRST).start()

    def out_part(n):
        return dot(wo[...], hid[:, lanes(n)], ((1,), (0,)))

    meet([(p, mp) for p in peers] + [other] + ([(sibling, mp)] if extra > 1 else []))
    c_far.start()
    w_copy.start()
    tok_copy(0).start()
    tok_copy(1).start()
    for n in range(steps):
        for kind in range(3):
            weight_copy(kind, n).start()
    for n in range(2, 5):
        tok_copy(n).start()
    din[...] = jnp.zeros_like(din)
    stage[...] = jnp.zeros_like(stage)
    before = place(-1)[1]
    dg[0:BLK, before * BLK : (before + 1) * BLK] = jnp.zeros((BLK, BLK), BF)
    du[0:BLK, before * BLK : (before + 1) * BLK] = jnp.zeros((BLK, BLK), BF)
    tok_copy(0).wait()
    tok_copy(1).wait()
    count = 2 * chunks * steps
    far_end = 2 * steps + 4

    def step(u, carry):
        @pl.when(u < steps)
        def _():
            for kind in range(3):
                weight_copy(kind, u).wait()

        @pl.when(u == steps)
        def _():
            tok_copy(2).wait()
            tok_copy(3).wait()

        @pl.when(u == steps + 4)
        def _():
            tok_copy(4).wait()
            c_far.wait()

        @pl.when(u < count)
        def _():
            substep(u)

        @pl.when(u == far_end)
        def _():
            xs[...] = din[:, far_part].astype(BF)
            x_copy.start()
            mid_copy.start()

        odd = u % 2 == 1
        late = (u >= 2 * steps + 5) * 1
        m = (u - 13) // 2 - 2 * ((u >= 2 * steps + 7) * 1)
        n = (u - 11) // 2 - 2 * late

        @pl.when(odd & ((u == 13) | (u == 15) | (u >= 2 * steps + 7)))
        def _():
            absorb_first(m)

        for at, events in (
            (21, ((1, 0),)), (23, ((1, 1),)), (25, ((2, 0),)), (27, ((1, 2),)),
        ):
            @pl.when(u == at)
            def _():
                for level, block in events:
                    absorb(level, block)

        @pl.when(odd & ((u == 11) | (u == 13) | (u >= 2 * steps + 5)))
        def _():
            grads(n)

        @pl.when(u == far_end + 5)
        def _():
            w_copy.wait()
            w_pass.start()

        return carry

    lax.fori_loop(0, count, step, 0)
    pj, pc = place(count - 1)
    backward(lanes(pj), lanes(pc))

    def far_out(n, carry):
        of[:, lanes(n)] = out_part(n + chunks).astype(BF)
        return carry

    lax.fori_loop(0, chunks, far_out, 0)
    absorb(2, 1)
    far_copy = pltpu.make_async_copy(of, far_hbm, osem.at[0])
    far_copy.start()
    mid_copy.wait()

    def near_out(n, carry):
        at = lanes(n + chunks)
        din[:, at] = din[:, at] + out_part(n)
        return carry

    lax.fori_loop(0, chunks, near_out, 0)
    near_copy = pltpu.make_async_copy(din.at[:, far_part], near_hbm, osem.at[1])
    near_copy.start()
    absorb_first(end)
    x_copy.wait()
    din[:, near_part] += xr[...].astype(F32)
    din_copy = pltpu.make_async_copy(din.at[:, near_part], din_hbm, osem.at[2])
    din_copy.start()
    absorb(3, 0)
    absorb(2, 2)
    absorb(1, 3)
    w_pass.wait()
    for n in range(1, steps):
        hand_copy(n).wait()
    far_copy.wait()
    near_copy.wait()
    din_copy.wait()


def ff_all(xt, ct, w2, wo, mid, wq, extra):
    d, total = xt.shape
    f = wo.shape[1]
    rows = total // 2
    steps = f // BLK
    deep = len(LEVELS)
    shard = d // 16
    spad = -(-shard // 16) * 16
    dma = pltpu.SemaphoreType.DMA
    any_spec = pl.BlockSpec(memory_space=pl.ANY)
    return pl.pallas_call(
        functools.partial(ff_kernel, steps, extra),
        in_specs=[any_spec] * 6,
        out_specs=[pl.BlockSpec(memory_space=pltpu.VMEM)] + [any_spec] * 7,
        out_shape=[
            jax.ShapeDtypeStruct((3, spad, BLK), F32),
            jax.ShapeDtypeStruct((d, rows), F32),
            jax.ShapeDtypeStruct((d, rows), F32),
            jax.ShapeDtypeStruct((d, rows), BF),
            jax.ShapeDtypeStruct((2, 2, 3, spad, BLK), BF),
            jax.ShapeDtypeStruct((4, 3, spad, BLK), BF),
            jax.ShapeDtypeStruct((steps - deep, 8, 3, spad, BLK), BF),
            jax.ShapeDtypeStruct(wq.shape, BF),
        ],
        scratch_shapes=[
            pltpu.VMEM((d, total), BF),
            pltpu.VMEM((d, total), BF),
            pltpu.VMEM((d, f), BF),
            pltpu.VMEM((d, f), BF),
            pltpu.VMEM((d, f), BF),
            pltpu.VMEM((f, total), BF),
            pltpu.VMEM((f, total), BF),
            pltpu.VMEM((f, total), BF),
            pltpu.VMEM((d, total), F32),
            pltpu.VMEM((16, 3, spad, BLK), BF),
            pltpu.VMEM((steps, 8, 3, spad, BLK), BF),
            pltpu.VMEM((4, 4, 3, spad, BLK), BF),
            pltpu.VMEM((3, 2, 3, spad, BLK), BF),
            pltpu.VMEM((1, 1, 3, spad, BLK), BF),
            pltpu.VMEM((d, rows), BF),
            pltpu.VMEM((d, rows), BF),
            pltpu.VMEM((d, rows), BF),
            dma((7,)),
            dma((3, steps)),
            dma((steps,)), dma((4,)), dma((3,)), dma((1,)),
            dma((steps,)), dma((4,)), dma((3,)), dma((1,)),
            dma((6,)),
            dma((4,)),
            dma((steps,)),
        ],
        compiler_params=pltpu.CompilerParams(
            vmem_limit_bytes=FF_VMEM, collective_id=0, has_side_effects=True
        ),
        cost_estimate=pl.CostEstimate(
            flops=18 * total * d * f,
            bytes_accessed=6 * d * f + 16 * total * d,
            transcendentals=total * f,
        ),
    )(xt, w2, ct, wo, mid, wq)


EVENTS = (
    ((0, 0), ((2, 3), (3, 2))),
    ((0, 2), ((1, 4),)),
    ((2, 0), ((3, 3),)),
    ((2, 1), ((2, 4),)),
    ((3, 2), ((1, 5),)),
)


def tail_kernel(
    heads, dk, buckets, blocks, extra,
    bid_ref, qkv_ref, e_ref, inv_ref, wall_ref, ctx_ref, ag_ref, fg_ref, early_ref,
    din_hbm, mid_hbm, cot_hbm, tok_hbm, nrm_hbm, wq_hbm, wfar_hbm, far_hbm,
    quarter_hbm, half_hbm, hand_hbm,
    ig_hbm, back_hbm, gq_ref, go_ref, small_ref, ffo_ref, ffi_ref,
    f1, f2, f3, nrm, wq, wn, wf, alow, dctx, dcs, osend, orecv, fsum, agc, fgc,
    dp_s, dkv, tally, dproj, dfar, grad,
    sa, sb_, a1, a2, a3, a4, b1, b2, b3, b4, hk, hm, hq, h2, h3, h4, sv, rv,
    lsem, ksem, xs_sem, xr_sem, cs_sem, cr_sem, bs_sem, br_sem, hs_sem, hr_sem,
):
    qb = pl.program_id(0)
    dp, x = lax.axis_index("dp"), lax.axis_index("mp")
    d, rows = f2.shape
    cols = heads * dk
    shard = d // 16
    a = group_coords(dp // extra)
    peers = [flip(dp, m * extra) for m in GROUP_MASKS]
    other = (dp, 1 - x)
    near_blocks = blocks // 2
    near_part, far_part = pl.ds(0, rows), pl.ds(rows, rows)
    halves = ((sa, a1, a2, a3, a4), (sb_, b1, b2, b3, b4))
    orders = (Y_FIRST, Y_FIRST)
    copies = (
        (din_hbm, f1), (mid_hbm, f2), (cot_hbm, f3), (tok_hbm, f2), (nrm_hbm, nrm), (wq_hbm, wq), (wfar_hbm, wq),
    )

    def local(i):
        return pltpu.make_async_copy(copies[i][0], copies[i][1], lsem.at[i])

    def x_copy(i, src, dst):
        return remote(src, dst, xs_sem.at[i], xr_sem.at[i], other)

    dctx_copy = x_copy(0, dcs, dctx.at[:, far_part])
    o_copy = x_copy(1, osend, orecv)
    dproj_copy = x_copy(2, dproj.at[:, far_part], dfar)

    def back_copy(i):
        part = pl.ds(i * 128, 128)
        return x_copy(3 + i, far_hbm.at[:, part], back_hbm.at[:, part])

    def hop(side, level):
        half = 8 >> level
        c = orders[side][level]
        away = pl.ds((1 - a[c]) * half, half)
        bufs = halves[side]
        return remote(
            bufs[level].at[away], bufs[level + 1], cs_sem.at[side, level], cr_sem.at[side, level], (peers[c], x)
        )

    def absorb(side, level):
        half = 8 >> level
        bufs = halves[side]
        hop(side, level).wait()
        kept = bufs[level][pl.ds(a[orders[side][level]] * half, half)]
        if level < 3:
            bufs[level + 1][...] = kept + bufs[level + 1][...]
            hop(side, level + 1).start()
            return
        both = (kept.astype(F32) + bufs[level + 1][...].astype(F32))[0, 0:shard]
        outs = (gq_ref.at[0], gq_ref.at[1]) if side == 0 else (gq_ref.at[2], go_ref)
        for i in range(2):
            outs[i][...] = both[:, i * cols : (i + 1) * cols]

    deep = len(LEVELS)
    handed = (3, 4, 2, 5, 6, 1)

    def keep_copy(block):
        level = levels_of(block)
        half = 8 >> level
        keep = pl.ds(a[order_of(block)[level]] * half, half)
        if level == 3:
            src, dst = quarter_hbm.at[block - 1, keep], hq.at[block - 1]
        elif level == 2:
            src, dst = half_hbm.at[keep], hm
        else:
            src, dst = hand_hbm.at[block - deep, keep], hk.at[block - deep]
        return pltpu.make_async_copy(src, dst, ksem.at[block])

    def hand_hop(level, block):
        half = 8 >> level
        c = order_of(block)[level]
        away = pl.ds((1 - a[c]) * half, half)
        fresh = level == levels_of(block)
        if level == 1:
            src, dst = hand_hbm.at[block - deep, away], h2.at[block - deep]
        elif level == 2:
            src, dst = half_hbm.at[away] if fresh else h2.at[block - deep, away], h3.at[block - 3]
        else:
            src, dst = quarter_hbm.at[block - 1, away] if fresh else h3.at[block - 3, away], h4.at[block - 1]
        return remote(src, dst, hs_sem.at[level, block], hr_sem.at[level, block], (peers[c], x))

    def put_grads(w, block, value):
        at = slice(block * BLK, (block + 1) * BLK)
        if w == 0:
            ffo_ref[:, at] = value
        else:
            ffi_ref[:, w - 1, at] = value

    def hand_absorb(level, block):
        half = 8 >> level
        keep = pl.ds(a[order_of(block)[level]] * half, half)
        hand_hop(level, block).wait()
        if level == levels_of(block):
            keep_copy(block).wait()
            kept = hk[block - deep] if level == 1 else (hm[...] if level == 2 else hq[block - 1])
        else:
            kept = h2[block - deep, keep] if level == 2 else h3[block - 3, keep]
        if level == 1:
            h2[block - deep] = kept + h2[block - deep]
        elif level == 2:
            h3[block - 3] = kept + h3[block - 3]
        else:
            both = kept.astype(F32) + h4[block - 1].astype(F32)
            for w in range(3):
                put_grads(w, block, both[0, w, 0:shard])
        if level < 3:
            hand_hop(level + 1, block).start()

    def round_copy(i):
        who = other if i == 4 else (peers[(0, 2, 3, 1)[i]], x)
        return remote(sv.at[i], rv.at[i], bs_sem.at[i], br_sem.at[i], who)

    def round_end(i):
        round_copy(i).wait()
        sv[i + 1] = sv[i] + rv[i]
        if i < 4:
            round_copy(i + 1).start()

    def out_copy(r):
        return pltpu.make_async_copy(f3.at[:, lanes(r)], ig_hbm.at[:, lanes(r)], lsem.at[len(copies) + r])

    def lane_sum(v):
        total = v[:, 0:128]
        for i in range(1, v.shape[1] // 128):
            total = total + v[:, i * 128 : (i + 1) * 128]
        return total

    @pl.when(qb == 0)
    def _():
        for i in range(3):
            local(i).start()
        meet([(p, x) for p in peers] + [other])
        back_copy(0).start()
        for block in handed[:-1]:
            hand_hop(levels_of(block), block).start()
        agc[...] = column(ag_ref[...])
        fgc[...] = column(fg_ref[...])
        dkv[...] = jnp.zeros_like(dkv)
        tally[...] = jnp.zeros_like(tally)
        sa[...] = jnp.zeros_like(sa)
        sb_[...] = jnp.zeros_like(sb_)
        fsum[...] = jnp.zeros_like(fsum)
        for i in range(3):
            local(i).wait()

        def norm_rows(r, carry):
            ls = lanes(r)
            v = f2[:, ls]
            c = f1[:, ls]
            scale = norm_scale(v)
            n = v * scale
            cg = c * fgc[...]
            m = jnp.mean(cg * n, axis=0, keepdims=True)
            gm = f3[:, ls] + scale * (cg - n * m)
            fsum[...] += lane_sum(c * n)
            f1[:, ls] = gm
            alow[:, ls] = gm.astype(BF)
            return carry

        lax.fori_loop(0, near_blocks, norm_rows, 0)
        dcs[...] = dot(wall_ref[cols : 2 * cols, :], alow[...], ((1,), (0,))).astype(BF)
        dctx_copy.start()
        for i in (3, 4, 5):
            local(i).start()
        for block in handed:
            keep_copy(block).start()
        dctx[:, near_part] = dot(wall_ref[0:cols, :], alow[...], ((1,), (0,))).astype(BF)
        osend[...] = dot(alow[...], ctx_ref[cols : 2 * cols, near_part], ((1,), (1,))).astype(BF)
        o_copy.start()
        grad[:, 3 * cols : 4 * cols] = dot(alow[...], ctx_ref[0:cols, near_part], ((1,), (1,)))
        for w in range(3):
            put_grads(w, 0, early_ref[w, 0:shard, :])
        dctx_copy.wait()
        back_copy(1).start()

    @pl.when(qb == 1)
    def _():
        local(5).wait()
        wn[...] = wq[...].astype(F32).T.astype(BF)
        local(6).start()

    @pl.when(qb == 2)
    def _():
        local(6).wait()
        wf[...] = wq[...].astype(F32).T.astype(BF)

    q_true = (qb + near_blocks * x) % blocks

    def head(h, carry):
        for at, events in EVENTS:
            @pl.when((qb == at[0]) & (h == at[1]))
            def _():
                for level, block in events:
                    hand_absorb(level, block)

        def head_rows(group):
            return pl.ds(pl.multiple_of(group * cols + h * dk, dk), dk)

        inv = inv_ref[h, 0]
        qh = qkv_ref[head_rows(0), lanes(qb)]
        scaled = (dctx[head_rows(0), lanes(qb)].astype(F32) * inv).astype(BF)
        inner = jnp.zeros((1, BLK), F32)
        for kb in range(blocks):
            krows = slice(kb * BLK, (kb + 1) * BLK)
            g = dot(qkv_ref[head_rows(2), krows], scaled, ((0,), (0,)))
            dp_s[krows, :] = g
            inner = inner + jnp.sum(e_ref[h, 0, krows, :].astype(F32) * g, axis=0, keepdims=True)
        inner = inner * inv
        dq = jnp.zeros((dk, BLK), F32)
        for kb in range(blocks):
            krows = slice(kb * BLK, (kb + 1) * BLK)
            e = e_ref[h, 0, krows, :]
            ds = (e.astype(F32) * (dp_s[krows, :] - inner)).astype(BF)
            dkv[head_rows(0), krows] += dot(qh, ds, ((1,), (1,)))
            dkv[head_rows(1), krows] += dot(scaled, e, ((1,), (1,)))
            dq = dq + dot(qkv_ref[head_rows(1), krows], ds, ((1,), (0,)))
            tally[h, near_diagonal((kb + near_blocks * x) % blocks - q_true)] += ds.astype(F32)
        dproj[head_rows(0), lanes(qb)] = dq.astype(BF)
        return carry

    lax.fori_loop(0, heads, head, 0)

    @pl.when(qb == blocks - 1)
    def _():
        dproj[cols : 3 * cols, :] = dkv[...].astype(BF)
        dproj_copy.start()
        back_copy(2).start()
        back_copy(3).start()
        local(3).wait()
        local(4).wait()
        per = 4 * shard

        def grad_rows(q, carry):
            rs = pl.ds(pl.multiple_of(q * per, 16), per)
            grad[rs, 0 : 3 * cols] = dot(nrm[rs, :], dproj[...], ((1,), (1,)))
            return carry

        lax.fori_loop(0, 4, grad_rows, 0)
        o_copy.wait()
        grad[:, 3 * cols : 4 * cols] += orecv[...].astype(F32)
        for side in range(2):
            for k in range(16):
                halves[side][0][block_position(k, orders[side]), 0:shard, :] = grad[
                    k * shard : (k + 1) * shard, 2 * side * cols : 2 * (side + 1) * cols
                ].astype(BF)
            hop(side, 0).start()
        hand_absorb(2, 5)

        def near_rows(r, carry):
            f3[:, lanes(r)] = dot(wn[...], dproj[:, lanes(r)], ((1,), (0,)))
            return carry

        lax.fori_loop(0, near_blocks, near_rows, 0)
        absorb(1, 0)
        absorb(0, 0)
        hand_hop(3, 1).start()
        hand_absorb(1, 6)
        ids = bid_ref[...]
        hot = ids == lax.broadcasted_iota(jnp.int32, (buckets, SPAN), 0)
        out_lane = lax.broadcasted_iota(jnp.int32, (buckets, 128), 1)
        sub = lax.broadcasted_iota(jnp.int32, (8, SPAN), 0)
        sv[0] = jnp.zeros(sv.shape[1:], F32)

        def bias_sums(hh, carry):
            line = jnp.zeros((8, SPAN), F32)
            for g in range(BLK // 8):
                group = slice(8 * g, 8 * g + 8)
                parts = [tally[hh, i, group, :] for i in (4, 3, 2, 1, 0)]
                strip = jnp.concatenate(parts + [jnp.zeros((8, BLK), F32)], axis=1)
                line = line + (strip if g == 0 else pltpu.roll(strip, SPAN - 8 * g, 1))
            for bit in (1, 2, 4):
                line = jnp.where((sub // bit) % 2 == 1, pltpu.roll(line, SPAN - bit, 1), line)
            sums = jnp.sum(line, axis=0, keepdims=True)
            col = jnp.sum(jnp.where(hot, sums, 0.0), axis=1, keepdims=True)
            sv[0, 0:buckets, :] = jnp.where(out_lane == x * heads + hh, col, sv[0, 0:buckets, :])
            return carry

        lax.fori_loop(0, heads, bias_sums, 0)
        product = wn[...].astype(F32) * grad[:, 0 : 3 * cols]
        again = lane_sum(product[:, 0:512]).T
        rest = product[:, 512 : 3 * cols]
        again = jnp.sum(again, axis=0, keepdims=True) + jnp.sum(rest.T, axis=0, keepdims=True)
        again = again / ag_ref[...]
        fgain = jnp.sum(fsum[...].T, axis=0, keepdims=True)
        lines = -(-d // 128)
        for i in range(lines):
            n = min(128, d - 128 * i)
            sv[0, buckets + i : buckets + i + 1, 0:n] = again[:, 128 * i : 128 * i + n]
            sv[0, buckets + lines + i : buckets + lines + i + 1, 0:n] = fgain[:, 128 * i : 128 * i + n]
        round_copy(0).start()
        hand_absorb(3, 4)
        round_end(0)
        absorb(1, 1)
        dproj_copy.wait()

        def last_norm(r, carry):
            ls = lanes(r)
            c = f3[:, ls] + dot(wf[...], dfar[:, ls], ((1,), (0,)))
            v = f2[:, ls]
            scale = norm_scale(v)
            n = v * scale
            cg = c * agc[...]
            m = jnp.mean(cg * n, axis=0, keepdims=True)
            f3[:, ls] = f1[:, ls] + scale * (cg - n * m)
            out_copy(r).start()
            return carry

        lax.fori_loop(0, near_blocks, last_norm, 0)
        absorb(0, 1)
        hand_absorb(3, 5)
        round_end(1)
        hand_absorb(2, 6)
        absorb(1, 2)
        round_end(2)
        absorb(0, 2)
        hand_absorb(3, 1)
        hand_absorb(3, 6)
        absorb(1, 3)
        round_end(3)
        absorb(0, 3)
        round_end(4)
        small_ref[...] = sv[5]
        for i in range(4):
            back_copy(i).wait()
        for r in range(near_blocks):
            out_copy(r).wait()


def tail(qkv, e, inv, wall, ctx, again, fgain, early, din, mid, cot, tok, nrm, wq, wfar, far,
         quarter, half_way, hand, buckets, heads, dk, extra, f):
    d, rows = tok.shape
    seq = 2 * rows
    cols = heads * dk
    blocks = seq // BLK
    near = blocks // 2
    shard = d // 16
    spad = -(-shard // 16) * 16
    deep = hand.shape[0]
    later = deep + len(LEVELS)
    lines = -(-(buckets + 2 * -(-d // 128)) // 8) * 8
    bids = jnp.asarray(lane_buckets(buckets))
    one = pl.Buffered(1)
    dma = pltpu.SemaphoreType.DMA
    any_spec = pl.BlockSpec(memory_space=pl.ANY)

    def full(v):
        return pl.BlockSpec(v.shape, lambda i: (0,) * len(v.shape), pipeline_mode=one)

    def chain(width):
        return [pltpu.VMEM((n, spad, width), BF) for n in (16, 8, 4, 2, 1)]

    outs = [
        jax.ShapeDtypeStruct((3, shard, cols), F32),
        jax.ShapeDtypeStruct((shard, cols), F32),
        jax.ShapeDtypeStruct((lines, 128), F32),
        jax.ShapeDtypeStruct((shard, f), F32),
        jax.ShapeDtypeStruct((shard, 2, f), F32),
    ]
    a_chain, b_chain = chain(2 * cols), chain(2 * cols)
    return pl.pallas_call(
        functools.partial(tail_kernel, heads, dk, buckets, blocks, extra),
        grid=(blocks,),
        in_specs=[
            full(bids),
            full(qkv),
            pl.BlockSpec((heads, 1, seq, BLK), lambda i: (0, i, 0, 0)),
            pl.BlockSpec((heads, 1, 1, BLK), lambda i: (0, i, 0, 0)),
            full(wall),
            full(ctx),
            full(again),
            full(fgain),
            full(early),
        ]
        + [any_spec] * 11,
        out_specs=[any_spec, any_spec] + [full(v) for v in outs],
        out_shape=[jax.ShapeDtypeStruct((d, rows), F32), jax.ShapeDtypeStruct((d, rows), BF)] + outs,
        scratch_shapes=[
            pltpu.VMEM((d, rows), F32),
            pltpu.VMEM((d, rows), F32),
            pltpu.VMEM((d, rows), F32),
            pltpu.VMEM((d, seq), BF),
            pltpu.VMEM((3 * cols, d), BF),
            pltpu.VMEM((d, 3 * cols), BF),
            pltpu.VMEM((d, 3 * cols), BF),
            pltpu.VMEM((d, rows), BF),
            pltpu.VMEM((cols, seq), BF),
            pltpu.VMEM((cols, rows), BF),
            pltpu.VMEM((d, cols), BF),
            pltpu.VMEM((d, cols), BF),
            pltpu.VMEM((d, 128), F32),
            pltpu.VMEM((d, 1), F32),
            pltpu.VMEM((d, 1), F32),
            pltpu.VMEM((seq, BLK), F32),
            pltpu.VMEM((2 * cols, seq), F32),
            pltpu.VMEM((heads, 5, BLK, BLK), F32),
            pltpu.VMEM((3 * cols, seq), BF),
            pltpu.VMEM((3 * cols, rows), BF),
            pltpu.VMEM((d, 4 * cols), F32),
            a_chain[0],
            b_chain[0],
        ]
        + a_chain[1:]
        + b_chain[1:]
        + [
            pltpu.VMEM((deep, 4, 3, spad, BLK), BF),
            pltpu.VMEM((2, 3, spad, BLK), BF),
            pltpu.VMEM((2, 1, 3, spad, BLK), BF),
            pltpu.VMEM((deep, 4, 3, spad, BLK), BF),
            pltpu.VMEM((deep + 1, 2, 3, spad, BLK), BF),
            pltpu.VMEM((later - 1, 1, 3, spad, BLK), BF),
            pltpu.VMEM((6, lines, 128), F32),
            pltpu.VMEM((5, lines, 128), F32),
            dma((7 + near,)),
            dma((later,)),
            dma((7,)), dma((7,)),
            dma((2, 4)), dma((2, 4)),
            dma((5,)), dma((5,)),
            dma((4, later)), dma((4, later)),
        ],
        compiler_params=pltpu.CompilerParams(
            vmem_limit_bytes=FF_VMEM, collective_id=1, has_side_effects=True
        ),
        cost_estimate=pl.CostEstimate(
            flops=32 * heads * seq * seq * dk + 8 * seq * d * 3 * cols,
            bytes_accessed=2 * heads * seq * seq + 30 * rows * d,
            transcendentals=0,
        ),
    )(bids, qkv, e, inv, wall, ctx, again, fgain, early, din, mid, cot, tok, nrm, wq, wfar, far,
      quarter, half_way, hand)


def outputs_kernel(near_ref, back_ref, ig_ref, ffi_ref, rel_ref, *refs):
    n = (len(refs) - 4) // 2
    refs, rel_out = refs[:-1], refs[-1]
    sources, res_ref, ig_out, ffi_out, targets = refs[:n], refs[n], refs[n + 1], refs[n + 2], refs[n + 3 :]
    res_ref[...] = near_ref[...] + back_ref[...].astype(F32)
    ig_out[...] = ig_ref[...]
    ffi_out[...] = ffi_ref[...]

    @pl.when(pl.program_id(0) == 0)
    def _():
        for i in range(n):
            targets[i][...] = sources[i][...]
        rel_out[...] = rel_ref[...].T[0 : rel_out.shape[0], 0 : rel_out.shape[1]]


def outputs(near, back, ig, ffi, small, rel_shape, *grads):
    d, rows = near.shape
    block = pl.BlockSpec((d // 4, rows), lambda i: (i, 0))
    shard, two, f = ffi.shape
    part = pl.BlockSpec((shard // 4, two, f), lambda i: (i, 0, 0))
    one = pl.Buffered(1)
    whole = [pl.BlockSpec(v.shape, lambda i, n=v.ndim: (0,) * n, pipeline_mode=one) for v in grads]
    return pl.pallas_call(
        outputs_kernel,
        grid=(4,),
        in_specs=[block] * 3 + [part, pl.BlockSpec((rel_shape[1], 128), lambda i: (0, 0))] + whole,
        out_specs=[block] * 2 + [part] + whole + [pl.BlockSpec(rel_shape, lambda i: (0, 0))],
        out_shape=[jax.ShapeDtypeStruct(v.shape, F32) for v in (near, ig, ffi) + grads]
        + [jax.ShapeDtypeStruct(rel_shape, F32)],
        compiler_params=pltpu.CompilerParams(vmem_limit_bytes=FF_VMEM),
    )(near, back, ig, ffi, small, *grads)


def take(array, index):
    return lax.dynamic_index_in_dim(array, index, 0, keepdims=False)


def per_device(
    tokens,
    cotangent,
    doc_lengths,
    pad_mask,
    attn_gain,
    qkv_weight,
    rel_table,
    out_weight,
    ff_gain,
    ff_in_weight,
    ff_out_weight,
):
    rows, d = tokens.shape
    n_dp = lax.axis_size("dp")
    n_mp = lax.axis_size("mp")
    cols = qkv_weight.shape[2]
    buckets, heads = rel_table.shape
    dk = cols // heads
    me = lax.axis_index("dp")
    shard = d // n_dp
    extra = n_dp // 16

    def hop(v, mask):
        return lax.ppermute(v, "dp", [(i, i ^ mask) for i in range(n_dp)])

    def bit(b):
        return (me >> b) & 1

    def finish(g):
        parts = [g.reshape((extra, shard) + g.shape[1:])]
        for b in reversed(range(extra.bit_length() - 1)):
            halves = [p.reshape((2, p.shape[0] // 2) + p.shape[1:]) for p in parts]
            away = sum(take(p, 1 - bit(b)).astype(F32) for p in halves).astype(BF)
            parts = [take(p, bit(b)) for p in halves] + [hop(away, 1 << b)]
        return sum(p.astype(F32) for p in parts)[0]

    tok = tokens.T
    cot = cotangent.T
    far = lax.ppermute(tok.astype(BF), "mp", [(0, 1), (1, 0)])
    w2 = jnp.transpose(ff_in_weight, (1, 0, 2))
    wq = jnp.transpose(qkv_weight, (1, 2, 0)).reshape(3 * cols, d)
    again, fgain = attn_gain.reshape(1, d), ff_gain.reshape(1, d)

    e, inv, qkv, ctx, nrm, xt, mid, ct, wall = front(
        rel_table, doc_lengths, pad_mask, again, fgain, wq, out_weight.T, tok, far, cot, heads, dk
    )
    early, din, near_out, far_out, quarter, half_way, hand, wfar = ff_all(
        xt, ct, w2, ff_out_weight, mid, wq, extra
    )
    input_grad, back, grad_qkv, grad_out, small, ffo, ffi = tail(
        qkv, e, inv, wall, ctx, again, fgain, early, din, mid, cot, tok, nrm, wq, wfar, far_out,
        quarter, half_way, hand, buckets, heads, dk, extra, ff_out_weight.shape[1],
    )
    for b in range(extra.bit_length() - 1):
        small = small + hop(small, 1 << b)
    result, input_grad, ffi, grad_qkv, grad_out, ffo, rel_grad = outputs(
        near_out, back, input_grad, ffi, small, (heads * n_mp, buckets), grad_qkv, grad_out, ffo
    )
    grad_qkv = jnp.transpose(grad_qkv, (1, 0, 2))
    if extra > 1:
        grad_qkv, grad_out, ffo, ffi = (finish(g) for g in (grad_qkv, grad_out, ffo, ffi))
    lines = -(-d // 128)
    return (
        result.T,
        input_grad.T,
        small[buckets : buckets + lines].reshape(-1)[:d],
        grad_qkv,
        rel_grad.T,
        grad_out,
        small[buckets + lines : buckets + 2 * lines].reshape(-1)[:d],
        ffi,
        ffo,
    )


def solution(mesh):
    return jax.shard_map(
        per_device,
        mesh=mesh,
        in_specs=(
            P(("dp", "mp"), None),
            P(("dp", "mp"), None),
            P("dp", None),
            P("dp", None),
            P(),
            P(None, None, "mp"),
            P(None, "mp"),
            P(None, "mp"),
            P(),
            P(None, None, "mp"),
            P(None, "mp"),
        ),
        out_specs=(
            P(("dp", "mp"), None),
            P(("dp", "mp"), None),
            P(),
            P("dp", None, "mp"),
            P(),
            P("dp", "mp"),
            P(),
            P("dp", None, "mp"),
            P("dp", "mp"),
        ),
        check_vma=False,
    )
```

```python
import functools

import jax
import jax.numpy as jnp
import numpy as np
from jax import lax
from jax.experimental import pallas as pl
from jax.experimental.pallas import tpu as pltpu
from jax.sharding import PartitionSpec as P

MAXDIST = 128
norm_eps = 1e-06
BLK = 256
SPAN = 6 * BLK
REACH = 2
BF = jnp.bfloat16
F32 = jnp.float32
FF_VMEM = 63 << 20


def bucket_of(offsets, buckets, reach):
    half_range = buckets // 2
    upper_half = (offsets > 0).astype(np.int32) * half_range
    distance = np.abs(offsets)
    exact_range = half_range // 2
    safe_dist = np.maximum(distance, 1)
    log_bucket = exact_range + (
        np.log(safe_dist / exact_range) / np.log(reach / exact_range) * (half_range - exact_range)
    ).astype(np.int32)
    log_bucket = np.minimum(log_bucket, half_range - 1)
    return (upper_half + np.where(distance < exact_range, distance, log_bucket)).astype(np.int32)


def lane_buckets(buckets):
    lanes = np.arange(SPAN)
    shifted = np.where(lanes < 5 * BLK, lanes, lanes - SPAN)
    return bucket_of(REACH * BLK - shifted, buckets, MAXDIST).reshape(1, SPAN)


def dot(a, b, contract):
    return lax.dot_general(a, b, (contract, ((), ())), preferred_element_type=F32)


def flip(index, mask):
    out = index
    bit = 1
    while bit <= mask:
        if mask & bit:
            out = out + bit * (1 - 2 * (index // bit % 2))
        bit *= 2
    return out


GROUP_MASKS = (1, 2, 4, 12)


def group_coords(g):
    b = [g // (1 << i) % 2 for i in range(4)]
    return [b[0], b[1], (b[2] + b[3]) % 2, b[3]]


Y_FIRST = (0, 1, 2, 3)
Z_FIRST = (0, 2, 3, 1)
Z_BLOCK = 1
LEVELS = (4, 3, 3, 2)


def order_of(block):
    return Z_FIRST if block == Z_BLOCK else Y_FIRST


def levels_of(block):
    return LEVELS[block] if block < len(LEVELS) else 1


def block_position(k, order):
    b = [k >> i & 1 for i in range(4)]
    c = [b[0], b[1], b[2] ^ b[3], b[3]]
    return sum(c[order[i]] << (3 - i) for i in range(4))


def column(line):
    return jnp.broadcast_to(line, (8, line.shape[1])).T[:, 0:1]


def norm_scale(v):
    return lax.rsqrt(jnp.mean(v * v, axis=0, keepdims=True) + norm_eps)


def lanes(block):
    return pl.ds(pl.multiple_of(block * BLK, BLK), BLK)


def remote(src, dst, send, recv, who):
    return pltpu.make_async_remote_copy(
        src_ref=src,
        dst_ref=dst,
        send_sem=send,
        recv_sem=recv,
        device_id=who,
        device_id_type=pl.DeviceIdType.MESH,
    )


def meet(devices):
    barrier = pltpu.get_barrier_semaphore()
    for who in devices:
        pl.semaphore_signal(barrier, inc=1, device_id=who, device_id_type=pl.DeviceIdType.MESH)
    pl.semaphore_wait(barrier, len(devices))


def near_diagonal(offset):
    i = offset + 3
    return i + (6 - i) // 6 - i // 6 - 1


def front_kernel(
    heads, dk, buckets, blocks,
    rel_ref, len_ref, bid_ref, pad_ref, ag_ref, fg_ref, wq_ref, wo_ref,
    tok_hbm, far_hbm, cot_hbm,
    e_ref, inv_ref, qkv_ref, ctx_hbm, nrm_hbm, xt_hbm, mid_hbm, ct_hbm, wall_hbm,
    f1, fb, f3, cl, nrm, table, padc, mask, score, agc, fgc, wall, wn, call, xo,
    lsem, osem, wsend, wrecv, csend, crecv,
):
    qb = pl.program_id(0)
    dp, x = lax.axis_index("dp"), lax.axis_index("mp")
    d, rows = f1.shape
    cols = heads * dk
    half = cols // 2
    core = dp % 2
    other = (dp, 1 - x)
    sibling = (dp + 1 - 2 * core, x)
    near_blocks = blocks // 2
    part = pl.ds(core * half, half)
    far_part = pl.ds(cols + core * half, half)

    def local(i):
        src, dst = ((tok_hbm, f1), (far_hbm, fb), (cot_hbm, f3))[i]
        return pltpu.make_async_copy(src, dst, lsem.at[i])

    def out(i):
        src, dst = (
            (call, ctx_hbm), (nrm, nrm_hbm), (f1.at[:, lanes(0)], mid_hbm.at[:, lanes(0)]), (cl, ct_hbm.at[:, pl.ds(0, rows)]), (wall, wall_hbm),
            (f1.at[:, pl.ds(BLK, rows - BLK)], mid_hbm.at[:, pl.ds(BLK, rows - BLK)]),
        )[i]
        return pltpu.make_async_copy(src, dst, osem.at[i])

    def xt_out(b):
        return pltpu.make_async_copy(xo.at[:, lanes(b)], xt_hbm.at[:, lanes(b)], osem.at[6 + b])

    w_copy = remote(wo_ref.at[part], wall.at[far_part], wsend.at[0], wrecv.at[0], other)
    w_pass = remote(wall.at[far_part], wall.at[far_part], wsend.at[1], wrecv.at[1], sibling)
    piece = d // 4

    def c_copy(i):
        rs = pl.ds(i * piece, piece)
        return remote(
            cl.at[rs, pl.ds(0, BLK)], ct_hbm.at[rs, pl.ds(rows, BLK)], wsend.at[2 + i], wrecv.at[2 + i], other
        )

    def ctx_copy(b):
        there = (b + near_blocks) % blocks
        return remote(
            call.at[pl.ds(0, cols), lanes(b)], call.at[pl.ds(cols, cols), lanes(there)],
            csend.at[b], crecv.at[b], other,
        )

    @pl.when(qb == 0)
    def _():
        for i in (2, 0, 1):
            local(i).start()
        meet([other, sibling])
        w_copy.start()
        wall[0:cols, :] = wo_ref[...]
        local(2).wait()
        cl[...] = f3[...].astype(BF)
        c_copy(0).start()
        c_copy(1).start()
        out(3).start()
        agc[...] = column(ag_ref[...])
        fgc[...] = column(fg_ref[...])
        local(0).wait()
        local(1).wait()
        for b in range(blocks):
            ls = slice(b * BLK, (b + 1) * BLK)
            v = f1[:, ls] if b < near_blocks else fb[:, b * BLK - rows : (b + 1) * BLK - rows].astype(F32)
            nrm[:, ls] = (v * norm_scale(v) * agc[...]).astype(BF)
            qkv_ref[:, ls] = dot(wq_ref[...], nrm[:, ls], ((1,), (0,))).astype(BF)
        out(1).start()
        for i in range(2):
            start = (1 - x) * rows if i else x * rows
            line = pad_ref[:, pl.ds(pl.multiple_of(start, BLK), rows)].astype(F32)
            padc[i * rows : (i + 1) * rows, :] = jnp.broadcast_to(line, (8, rows)).T
        ids = bid_ref[...]
        for hh in range(heads):
            line = jnp.zeros((1, SPAN), F32)
            for b in range(buckets):
                line = jnp.where(ids == b, rel_ref[b, hh], line)
            turned = pltpu.roll(
                jnp.broadcast_to(line, (BLK, SPAN)), 0, 1, stride=1, stride_axis=0
            )
            for g in range(5):
                table[hh, g] = turned[:, BLK * (4 - g) : BLK * (5 - g)]

    @pl.when(qb == 1)
    def _():
        w_copy.wait()
        w_pass.start()

    q_true = (qb + near_blocks * x) % blocks

    q_pos = q_true * BLK + lax.broadcasted_iota(jnp.int32, (1, BLK), 1)
    k_iota = lax.broadcasted_iota(jnp.int32, (BLK, BLK), 0)
    for kb in range(blocks):
        k_pos = (kb + near_blocks * x) % blocks * BLK + k_iota
        bound = 0
        q_doc = jnp.zeros((1, BLK), jnp.int32)
        k_doc = jnp.zeros((BLK, BLK), jnp.int32)
        for i in range(len_ref.shape[1]):
            bound = bound + len_ref[0, i]
            q_doc = q_doc + (q_pos >= bound).astype(jnp.int32)
            k_doc = k_doc + (k_pos >= bound).astype(jnp.int32)
        krows = slice(kb * BLK, (kb + 1) * BLK)
        seen = (padc[krows, 0:1] > 0.5) | (k_pos == q_pos)
        mask[krows, :] = jnp.where((k_doc == q_doc) & seen, 0.0, -1000000000.0)

    def head_rows(h, group):
        return pl.ds(pl.multiple_of(group * cols + h * dk, dk), dk)

    def diagonal(kb):
        return near_diagonal((kb + near_blocks * x) % blocks - q_true)

    def head(h, carry):
        qh = qkv_ref[head_rows(h, 0), lanes(qb)]
        peak = None
        for kb in range(blocks):
            krows = slice(kb * BLK, (kb + 1) * BLK)
            s = dot(qkv_ref[head_rows(h, 1), krows], qh, ((0,), (0,)))
            diag = diagonal(kb)
            s = s + table[h, diag] + mask[krows, :]
            score[krows, :] = s
            top = jnp.max(s, axis=0, keepdims=True)
            peak = top if peak is None else jnp.maximum(peak, top)
        total = jnp.zeros((1, BLK), F32)
        ctx = jnp.zeros((dk, BLK), F32)
        for kb in range(blocks):
            krows = slice(kb * BLK, (kb + 1) * BLK)
            e = jnp.exp(score[krows, :] - peak)
            total = total + jnp.sum(e, axis=0, keepdims=True)
            e_low = e.astype(BF)
            e_ref[h, 0, krows, :] = e_low
            ctx = ctx + dot(qkv_ref[head_rows(h, 2), krows], e_low, ((1,), (0,)))
        inv = 1.0 / total
        inv_ref[h, 0] = inv
        call[head_rows(h, 0), lanes(qb)] = (ctx * inv).astype(BF)
        return carry

    lax.fori_loop(0, heads, head, 0)
    ctx_copy(qb).start()

    @pl.when(qb == 1)
    def _():
        c_copy(2).start()

    @pl.when(qb == blocks - 1)
    def _():
        c_copy(3).start()
        w_pass.wait()
        wn[...] = wall[...].astype(F32).T.astype(BF)
        out(4).start()
        for i in range(blocks):
            b = (i + near_blocks) % blocks
            ctx_copy(i).wait()
            ls = slice(b * BLK, (b + 1) * BLK)
            v = dot(wn[...], call[:, ls], ((1,), (0,)))
            if b < near_blocks:
                v = v + f1[:, ls]
                f1[:, ls] = v
                if b == 0:
                    out(2).start()
            else:
                v = v + fb[:, b * BLK - rows : (b + 1) * BLK - rows].astype(F32)
            xo[:, ls] = (v * norm_scale(v) * fgc[...]).astype(BF)
            xt_out(b).start()
        out(0).start()
        out(5).start()
        for i in range(4):
            c_copy(i).wait()
        for i in range(6):
            out(i).wait()
        for b in range(blocks):
            xt_out(b).wait()


def front(rel, lengths, pad, again, fgain, wq, wo, tok, far, cot, heads, dk):
    d, rows = tok.shape
    seq = 2 * rows
    cols = heads * dk
    blocks = seq // BLK
    buckets = rel.shape[0]
    bids = jnp.asarray(lane_buckets(buckets))
    one = pl.Buffered(1)
    dma = pltpu.SemaphoreType.DMA
    any_spec = pl.BlockSpec(memory_space=pl.ANY)
    smem = pl.BlockSpec(memory_space=pltpu.SMEM)

    def full(v):
        return pl.BlockSpec(v.shape, lambda i: (0, 0), pipeline_mode=one)

    return pl.pallas_call(
        functools.partial(front_kernel, heads, dk, buckets, blocks),
        grid=(blocks,),
        in_specs=[smem, smem, full(bids), full(pad), full(again), full(fgain), full(wq), full(wo)]
        + [any_spec] * 3,
        out_specs=[
            pl.BlockSpec((heads, 1, seq, BLK), lambda i: (0, i, 0, 0)),
            pl.BlockSpec((heads, 1, 1, BLK), lambda i: (0, i, 0, 0)),
            pl.BlockSpec((3 * cols, seq), lambda i: (0, 0)),
        ]
        + [any_spec] * 6,
        out_shape=[
            jax.ShapeDtypeStruct((heads, blocks, seq, BLK), BF),
            jax.ShapeDtypeStruct((heads, blocks, 1, BLK), F32),
            jax.ShapeDtypeStruct((3 * cols, seq), BF),
            jax.ShapeDtypeStruct((2 * cols, seq), BF),
            jax.ShapeDtypeStruct((d, seq), BF),
            jax.ShapeDtypeStruct((d, seq), BF),
            jax.ShapeDtypeStruct((d, rows), F32),
            jax.ShapeDtypeStruct((d, seq), BF),
            jax.ShapeDtypeStruct((2 * cols, d), BF),
        ],
        scratch_shapes=[
            pltpu.VMEM((d, rows), F32),
            pltpu.VMEM((d, rows), BF),
            pltpu.VMEM((d, rows), F32),
            pltpu.VMEM((d, rows), BF),
            pltpu.VMEM((d, seq), BF),
            pltpu.VMEM((heads, 5, BLK, BLK), F32),
            pltpu.VMEM((seq, 8), F32),
            pltpu.VMEM((seq, BLK), F32),
            pltpu.VMEM((seq, BLK), F32),
            pltpu.VMEM((d, 1), F32),
            pltpu.VMEM((d, 1), F32),
            pltpu.VMEM((2 * cols, d), BF),
            pltpu.VMEM((d, 2 * cols), BF),
            pltpu.VMEM((2 * cols, seq), BF),
            pltpu.VMEM((d, seq), BF),
            dma((3,)), dma((6 + blocks,)), dma((6,)), dma((6,)), dma((blocks,)), dma((blocks,)),
        ],
        compiler_params=pltpu.CompilerParams(
            vmem_limit_bytes=FF_VMEM, collective_id=2, has_side_effects=True
        ),
        cost_estimate=pl.CostEstimate(
            flops=16 * heads * seq * seq * dk + 10 * seq * d * cols,
            bytes_accessed=2 * heads * seq * seq + 30 * rows * d,
            transcendentals=heads * seq * seq,
        ),
    )(rel, lengths, bids, pad, again, fgain, wq, wo, tok, far, cot)


def ff_kernel(
    steps, extra,
    xt_hbm, w_hbm, ct_hbm, wo_hbm, mid_hbm, wq_hbm,
    grads_ref, din_hbm, near_hbm, far_hbm, quarter_hbm, half_hbm, hand_hbm, wfar_hbm,
    xt, ct, wg, wu, wo, hid, dg, du, din, stage, r1, r2, r3, r4, xs, xr, of,
    csem, wsem, s1, s2, s3, s4, t1, t2, t3, t4, xsem, osem, hsem,
):
    f, total = hid.shape
    rows = total // 2
    chunks = rows // BLK
    d = xt.shape[0]
    shard = d // 16
    dp, mp = lax.axis_index("dp"), lax.axis_index("mp")
    a = group_coords(dp // extra)
    peers = [flip(dp, m * extra) for m in GROUP_MASKS]
    other = (dp, 1 - mp)
    core = dp % 2
    sibling = dp + 1 - 2 * core
    bufs = (r1, r2, r3, r4)
    sends, recvs = (s1, s2, s3, s4), (t1, t2, t3, t4)
    end = steps - 1

    def weight_copy(kind, n):
        src, dst = ((w_hbm.at[0], wg), (w_hbm.at[1], wu), (wo_hbm, wo))[kind]
        return pltpu.make_async_copy(src.at[:, lanes(n)], dst.at[:, lanes(n)], wsem.at[kind, n])

    def tok_copy(n):
        src, dst, start, size = (
            (xt_hbm, xt, rows, BLK), (ct_hbm, ct, rows, BLK),
            (xt_hbm, xt, 0, rows), (ct_hbm, ct, 0, rows), (xt_hbm, xt, rows + BLK, BLK),
        )[n]
        part = pl.ds(start, size)
        return pltpu.make_async_copy(src.at[:, part], dst.at[:, part], csem.at[n])

    near_part, far_part = pl.ds(0, rows), pl.ds(rows, rows)
    c_far = remote(
        ct_hbm.at[:, pl.ds(BLK, BLK)], ct.at[:, pl.ds(rows + BLK, BLK)], csem.at[5], csem.at[6], other
    )
    x_copy = remote(xs, xr, xsem.at[0], xsem.at[1], other)
    wq_rows = wq_hbm.shape[0] // 2
    wq_part = pl.ds(core * wq_rows, wq_rows)
    w_copy = remote(wq_hbm.at[wq_part], wfar_hbm.at[wq_part], xsem.at[2], xsem.at[3], other)
    w_pass = remote(wfar_hbm.at[wq_part], wfar_hbm.at[wq_part], xsem.at[4], xsem.at[5], (sibling, mp))
    mid_copy = pltpu.make_async_copy(mid_hbm, din.at[:, far_part], osem.at[3])

    deep = len(LEVELS)

    def hop(level, n, order):
        half = 8 >> level
        c = order[level]
        away = pl.ds((1 - a[c]) * half, half)
        src = stage.at[away] if level == 0 else bufs[level - 1].at[n, away]
        return remote(src, bufs[level].at[n], sends[level].at[n], recvs[level].at[n], (peers[c], mp))

    def hand_copy(n):
        level = levels_of(n) if isinstance(n, int) else 1
        dst = (hand_hbm.at[n - deep], half_hbm, quarter_hbm.at[n - 1])[level - 1]
        return pltpu.make_async_copy(bufs[level - 1].at[n], dst, hsem.at[n])

    def absorb_first(n):
        hop(0, n, Y_FIRST).wait()
        r1[n] = stage[pl.ds(a[0] * 8, 8)] + r1[n]
        if isinstance(n, int):
            hand_copy(n).start()
            return

        @pl.when(n == Z_BLOCK)
        def _():
            hop(1, n, Z_FIRST).start()

        @pl.when((n < deep) & (n != Z_BLOCK))
        def _():
            hop(1, n, Y_FIRST).start()

        @pl.when(n >= deep)
        def _():
            hand_copy(n).start()

    def absorb(level, n):
        half = 8 >> level
        order = order_of(n)
        hop(level, n, order).wait()
        kept = bufs[level - 1][n, pl.ds(a[order[level]] * half, half)]
        if level < 3:
            bufs[level][n] = kept + bufs[level][n]
            if level + 1 < levels_of(n):
                hop(level + 1, n, order).start()
            else:
                hand_copy(n).start()
        else:
            both = kept.astype(F32) + bufs[level][n].astype(F32)
            for w in range(3):
                grads_ref[w, :, n * BLK : (n + 1) * BLK] = both[0, w]

    scale = np.float32(np.sqrt(2 / np.pi))

    def place(u):
        early, late = u // steps, (u - 4) // steps
        is_far0 = (early == 0) * 1
        is_far1 = (late == 1) * 1
        v = u - steps
        n = v - steps * (u // (2 * steps + 4))
        near_j, near_c = n // 2, n % 2
        j = is_far0 * u + is_far1 * (u - steps - 4) + (1 - is_far0 - is_far1) * near_j
        c = is_far0 * chunks + is_far1 * (chunks + 1) + (1 - is_far0 - is_far1) * near_c
        return j, c

    def substep(u):
        j, c = place(u)
        pj, pc = place(u - 1)
        pj = pj + (u == 0) * 1
        fcols, tok = lanes(j), lanes(c)
        pcols, ptok = lanes(pj), lanes(pc)
        gate = dot(wg[:, fcols], xt[:, tok], ((0,), (0,)))
        up = dot(wu[:, fcols], xt[:, tok], ((0,), (0,)))
        dh = dot(wo[:, fcols], ct[:, tok], ((0,), (0,)))
        backward(pcols, ptok)
        sq = gate * gate
        t = jnp.tanh(scale * gate * (1.0 + 0.044715 * sq))
        half = 0.5 * (1.0 + t)
        act = gate * half
        slope = half + 0.5 * gate * (1.0 - t * t) * (scale * (1.0 + (3 * 0.044715) * sq))
        hid[fcols, tok] = (act * up).astype(BF)
        dg[fcols, tok] = (dh * (up * slope)).astype(BF)
        du[fcols, tok] = (dh * act).astype(BF)

    def backward(rs, tok):
        din[:, tok] += dot(wg[:, rs], dg[rs, tok], ((1,), (0,))) + dot(wu[:, rs], du[rs, tok], ((1,), (0,)))

    per = 4 * shard

    def grads(j):
        z = (j == Z_BLOCK) * 1
        for w in range(3):
            right = (hid, dg, du)[w][lanes(j), :]
            for q in range(4):
                rs = slice(q * per, (q + 1) * per)
                left = ct[rs, :] if w == 0 else xt[rs, :]
                part = dot(left, right, ((1,), (1,)))
                for k in range(4):
                    at = block_position(4 * q + k, Y_FIRST)
                    at = at + z * (block_position(4 * q + k, Z_FIRST) - at)
                    stage[at, w, 0:shard, :] = part[k * shard : (k + 1) * shard].astype(BF)
        hop(0, j, Y_FIRST).start()

    def out_part(n):
        return dot(wo[...], hid[:, lanes(n)], ((1,), (0,)))

    meet([(p, mp) for p in peers] + [other] + ([(sibling, mp)] if extra > 1 else []))
    c_far.start()
    w_copy.start()
    tok_copy(0).start()
    tok_copy(1).start()
    for n in range(steps):
        for kind in range(3):
            weight_copy(kind, n).start()
    for n in range(2, 5):
        tok_copy(n).start()
    din[...] = jnp.zeros_like(din)
    stage[...] = jnp.zeros_like(stage)
    before = place(-1)[1]
    dg[0:BLK, before * BLK : (before + 1) * BLK] = jnp.zeros((BLK, BLK), BF)
    du[0:BLK, before * BLK : (before + 1) * BLK] = jnp.zeros((BLK, BLK), BF)
    tok_copy(0).wait()
    tok_copy(1).wait()
    count = 2 * chunks * steps
    far_end = 2 * steps + 4

    def step(u, carry):
        @pl.when(u < steps)
        def _():
            for kind in range(3):
                weight_copy(kind, u).wait()

        @pl.when(u == steps)
        def _():
            tok_copy(2).wait()
            tok_copy(3).wait()

        @pl.when(u == steps + 4)
        def _():
            tok_copy(4).wait()
            c_far.wait()

        @pl.when(u < count)
        def _():
            substep(u)

        @pl.when(u == far_end)
        def _():
            xs[...] = din[:, far_part].astype(BF)
            x_copy.start()
            mid_copy.start()

        odd = u % 2 == 1
        late = (u >= 2 * steps + 5) * 1
        m = (u - 13) // 2 - 2 * ((u >= 2 * steps + 7) * 1)
        n = (u - 11) // 2 - 2 * late

        @pl.when(odd & ((u == 13) | (u == 15) | (u >= 2 * steps + 7)))
        def _():
            absorb_first(m)

        for at, events in (
            (21, ((1, 0),)), (23, ((1, 1),)), (25, ((2, 0),)), (27, ((1, 2),)),
        ):
            @pl.when(u == at)
            def _():
                for level, block in events:
                    absorb(level, block)

        @pl.when(odd & ((u == 11) | (u == 13) | (u >= 2 * steps + 5)))
        def _():
            grads(n)

        @pl.when(u == far_end + 5)
        def _():
            w_copy.wait()
            w_pass.start()

        return carry

    lax.fori_loop(0, count, step, 0)
    pj, pc = place(count - 1)
    backward(lanes(pj), lanes(pc))

    def far_out(n, carry):
        of[:, lanes(n)] = out_part(n + chunks).astype(BF)
        return carry

    lax.fori_loop(0, chunks, far_out, 0)
    absorb(2, 1)
    far_copy = pltpu.make_async_copy(of, far_hbm, osem.at[0])
    far_copy.start()
    mid_copy.wait()

    def near_out(n, carry):
        at = lanes(n + chunks)
        din[:, at] = din[:, at] + out_part(n)
        return carry

    lax.fori_loop(0, chunks, near_out, 0)
    near_copy = pltpu.make_async_copy(din.at[:, far_part], near_hbm, osem.at[1])
    near_copy.start()
    absorb_first(end)
    x_copy.wait()
    din[:, near_part] += xr[...].astype(F32)
    din_copy = pltpu.make_async_copy(din.at[:, near_part], din_hbm, osem.at[2])
    din_copy.start()
    absorb(3, 0)
    absorb(2, 2)
    absorb(1, 3)
    w_pass.wait()
    for n in range(1, steps):
        hand_copy(n).wait()
    far_copy.wait()
    near_copy.wait()
    din_copy.wait()


def ff_all(xt, ct, w2, wo, mid, wq, extra):
    d, total = xt.shape
    f = wo.shape[1]
    rows = total // 2
    steps = f // BLK
    deep = len(LEVELS)
    shard = d // 16
    spad = -(-shard // 16) * 16
    dma = pltpu.SemaphoreType.DMA
    any_spec = pl.BlockSpec(memory_space=pl.ANY)
    return pl.pallas_call(
        functools.partial(ff_kernel, steps, extra),
        in_specs=[any_spec] * 6,
        out_specs=[pl.BlockSpec(memory_space=pltpu.VMEM)] + [any_spec] * 7,
        out_shape=[
            jax.ShapeDtypeStruct((3, spad, BLK), F32),
            jax.ShapeDtypeStruct((d, rows), F32),
            jax.ShapeDtypeStruct((d, rows), F32),
            jax.ShapeDtypeStruct((d, rows), BF),
            jax.ShapeDtypeStruct((2, 2, 3, spad, BLK), BF),
            jax.ShapeDtypeStruct((4, 3, spad, BLK), BF),
            jax.ShapeDtypeStruct((steps - deep, 8, 3, spad, BLK), BF),
            jax.ShapeDtypeStruct(wq.shape, BF),
        ],
        scratch_shapes=[
            pltpu.VMEM((d, total), BF),
            pltpu.VMEM((d, total), BF),
            pltpu.VMEM((d, f), BF),
            pltpu.VMEM((d, f), BF),
            pltpu.VMEM((d, f), BF),
            pltpu.VMEM((f, total), BF),
            pltpu.VMEM((f, total), BF),
            pltpu.VMEM((f, total), BF),
            pltpu.VMEM((d, total), F32),
            pltpu.VMEM((16, 3, spad, BLK), BF),
            pltpu.VMEM((steps, 8, 3, spad, BLK), BF),
            pltpu.VMEM((4, 4, 3, spad, BLK), BF),
            pltpu.VMEM((3, 2, 3, spad, BLK), BF),
            pltpu.VMEM((1, 1, 3, spad, BLK), BF),
            pltpu.VMEM((d, rows), BF),
            pltpu.VMEM((d, rows), BF),
            pltpu.VMEM((d, rows), BF),
            dma((7,)),
            dma((3, steps)),
            dma((steps,)), dma((4,)), dma((3,)), dma((1,)),
            dma((steps,)), dma((4,)), dma((3,)), dma((1,)),
            dma((6,)),
            dma((4,)),
            dma((steps,)),
        ],
        compiler_params=pltpu.CompilerParams(
            vmem_limit_bytes=FF_VMEM, collective_id=0, has_side_effects=True
        ),
        cost_estimate=pl.CostEstimate(
            flops=18 * total * d * f,
            bytes_accessed=6 * d * f + 16 * total * d,
            transcendentals=total * f,
        ),
    )(xt, w2, ct, wo, mid, wq)


EVENTS = (
    ((0, 0), ((2, 3), (3, 2))),
    ((0, 2), ((1, 4),)),
    ((2, 0), ((3, 3),)),
    ((2, 1), ((2, 4),)),
    ((3, 2), ((1, 5),)),
)


def tail_kernel(
    heads, dk, buckets, blocks, extra,
    bid_ref, qkv_ref, e_ref, inv_ref, wall_ref, ctx_ref, ag_ref, fg_ref, early_ref,
    din_hbm, mid_hbm, cot_hbm, tok_hbm, nrm_hbm, wq_hbm, wfar_hbm, far_hbm,
    quarter_hbm, half_hbm, hand_hbm,
    ig_hbm, back_hbm, gq_ref, go_ref, small_ref, ffo_ref, ffi_ref,
    f1, f2, f3, nrm, wq, wn, wf, alow, dctx, dcs, osend, orecv, fsum, agc, fgc,
    dp_s, dkv, tally, dproj, dfar, grad,
    sa, sb_, a1, a2, a3, a4, b1, b2, b3, b4, hk, hm, hq, h2, h3, h4, sv, rv,
    lsem, ksem, xs_sem, xr_sem, cs_sem, cr_sem, bs_sem, br_sem, hs_sem, hr_sem,
):
    qb = pl.program_id(0)
    dp, x = lax.axis_index("dp"), lax.axis_index("mp")
    d, rows = f2.shape
    cols = heads * dk
    shard = d // 16
    a = group_coords(dp // extra)
    peers = [flip(dp, m * extra) for m in GROUP_MASKS]
    other = (dp, 1 - x)
    near_blocks = blocks // 2
    near_part, far_part = pl.ds(0, rows), pl.ds(rows, rows)
    halves = ((sa, a1, a2, a3, a4), (sb_, b1, b2, b3, b4))
    orders = (Y_FIRST, Y_FIRST)
    copies = (
        (din_hbm, f1), (mid_hbm, f2), (cot_hbm, f3), (tok_hbm, f2), (nrm_hbm, nrm), (wq_hbm, wq), (wfar_hbm, wq),
    )

    def local(i):
        return pltpu.make_async_copy(copies[i][0], copies[i][1], lsem.at[i])

    def x_copy(i, src, dst):
        return remote(src, dst, xs_sem.at[i], xr_sem.at[i], other)

    dctx_copy = x_copy(0, dcs, dctx.at[:, far_part])
    o_copy = x_copy(1, osend, orecv)
    dproj_copy = x_copy(2, dproj.at[:, far_part], dfar)

    def back_copy(i):
        part = pl.ds(i * 128, 128)
        return x_copy(3 + i, far_hbm.at[:, part], back_hbm.at[:, part])

    def hop(side, level):
        half = 8 >> level
        c = orders[side][level]
        away = pl.ds((1 - a[c]) * half, half)
        bufs = halves[side]
        return remote(
            bufs[level].at[away], bufs[level + 1], cs_sem.at[side, level], cr_sem.at[side, level], (peers[c], x)
        )

    def absorb(side, level):
        half = 8 >> level
        bufs = halves[side]
        hop(side, level).wait()
        kept = bufs[level][pl.ds(a[orders[side][level]] * half, half)]
        if level < 3:
            bufs[level + 1][...] = kept + bufs[level + 1][...]
            hop(side, level + 1).start()
            return
        both = (kept.astype(F32) + bufs[level + 1][...].astype(F32))[0, 0:shard]
        outs = (gq_ref.at[0], gq_ref.at[1]) if side == 0 else (gq_ref.at[2], go_ref)
        for i in range(2):
            outs[i][...] = both[:, i * cols : (i + 1) * cols]

    deep = len(LEVELS)
    handed = (3, 4, 2, 5, 6, 1)

    def keep_copy(block):
        level = levels_of(block)
        half = 8 >> level
        keep = pl.ds(a[order_of(block)[level]] * half, half)
        if level == 3:
            src, dst = quarter_hbm.at[block - 1, keep], hq.at[block - 1]
        elif level == 2:
            src, dst = half_hbm.at[keep], hm
        else:
            src, dst = hand_hbm.at[block - deep, keep], hk.at[block - deep]
        return pltpu.make_async_copy(src, dst, ksem.at[block])

    def hand_hop(level, block):
        half = 8 >> level
        c = order_of(block)[level]
        away = pl.ds((1 - a[c]) * half, half)
        fresh = level == levels_of(block)
        if level == 1:
            src, dst = hand_hbm.at[block - deep, away], h2.at[block - deep]
        elif level == 2:
            src, dst = half_hbm.at[away] if fresh else h2.at[block - deep, away], h3.at[block - 3]
        else:
            src, dst = quarter_hbm.at[block - 1, away] if fresh else h3.at[block - 3, away], h4.at[block - 1]
        return remote(src, dst, hs_sem.at[level, block], hr_sem.at[level, block], (peers[c], x))

    def put_grads(w, block, value):
        at = slice(block * BLK, (block + 1) * BLK)
        if w == 0:
            ffo_ref[:, at] = value
        else:
            ffi_ref[:, w - 1, at] = value

    def hand_absorb(level, block):
        half = 8 >> level
        keep = pl.ds(a[order_of(block)[level]] * half, half)
        hand_hop(level, block).wait()
        if level == levels_of(block):
            keep_copy(block).wait()
            kept = hk[block - deep] if level == 1 else (hm[...] if level == 2 else hq[block - 1])
        else:
            kept = h2[block - deep, keep] if level == 2 else h3[block - 3, keep]
        if level == 1:
            h2[block - deep] = kept + h2[block - deep]
        elif level == 2:
            h3[block - 3] = kept + h3[block - 3]
        else:
            both = kept.astype(F32) + h4[block - 1].astype(F32)
            for w in range(3):
                put_grads(w, block, both[0, w, 0:shard])
        if level < 3:
            hand_hop(level + 1, block).start()

    def round_copy(i):
        who = other if i == 4 else (peers[(0, 2, 3, 1)[i]], x)
        return remote(sv.at[i], rv.at[i], bs_sem.at[i], br_sem.at[i], who)

    def round_end(i):
        round_copy(i).wait()
        sv[i + 1] = sv[i] + rv[i]
        if i < 4:
            round_copy(i + 1).start()

    def out_copy(r):
        return pltpu.make_async_copy(f3.at[:, lanes(r)], ig_hbm.at[:, lanes(r)], lsem.at[len(copies) + r])

    def lane_sum(v):
        total = v[:, 0:128]
        for i in range(1, v.shape[1] // 128):
            total = total + v[:, i * 128 : (i + 1) * 128]
        return total

    @pl.when(qb == 0)
    def _():
        for i in range(3):
            local(i).start()
        meet([(p, x) for p in peers] + [other])
        back_copy(0).start()
        for block in handed[:-1]:
            hand_hop(levels_of(block), block).start()
        agc[...] = column(ag_ref[...])
        fgc[...] = column(fg_ref[...])
        dkv[...] = jnp.zeros_like(dkv)
        tally[...] = jnp.zeros_like(tally)
        sa[...] = jnp.zeros_like(sa)
        sb_[...] = jnp.zeros_like(sb_)
        fsum[...] = jnp.zeros_like(fsum)
        for i in range(3):
            local(i).wait()

        def norm_rows(r, carry):
            ls = lanes(r)
            v = f2[:, ls]
            c = f1[:, ls]
            scale = norm_scale(v)
            n = v * scale
            cg = c * fgc[...]
            m = jnp.mean(cg * n, axis=0, keepdims=True)
            gm = f3[:, ls] + scale * (cg - n * m)
            fsum[...] += lane_sum(c * n)
            f1[:, ls] = gm
            alow[:, ls] = gm.astype(BF)
            return carry

        lax.fori_loop(0, near_blocks, norm_rows, 0)
        dcs[...] = dot(wall_ref[cols : 2 * cols, :], alow[...], ((1,), (0,))).astype(BF)
        dctx_copy.start()
        for i in (3, 4, 5):
            local(i).start()
        for block in handed:
            keep_copy(block).start()
        dctx[:, near_part] = dot(wall_ref[0:cols, :], alow[...], ((1,), (0,))).astype(BF)
        osend[...] = dot(alow[...], ctx_ref[cols : 2 * cols, near_part], ((1,), (1,))).astype(BF)
        o_copy.start()
        grad[:, 3 * cols : 4 * cols] = dot(alow[...], ctx_ref[0:cols, near_part], ((1,), (1,)))
        for w in range(3):
            put_grads(w, 0, early_ref[w, 0:shard, :])
        dctx_copy.wait()
        back_copy(1).start()

    @pl.when(qb == 1)
    def _():
        local(5).wait()
        wn[...] = wq[...].astype(F32).T.astype(BF)
        local(6).start()

    @pl.when(qb == 2)
    def _():
        local(6).wait()
        wf[...] = wq[...].astype(F32).T.astype(BF)

    q_true = (qb + near_blocks * x) % blocks

    def head(h, carry):
        for at, events in EVENTS:
            @pl.when((qb == at[0]) & (h == at[1]))
            def _():
                for level, block in events:
                    hand_absorb(level, block)

        def head_rows(group):
            return pl.ds(pl.multiple_of(group * cols + h * dk, dk), dk)

        inv = inv_ref[h, 0]
        qh = qkv_ref[head_rows(0), lanes(qb)]
        scaled = (dctx[head_rows(0), lanes(qb)].astype(F32) * inv).astype(BF)
        inner = jnp.zeros((1, BLK), F32)
        for kb in range(blocks):
            krows = slice(kb * BLK, (kb + 1) * BLK)
            g = dot(qkv_ref[head_rows(2), krows], scaled, ((0,), (0,)))
            dp_s[krows, :] = g
            inner = inner + jnp.sum(e_ref[h, 0, krows, :].astype(F32) * g, axis=0, keepdims=True)
        inner = inner * inv
        dq = jnp.zeros((dk, BLK), F32)
        for kb in range(blocks):
            krows = slice(kb * BLK, (kb + 1) * BLK)
            e = e_ref[h, 0, krows, :]
            ds = (e.astype(F32) * (dp_s[krows, :] - inner)).astype(BF)
            dkv[head_rows(0), krows] += dot(qh, ds, ((1,), (1,)))
            dkv[head_rows(1), krows] += dot(scaled, e, ((1,), (1,)))
            dq = dq + dot(qkv_ref[head_rows(1), krows], ds, ((1,), (0,)))
            tally[h, near_diagonal((kb + near_blocks * x) % blocks - q_true)] += ds.astype(F32)
        dproj[head_rows(0), lanes(qb)] = dq.astype(BF)
        return carry

    lax.fori_loop(0, heads, head, 0)

    @pl.when(qb == blocks - 1)
    def _():
        dproj[cols : 3 * cols, :] = dkv[...].astype(BF)
        dproj_copy.start()
        back_copy(2).start()
        back_copy(3).start()
        local(3).wait()
        local(4).wait()
        per = 4 * shard

        def grad_rows(q, carry):
            rs = pl.ds(pl.multiple_of(q * per, 16), per)
            grad[rs, 0 : 3 * cols] = dot(nrm[rs, :], dproj[...], ((1,), (1,)))
            return carry

        lax.fori_loop(0, 4, grad_rows, 0)
        o_copy.wait()
        grad[:, 3 * cols : 4 * cols] += orecv[...].astype(F32)
        for side in range(2):
            for k in range(16):
                halves[side][0][block_position(k, orders[side]), 0:shard, :] = grad[
                    k * shard : (k + 1) * shard, 2 * side * cols : 2 * (side + 1) * cols
                ].astype(BF)
            hop(side, 0).start()
        hand_absorb(2, 5)

        def near_rows(r, carry):
            f3[:, lanes(r)] = dot(wn[...], dproj[:, lanes(r)], ((1,), (0,)))
            return carry

        lax.fori_loop(0, near_blocks, near_rows, 0)
        absorb(1, 0)
        absorb(0, 0)
        hand_hop(3, 1).start()
        hand_absorb(1, 6)
        ids = bid_ref[...]
        hot = ids == lax.broadcasted_iota(jnp.int32, (buckets, SPAN), 0)
        out_lane = lax.broadcasted_iota(jnp.int32, (buckets, 128), 1)
        sub = lax.broadcasted_iota(jnp.int32, (8, SPAN), 0)
        sv[0] = jnp.zeros(sv.shape[1:], F32)

        def bias_sums(hh, carry):
            line = jnp.zeros((8, SPAN), F32)
            for g in range(BLK // 8):
                group = slice(8 * g, 8 * g + 8)
                parts = [tally[hh, i, group, :] for i in (4, 3, 2, 1, 0)]
                strip = jnp.concatenate(parts + [jnp.zeros((8, BLK), F32)], axis=1)
                line = line + (strip if g == 0 else pltpu.roll(strip, SPAN - 8 * g, 1))
            for bit in (1, 2, 4):
                line = jnp.where((sub // bit) % 2 == 1, pltpu.roll(line, SPAN - bit, 1), line)
            sums = jnp.sum(line, axis=0, keepdims=True)
            col = jnp.sum(jnp.where(hot, sums, 0.0), axis=1, keepdims=True)
            sv[0, 0:buckets, :] = jnp.where(out_lane == x * heads + hh, col, sv[0, 0:buckets, :])
            return carry

        lax.fori_loop(0, heads, bias_sums, 0)
        product = wn[...].astype(F32) * grad[:, 0 : 3 * cols]
        again = lane_sum(product[:, 0:512]).T
        rest = product[:, 512 : 3 * cols]
        again = jnp.sum(again, axis=0, keepdims=True) + jnp.sum(rest.T, axis=0, keepdims=True)
        again = again / ag_ref[...]
        fgain = jnp.sum(fsum[...].T, axis=0, keepdims=True)
        lines = -(-d // 128)
        for i in range(lines):
            n = min(128, d - 128 * i)
            sv[0, buckets + i : buckets + i + 1, 0:n] = again[:, 128 * i : 128 * i + n]
            sv[0, buckets + lines + i : buckets + lines + i + 1, 0:n] = fgain[:, 128 * i : 128 * i + n]
        round_copy(0).start()
        hand_absorb(3, 4)
        round_end(0)
        absorb(1, 1)
        dproj_copy.wait()

        def last_norm(r, carry):
            ls = lanes(r)
            c = f3[:, ls] + dot(wf[...], dfar[:, ls], ((1,), (0,)))
            v = f2[:, ls]
            scale = norm_scale(v)
            n = v * scale
            cg = c * agc[...]
            m = jnp.mean(cg * n, axis=0, keepdims=True)
            f3[:, ls] = f1[:, ls] + scale * (cg - n * m)
            out_copy(r).start()
            return carry

        lax.fori_loop(0, near_blocks, last_norm, 0)
        absorb(0, 1)
        hand_absorb(3, 5)
        round_end(1)
        hand_absorb(2, 6)
        absorb(1, 2)
        round_end(2)
        absorb(0, 2)
        hand_absorb(3, 1)
        hand_absorb(3, 6)
        absorb(1, 3)
        round_end(3)
        absorb(0, 3)
        round_end(4)
        small_ref[...] = sv[5]
        for i in range(4):
            back_copy(i).wait()
        for r in range(near_blocks):
            out_copy(r).wait()


def tail(qkv, e, inv, wall, ctx, again, fgain, early, din, mid, cot, tok, nrm, wq, wfar, far,
         quarter, half_way, hand, buckets, heads, dk, extra, f):
    d, rows = tok.shape
    seq = 2 * rows
    cols = heads * dk
    blocks = seq // BLK
    near = blocks // 2
    shard = d // 16
    spad = -(-shard // 16) * 16
    deep = hand.shape[0]
    later = deep + len(LEVELS)
    lines = -(-(buckets + 2 * -(-d // 128)) // 8) * 8
    bids = jnp.asarray(lane_buckets(buckets))
    one = pl.Buffered(1)
    dma = pltpu.SemaphoreType.DMA
    any_spec = pl.BlockSpec(memory_space=pl.ANY)

    def full(v):
        return pl.BlockSpec(v.shape, lambda i: (0,) * len(v.shape), pipeline_mode=one)

    def chain(width):
        return [pltpu.VMEM((n, spad, width), BF) for n in (16, 8, 4, 2, 1)]

    outs = [
        jax.ShapeDtypeStruct((3, shard, cols), F32),
        jax.ShapeDtypeStruct((shard, cols), F32),
        jax.ShapeDtypeStruct((lines, 128), F32),
        jax.ShapeDtypeStruct((shard, f), F32),
        jax.ShapeDtypeStruct((shard, 2, f), F32),
    ]
    a_chain, b_chain = chain(2 * cols), chain(2 * cols)
    return pl.pallas_call(
        functools.partial(tail_kernel, heads, dk, buckets, blocks, extra),
        grid=(blocks,),
        in_specs=[
            full(bids),
            full(qkv),
            pl.BlockSpec((heads, 1, seq, BLK), lambda i: (0, i, 0, 0)),
            pl.BlockSpec((heads, 1, 1, BLK), lambda i: (0, i, 0, 0)),
            full(wall),
            full(ctx),
            full(again),
            full(fgain),
            full(early),
        ]
        + [any_spec] * 11,
        out_specs=[any_spec, any_spec] + [full(v) for v in outs],
        out_shape=[jax.ShapeDtypeStruct((d, rows), F32), jax.ShapeDtypeStruct((d, rows), BF)] + outs,
        scratch_shapes=[
            pltpu.VMEM((d, rows), F32),
            pltpu.VMEM((d, rows), F32),
            pltpu.VMEM((d, rows), F32),
            pltpu.VMEM((d, seq), BF),
            pltpu.VMEM((3 * cols, d), BF),
            pltpu.VMEM((d, 3 * cols), BF),
            pltpu.VMEM((d, 3 * cols), BF),
            pltpu.VMEM((d, rows), BF),
            pltpu.VMEM((cols, seq), BF),
            pltpu.VMEM((cols, rows), BF),
            pltpu.VMEM((d, cols), BF),
            pltpu.VMEM((d, cols), BF),
            pltpu.VMEM((d, 128), F32),
            pltpu.VMEM((d, 1), F32),
            pltpu.VMEM((d, 1), F32),
            pltpu.VMEM((seq, BLK), F32),
            pltpu.VMEM((2 * cols, seq), F32),
            pltpu.VMEM((heads, 5, BLK, BLK), F32),
            pltpu.VMEM((3 * cols, seq), BF),
            pltpu.VMEM((3 * cols, rows), BF),
            pltpu.VMEM((d, 4 * cols), F32),
            a_chain[0],
            b_chain[0],
        ]
        + a_chain[1:]
        + b_chain[1:]
        + [
            pltpu.VMEM((deep, 4, 3, spad, BLK), BF),
            pltpu.VMEM((2, 3, spad, BLK), BF),
            pltpu.VMEM((2, 1, 3, spad, BLK), BF),
            pltpu.VMEM((deep, 4, 3, spad, BLK), BF),
            pltpu.VMEM((deep + 1, 2, 3, spad, BLK), BF),
            pltpu.VMEM((later - 1, 1, 3, spad, BLK), BF),
            pltpu.VMEM((6, lines, 128), F32),
            pltpu.VMEM((5, lines, 128), F32),
            dma((7 + near,)),
            dma((later,)),
            dma((7,)), dma((7,)),
            dma((2, 4)), dma((2, 4)),
            dma((5,)), dma((5,)),
            dma((4, later)), dma((4, later)),
        ],
        compiler_params=pltpu.CompilerParams(
            vmem_limit_bytes=FF_VMEM, collective_id=1, has_side_effects=True
        ),
        cost_estimate=pl.CostEstimate(
            flops=32 * heads * seq * seq * dk + 8 * seq * d * 3 * cols,
            bytes_accessed=2 * heads * seq * seq + 30 * rows * d,
            transcendentals=0,
        ),
    )(bids, qkv, e, inv, wall, ctx, again, fgain, early, din, mid, cot, tok, nrm, wq, wfar, far,
      quarter, half_way, hand)


def outputs_kernel(near_ref, back_ref, ig_ref, ffi_ref, rel_ref, *refs):
    n = (len(refs) - 4) // 2
    refs, rel_out = refs[:-1], refs[-1]
    sources, res_ref, ig_out, ffi_out, targets = refs[:n], refs[n], refs[n + 1], refs[n + 2], refs[n + 3 :]
    res_ref[...] = near_ref[...] + back_ref[...].astype(F32)
    ig_out[...] = ig_ref[...]
    ffi_out[...] = ffi_ref[...]

    @pl.when(pl.program_id(0) == 0)
    def _():
        for i in range(n):
            targets[i][...] = sources[i][...]
        rel_out[...] = rel_ref[...].T[0 : rel_out.shape[0], 0 : rel_out.shape[1]]


def outputs(near, back, ig, ffi, small, rel_shape, *grads):
    d, rows = near.shape
    block = pl.BlockSpec((d // 2, rows), lambda i: (i, 0))
    shard, two, f = ffi.shape
    part = pl.BlockSpec((shard // 2, two, f), lambda i: (i, 0, 0))
    one = pl.Buffered(1)
    whole = [pl.BlockSpec(v.shape, lambda i, n=v.ndim: (0,) * n, pipeline_mode=one) for v in grads]
    return pl.pallas_call(
        outputs_kernel,
        grid=(2,),
        in_specs=[block] * 3 + [part, pl.BlockSpec((rel_shape[1], 128), lambda i: (0, 0))] + whole,
        out_specs=[block] * 2 + [part] + whole + [pl.BlockSpec(rel_shape, lambda i: (0, 0))],
        out_shape=[jax.ShapeDtypeStruct(v.shape, F32) for v in (near, ig, ffi) + grads]
        + [jax.ShapeDtypeStruct(rel_shape, F32)],
        compiler_params=pltpu.CompilerParams(vmem_limit_bytes=FF_VMEM),
    )(near, back, ig, ffi, small, *grads)


def take(array, index):
    return lax.dynamic_index_in_dim(array, index, 0, keepdims=False)


def per_device(
    tokens,
    cotangent,
    doc_lengths,
    pad_mask,
    attn_gain,
    qkv_weight,
    rel_table,
    out_weight,
    ff_gain,
    ff_in_weight,
    ff_out_weight,
):
    rows, d = tokens.shape
    n_dp = lax.axis_size("dp")
    n_mp = lax.axis_size("mp")
    cols = qkv_weight.shape[2]
    buckets, heads = rel_table.shape
    dk = cols // heads
    me = lax.axis_index("dp")
    shard = d // n_dp
    extra = n_dp // 16

    def hop(v, mask):
        return lax.ppermute(v, "dp", [(i, i ^ mask) for i in range(n_dp)])

    def bit(b):
        return (me >> b) & 1

    def finish(g):
        parts = [g.reshape((extra, shard) + g.shape[1:])]
        for b in reversed(range(extra.bit_length() - 1)):
            halves = [p.reshape((2, p.shape[0] // 2) + p.shape[1:]) for p in parts]
            away = sum(take(p, 1 - bit(b)).astype(F32) for p in halves).astype(BF)
            parts = [take(p, bit(b)) for p in halves] + [hop(away, 1 << b)]
        return sum(p.astype(F32) for p in parts)[0]

    tok = tokens.T
    cot = cotangent.T
    far = lax.ppermute(tok.astype(BF), "mp", [(0, 1), (1, 0)])
    w2 = jnp.transpose(ff_in_weight, (1, 0, 2))
    wq = jnp.transpose(qkv_weight, (1, 2, 0)).reshape(3 * cols, d)
    again, fgain = attn_gain.reshape(1, d), ff_gain.reshape(1, d)

    e, inv, qkv, ctx, nrm, xt, mid, ct, wall = front(
        rel_table, doc_lengths, pad_mask, again, fgain, wq, out_weight.T, tok, far, cot, heads, dk
    )
    early, din, near_out, far_out, quarter, half_way, hand, wfar = ff_all(
        xt, ct, w2, ff_out_weight, mid, wq, extra
    )
    input_grad, back, grad_qkv, grad_out, small, ffo, ffi = tail(
        qkv, e, inv, wall, ctx, again, fgain, early, din, mid, cot, tok, nrm, wq, wfar, far_out,
        quarter, half_way, hand, buckets, heads, dk, extra, ff_out_weight.shape[1],
    )
    for b in range(extra.bit_length() - 1):
        small = small + hop(small, 1 << b)
    result, input_grad, ffi, grad_qkv, grad_out, ffo, rel_grad = outputs(
        near_out, back, input_grad, ffi, small, (heads * n_mp, buckets), grad_qkv, grad_out, ffo
    )
    grad_qkv = jnp.transpose(grad_qkv, (1, 0, 2))
    if extra > 1:
        grad_qkv, grad_out, ffo, ffi = (finish(g) for g in (grad_qkv, grad_out, ffo, ffi))
    lines = -(-d // 128)
    return (
        result.T,
        input_grad.T,
        small[buckets : buckets + lines].reshape(-1)[:d],
        grad_qkv,
        rel_grad.T,
        grad_out,
        small[buckets + lines : buckets + 2 * lines].reshape(-1)[:d],
        ffi,
        ffo,
    )


def solution(mesh):
    return jax.shard_map(
        per_device,
        mesh=mesh,
        in_specs=(
            P(("dp", "mp"), None),
            P(("dp", "mp"), None),
            P("dp", None),
            P("dp", None),
            P(),
            P(None, None, "mp"),
            P(None, "mp"),
            P(None, "mp"),
            P(),
            P(None, None, "mp"),
            P(None, "mp"),
        ),
        out_specs=(
            P(("dp", "mp"), None),
            P(("dp", "mp"), None),
            P(),
            P("dp", None, "mp"),
            P(),
            P("dp", "mp"),
            P(),
            P("dp", None, "mp"),
            P("dp", "mp"),
        ),
        check_vma=False,
    )
```

```python
import functools

import jax
import jax.numpy as jnp
import numpy as np
from jax import lax
from jax.experimental import pallas as pl
from jax.experimental.pallas import tpu as pltpu
from jax.sharding import PartitionSpec as P

MAXDIST = 128
norm_eps = 1e-06
BLK = 256
SPAN = 6 * BLK
REACH = 2
BF = jnp.bfloat16
F32 = jnp.float32
FF_VMEM = 63 << 20


def bucket_of(offsets, buckets, reach):
    half_range = buckets // 2
    upper_half = (offsets > 0).astype(np.int32) * half_range
    distance = np.abs(offsets)
    exact_range = half_range // 2
    safe_dist = np.maximum(distance, 1)
    log_bucket = exact_range + (
        np.log(safe_dist / exact_range) / np.log(reach / exact_range) * (half_range - exact_range)
    ).astype(np.int32)
    log_bucket = np.minimum(log_bucket, half_range - 1)
    return (upper_half + np.where(distance < exact_range, distance, log_bucket)).astype(np.int32)


def lane_buckets(buckets):
    lanes = np.arange(SPAN)
    shifted = np.where(lanes < 5 * BLK, lanes, lanes - SPAN)
    return bucket_of(REACH * BLK - shifted, buckets, MAXDIST).reshape(1, SPAN)


def dot(a, b, contract):
    return lax.dot_general(a, b, (contract, ((), ())), preferred_element_type=F32)


def flip(index, mask):
    out = index
    bit = 1
    while bit <= mask:
        if mask & bit:
            out = out + bit * (1 - 2 * (index // bit % 2))
        bit *= 2
    return out


GROUP_MASKS = (1, 2, 4, 12)


def group_coords(g):
    b = [g // (1 << i) % 2 for i in range(4)]
    return [b[0], b[1], (b[2] + b[3]) % 2, b[3]]


Y_FIRST = (0, 1, 2, 3)
Z_FIRST = (0, 2, 3, 1)
Z_BLOCK = 1
LEVELS = (4, 3, 3, 2)


def order_of(block):
    return Z_FIRST if block == Z_BLOCK else Y_FIRST


def levels_of(block):
    return LEVELS[block] if block < len(LEVELS) else 1


def block_position(k, order):
    b = [k >> i & 1 for i in range(4)]
    c = [b[0], b[1], b[2] ^ b[3], b[3]]
    return sum(c[order[i]] << (3 - i) for i in range(4))


def column(line):
    return jnp.broadcast_to(line, (8, line.shape[1])).T[:, 0:1]


def norm_scale(v):
    return lax.rsqrt(jnp.mean(v * v, axis=0, keepdims=True) + norm_eps)


def lanes(block):
    return pl.ds(pl.multiple_of(block * BLK, BLK), BLK)


def remote(src, dst, send, recv, who):
    return pltpu.make_async_remote_copy(
        src_ref=src,
        dst_ref=dst,
        send_sem=send,
        recv_sem=recv,
        device_id=who,
        device_id_type=pl.DeviceIdType.MESH,
    )


def meet(devices):
    barrier = pltpu.get_barrier_semaphore()
    for who in devices:
        pl.semaphore_signal(barrier, inc=1, device_id=who, device_id_type=pl.DeviceIdType.MESH)
    pl.semaphore_wait(barrier, len(devices))


def near_diagonal(offset):
    i = offset + 3
    return i + (6 - i) // 6 - i // 6 - 1


def front_kernel(
    heads, dk, buckets, blocks,
    rel_ref, len_ref, bid_ref, pad_ref, ag_ref, fg_ref, wq_ref, wo_ref,
    tok_hbm, far_hbm, cot_hbm,
    e_ref, inv_ref, qkv_ref, ctx_hbm, nrm_hbm, xt_hbm, mid_hbm, ct_hbm, wall_hbm,
    f1, fb, f3, cl, nrm, table, padc, mask, score, agc, fgc, wall, wn, call, xo,
    lsem, osem, wsend, wrecv, csend, crecv,
):
    qb = pl.program_id(0)
    dp, x = lax.axis_index("dp"), lax.axis_index("mp")
    d, rows = f1.shape
    cols = heads * dk
    half = cols // 2
    core = dp % 2
    other = (dp, 1 - x)
    sibling = (dp + 1 - 2 * core, x)
    near_blocks = blocks // 2
    part = pl.ds(core * half, half)
    far_part = pl.ds(cols + core * half, half)

    def local(i):
        src, dst = ((tok_hbm, f1), (far_hbm, fb), (cot_hbm, f3))[i]
        return pltpu.make_async_copy(src, dst, lsem.at[i])

    def out(i):
        src, dst = (
            (call, ctx_hbm), (nrm, nrm_hbm), (f1.at[:, lanes(0)], mid_hbm.at[:, lanes(0)]), (cl, ct_hbm.at[:, pl.ds(0, rows)]), (wall, wall_hbm),
            (f1.at[:, pl.ds(BLK, rows - BLK)], mid_hbm.at[:, pl.ds(BLK, rows - BLK)]),
        )[i]
        return pltpu.make_async_copy(src, dst, osem.at[i])

    def xt_out(b):
        return pltpu.make_async_copy(xo.at[:, lanes(b)], xt_hbm.at[:, lanes(b)], osem.at[6 + b])

    w_copy = remote(wo_ref.at[part], wall.at[far_part], wsend.at[0], wrecv.at[0], other)
    w_pass = remote(wall.at[far_part], wall.at[far_part], wsend.at[1], wrecv.at[1], sibling)
    piece = d // 4

    def c_copy(i):
        rs = pl.ds(i * piece, piece)
        return remote(
            cl.at[rs, pl.ds(0, BLK)], ct_hbm.at[rs, pl.ds(rows, BLK)], wsend.at[2 + i], wrecv.at[2 + i], other
        )

    def ctx_copy(b):
        there = (b + near_blocks) % blocks
        return remote(
            call.at[pl.ds(0, cols), lanes(b)], call.at[pl.ds(cols, cols), lanes(there)],
            csend.at[b], crecv.at[b], other,
        )

    @pl.when(qb == 0)
    def _():
        for i in (2, 0, 1):
            local(i).start()
        meet([other, sibling])
        w_copy.start()
        wall[0:cols, :] = wo_ref[...]
        local(2).wait()
        cl[...] = f3[...].astype(BF)
        c_copy(0).start()
        c_copy(1).start()
        out(3).start()
        agc[...] = column(ag_ref[...])
        fgc[...] = column(fg_ref[...])
        local(0).wait()
        local(1).wait()
        for b in range(blocks):
            ls = slice(b * BLK, (b + 1) * BLK)
            v = f1[:, ls] if b < near_blocks else fb[:, b * BLK - rows : (b + 1) * BLK - rows].astype(F32)
            nrm[:, ls] = (v * norm_scale(v) * agc[...]).astype(BF)
            qkv_ref[:, ls] = dot(wq_ref[...], nrm[:, ls], ((1,), (0,))).astype(BF)
        out(1).start()
        for i in range(2):
            start = (1 - x) * rows if i else x * rows
            line = pad_ref[:, pl.ds(pl.multiple_of(start, BLK), rows)].astype(F32)
            padc[i * rows : (i + 1) * rows, :] = jnp.broadcast_to(line, (8, rows)).T
        ids = bid_ref[...]
        for hh in range(heads):
            line = jnp.zeros((1, SPAN), F32)
            for b in range(buckets):
                line = jnp.where(ids == b, rel_ref[b, hh], line)
            turned = pltpu.roll(
                jnp.broadcast_to(line, (BLK, SPAN)), 0, 1, stride=1, stride_axis=0
            )
            for g in range(5):
                table[hh, g] = turned[:, BLK * (4 - g) : BLK * (5 - g)]

    @pl.when(qb == 1)
    def _():
        w_copy.wait()
        w_pass.start()

    q_true = (qb + near_blocks * x) % blocks

    q_pos = q_true * BLK + lax.broadcasted_iota(jnp.int32, (1, BLK), 1)
    k_iota = lax.broadcasted_iota(jnp.int32, (BLK, BLK), 0)
    for kb in range(blocks):
        k_pos = (kb + near_blocks * x) % blocks * BLK + k_iota
        bound = 0
        q_doc = jnp.zeros((1, BLK), jnp.int32)
        k_doc = jnp.zeros((BLK, BLK), jnp.int32)
        for i in range(len_ref.shape[1]):
            bound = bound + len_ref[0, i]
            q_doc = q_doc + (q_pos >= bound).astype(jnp.int32)
            k_doc = k_doc + (k_pos >= bound).astype(jnp.int32)
        krows = slice(kb * BLK, (kb + 1) * BLK)
        seen = (padc[krows, 0:1] > 0.5) | (k_pos == q_pos)
        mask[krows, :] = jnp.where((k_doc == q_doc) & seen, 0.0, -1000000000.0)

    def head_rows(h, group):
        return pl.ds(pl.multiple_of(group * cols + h * dk, dk), dk)

    def diagonal(kb):
        return near_diagonal((kb + near_blocks * x) % blocks - q_true)

    def head(h, carry):
        qh = qkv_ref[head_rows(h, 0), lanes(qb)]
        peak = None
        for kb in range(blocks):
            krows = slice(kb * BLK, (kb + 1) * BLK)
            s = dot(qkv_ref[head_rows(h, 1), krows], qh, ((0,), (0,)))
            diag = diagonal(kb)
            s = s + table[h, diag] + mask[krows, :]
            score[krows, :] = s
            top = jnp.max(s, axis=0, keepdims=True)
            peak = top if peak is None else jnp.maximum(peak, top)
        total = jnp.zeros((1, BLK), F32)
        ctx = jnp.zeros((dk, BLK), F32)
        for kb in range(blocks):
            krows = slice(kb * BLK, (kb + 1) * BLK)
            e = jnp.exp(score[krows, :] - peak)
            total = total + jnp.sum(e, axis=0, keepdims=True)
            e_low = e.astype(BF)
            e_ref[h, 0, krows, :] = e_low
            ctx = ctx + dot(qkv_ref[head_rows(h, 2), krows], e_low, ((1,), (0,)))
        inv = 1.0 / total
        inv_ref[h, 0] = inv
        call[head_rows(h, 0), lanes(qb)] = (ctx * inv).astype(BF)
        return carry

    lax.fori_loop(0, heads, head, 0)
    ctx_copy(qb).start()

    @pl.when(qb == 1)
    def _():
        c_copy(2).start()

    @pl.when(qb == blocks - 1)
    def _():
        c_copy(3).start()
        w_pass.wait()
        wn[...] = wall[...].astype(F32).T.astype(BF)
        out(4).start()
        for i in range(blocks):
            b = (i + near_blocks) % blocks
            ctx_copy(i).wait()
            ls = slice(b * BLK, (b + 1) * BLK)
            v = dot(wn[...], call[:, ls], ((1,), (0,)))
            if b < near_blocks:
                v = v + f1[:, ls]
                f1[:, ls] = v
                if b == 0:
                    out(2).start()
            else:
                v = v + fb[:, b * BLK - rows : (b + 1) * BLK - rows].astype(F32)
            xo[:, ls] = (v * norm_scale(v) * fgc[...]).astype(BF)
            xt_out(b).start()
        out(0).start()
        out(5).start()
        for i in range(4):
            c_copy(i).wait()
        for i in range(6):
            out(i).wait()
        for b in range(blocks):
            xt_out(b).wait()


def front(rel, lengths, pad, again, fgain, wq, wo, tok, far, cot, heads, dk):
    d, rows = tok.shape
    seq = 2 * rows
    cols = heads * dk
    blocks = seq // BLK
    buckets = rel.shape[0]
    bids = jnp.asarray(lane_buckets(buckets))
    one = pl.Buffered(1)
    dma = pltpu.SemaphoreType.DMA
    any_spec = pl.BlockSpec(memory_space=pl.ANY)
    smem = pl.BlockSpec(memory_space=pltpu.SMEM)

    def full(v):
        return pl.BlockSpec(v.shape, lambda i: (0, 0), pipeline_mode=one)

    return pl.pallas_call(
        functools.partial(front_kernel, heads, dk, buckets, blocks),
        grid=(blocks,),
        in_specs=[smem, smem, full(bids), full(pad), full(again), full(fgain), full(wq), full(wo)]
        + [any_spec] * 3,
        out_specs=[
            pl.BlockSpec((heads, 1, seq, BLK), lambda i: (0, i, 0, 0)),
            pl.BlockSpec((heads, 1, 1, BLK), lambda i: (0, i, 0, 0)),
            pl.BlockSpec((3 * cols, seq), lambda i: (0, 0)),
        ]
        + [any_spec] * 6,
        out_shape=[
            jax.ShapeDtypeStruct((heads, blocks, seq, BLK), BF),
            jax.ShapeDtypeStruct((heads, blocks, 1, BLK), F32),
            jax.ShapeDtypeStruct((3 * cols, seq), BF),
            jax.ShapeDtypeStruct((2 * cols, seq), BF),
            jax.ShapeDtypeStruct((d, seq), BF),
            jax.ShapeDtypeStruct((d, seq), BF),
            jax.ShapeDtypeStruct((d, rows), F32),
            jax.ShapeDtypeStruct((d, seq), BF),
            jax.ShapeDtypeStruct((2 * cols, d), BF),
        ],
        scratch_shapes=[
            pltpu.VMEM((d, rows), F32),
            pltpu.VMEM((d, rows), BF),
            pltpu.VMEM((d, rows), F32),
            pltpu.VMEM((d, rows), BF),
            pltpu.VMEM((d, seq), BF),
            pltpu.VMEM((heads, 5, BLK, BLK), F32),
            pltpu.VMEM((seq, 8), F32),
            pltpu.VMEM((seq, BLK), F32),
            pltpu.VMEM((seq, BLK), F32),
            pltpu.VMEM((d, 1), F32),
            pltpu.VMEM((d, 1), F32),
            pltpu.VMEM((2 * cols, d), BF),
            pltpu.VMEM((d, 2 * cols), BF),
            pltpu.VMEM((2 * cols, seq), BF),
            pltpu.VMEM((d, seq), BF),
            dma((3,)), dma((6 + blocks,)), dma((6,)), dma((6,)), dma((blocks,)), dma((blocks,)),
        ],
        compiler_params=pltpu.CompilerParams(
            vmem_limit_bytes=FF_VMEM, collective_id=2, has_side_effects=True
        ),
        cost_estimate=pl.CostEstimate(
            flops=16 * heads * seq * seq * dk + 10 * seq * d * cols,
            bytes_accessed=2 * heads * seq * seq + 30 * rows * d,
            transcendentals=heads * seq * seq,
        ),
    )(rel, lengths, bids, pad, again, fgain, wq, wo, tok, far, cot)


def ff_kernel(
    steps, extra,
    xt_hbm, w_hbm, ct_hbm, wo_hbm, mid_hbm, wq_hbm,
    grads_ref, din_hbm, near_hbm, far_hbm, quarter_hbm, half_hbm, hand_hbm, wfar_hbm,
    xt, ct, wg, wu, wo, hid, dg, du, din, stage, r1, r2, r3, r4, xs, xr, of,
    csem, wsem, s1, s2, s3, s4, t1, t2, t3, t4, xsem, osem, hsem,
):
    f, total = hid.shape
    rows = total // 2
    chunks = rows // BLK
    d = xt.shape[0]
    shard = d // 16
    dp, mp = lax.axis_index("dp"), lax.axis_index("mp")
    a = group_coords(dp // extra)
    peers = [flip(dp, m * extra) for m in GROUP_MASKS]
    other = (dp, 1 - mp)
    core = dp % 2
    sibling = dp + 1 - 2 * core
    bufs = (r1, r2, r3, r4)
    sends, recvs = (s1, s2, s3, s4), (t1, t2, t3, t4)
    end = steps - 1

    def weight_copy(kind, n):
        src, dst = ((w_hbm.at[0], wg), (w_hbm.at[1], wu), (wo_hbm, wo))[kind]
        return pltpu.make_async_copy(src.at[:, lanes(n)], dst.at[:, lanes(n)], wsem.at[kind, n])

    def tok_copy(n):
        src, dst, start, size = (
            (xt_hbm, xt, rows, BLK), (ct_hbm, ct, rows, BLK),
            (xt_hbm, xt, 0, rows), (ct_hbm, ct, 0, rows), (xt_hbm, xt, rows + BLK, BLK),
        )[n]
        part = pl.ds(start, size)
        return pltpu.make_async_copy(src.at[:, part], dst.at[:, part], csem.at[n])

    near_part, far_part = pl.ds(0, rows), pl.ds(rows, rows)
    c_far = remote(
        ct_hbm.at[:, pl.ds(BLK, BLK)], ct.at[:, pl.ds(rows + BLK, BLK)], csem.at[5], csem.at[6], other
    )
    x_copy = remote(xs, xr, xsem.at[0], xsem.at[1], other)
    wq_rows = wq_hbm.shape[0] // 2
    wq_part = pl.ds(core * wq_rows, wq_rows)
    w_copy = remote(wq_hbm.at[wq_part], wfar_hbm.at[wq_part], xsem.at[2], xsem.at[3], other)
    w_pass = remote(wfar_hbm.at[wq_part], wfar_hbm.at[wq_part], xsem.at[4], xsem.at[5], (sibling, mp))
    mid_copy = pltpu.make_async_copy(mid_hbm, din.at[:, far_part], osem.at[3])

    deep = len(LEVELS)

    def hop(level, n, order):
        half = 8 >> level
        c = order[level]
        away = pl.ds((1 - a[c]) * half, half)
        src = stage.at[away] if level == 0 else bufs[level - 1].at[n, away]
        return remote(src, bufs[level].at[n], sends[level].at[n], recvs[level].at[n], (peers[c], mp))

    def hand_copy(n):
        level = levels_of(n) if isinstance(n, int) else 1
        dst = (hand_hbm.at[n - deep], half_hbm, quarter_hbm.at[n - 1])[level - 1]
        return pltpu.make_async_copy(bufs[level - 1].at[n], dst, hsem.at[n])

    def absorb_first(n):
        hop(0, n, Y_FIRST).wait()
        r1[n] = stage[pl.ds(a[0] * 8, 8)] + r1[n]
        if isinstance(n, int):
            hand_copy(n).start()
            return

        @pl.when(n == Z_BLOCK)
        def _():
            hop(1, n, Z_FIRST).start()

        @pl.when((n < deep) & (n != Z_BLOCK))
        def _():
            hop(1, n, Y_FIRST).start()

        @pl.when(n >= deep)
        def _():
            hand_copy(n).start()

    def absorb(level, n):
        half = 8 >> level
        order = order_of(n)
        hop(level, n, order).wait()
        kept = bufs[level - 1][n, pl.ds(a[order[level]] * half, half)]
        if level < 3:
            bufs[level][n] = kept + bufs[level][n]
            if level + 1 < levels_of(n):
                hop(level + 1, n, order).start()
            else:
                hand_copy(n).start()
        else:
            both = kept.astype(F32) + bufs[level][n].astype(F32)
            for w in range(3):
                grads_ref[w, :, n * BLK : (n + 1) * BLK] = both[0, w]

    scale = np.float32(np.sqrt(2 / np.pi))

    def place(u):
        early, late = u // steps, (u - 4) // steps
        is_far0 = (early == 0) * 1
        is_far1 = (late == 1) * 1
        v = u - steps
        n = v - steps * (u // (2 * steps + 4))
        near_j, near_c = n // 2, n % 2
        j = is_far0 * u + is_far1 * (u - steps - 4) + (1 - is_far0 - is_far1) * near_j
        c = is_far0 * chunks + is_far1 * (chunks + 1) + (1 - is_far0 - is_far1) * near_c
        return j, c

    def substep(u):
        j, c = place(u)
        pj, pc = place(u - 1)
        pj = pj + (u == 0) * 1
        fcols, tok = lanes(j), lanes(c)
        pcols, ptok = lanes(pj), lanes(pc)
        gate = dot(wg[:, fcols], xt[:, tok], ((0,), (0,)))
        up = dot(wu[:, fcols], xt[:, tok], ((0,), (0,)))
        dh = dot(wo[:, fcols], ct[:, tok], ((0,), (0,)))
        backward(pcols, ptok)
        sq = gate * gate
        t = jnp.tanh(scale * gate * (1.0 + 0.044715 * sq))
        half = 0.5 * (1.0 + t)
        act = gate * half
        slope = half + 0.5 * gate * (1.0 - t * t) * (scale * (1.0 + (3 * 0.044715) * sq))
        hid[fcols, tok] = (act * up).astype(BF)
        dg[fcols, tok] = (dh * (up * slope)).astype(BF)
        du[fcols, tok] = (dh * act).astype(BF)

    def backward(rs, tok):
        din[:, tok] += dot(wg[:, rs], dg[rs, tok], ((1,), (0,))) + dot(wu[:, rs], du[rs, tok], ((1,), (0,)))

    per = 4 * shard

    def grads(j):
        z = (j == Z_BLOCK) * 1
        for w in range(3):
            right = (hid, dg, du)[w][lanes(j), :]
            for q in range(4):
                rs = slice(q * per, (q + 1) * per)
                left = ct[rs, :] if w == 0 else xt[rs, :]
                part = dot(left, right, ((1,), (1,)))
                for k in range(4):
                    at = block_position(4 * q + k, Y_FIRST)
                    at = at + z * (block_position(4 * q + k, Z_FIRST) - at)
                    stage[at, w, 0:shard, :] = part[k * shard : (k + 1) * shard].astype(BF)
        hop(0, j, Y_FIRST).start()

    def out_part(n):
        return dot(wo[...], hid[:, lanes(n)], ((1,), (0,)))

    meet([(p, mp) for p in peers] + [other] + ([(sibling, mp)] if extra > 1 else []))
    c_far.start()
    w_copy.start()
    tok_copy(0).start()
    tok_copy(1).start()
    for n in range(steps):
        for kind in range(3):
            weight_copy(kind, n).start()
    for n in range(2, 5):
        tok_copy(n).start()
    din[...] = jnp.zeros_like(din)
    stage[...] = jnp.zeros_like(stage)
    before = place(-1)[1]
    dg[0:BLK, before * BLK : (before + 1) * BLK] = jnp.zeros((BLK, BLK), BF)
    du[0:BLK, before * BLK : (before + 1) * BLK] = jnp.zeros((BLK, BLK), BF)
    tok_copy(0).wait()
    tok_copy(1).wait()
    count = 2 * chunks * steps
    far_end = 2 * steps + 4

    def step(u, carry):
        @pl.when(u < steps)
        def _():
            for kind in range(3):
                weight_copy(kind, u).wait()

        @pl.when(u == steps)
        def _():
            tok_copy(2).wait()
            tok_copy(3).wait()

        @pl.when(u == steps + 4)
        def _():
            tok_copy(4).wait()
            c_far.wait()

        @pl.when(u < count)
        def _():
            substep(u)

        @pl.when(u == far_end)
        def _():
            xs[...] = din[:, far_part].astype(BF)
            x_copy.start()
            mid_copy.start()

        odd = u % 2 == 1
        late = (u >= 2 * steps + 5) * 1
        m = (u - 13) // 2 - 2 * ((u >= 2 * steps + 7) * 1)
        n = (u - 11) // 2 - 2 * late

        @pl.when(odd & ((u == 13) | (u == 15) | (u >= 2 * steps + 7)))
        def _():
            absorb_first(m)

        for at, events in (
            (21, ((1, 0),)), (23, ((1, 1),)), (25, ((2, 0),)), (27, ((1, 2),)),
        ):
            @pl.when(u == at)
            def _():
                for level, block in events:
                    absorb(level, block)

        @pl.when(odd & ((u == 11) | (u == 13) | (u >= 2 * steps + 5)))
        def _():
            grads(n)

        @pl.when(u == far_end + 5)
        def _():
            w_copy.wait()
            w_pass.start()

        return carry

    lax.fori_loop(0, count, step, 0)
    pj, pc = place(count - 1)
    backward(lanes(pj), lanes(pc))

    def far_out(n, carry):
        of[:, lanes(n)] = out_part(n + chunks).astype(BF)
        return carry

    lax.fori_loop(0, chunks, far_out, 0)
    absorb(2, 1)
    far_copy = pltpu.make_async_copy(of, far_hbm, osem.at[0])
    far_copy.start()
    mid_copy.wait()

    def near_out(n, carry):
        at = lanes(n + chunks)
        din[:, at] = din[:, at] + out_part(n)
        return carry

    lax.fori_loop(0, chunks, near_out, 0)
    near_copy = pltpu.make_async_copy(din.at[:, far_part], near_hbm, osem.at[1])
    near_copy.start()
    absorb_first(end)
    x_copy.wait()
    din[:, near_part] += xr[...].astype(F32)
    din_copy = pltpu.make_async_copy(din.at[:, near_part], din_hbm, osem.at[2])
    din_copy.start()
    absorb(3, 0)
    absorb(2, 2)
    absorb(1, 3)
    w_pass.wait()
    for n in range(1, steps):
        hand_copy(n).wait()
    far_copy.wait()
    near_copy.wait()
    din_copy.wait()


def ff_all(xt, ct, w2, wo, mid, wq, extra):
    d, total = xt.shape
    f = wo.shape[1]
    rows = total // 2
    steps = f // BLK
    deep = len(LEVELS)
    shard = d // 16
    spad = -(-shard // 16) * 16
    dma = pltpu.SemaphoreType.DMA
    any_spec = pl.BlockSpec(memory_space=pl.ANY)
    return pl.pallas_call(
        functools.partial(ff_kernel, steps, extra),
        in_specs=[any_spec] * 6,
        out_specs=[pl.BlockSpec(memory_space=pltpu.VMEM)] + [any_spec] * 7,
        out_shape=[
            jax.ShapeDtypeStruct((3, spad, BLK), F32),
            jax.ShapeDtypeStruct((d, rows), F32),
            jax.ShapeDtypeStruct((d, rows), F32),
            jax.ShapeDtypeStruct((d, rows), BF),
            jax.ShapeDtypeStruct((2, 2, 3, spad, BLK), BF),
            jax.ShapeDtypeStruct((4, 3, spad, BLK), BF),
            jax.ShapeDtypeStruct((steps - deep, 8, 3, spad, BLK), BF),
            jax.ShapeDtypeStruct(wq.shape, BF),
        ],
        scratch_shapes=[
            pltpu.VMEM((d, total), BF),
            pltpu.VMEM((d, total), BF),
            pltpu.VMEM((d, f), BF),
            pltpu.VMEM((d, f), BF),
            pltpu.VMEM((d, f), BF),
            pltpu.VMEM((f, total), BF),
            pltpu.VMEM((f, total), BF),
            pltpu.VMEM((f, total), BF),
            pltpu.VMEM((d, total), F32),
            pltpu.VMEM((16, 3, spad, BLK), BF),
            pltpu.VMEM((steps, 8, 3, spad, BLK), BF),
            pltpu.VMEM((4, 4, 3, spad, BLK), BF),
            pltpu.VMEM((3, 2, 3, spad, BLK), BF),
            pltpu.VMEM((1, 1, 3, spad, BLK), BF),
            pltpu.VMEM((d, rows), BF),
            pltpu.VMEM((d, rows), BF),
            pltpu.VMEM((d, rows), BF),
            dma((7,)),
            dma((3, steps)),
            dma((steps,)), dma((4,)), dma((3,)), dma((1,)),
            dma((steps,)), dma((4,)), dma((3,)), dma((1,)),
            dma((6,)),
            dma((4,)),
            dma((steps,)),
        ],
        compiler_params=pltpu.CompilerParams(
            vmem_limit_bytes=FF_VMEM, collective_id=0, has_side_effects=True
        ),
        cost_estimate=pl.CostEstimate(
            flops=18 * total * d * f,
            bytes_accessed=6 * d * f + 16 * total * d,
            transcendentals=total * f,
        ),
    )(xt, w2, ct, wo, mid, wq)


EVENTS = (
    ((0, 0), ((2, 3), (3, 2))),
    ((0, 2), ((1, 4),)),
    ((2, 0), ((3, 3),)),
    ((2, 1), ((2, 4),)),
    ((3, 2), ((1, 5),)),
)


def tail_kernel(
    heads, dk, buckets, blocks, extra,
    bid_ref, qkv_ref, e_ref, inv_ref, wall_ref, ctx_ref, ag_ref, fg_ref, early_ref,
    din_hbm, mid_hbm, cot_hbm, tok_hbm, nrm_hbm, wq_hbm, wfar_hbm, far_hbm,
    quarter_hbm, half_hbm, hand_hbm,
    ig_hbm, back_hbm, gq_ref, go_ref, small_ref, ffo_ref, ffi_ref,
    f1, f2, f3, nrm, wq, wn, wf, alow, dctx, dcs, osend, orecv, fsum, agc, fgc,
    dp_s, dkv, tally, dproj, dfar, grad,
    sa, sb_, a1, a2, a3, a4, b1, b2, b3, b4, hk, hm, hq, h2, h3, h4, sv, rv,
    lsem, ksem, xs_sem, xr_sem, cs_sem, cr_sem, bs_sem, br_sem, hs_sem, hr_sem,
):
    qb = pl.program_id(0)
    dp, x = lax.axis_index("dp"), lax.axis_index("mp")
    d, rows = f2.shape
    cols = heads * dk
    shard = d // 16
    a = group_coords(dp // extra)
    peers = [flip(dp, m * extra) for m in GROUP_MASKS]
    other = (dp, 1 - x)
    near_blocks = blocks // 2
    near_part, far_part = pl.ds(0, rows), pl.ds(rows, rows)
    halves = ((sa, a1, a2, a3, a4), (sb_, b1, b2, b3, b4))
    orders = (Y_FIRST, Y_FIRST)
    copies = (
        (din_hbm, f1), (mid_hbm, f2), (cot_hbm, f3), (tok_hbm, f2), (nrm_hbm, nrm), (wq_hbm, wq), (wfar_hbm, wq),
    )

    def local(i):
        return pltpu.make_async_copy(copies[i][0], copies[i][1], lsem.at[i])

    def x_copy(i, src, dst):
        return remote(src, dst, xs_sem.at[i], xr_sem.at[i], other)

    dctx_copy = x_copy(0, dcs, dctx.at[:, far_part])
    o_copy = x_copy(1, osend, orecv)
    dproj_copy = x_copy(2, dproj.at[:, far_part], dfar)

    def back_copy(i):
        part = pl.ds(i * 128, 128)
        return x_copy(3 + i, far_hbm.at[:, part], back_hbm.at[:, part])

    def hop(side, level):
        half = 8 >> level
        c = orders[side][level]
        away = pl.ds((1 - a[c]) * half, half)
        bufs = halves[side]
        return remote(
            bufs[level].at[away], bufs[level + 1], cs_sem.at[side, level], cr_sem.at[side, level], (peers[c], x)
        )

    def absorb(side, level):
        half = 8 >> level
        bufs = halves[side]
        hop(side, level).wait()
        kept = bufs[level][pl.ds(a[orders[side][level]] * half, half)]
        if level < 3:
            bufs[level + 1][...] = kept + bufs[level + 1][...]
            hop(side, level + 1).start()
            return
        both = (kept.astype(F32) + bufs[level + 1][...].astype(F32))[0, 0:shard]
        outs = (gq_ref.at[0], gq_ref.at[1]) if side == 0 else (gq_ref.at[2], go_ref)
        for i in range(2):
            outs[i][...] = both[:, i * cols : (i + 1) * cols]

    deep = len(LEVELS)
    handed = (3, 4, 2, 5, 6, 1)

    def keep_copy(block):
        level = levels_of(block)
        half = 8 >> level
        keep = pl.ds(a[order_of(block)[level]] * half, half)
        if level == 3:
            src, dst = quarter_hbm.at[block - 1, keep], hq.at[block - 1]
        elif level == 2:
            src, dst = half_hbm.at[keep], hm
        else:
            src, dst = hand_hbm.at[block - deep, keep], hk.at[block - deep]
        return pltpu.make_async_copy(src, dst, ksem.at[block])

    def hand_hop(level, block):
        half = 8 >> level
        c = order_of(block)[level]
        away = pl.ds((1 - a[c]) * half, half)
        fresh = level == levels_of(block)
        if level == 1:
            src, dst = hand_hbm.at[block - deep, away], h2.at[block - deep]
        elif level == 2:
            src, dst = half_hbm.at[away] if fresh else h2.at[block - deep, away], h3.at[block - 3]
        else:
            src, dst = quarter_hbm.at[block - 1, away] if fresh else h3.at[block - 3, away], h4.at[block - 1]
        return remote(src, dst, hs_sem.at[level, block], hr_sem.at[level, block], (peers[c], x))

    def put_grads(w, block, value):
        at = slice(block * BLK, (block + 1) * BLK)
        if w == 0:
            ffo_ref[:, at] = value
        else:
            ffi_ref[:, w - 1, at] = value

    def hand_absorb(level, block):
        half = 8 >> level
        keep = pl.ds(a[order_of(block)[level]] * half, half)
        hand_hop(level, block).wait()
        if level == levels_of(block):
            keep_copy(block).wait()
            kept = hk[block - deep] if level == 1 else (hm[...] if level == 2 else hq[block - 1])
        else:
            kept = h2[block - deep, keep] if level == 2 else h3[block - 3, keep]
        if level == 1:
            h2[block - deep] = kept + h2[block - deep]
        elif level == 2:
            h3[block - 3] = kept + h3[block - 3]
        else:
            both = kept.astype(F32) + h4[block - 1].astype(F32)
            for w in range(3):
                put_grads(w, block, both[0, w, 0:shard])
        if level < 3:
            hand_hop(level + 1, block).start()

    def round_copy(i):
        who = other if i == 4 else (peers[(0, 2, 3, 1)[i]], x)
        return remote(sv.at[i], rv.at[i], bs_sem.at[i], br_sem.at[i], who)

    def round_end(i):
        round_copy(i).wait()
        sv[i + 1] = sv[i] + rv[i]
        if i < 4:
            round_copy(i + 1).start()

    def out_copy(r):
        return pltpu.make_async_copy(f3.at[:, lanes(r)], ig_hbm.at[:, lanes(r)], lsem.at[len(copies) + r])

    def lane_sum(v):
        total = v[:, 0:128]
        for i in range(1, v.shape[1] // 128):
            total = total + v[:, i * 128 : (i + 1) * 128]
        return total

    @pl.when(qb == 0)
    def _():
        for i in range(3):
            local(i).start()
        meet([(p, x) for p in peers] + [other])
        back_copy(0).start()
        for block in handed[:-1]:
            hand_hop(levels_of(block), block).start()
        agc[...] = column(ag_ref[...])
        fgc[...] = column(fg_ref[...])
        dkv[...] = jnp.zeros_like(dkv)
        tally[...] = jnp.zeros_like(tally)
        sa[...] = jnp.zeros_like(sa)
        sb_[...] = jnp.zeros_like(sb_)
        fsum[...] = jnp.zeros_like(fsum)
        for i in range(3):
            local(i).wait()

        def norm_rows(r, carry):
            ls = lanes(r)
            v = f2[:, ls]
            c = f1[:, ls]
            scale = norm_scale(v)
            n = v * scale
            cg = c * fgc[...]
            m = jnp.mean(cg * n, axis=0, keepdims=True)
            gm = f3[:, ls] + scale * (cg - n * m)
            fsum[...] += lane_sum(c * n)
            f1[:, ls] = gm
            alow[:, ls] = gm.astype(BF)
            return carry

        lax.fori_loop(0, near_blocks, norm_rows, 0)
        dcs[...] = dot(wall_ref[cols : 2 * cols, :], alow[...], ((1,), (0,))).astype(BF)
        dctx_copy.start()
        for i in (3, 4, 5):
            local(i).start()
        for block in handed:
            keep_copy(block).start()
        dctx[:, near_part] = dot(wall_ref[0:cols, :], alow[...], ((1,), (0,))).astype(BF)
        osend[...] = dot(alow[...], ctx_ref[cols : 2 * cols, near_part], ((1,), (1,))).astype(BF)
        o_copy.start()
        grad[:, 3 * cols : 4 * cols] = dot(alow[...], ctx_ref[0:cols, near_part], ((1,), (1,)))
        for w in range(3):
            put_grads(w, 0, early_ref[w, 0:shard, :])
        dctx_copy.wait()
        back_copy(1).start()

    @pl.when(qb == 1)
    def _():
        local(5).wait()
        wn[...] = wq[...].astype(F32).T.astype(BF)
        local(6).start()

    @pl.when(qb == 2)
    def _():
        local(6).wait()
        wf[...] = wq[...].astype(F32).T.astype(BF)

    q_true = (qb + near_blocks * x) % blocks

    def head(h, carry):
        for at, events in EVENTS:
            @pl.when((qb == at[0]) & (h == at[1]))
            def _():
                for level, block in events:
                    hand_absorb(level, block)

        def head_rows(group):
            return pl.ds(pl.multiple_of(group * cols + h * dk, dk), dk)

        inv = inv_ref[h, 0]
        qh = qkv_ref[head_rows(0), lanes(qb)]
        scaled = (dctx[head_rows(0), lanes(qb)].astype(F32) * inv).astype(BF)
        inner = jnp.zeros((1, BLK), F32)
        for kb in range(blocks):
            krows = slice(kb * BLK, (kb + 1) * BLK)
            g = dot(qkv_ref[head_rows(2), krows], scaled, ((0,), (0,)))
            dp_s[krows, :] = g
            inner = inner + jnp.sum(e_ref[h, 0, krows, :].astype(F32) * g, axis=0, keepdims=True)
        inner = inner * inv
        dq = jnp.zeros((dk, BLK), F32)
        for kb in range(blocks):
            krows = slice(kb * BLK, (kb + 1) * BLK)
            e = e_ref[h, 0, krows, :]
            ds = (e.astype(F32) * (dp_s[krows, :] - inner)).astype(BF)
            dkv[head_rows(0), krows] += dot(qh, ds, ((1,), (1,)))
            dkv[head_rows(1), krows] += dot(scaled, e, ((1,), (1,)))
            dq = dq + dot(qkv_ref[head_rows(1), krows], ds, ((1,), (0,)))
            tally[h, near_diagonal((kb + near_blocks * x) % blocks - q_true)] += ds.astype(F32)
        dproj[head_rows(0), lanes(qb)] = dq.astype(BF)
        return carry

    lax.fori_loop(0, heads, head, 0)

    @pl.when(qb == blocks - 1)
    def _():
        dproj[cols : 3 * cols, :] = dkv[...].astype(BF)
        dproj_copy.start()
        back_copy(2).start()
        back_copy(3).start()
        local(3).wait()
        local(4).wait()
        per = 4 * shard

        def grad_rows(q, carry):
            rs = pl.ds(pl.multiple_of(q * per, 16), per)
            grad[rs, 0 : 3 * cols] = dot(nrm[rs, :], dproj[...], ((1,), (1,)))
            return carry

        lax.fori_loop(0, 4, grad_rows, 0)
        o_copy.wait()
        grad[:, 3 * cols : 4 * cols] += orecv[...].astype(F32)
        for side in range(2):
            for k in range(16):
                halves[side][0][block_position(k, orders[side]), 0:shard, :] = grad[
                    k * shard : (k + 1) * shard, 2 * side * cols : 2 * (side + 1) * cols
                ].astype(BF)
            hop(side, 0).start()
        hand_absorb(2, 5)

        def near_rows(r, carry):
            f3[:, lanes(r)] = dot(wn[...], dproj[:, lanes(r)], ((1,), (0,)))
            return carry

        lax.fori_loop(0, near_blocks, near_rows, 0)
        absorb(1, 0)
        absorb(0, 0)
        hand_hop(3, 1).start()
        hand_absorb(1, 6)
        ids = bid_ref[...]
        hot = ids == lax.broadcasted_iota(jnp.int32, (buckets, SPAN), 0)
        out_lane = lax.broadcasted_iota(jnp.int32, (buckets, 128), 1)
        sub = lax.broadcasted_iota(jnp.int32, (8, SPAN), 0)
        sv[0] = jnp.zeros(sv.shape[1:], F32)

        def bias_sums(hh, carry):
            line = jnp.zeros((8, SPAN), F32)
            for g in range(BLK // 8):
                group = slice(8 * g, 8 * g + 8)
                parts = [tally[hh, i, group, :] for i in (4, 3, 2, 1, 0)]
                strip = jnp.concatenate(parts + [jnp.zeros((8, BLK), F32)], axis=1)
                line = line + (strip if g == 0 else pltpu.roll(strip, SPAN - 8 * g, 1))
            for bit in (1, 2, 4):
                line = jnp.where((sub // bit) % 2 == 1, pltpu.roll(line, SPAN - bit, 1), line)
            sums = jnp.sum(line, axis=0, keepdims=True)
            col = jnp.sum(jnp.where(hot, sums, 0.0), axis=1, keepdims=True)
            sv[0, 0:buckets, :] = jnp.where(out_lane == x * heads + hh, col, sv[0, 0:buckets, :])
            return carry

        lax.fori_loop(0, heads, bias_sums, 0)
        product = wn[...].astype(F32) * grad[:, 0 : 3 * cols]
        again = lane_sum(product[:, 0:512]).T
        rest = product[:, 512 : 3 * cols]
        again = jnp.sum(again, axis=0, keepdims=True) + jnp.sum(rest.T, axis=0, keepdims=True)
        again = again / ag_ref[...]
        fgain = jnp.sum(fsum[...].T, axis=0, keepdims=True)
        lines = -(-d // 128)
        for i in range(lines):
            n = min(128, d - 128 * i)
            sv[0, buckets + i : buckets + i + 1, 0:n] = again[:, 128 * i : 128 * i + n]
            sv[0, buckets + lines + i : buckets + lines + i + 1, 0:n] = fgain[:, 128 * i : 128 * i + n]
        round_copy(0).start()
        hand_absorb(3, 4)
        round_end(0)
        absorb(1, 1)
        dproj_copy.wait()

        def last_norm(r, carry):
            ls = lanes(r)
            c = f3[:, ls] + dot(wf[...], dfar[:, ls], ((1,), (0,)))
            v = f2[:, ls]
            scale = norm_scale(v)
            n = v * scale
            cg = c * agc[...]
            m = jnp.mean(cg * n, axis=0, keepdims=True)
            f3[:, ls] = f1[:, ls] + scale * (cg - n * m)
            out_copy(r).start()
            return carry

        lax.fori_loop(0, near_blocks, last_norm, 0)
        absorb(0, 1)
        hand_absorb(3, 5)
        round_end(1)
        hand_absorb(2, 6)
        absorb(1, 2)
        round_end(2)
        absorb(0, 2)
        hand_absorb(3, 1)
        hand_absorb(3, 6)
        absorb(1, 3)
        round_end(3)
        absorb(0, 3)
        round_end(4)
        small_ref[...] = sv[5]
        for i in range(4):
            back_copy(i).wait()
        for r in range(near_blocks):
            out_copy(r).wait()


def tail(qkv, e, inv, wall, ctx, again, fgain, early, din, mid, cot, tok, nrm, wq, wfar, far,
         quarter, half_way, hand, buckets, heads, dk, extra, f):
    d, rows = tok.shape
    seq = 2 * rows
    cols = heads * dk
    blocks = seq // BLK
    near = blocks // 2
    shard = d // 16
    spad = -(-shard // 16) * 16
    deep = hand.shape[0]
    later = deep + len(LEVELS)
    lines = -(-(buckets + 2 * -(-d // 128)) // 8) * 8
    bids = jnp.asarray(lane_buckets(buckets))
    one = pl.Buffered(1)
    dma = pltpu.SemaphoreType.DMA
    any_spec = pl.BlockSpec(memory_space=pl.ANY)

    def full(v):
        return pl.BlockSpec(v.shape, lambda i: (0,) * len(v.shape), pipeline_mode=one)

    def chain(width):
        return [pltpu.VMEM((n, spad, width), BF) for n in (16, 8, 4, 2, 1)]

    outs = [
        jax.ShapeDtypeStruct((3, shard, cols), F32),
        jax.ShapeDtypeStruct((shard, cols), F32),
        jax.ShapeDtypeStruct((lines, 128), F32),
        jax.ShapeDtypeStruct((shard, f), F32),
        jax.ShapeDtypeStruct((shard, 2, f), F32),
    ]
    a_chain, b_chain = chain(2 * cols), chain(2 * cols)
    return pl.pallas_call(
        functools.partial(tail_kernel, heads, dk, buckets, blocks, extra),
        grid=(blocks,),
        in_specs=[
            full(bids),
            full(qkv),
            pl.BlockSpec((heads, 1, seq, BLK), lambda i: (0, i, 0, 0)),
            pl.BlockSpec((heads, 1, 1, BLK), lambda i: (0, i, 0, 0)),
            full(wall),
            full(ctx),
            full(again),
            full(fgain),
            full(early),
        ]
        + [any_spec] * 11,
        out_specs=[any_spec, any_spec] + [full(v) for v in outs],
        out_shape=[jax.ShapeDtypeStruct((d, rows), F32), jax.ShapeDtypeStruct((d, rows), BF)] + outs,
        scratch_shapes=[
            pltpu.VMEM((d, rows), F32),
            pltpu.VMEM((d, rows), F32),
            pltpu.VMEM((d, rows), F32),
            pltpu.VMEM((d, seq), BF),
            pltpu.VMEM((3 * cols, d), BF),
            pltpu.VMEM((d, 3 * cols), BF),
            pltpu.VMEM((d, 3 * cols), BF),
            pltpu.VMEM((d, rows), BF),
            pltpu.VMEM((cols, seq), BF),
            pltpu.VMEM((cols, rows), BF),
            pltpu.VMEM((d, cols), BF),
            pltpu.VMEM((d, cols), BF),
            pltpu.VMEM((d, 128), F32),
            pltpu.VMEM((d, 1), F32),
            pltpu.VMEM((d, 1), F32),
            pltpu.VMEM((seq, BLK), F32),
            pltpu.VMEM((2 * cols, seq), F32),
            pltpu.VMEM((heads, 5, BLK, BLK), F32),
            pltpu.VMEM((3 * cols, seq), BF),
            pltpu.VMEM((3 * cols, rows), BF),
            pltpu.VMEM((d, 4 * cols), F32),
            a_chain[0],
            b_chain[0],
        ]
        + a_chain[1:]
        + b_chain[1:]
        + [
            pltpu.VMEM((deep, 4, 3, spad, BLK), BF),
            pltpu.VMEM((2, 3, spad, BLK), BF),
            pltpu.VMEM((2, 1, 3, spad, BLK), BF),
            pltpu.VMEM((deep, 4, 3, spad, BLK), BF),
            pltpu.VMEM((deep + 1, 2, 3, spad, BLK), BF),
            pltpu.VMEM((later - 1, 1, 3, spad, BLK), BF),
            pltpu.VMEM((6, lines, 128), F32),
            pltpu.VMEM((5, lines, 128), F32),
            dma((7 + near,)),
            dma((later,)),
            dma((7,)), dma((7,)),
            dma((2, 4)), dma((2, 4)),
            dma((5,)), dma((5,)),
            dma((4, later)), dma((4, later)),
        ],
        compiler_params=pltpu.CompilerParams(
            vmem_limit_bytes=FF_VMEM, collective_id=1, has_side_effects=True
        ),
        cost_estimate=pl.CostEstimate(
            flops=32 * heads * seq * seq * dk + 8 * seq * d * 3 * cols,
            bytes_accessed=2 * heads * seq * seq + 30 * rows * d,
            transcendentals=0,
        ),
    )(bids, qkv, e, inv, wall, ctx, again, fgain, early, din, mid, cot, tok, nrm, wq, wfar, far,
      quarter, half_way, hand)


def outputs_kernel(near_ref, back_ref, ig_ref, ffi_ref, rel_ref, *refs):
    n = (len(refs) - 4) // 2
    refs, rel_out = refs[:-1], refs[-1]
    sources, res_ref, ig_out, ffi_out, targets = refs[:n], refs[n], refs[n + 1], refs[n + 2], refs[n + 3 :]
    res_ref[...] = near_ref[...] + back_ref[...].astype(F32)
    ig_out[...] = ig_ref[...]
    ffi_out[...] = ffi_ref[...]

    targets[-1][...] = sources[-1][...]

    @pl.when(pl.program_id(0) == 0)
    def _():
        for i in range(n - 1):
            targets[i][...] = sources[i][...]
        rel_out[...] = rel_ref[...].T[0 : rel_out.shape[0], 0 : rel_out.shape[1]]


def outputs(near, back, ig, ffi, small, rel_shape, *grads):
    d, rows = near.shape
    block = pl.BlockSpec((d // 2, rows), lambda i: (i, 0))
    shard, two, f = ffi.shape
    part = pl.BlockSpec((shard // 2, two, f), lambda i: (i, 0, 0))
    one = pl.Buffered(1)
    whole = [pl.BlockSpec(v.shape, lambda i, n=v.ndim: (0,) * n, pipeline_mode=one) for v in grads]
    whole[-1] = pl.BlockSpec((shard, f // 2), lambda i: (0, i))
    return pl.pallas_call(
        outputs_kernel,
        grid=(2,),
        in_specs=[block] * 3 + [part, pl.BlockSpec((rel_shape[1], 128), lambda i: (0, 0))] + whole,
        out_specs=[block] * 2 + [part] + whole + [pl.BlockSpec(rel_shape, lambda i: (0, 0))],
        out_shape=[jax.ShapeDtypeStruct(v.shape, F32) for v in (near, ig, ffi) + grads]
        + [jax.ShapeDtypeStruct(rel_shape, F32)],
        compiler_params=pltpu.CompilerParams(vmem_limit_bytes=FF_VMEM),
    )(near, back, ig, ffi, small, *grads)


def take(array, index):
    return lax.dynamic_index_in_dim(array, index, 0, keepdims=False)


def per_device(
    tokens,
    cotangent,
    doc_lengths,
    pad_mask,
    attn_gain,
    qkv_weight,
    rel_table,
    out_weight,
    ff_gain,
    ff_in_weight,
    ff_out_weight,
):
    rows, d = tokens.shape
    n_dp = lax.axis_size("dp")
    n_mp = lax.axis_size("mp")
    cols = qkv_weight.shape[2]
    buckets, heads = rel_table.shape
    dk = cols // heads
    me = lax.axis_index("dp")
    shard = d // n_dp
    extra = n_dp // 16

    def hop(v, mask):
        return lax.ppermute(v, "dp", [(i, i ^ mask) for i in range(n_dp)])

    def bit(b):
        return (me >> b) & 1

    def finish(g):
        parts = [g.reshape((extra, shard) + g.shape[1:])]
        for b in reversed(range(extra.bit_length() - 1)):
            halves = [p.reshape((2, p.shape[0] // 2) + p.shape[1:]) for p in parts]
            away = sum(take(p, 1 - bit(b)).astype(F32) for p in halves).astype(BF)
            parts = [take(p, bit(b)) for p in halves] + [hop(away, 1 << b)]
        return sum(p.astype(F32) for p in parts)[0]

    tok = tokens.T
    cot = cotangent.T
    far = lax.ppermute(tok.astype(BF), "mp", [(0, 1), (1, 0)])
    w2 = jnp.transpose(ff_in_weight, (1, 0, 2))
    wq = jnp.transpose(qkv_weight, (1, 2, 0)).reshape(3 * cols, d)
    again, fgain = attn_gain.reshape(1, d), ff_gain.reshape(1, d)

    e, inv, qkv, ctx, nrm, xt, mid, ct, wall = front(
        rel_table, doc_lengths, pad_mask, again, fgain, wq, out_weight.T, tok, far, cot, heads, dk
    )
    early, din, near_out, far_out, quarter, half_way, hand, wfar = ff_all(
        xt, ct, w2, ff_out_weight, mid, wq, extra
    )
    input_grad, back, grad_qkv, grad_out, small, ffo, ffi = tail(
        qkv, e, inv, wall, ctx, again, fgain, early, din, mid, cot, tok, nrm, wq, wfar, far_out,
        quarter, half_way, hand, buckets, heads, dk, extra, ff_out_weight.shape[1],
    )
    for b in range(extra.bit_length() - 1):
        small = small + hop(small, 1 << b)
    result, input_grad, ffi, grad_qkv, grad_out, ffo, rel_grad = outputs(
        near_out, back, input_grad, ffi, small, (heads * n_mp, buckets), grad_qkv, grad_out, ffo
    )
    grad_qkv = jnp.transpose(grad_qkv, (1, 0, 2))
    if extra > 1:
        grad_qkv, grad_out, ffo, ffi = (finish(g) for g in (grad_qkv, grad_out, ffo, ffi))
    lines = -(-d // 128)
    return (
        result.T,
        input_grad.T,
        small[buckets : buckets + lines].reshape(-1)[:d],
        grad_qkv,
        rel_grad.T,
        grad_out,
        small[buckets + lines : buckets + 2 * lines].reshape(-1)[:d],
        ffi,
        ffo,
    )


def solution(mesh):
    return jax.shard_map(
        per_device,
        mesh=mesh,
        in_specs=(
            P(("dp", "mp"), None),
            P(("dp", "mp"), None),
            P("dp", None),
            P("dp", None),
            P(),
            P(None, None, "mp"),
            P(None, "mp"),
            P(None, "mp"),
            P(),
            P(None, None, "mp"),
            P(None, "mp"),
        ),
        out_specs=(
            P(("dp", "mp"), None),
            P(("dp", "mp"), None),
            P(),
            P("dp", None, "mp"),
            P(),
            P("dp", "mp"),
            P(),
            P("dp", None, "mp"),
            P("dp", "mp"),
        ),
        check_vma=False,
    )
```
